32 devices in a mesh: seq: 2 (over core), batch: 16 (over z, y, x).
Axes of the slice: x: 2, y: 2, z: 4, core: 2. Of those that a mesh axis runs over, the one named last changes fastest.
Arguments:
- first_layer_input: bfloat16 [48, 512, 768], P('batch', 'seq'), may hold values from -6 to 6
- output_gradient: bfloat16 [48, 512, 768], P('batch', 'seq'), may hold values from -6 to 6
- sentence_pair_index: int32 [48, 512], P('batch', 'seq'), may hold values from 0 to 15, never falling along the last dimension, each value on 1 to 96 neighbouring positions
- sequence_live_length: int32 [48], P('batch'), may hold values from 256 to 512, as said below
- optimizer_step_count: int32 [2, 2, 2], replicated, may hold values from 1 to 4
- query_key_value_weight: bfloat16 [2, 768, 2304], replicated, may hold values from -0.21875 to 0.21875
- attention_output_weight: bfloat16 [2, 768, 768], replicated, may hold values from -0.4375 to 0.4375
- feedforward_up_weight: bfloat16 [2, 768, 3072], replicated, may hold values from -0.21875 to 0.21875
- feedforward_down_weight: bfloat16 [2, 3072, 768], replicated, may hold values from -0.109375 to 0.109375
- layer_bias_gain_rows: bfloat16 [2, 8, 768], replicated, may hold values from -1.5 to 1.5, as said below
- feedforward_up_bias: bfloat16 [2, 3072], replicated, may hold values from -3 to 3
- adapter_down_factors: float32 [2, 2, 8, 768], replicated, may hold values from -0.21875 to 0.21875
- adapter_up_factors: float32 [2, 2, 768, 8], replicated, may hold values from -1 to 1
- first_moment_down: float32 [2, 2, 8, 768], replicated, may hold values from -0.046875 to 0.046875
- second_moment_down: float32 [2, 2, 8, 768], replicated, may hold values from 8.138021e-07 to 2.0345053e-05
- first_moment_up: float32 [2, 2, 768, 8], replicated, may hold values from -0.046875 to 0.046875
- second_moment_up: float32 [2, 2, 768, 8], replicated, may hold values from 8.138021e-07 to 2.0345053e-05
Outputs:
- hidden_out: bfloat16 [48, 512, 768], P('batch', 'seq')
- grad_in: float32 [48, 512, 768], P('batch', 'seq')
- updated_down_factors: float32 [2, 2, 8, 768], replicated
- updated_up_factors: float32 [2, 2, 768, 8], replicated
- updated_first_moment_down: float32 [2, 2, 8, 768], replicated
- updated_second_moment_down: float32 [2, 2, 8, 768], replicated
- updated_first_moment_up: float32 [2, 2, 768, 8], replicated
- updated_second_moment_up: float32 [2, 2, 768, 8], replicated
The draws below stay inside these ranges and needn't reach their ends.
Inputs may be any that keep to these rules, and one draw needn't show every extreme that they name: `sentence_pair_index`: ids never fall along a sequence; each sentence pair covers at most 96 positions. `sequence_live_length`: every sequence has 256 live positions or more, and some sequence has all 512. `layer_bias_gain_rows`: rows 4 and 6 lie between 0.55 and 1.45.
All inputs are finite; a program needn't handle non-finite values.
Results may differ from the reference program's by a relative error of at most 0.04.
Values may be sent and summed in bfloat16 or wider, within the bound.
No kernel may reach another device: no remote copies, remote signals or barrier semaphores. Data moves between devices by JAX's collectives and lax.ppermute only.
A program may use at most 256 MiB of HBM per device.

```python
import math
import jax
import jax.numpy as jnp
import numpy as np
from jax import lax

MODEL_DIMENSION = 768
HEADS = 12
HDIM = 64
FF = 3072
ADAPTER_RANK = 8
ENCODER_LAYERS = 2
LEN = 512
DOCS = 16
DOC_MOST = 96
SEQS = 3
SEQUENCES = 48
TOKEN_SLOTS_ALL = 24576


def draw_sequence_live_length(key, part):
    lengths = jax.random.randint(key, (SEQUENCES,), LEN // 2, LEN + 1, dtype=jnp.int32)
    return lengths.at[0].set(LEN).at[1].set(LEN // 2)


def draw_layer_bias_gain_rows(key, part):
    first_key, second_key = jax.random.split(jax.random.fold_in(key, 11))
    rows = jnp.arange(8, dtype=jnp.int32)[None, :, None]
    gain_rows = (rows == 4) | (rows == 6)
    base = 0.5 * jnp.clip(jax.random.normal(first_key, (ENCODER_LAYERS, 8, MODEL_DIMENSION), jnp.float32), -3.0, 3.0)
    spread = 0.15 * jnp.clip(jax.random.normal(second_key, (ENCODER_LAYERS, 8, MODEL_DIMENSION), jnp.float32), -3.0, 3.0)
    return jnp.where(gain_rows, 1.0 + spread, base).astype(jnp.bfloat16)


def plant(drawn, key, smallest, largest):
    dims = drawn.shape
    spot = [jax.random.randint(jax.random.fold_in(key, axis), (), 0, dims[axis]) for axis in range(len(dims))]
    drawn = drawn.at[tuple(spot)].set(smallest)
    longest = dims.index(max(dims))
    spot[longest] = (spot[longest] + 1) % dims[longest]
    return drawn.at[tuple(spot)].set(largest)


def steps_of(rng, shape, shards, least, high):
    level = 1.0
    for position, blocks in shards:
        steps = jax.random.uniform(jax.random.fold_in(jax.random.fold_in(rng, 6), position), (blocks,), jnp.float32, least / len(shards), high / len(shards))
        level = level * jnp.repeat(jnp.exp(steps), shape[position] // blocks).reshape((-1,) + (1,) * (len(shape) - 1 - position))
    return level


def profile(amount, total, bound, skew):
    weights = [(1 << 20) // math.isqrt(standing ** skew) + 1 for standing in range(2, amount + 1)]
    surplus, given = total - bound - (amount - 1), [1] * (amount - 1)
    while surplus > 0:
        movable = [i for i in range(amount - 1) if given[i] < bound]
        pool, remaining = sum([weights[i] for i in movable]), surplus
        for i in movable:
            extra = min(bound - given[i], max(1, remaining * weights[i] // pool), surplus)
            given[i] = given[i] + extra
            surplus = surplus - extra
    return np.array([bound] + given)


def uneven(key, amount, total, limit, skew):
    if amount == 2:
        one = jax.random.randint(key, (), max(1, total - limit), min(limit, total - 1) + 1)
        return jnp.stack([one, total - one])
    sizes = jnp.asarray(profile(amount, total, limit, skew), jnp.int32)
    pairs = (amount - 1) // 2
    donor, taker = sizes[1:1 + 2 * pairs:2], sizes[2:2 + 2 * pairs:2]
    slack = jnp.minimum(donor - 1, limit - taker)
    passed = jax.random.randint(jax.random.fold_in(key, 1), (pairs,), 0, 1 << 20) % (slack + 1)
    sizes = sizes.at[1:1 + 2 * pairs:2].set(donor - passed).at[2:2 + 2 * pairs:2].set(taker + passed)
    return sizes[jax.random.permutation(jax.random.fold_in(key, 2), amount)]


def normal_values(key, dims, deviation, limit, cuts=(), kind=jnp.bfloat16):
    factor_of = steps_of(key, dims, cuts, -0.22, 0.18) if cuts else 1.0
    drawn = jax.random.normal(key, dims, jnp.float32) * deviation * factor_of
    return jnp.minimum(jnp.maximum(drawn, -limit), limit).astype(kind)


def setup_inputs(seed: int = 0) -> dict:
    key_list = jax.random.split(jax.random.key(seed), 18)
    return {
        "first_layer_input": normal_values(key_list[0], (SEQUENCES, LEN, MODEL_DIMENSION), 1.0, 6.0, ((0, 16), (1, 2))),
        "output_gradient": normal_values(key_list[1], (SEQUENCES, LEN, MODEL_DIMENSION), 1.0, 6.0, ((0, 16), (1, 2))),
        "sentence_pair_index": jax.vmap(lambda own: jnp.searchsorted(jnp.cumsum(uneven(own, DOCS, LEN, DOC_MOST, 1)), jnp.arange(LEN), side="right"))(jax.random.split(key_list[2], SEQUENCES)).reshape((SEQUENCES, LEN)).astype(jnp.int32),
        "sequence_live_length": draw_sequence_live_length(jax.random.fold_in(key_list[17], 71), 0),
        "optimizer_step_count": plant(jax.random.randint(key_list[4], (ENCODER_LAYERS, 2, 2), 1, 5), jax.random.fold_in(key_list[4], 1), 1, 4).astype(jnp.int32),
        "query_key_value_weight": normal_values(key_list[5], (ENCODER_LAYERS, MODEL_DIMENSION, 3 * MODEL_DIMENSION), MODEL_DIMENSION ** -0.5, 0.21875),
        "attention_output_weight": normal_values(key_list[6], (ENCODER_LAYERS, MODEL_DIMENSION, MODEL_DIMENSION), (MODEL_DIMENSION // 4) ** -0.5, 0.4375),
        "feedforward_up_weight": normal_values(key_list[7], (ENCODER_LAYERS, MODEL_DIMENSION, FF), MODEL_DIMENSION ** -0.5, 0.21875),
        "feedforward_down_weight": normal_values(key_list[8], (ENCODER_LAYERS, FF, MODEL_DIMENSION), FF ** -0.5, 0.109375),
        "layer_bias_gain_rows": draw_layer_bias_gain_rows(jax.random.fold_in(key_list[17], 71), 0),
        "feedforward_up_bias": normal_values(key_list[10], (ENCODER_LAYERS, FF), 0.5, 3.0),
        "adapter_down_factors": normal_values(key_list[11], (ENCODER_LAYERS, 2, ADAPTER_RANK, MODEL_DIMENSION), MODEL_DIMENSION ** -0.5, 0.21875, (), jnp.float32),
        "adapter_up_factors": normal_values(key_list[12], (ENCODER_LAYERS, 2, MODEL_DIMENSION, ADAPTER_RANK), (4 * ADAPTER_RANK) ** -0.5, 1.0, (), jnp.float32),
        "first_moment_down": normal_values(key_list[13], (ENCODER_LAYERS, 2, ADAPTER_RANK, MODEL_DIMENSION), (0.5 / TOKEN_SLOTS_ALL ** 0.5), 0.046875, (), jnp.float32),
        "second_moment_down": jnp.clip(jnp.exp(jax.random.uniform(key_list[14], (ENCODER_LAYERS, 2, ADAPTER_RANK, MODEL_DIMENSION), jnp.float32, math.log(8.138021030390519e-07), math.log(2.0345052689663135e-05))), 8.138021030390519e-07, 2.0345052689663135e-05),
        "first_moment_up": normal_values(key_list[15], (ENCODER_LAYERS, 2, MODEL_DIMENSION, ADAPTER_RANK), (0.5 / TOKEN_SLOTS_ALL ** 0.5), 0.046875, (), jnp.float32),
        "second_moment_up": jnp.clip(jnp.exp(jax.random.uniform(key_list[16], (ENCODER_LAYERS, 2, MODEL_DIMENSION, ADAPTER_RANK), jnp.float32, math.log(8.138021030390519e-07), math.log(2.0345052689663135e-05))), 8.138021030390519e-07, 2.0345052689663135e-05),
    }


@jax.custom_vjp
def low(v):
    return lax.optimization_barrier(v.astype(jnp.bfloat16)).astype(jnp.float32)

@jax.custom_vjp
def low_back(v):
    return v

def low_keep(v):
    return (low(v), None)

def low_pass(kept, grad):
    return (grad,)

def back_keep(v):
    return (v, None)

def back_low(kept, grad):
    return (low(grad),)
low.defvjp(low_keep, low_pass)
low_back.defvjp(back_keep, back_low)

def product(left_side, right_side):
    return jnp.einsum('...d,df->...f', left_side, right_side, precision=lax.Precision.HIGHEST)

def normalize(values, gain_row, shift_row):
    center = values - lax.optimization_barrier(jnp.mean(values, axis=-1, keepdims=True))
    spread = lax.optimization_barrier(jnp.mean(center * center, axis=-1, keepdims=True))
    return center * lax.rsqrt(spread + 1e-05) * gain_row + shift_row

def encoder_layer(current, factor_a, factor_b, allowed, weights_qkv, weights_out, weights_up, weights_down, vectors, bias_up):
    rows_count = current.shape[0]
    layer_in = low(current)
    query_down = low(factor_a[0])
    value_down = low(factor_a[1])
    query_up = low(factor_b[0])
    value_up = low(factor_b[1])
    joined = product(layer_in, weights_qkv)
    inner_query = low(low_back(product(layer_in, query_down.T)))
    inner_value = low(low_back(product(layer_in, value_down.T)))
    queries = low(low_back(joined[..., :MODEL_DIMENSION] + vectors[0] + 2.0 * product(inner_query, query_up.T)))
    key_rows = low(low_back(joined[..., MODEL_DIMENSION:2 * MODEL_DIMENSION]))
    values = low(low_back(joined[..., 2 * MODEL_DIMENSION:] + vectors[1] + 2.0 * product(inner_value, value_up.T)))
    query_heads = queries.reshape(rows_count, LEN, HEADS, HDIM)
    key_heads = key_rows.reshape(rows_count, LEN, HEADS, HDIM)
    value_heads = values.reshape(rows_count, LEN, HEADS, HDIM)
    scores = jnp.einsum('gqhe,gkhe->ghqk', query_heads, key_heads, precision=lax.Precision.HIGHEST)
    scores = low_back(scores * (1.0 / math.sqrt(HDIM)))
    scores = jnp.where(allowed, scores, -1000000000.0)
    weights = low(jax.nn.softmax(scores, axis=-1))
    mixture = jnp.einsum('ghqk,gkhe->gqhe', weights, value_heads, precision=lax.Precision.HIGHEST)
    mixture = low(low_back(mixture.reshape(rows_count, LEN, MODEL_DIMENSION)))
    attended = low_back(product(mixture, weights_out)) + vectors[2] + current
    normed_one = normalize(attended, vectors[4], vectors[5])
    gate_in = low_back(product(low(normed_one), weights_up) + bias_up)
    active = low(jax.nn.gelu(gate_in, approximate=False))
    summed_two = low_back(product(active, weights_down)) + vectors[3] + normed_one
    return normalize(summed_two, vectors[6], vectors[7])

def adamw_step_update(weight, gradient, moment, velocity, bias_correction, learn_rate, decay_rate):
    moment = 0.5 * moment + 0.5 * gradient
    velocity = 0.5 * velocity + 0.5 * gradient * gradient
    step_size = moment / bias_correction / (jnp.sqrt(velocity / bias_correction) + 1e-08)
    return (weight - learn_rate * (step_size + decay_rate * weight), moment, velocity)

def reference(first_layer_input, output_gradient, sentence_pair_index, sequence_live_length, optimizer_step_count, query_key_value_weight, attention_output_weight, feedforward_up_weight, feedforward_down_weight, layer_bias_gain_rows, feedforward_up_bias, adapter_down_factors, adapter_up_factors, first_moment_down, second_moment_down, first_moment_up, second_moment_up):
    weights_qkv = query_key_value_weight.astype(jnp.float32)
    weights_out = attention_output_weight.astype(jnp.float32)
    weights_up = feedforward_up_weight.astype(jnp.float32)
    weights_down = feedforward_down_weight.astype(jnp.float32)
    vectors = layer_bias_gain_rows.astype(jnp.float32)
    bias_up = feedforward_up_bias.astype(jnp.float32)
    positions = jnp.arange(LEN, dtype=jnp.int32)
    itself = positions[:, None] == positions[None, :]

    def one_group(running, batch_rows):
        down_gradient_total, up_gradient_total = running
        hidden_state, cotangent, doc_rows, lengths = batch_rows
        same_doc = doc_rows[:, :, None] == doc_rows[:, None, :]
        visible = (positions[None, None, :] < lengths[:, None, None]) | itself[None]
        allowed = (same_doc & visible)[:, None]
        live_rows = (positions[None, :] < lengths[:, None]).astype(jnp.float32)[:, :, None]

        def forward_encoder(current, factors_a, factors_b):
            for layer_number in range(ENCODER_LAYERS):
                current = encoder_layer(current, factors_a[layer_number], factors_b[layer_number], allowed, weights_qkv[layer_number], weights_out[layer_number], weights_up[layer_number], weights_down[layer_number], vectors[layer_number], bias_up[layer_number])
            return current
        final_output, backward_function = jax.vjp(forward_encoder, hidden_state.astype(jnp.float32), adapter_down_factors, adapter_up_factors)
        input_grad, grad_a, grad_b = backward_function(cotangent.astype(jnp.float32) * live_rows)
        return ((down_gradient_total + grad_a, up_gradient_total + grad_b), (final_output.astype(jnp.bfloat16), input_grad))
    groups = SEQUENCES // SEQS
    inputs = (first_layer_input.reshape(groups, SEQS, LEN, MODEL_DIMENSION), output_gradient.reshape(groups, SEQS, LEN, MODEL_DIMENSION), sentence_pair_index.reshape(groups, SEQS, LEN), sequence_live_length.reshape(groups, SEQS))
    initial_state = (jnp.zeros_like(adapter_down_factors), jnp.zeros_like(adapter_up_factors))
    (down_gradient_total, up_gradient_total), (outputs, in_grads) = lax.scan(one_group, initial_state, inputs)
    corrections = 1.0 - jnp.power(0.5, optimizer_step_count.astype(jnp.float32))
    correction_down = corrections[:, :, 0][:, :, None, None]
    correction_up = corrections[:, :, 1][:, :, None, None]
    updated_down_factors, updated_first_moment_down, updated_second_moment_down = adamw_step_update(adapter_down_factors, down_gradient_total / TOKEN_SLOTS_ALL, first_moment_down, second_moment_down, correction_down, 0.03125, 0.1)
    updated_up_factors, updated_first_moment_up, updated_second_moment_up = adamw_step_update(adapter_up_factors, up_gradient_total / TOKEN_SLOTS_ALL, first_moment_up, second_moment_up, correction_up, 0.5, 0.0)
    return (outputs.reshape(SEQUENCES, LEN, MODEL_DIMENSION), in_grads.reshape(SEQUENCES, LEN, MODEL_DIMENSION), updated_down_factors, updated_up_factors, updated_first_moment_down, updated_second_moment_down, updated_first_moment_up, updated_second_moment_up)
```

```python
import jax
import jax.numpy as jnp
from jax import lax
from jax.experimental import pallas as pl
from jax.experimental.pallas import tpu as pltpu
from jax.sharding import PartitionSpec as P

HEADS = 12
ENCODER_LAYERS = 2
HALO = 96
BLOCK = 128
MASKED = -1000000000.0
F32 = jnp.float32
BF16 = jnp.bfloat16
VMEM_LIMIT = 63 * 1024 * 1024


def dot_nn(a, b):
    return lax.dot_general(a, b, (((1,), (0,)), ((), ())), preferred_element_type=F32)


def dot_nt(a, b):
    return lax.dot_general(a, b, (((1,), (1,)), ((), ())), preferred_element_type=F32)


def dot_tn(a, b):
    return lax.dot_general(a, b, (((0,), (0,)), ((), ())), preferred_element_type=F32)


def rows_at(start, size, multiple):
    return pl.ds(pl.multiple_of(start, multiple), size)


def start_copies(pairs, sems):
    copies = [pltpu.make_async_copy(src, dst, sems.at[i]) for i, (src, dst) in enumerate(pairs)]
    for copy in copies:
        copy.start()
    return copies


def column_of(row):
    n = row.shape[1]
    eye = lax.broadcasted_iota(jnp.int32, (n, n), 0) == lax.broadcasted_iota(jnp.int32, (n, n), 1)
    return jnp.sum(jnp.where(eye, row, 0.0), axis=1, keepdims=True)


def key_rows_of(s, side, length, ids_ref, halo_ids_ref, live_ref):
    live = live_ref[s]
    own = ids_ref[pl.ds(s, 1), :].astype(F32)
    places = lax.broadcasted_iota(jnp.int32, (1, length), 1) + side * length
    own = jnp.where(places < live, own, -1.0)
    if halo_ids_ref is None:
        return own, None
    halo = halo_ids_ref[pl.ds(s, 1), :].astype(F32)
    places = lax.broadcasted_iota(jnp.int32, (1, HALO), 1) + jnp.where(
        side == 0, length, length - HALO
    )
    halo = jnp.where(places < live, halo, -1.0)
    return own, halo


def query_row_of(s, row0, ids_ref):
    row = ids_ref[pl.ds(s, 1), :].astype(F32)
    return jnp.where(row0 == 0, row[:, :BLOCK], row[:, BLOCK:])


def stack_heads(tile, first):
    zero = jnp.zeros_like(tile)
    return jnp.concatenate([jnp.where(first, tile, zero), jnp.where(first, zero, tile)], axis=0)


def attention_forward(near, side, sequences, length, q_ref, k_ref, v_ref, halo_ref, ids_ref,
                      halo_ids_ref, live_ref, out_ref, out_row):
    width = q_ref.shape[1]
    first = lax.broadcasted_iota(jnp.int32, (BLOCK, 2 * 64), 1) < 64
    row0 = pl.multiple_of(BLOCK * ((1 - side) if near else side), BLOCK)

    def one(s, carry):
        own_ids, halo_ids = key_rows_of(s, side, length, ids_ref, halo_ids_ref, live_ref)
        query_ids = column_of(query_row_of(s, row0, ids_ref))
        itself = (lax.broadcasted_iota(jnp.int32, (BLOCK, length), 0) + row0
                  == lax.broadcasted_iota(jnp.int32, (BLOCK, length), 1))
        bias = jnp.where((query_ids == own_ids) | itself, 0.0, MASKED)
        bias = jnp.concatenate([bias, bias], axis=0)
        if near:
            bias_h = jnp.where(query_ids == halo_ids, 0.0, MASKED)
            bias_h = jnp.concatenate([bias_h, bias_h], axis=0)
        rows = rows_at(s * length + row0, BLOCK, BLOCK)
        keys = rows_at(s * length, length, BLOCK)
        hrows = rows_at(s * HALO, HALO, 32)
        outs = rows_at(out_row(s), BLOCK, BLOCK)
        for pair in range(width // 128):
            cols = slice(128 * pair, 128 * pair + 128)
            q2 = stack_heads(q_ref[rows, cols], first)
            s1 = dot_nt(q2, k_ref[keys, cols]) + bias
            top = jnp.max(s1, axis=1, keepdims=True)
            if near:
                s2 = dot_nt(q2, halo_ref[0, hrows, cols]) + bias_h
                top = jnp.maximum(top, jnp.max(s2, axis=1, keepdims=True))
            e1 = jnp.exp(s1 - top)
            total = jnp.sum(e1, axis=1, keepdims=True)
            o = dot_nn(e1.astype(BF16), v_ref[keys, cols])
            if near:
                e2 = jnp.exp(s2 - top)
                total = total + jnp.sum(e2, axis=1, keepdims=True)
                o = o + dot_nn(e2.astype(BF16), halo_ref[1, hrows, cols])
            o = o / total
            out_ref[outs, cols] = jnp.where(first, o[:BLOCK], o[BLOCK:]).astype(BF16)
        return carry

    lax.fori_loop(0, sequences, one, 0)


def attention_backward(near, side, sequences, length, q_ref, k_ref, v_ref, halo_ref, dmix_ref,
                       ids_ref, halo_ids_ref, live_ref, dq_ref, dk_ref, dv_ref, dhalo_ref,
                       dkn_ref=None, dvn_ref=None, dmix_row=None, dq_row=None):
    width = q_ref.shape[1]
    first = lax.broadcasted_iota(jnp.int32, (BLOCK, 2 * 64), 1) < 64
    row0 = pl.multiple_of(BLOCK * ((1 - side) if near else side), BLOCK)

    def one(s, carry):
        own_ids, halo_ids = key_rows_of(s, side, length, ids_ref, halo_ids_ref, live_ref)
        query_ids = query_row_of(s, row0, ids_ref)
        own_col = jnp.concatenate(
            [column_of(own_ids[:, i:i + BLOCK]) for i in range(0, length, BLOCK)], axis=0)
        itself = (lax.broadcasted_iota(jnp.int32, (length, BLOCK), 1) + row0
                  == lax.broadcasted_iota(jnp.int32, (length, BLOCK), 0))
        bias = jnp.where((own_col == query_ids) | itself, 0.0, MASKED)
        bias = jnp.concatenate([bias, bias], axis=1)
        if near:
            bias_h = jnp.where(column_of(halo_ids) == query_ids, 0.0, MASKED)
            bias_h = jnp.concatenate([bias_h, bias_h], axis=1)
        rows = rows_at(s * length + row0, BLOCK, BLOCK)
        keys = rows_at(s * length, length, BLOCK)
        hrows = rows_at(s * HALO, HALO, 32)
        mrows = rows if dmix_row is None else rows_at(dmix_row(s), BLOCK, BLOCK)
        qrows = rows if dq_row is None else rows_at(dq_row(s), BLOCK, BLOCK)
        for pair in range(width // 128):
            cols = slice(128 * pair, 128 * pair + 128)
            q2 = stack_heads(q_ref[rows, cols], first)
            d2 = stack_heads(dmix_ref[mrows, cols], first)
            kt, vt = k_ref[keys, cols], v_ref[keys, cols]
            s1 = dot_nt(kt, q2) + bias
            top = jnp.max(s1, axis=0, keepdims=True)
            if near:
                kh, vh = halo_ref[0, hrows, cols], halo_ref[1, hrows, cols]
                s2 = dot_nt(kh, q2) + bias_h
                top = jnp.maximum(top, jnp.max(s2, axis=0, keepdims=True))
            p1 = jnp.exp(s1 - top)
            total = jnp.sum(p1, axis=0, keepdims=True)
            if near:
                p2 = jnp.exp(s2 - top)
                total = total + jnp.sum(p2, axis=0, keepdims=True)
            share = 1.0 / total
            p1 = p1 * share
            g1 = dot_nt(vt, d2)
            delta = jnp.sum(p1 * g1, axis=0, keepdims=True)
            if near:
                p2 = p2 * share
                g2 = dot_nt(vh, d2)
                delta = delta + jnp.sum(p2 * g2, axis=0, keepdims=True)
            ds1 = (p1 * (g1 - delta)).astype(BF16)
            dv = dot_nn(p1.astype(BF16), d2)
            dk = dot_nn(ds1, q2)
            if dkn_ref is not None:
                dv = dv + dvn_ref[keys, cols]
                dk = dk + dkn_ref[keys, cols]
            dv_ref[keys, cols] = dv.astype(dv_ref.dtype)
            dk_ref[keys, cols] = dk.astype(dk_ref.dtype)
            dq = dot_tn(ds1, kt)
            if near:
                ds2 = (p2 * (g2 - delta)).astype(BF16)
                dhalo_ref[1, hrows, cols] = dot_nn(p2.astype(BF16), d2).astype(BF16)
                dhalo_ref[0, hrows, cols] = dot_nn(ds2, q2).astype(BF16)
                dq = dq + dot_tn(ds2, kh)
            dq = jnp.where(first, dq[:BLOCK], dq[BLOCK:]) * 0.125
            dq_ref[qrows, cols] = dq.astype(BF16)
        return carry

    lax.fori_loop(0, sequences, one, 0)


def norm_forward(values, gain, shift):
    center = values - jnp.mean(values, axis=1, keepdims=True)
    spread = jnp.mean(center * center, axis=1, keepdims=True)
    inverse = lax.rsqrt(spread + 1e-05)
    scaled = center * inverse
    return scaled * gain + shift, scaled, inverse


def norm_backward(gradient, scaled, inverse, gain):
    inner = gradient * gain
    return inverse * (
        inner
        - jnp.mean(inner, axis=1, keepdims=True)
        - scaled * jnp.mean(inner * scaled, axis=1, keepdims=True)
    )


def low_rank(a_ref, b_ref):
    down = jnp.concatenate([a_ref[0], a_ref[1]], axis=0).astype(BF16)
    zero = jnp.zeros_like(b_ref[0])
    up_q = jnp.concatenate([b_ref[0], zero], axis=0).astype(BF16)
    up_v = jnp.concatenate([zero, b_ref[1]], axis=0).astype(BF16)
    return down, up_q, up_v


def project_in(layer, side, sequences, length, x_ref, w_ref, wait, a_ref, b_ref, vec_ref, q_ref, k_ref,
               v_ref, u_ref, send_ref):
    width = x_ref.shape[1]
    down, up_q, up_v = low_rank(a_ref.at[layer], b_ref.at[layer])
    vec = vec_ref[layer].astype(F32)
    bias_q, bias_v = vec[0:1], vec[1:2]
    wait()
    for s in range(sequences):
        rows = slice(s * length, (s + 1) * length)
        x = x_ref[rows, :]
        inner = dot_nt(x, down).astype(BF16)
        u_ref[rows, :] = inner
        q = dot_nn(x, w_ref[:, :width]) + bias_q + 2.0 * dot_nn(inner, up_q)
        q_ref[rows, :] = q.astype(BF16) * jnp.asarray(0.125, BF16)
        k_ref[rows, :] = dot_nn(x, w_ref[:, width:2 * width]).astype(BF16)
        v = dot_nn(x, w_ref[:, 2 * width:]) + bias_v + 2.0 * dot_nn(inner, up_v)
        v_ref[rows, :] = v.astype(BF16)
    for s in range(sequences):
        taken = rows_at(s * length + (1 - side) * (length - HALO), HALO, 32)
        send_ref[0, s * HALO:(s + 1) * HALO, :] = k_ref[taken, :]
        send_ref[1, s * HALO:(s + 1) * HALO, :] = v_ref[taken, :]


def any_spec():
    return pl.BlockSpec(memory_space=pl.ANY)


def vmem_spec():
    return pl.BlockSpec(memory_space=pltpu.VMEM)


def smem_spec():
    return pl.BlockSpec(memory_space=pltpu.SMEM)


def call(kernel, name, outs, in_specs, scratch, flops, nbytes):
    return pl.pallas_call(
        kernel,
        name=name,
        out_shape=outs,
        in_specs=in_specs,
        out_specs=jax.tree.map(lambda _: vmem_spec(), outs),
        scratch_shapes=scratch,
        compiler_params=pltpu.CompilerParams(vmem_limit_bytes=VMEM_LIMIT),
        cost_estimate=pl.CostEstimate(flops=flops, bytes_accessed=nbytes, transcendentals=0),
    )


def sds(shape, dtype):
    return jax.ShapeDtypeStruct(shape, dtype)


def qkv_call(layer, sequences, length, x, w, a, b, vec):
    tokens, width = x.shape
    rank = a.shape[2]

    def kernel(x_ref, w_hbm, a_ref, b_ref, vec_ref, q_ref, k_ref, v_ref, u_ref, send_ref, w_ref,
               sems):
        side = lax.axis_index("seq")
        copies = start_copies([(w_hbm.at[layer], w_ref)], sems)
        project_in(layer, side, sequences, length, x_ref, w_ref, copies[0].wait, a_ref, b_ref, vec_ref,
                   q_ref, k_ref, v_ref, u_ref, send_ref)

    act = sds((tokens, width), BF16)
    return call(
        kernel, "qkv_forward",
        (act, act, act, sds((tokens, 2 * rank), BF16), sds((2, sequences * HALO, width), BF16)),
        [vmem_spec(), any_spec(), vmem_spec(),
         vmem_spec(), vmem_spec()],
        [pltpu.VMEM((width, 3 * width), BF16), pltpu.SemaphoreType.DMA((1,))],
        2 * tokens * width * width * 3, 12000000,
    )(x, w, a, b, vec)


def far_call(sequences, length, q, k, v, ids, live):
    tokens, width = q.shape

    def kernel(q_ref, k_ref, v_ref, ids_ref, live_ref, out_ref):
        side = lax.axis_index("seq")
        attention_forward(False, side, sequences, length, q_ref, k_ref, v_ref, None, ids_ref,
                          None, live_ref, out_ref, lambda s: s * BLOCK)

    return call(
        kernel, "attention_far", sds((sequences * BLOCK, width), BF16),
        [vmem_spec()] * 4 + [smem_spec()], [], 2000000000, 6000000,
    )(q, k, v, ids, live)


def near_post_call(layer, sequences, length, far, q, k, v, halo, ids, halo_ids, live, h, wo, wu,
                   wd, vec, bias_up):
    tokens, width = q.shape
    hidden = wu.shape[2]
    last = layer == ENCODER_LAYERS - 1

    def kernel(far_ref, q_ref, k_ref, v_ref, halo_ref, ids_ref, halo_ids_ref, live_ref, h_ref,
               wo_hbm, wu_hbm, wd_hbm, vec_ref, bu_ref, n1_ref, r1_ref, dg_ref, n2_ref, r2_ref,
               *rest):
        h_outs, (wo_ref, wu_ref, wd_ref, mix_ref, one_ref, low_ref, act_ref, sems) = (
            rest[:-8], rest[-8:])
        side = lax.axis_index("seq")
        copies = start_copies(
            [(wo_hbm.at[layer], wo_ref), (wu_hbm.at[layer], wu_ref), (wd_hbm.at[layer], wd_ref)],
            sems)
        attention_forward(True, side, sequences, length, q_ref, k_ref, v_ref, halo_ref, ids_ref,
                          halo_ids_ref, live_ref, mix_ref,
                          lambda s: s * length + (1 - side) * BLOCK)
        for s in range(sequences):
            mix_ref[rows_at(s * length + side * BLOCK, BLOCK, BLOCK), :] = far_ref[
                s * BLOCK:(s + 1) * BLOCK, :]
        vec = vec_ref[layer].astype(F32)
        copies[0].wait()
        for s in range(sequences):
            rows = slice(s * length, (s + 1) * length)
            attended = dot_nn(mix_ref[rows, :], wo_ref[...]) + vec[2:3] + h_ref[rows, :].astype(F32)
            one, scaled, inverse = norm_forward(attended, vec[4:5], vec[5:6])
            n1_ref[rows, :] = scaled.astype(n1_ref.dtype)
            r1_ref[rows, :] = jnp.broadcast_to(inverse, (length, 128))
            one_ref[rows, :] = one
            low_ref[rows, :] = one.astype(BF16)
        copies[1].wait()
        tile = 512

        def up(j, carry):
            cols = rows_at(j * tile, tile, tile)
            bias = bu_ref[layer, :, cols].astype(F32)
            weights = wu_ref[:, cols]
            for s in range(sequences):
                rows = slice(s * length, (s + 1) * length)
                gate = dot_nn(low_ref[rows, :], weights) + bias
                below = 0.5 * lax.erf(gate * 0.7071067811865476) + 0.5
                act_ref[rows, cols] = (gate * below).astype(BF16)
                density = jnp.exp(gate * gate * -0.5) * 0.3989422804014327
                dg_ref[rows, cols] = (below + gate * density).astype(BF16)
            return carry

        lax.fori_loop(0, hidden // tile, up, 0)
        copies[2].wait()
        for s in range(sequences):
            rows = slice(s * length, (s + 1) * length)
            summed = dot_nn(act_ref[rows, :], wd_ref[...]) + vec[3:4] + one_ref[rows, :]
            out, scaled, inverse = norm_forward(summed, vec[6:7], vec[7:8])
            n2_ref[rows, :] = scaled.astype(n2_ref.dtype)
            r2_ref[rows, :] = jnp.broadcast_to(inverse, (length, 128))
            for h_out in h_outs:
                h_out[rows, :] = out.astype(h_out.dtype)

    act = sds((tokens, width), BF16)
    stat = sds((tokens, 128), F32)
    h_outs = (act,) if last else (act, sds((tokens, width), F32))
    return call(
        kernel, "near_post",
        (act, stat, sds((tokens, hidden), BF16), act, stat) + h_outs,
        [vmem_spec()] * 7 + [smem_spec()] + [vmem_spec()] + [any_spec()] * 3
        + [vmem_spec(), vmem_spec()],
        [pltpu.VMEM((width, width), BF16), pltpu.VMEM((width, hidden), BF16),
         pltpu.VMEM((hidden, width), BF16), pltpu.VMEM((tokens, width), BF16),
         pltpu.VMEM((tokens, width), F32), pltpu.VMEM((tokens, width), BF16),
         pltpu.VMEM((tokens, hidden), BF16), pltpu.SemaphoreType.DMA((3,))],
        2 * tokens * width * (2 * hidden + width), 24000000,
    )(far, q, k, v, halo, ids, halo_ids, live, h, wo, wu, wd, vec, bias_up)


def back_near_call(layer, sequences, length, grad, live_mask, q, k, v, halo, ids, halo_ids, live,
                   n1, r1, dg, n2, r2, wo, wu, wd, vec):
    tokens, width = q.shape
    hidden = wu.shape[2]

    def kernel(g_ref, q_ref, k_ref, v_ref, halo_ref, ids_ref, halo_ids_ref, live_ref, n1_ref,
               r1_ref, dg_ref, n2_ref, r2_ref, wo_hbm, wu_hbm, wd_hbm, vec_ref, datt_ref,
               dfar_ref, dq_ref, dk_ref, dv_ref, dhalo_ref, wo_ref, wu_ref, wd_ref, two_ref,
               low_ref, dmix_ref, gate_ref, sems):
        side = lax.axis_index("seq")
        copies = start_copies(
            [(wd_hbm.at[layer], wd_ref), (wu_hbm.at[layer], wu_ref), (wo_hbm.at[layer], wo_ref)],
            sems)
        vec = vec_ref[layer].astype(F32)
        for s in range(sequences):
            rows = slice(s * length, (s + 1) * length)
            g = g_ref[rows, :].astype(F32)
            if live_mask:
                places = lax.broadcasted_iota(jnp.int32, (length, 1), 0) + side * length
                g = jnp.where(places < live_ref[s], g, 0.0)
            two = norm_backward(g, n2_ref[rows, :].astype(F32), r2_ref[rows, 0:1], vec[6:7])
            two_ref[rows, :] = two
            low_ref[rows, :] = two.astype(BF16)
        copies[0].wait()
        tile = 512

        def down(j, carry):
            cols = rows_at(j * tile, tile, tile)
            weights = wd_ref[cols, :]
            for s in range(sequences):
                rows = slice(s * length, (s + 1) * length)
                gate = dot_nt(low_ref[rows, :], weights)
                gate_ref[rows, cols] = (gate * dg_ref[rows, cols].astype(F32)).astype(BF16)
            return carry

        lax.fori_loop(0, hidden // tile, down, 0)
        copies[1].wait()
        copies[2].wait()
        for s in range(sequences):
            rows = slice(s * length, (s + 1) * length)
            one = dot_nt(gate_ref[rows, :], wu_ref[...]) + two_ref[rows, :]
            att = norm_backward(one, n1_ref[rows, :].astype(F32), r1_ref[rows, 0:1], vec[4:5])
            datt_ref[rows, :] = att
            dmix_ref[rows, :] = dot_nt(att.astype(BF16), wo_ref[...]).astype(BF16)
        for s in range(sequences):
            dfar_ref[s * BLOCK:(s + 1) * BLOCK, :] = dmix_ref[
                rows_at(s * length + side * BLOCK, BLOCK, BLOCK), :]
        attention_backward(True, side, sequences, length, q_ref, k_ref, v_ref, halo_ref, dmix_ref,
                           ids_ref, halo_ids_ref, live_ref, dq_ref, dk_ref, dv_ref, dhalo_ref,
                           dq_row=lambda s: s * BLOCK)

    wide = sds((tokens, width), F32)
    block = sds((sequences * BLOCK, width), BF16)
    return call(
        kernel, "back_near",
        (wide, block, block, wide, wide, sds((2, sequences * HALO, width), BF16)),
        [vmem_spec()] * 7 + [smem_spec()] + [vmem_spec()] * 5 + [any_spec()] * 3
        + [vmem_spec()],
        [pltpu.VMEM((width, width), BF16), pltpu.VMEM((width, hidden), BF16),
         pltpu.VMEM((hidden, width), BF16), pltpu.VMEM((tokens, width), F32),
         pltpu.VMEM((tokens, width), BF16), pltpu.VMEM((tokens, width), BF16),
         pltpu.VMEM((tokens, hidden), BF16), pltpu.SemaphoreType.DMA((3,))],
        2 * tokens * width * (2 * hidden + width), 24000000,
    )(grad, q, k, v, halo, ids, halo_ids, live, n1, r1, dg, n2, r2, wo, wu, wd, vec)


def back_far_call(sequences, length, q, k, v, dfar, ids, live, dq_near, dk_near, dv_near):
    tokens, width = q.shape

    def kernel(q_ref, k_ref, v_ref, dfar_ref, ids_ref, live_ref, dqn_ref, dkn_ref, dvn_ref,
               dq_ref, dk_ref, dv_ref):
        side = lax.axis_index("seq")
        attention_backward(False, side, sequences, length, q_ref, k_ref, v_ref, None, dfar_ref,
                           ids_ref, None, live_ref, dq_ref, dk_ref, dv_ref, None, dkn_ref,
                           dvn_ref, dmix_row=lambda s: s * BLOCK)
        for s in range(sequences):
            dq_ref[rows_at(s * length + (1 - side) * BLOCK, BLOCK, BLOCK), :] = dqn_ref[
                s * BLOCK:(s + 1) * BLOCK, :]

    wide = sds((tokens, width), F32)
    return call(
        kernel, "back_far", (sds((tokens, width), BF16), wide, wide),
        [vmem_spec()] * 5 + [smem_spec()] + [vmem_spec()] * 3, [], 4000000000, 16000000,
    )(q, k, v, dfar, ids, live, dq_near, dk_near, dv_near)


def back_grads_call(layer, sequences, length, dq, dk, dv, dhalo, u, x, a, b):
    tokens, width = dq.shape
    rank = a.shape[2]

    def kernel(dq_ref, dk_ref, dv_ref, dhalo_ref, u_ref, x_ref, a_ref, b_ref, dkb_ref, dvb_ref,
               du_ref, grad_ref):
        side = lax.axis_index("seq")
        down, up_q, up_v = low_rank(a_ref.at[layer], b_ref.at[layer])
        for s in range(sequences):
            taken = rows_at(s * length + (1 - side) * (length - HALO), HALO, 32)
            hrows = slice(s * HALO, (s + 1) * HALO)
            dk_ref[taken, :] = dk_ref[taken, :] + dhalo_ref[0, hrows, :].astype(F32)
            dv_ref[taken, :] = dv_ref[taken, :] + dhalo_ref[1, hrows, :].astype(F32)
        dkb_ref[...] = dk_ref[...].astype(BF16)
        dv16 = dv_ref[...].astype(BF16)
        dvb_ref[...] = dv16
        dq16 = dq_ref[...]
        du = (2.0 * (dot_nt(dq16, up_q) + dot_nt(dv16, up_v))).astype(BF16)
        du_ref[...] = du
        u = u_ref[...]
        grad_ref[0:2 * rank, :] = dot_tn(du, x_ref[...])
        up = jnp.where(lax.broadcasted_iota(jnp.int32, (2 * rank, width), 0) < rank,
                       dot_tn(u, dq16), dot_tn(u, dv16))
        grad_ref[2 * rank:, :] = 2.0 * up

    act = sds((tokens, width), BF16)
    return call(
        kernel, "back_grads", (act, act, sds((tokens, 2 * rank), BF16), sds((4 * rank, width), F32)),
        [vmem_spec()] * 6 + [vmem_spec()] * 2, [], 500000000, 12000000,
    )(dq, dk, dv, dhalo, u, x, a, b)


def back_in_call(layer, sequences, length, datt, dq, dk, dv, du, w, a, b):
    tokens, width = dq.shape
    rank = a.shape[2]

    def kernel(datt_ref, dq_ref, dk_ref, dv_ref, du_ref, w_hbm, a_ref, b_ref, out_ref, w_ref,
               sems):
        copies = start_copies([(w_hbm.at[layer], w_ref)], sems)
        down, _, _ = low_rank(a_ref.at[layer], b_ref.at[layer])
        copies[0].wait()
        for s in range(sequences):
            rows = slice(s * length, (s + 1) * length)
            out = datt_ref[rows, :] + dot_nn(du_ref[rows, :], down)
            out = out + dot_nt(dq_ref[rows, :], w_ref[:, :width])
            out = out + dot_nt(dk_ref[rows, :], w_ref[:, width:2 * width])
            out_ref[rows, :] = out + dot_nt(dv_ref[rows, :], w_ref[:, 2 * width:])

    return call(
        kernel, "back_in", sds((tokens, width), F32),
        [vmem_spec()] * 5 + [any_spec()] + [vmem_spec()] * 2,
        [pltpu.VMEM((width, 3 * width), BF16), pltpu.SemaphoreType.DMA((1,))],
        2 * tokens * width * width * 3, 12000000,
    )(datt, dq, dk, dv, du, w, a, b)


def adam_call(total, count, token_slots, steps, down, up, m_down, v_down, m_up, v_up):
    layers, two, rank, width = down.shape

    def kernel(g_ref, steps_ref, down_ref, up_ref, md_ref, vd_ref, mu_ref, vu_ref, down_out,
               up_out, md_out, vd_out, mu_out, vu_out):
        for layer in range(layers):
            for which in range(two):
                for group, (w_ref, m_ref, v_ref, w_out, m_out, v_out, rate, decay) in enumerate((
                    (down_ref, md_ref, vd_ref, down_out, md_out, vd_out, 0.03125, 0.1),
                    (up_ref, mu_ref, vu_ref, up_out, mu_out, vu_out, 0.5, 0.0),
                )):
                    start = ((layer * 2 + group) * two + which) * rank
                    grad = g_ref[start:start + rank, :] / token_slots
                    step = jnp.full((rank, width), steps_ref[layer, which, group], jnp.int32)
                    correction = 1.0 - jnp.exp2(-step.astype(F32))
                    weight = w_ref[layer, which]
                    moment = 0.5 * m_ref[layer, which] + 0.5 * grad
                    velocity = 0.5 * v_ref[layer, which] + 0.5 * grad * grad
                    size = moment / correction / (jnp.sqrt(velocity / correction) + 1e-08)
                    w_out[layer, which] = weight - rate * (size + decay * weight)
                    m_out[layer, which] = moment
                    v_out[layer, which] = velocity

    shape = sds(down.shape, F32)
    return call(
        kernel, "adam", (shape,) * 6,
        [vmem_spec(), smem_spec()] + [vmem_spec()] * 6, [], 1000000, 2000000,
    )(total, steps, down, up, m_down, v_down, m_up, v_up)


def sum_over_devices(value):
    seq, batch = lax.axis_size("seq"), lax.axis_size("batch")
    if seq != 2 or batch & (batch - 1):
        return lax.psum(value, ("seq", "batch"))
    swap = [(0, 1), (1, 0)]
    half = value.shape[0] // 2
    side = lax.axis_index("seq")
    mine = lax.dynamic_slice_in_dim(value, side * half, half, 0)
    theirs = lax.dynamic_slice_in_dim(value, (1 - side) * half, half, 0)
    mine = mine + lax.ppermute(theirs, "seq", swap)
    step = 1
    while step < batch:
        mine = mine + lax.ppermute(mine, "batch", [(i, i ^ step) for i in range(batch)])
        step *= 2
    theirs = lax.ppermute(mine, "seq", swap)
    return jnp.where(side == 0, jnp.concatenate([mine, theirs]), jnp.concatenate([theirs, mine]))


def shards(
    first_layer_input,
    output_gradient,
    sentence_pair_index,
    sequence_live_length,
    optimizer_step_count,
    query_key_value_weight,
    attention_output_weight,
    feedforward_up_weight,
    feedforward_down_weight,
    layer_bias_gain_rows,
    feedforward_up_bias,
    adapter_down_factors,
    adapter_up_factors,
    first_moment_down,
    second_moment_down,
    first_moment_up,
    second_moment_up,
):
    sequences, length, width = first_layer_input.shape
    tokens = sequences * length
    swap = [(0, 1), (1, 0)]
    side = lax.axis_index("seq")
    ids, live = sentence_pair_index, sequence_live_length
    a, b = adapter_down_factors, jnp.swapaxes(adapter_up_factors, 2, 3)
    vec = layer_bias_gain_rows
    bias_up = feedforward_up_bias[:, None, :]
    wqkv, wo = query_key_value_weight, attention_output_weight
    wu, wd = feedforward_up_weight, feedforward_down_weight
    halo_ids = lax.ppermute(
        lax.dynamic_slice_in_dim(ids, (1 - side) * (length - HALO), HALO, 1), "seq", swap)

    x = first_layer_input.reshape(tokens, width)
    h = x
    kept = []
    for layer in range(ENCODER_LAYERS):
        q, k, v, u, send = qkv_call(layer, sequences, length, x, wqkv, a, b, vec)
        halo = lax.ppermute(send, "seq", swap)
        far = far_call(sequences, length, q, k, v, ids, live)
        n1, r1, dg, n2, r2, *outs = near_post_call(
            layer, sequences, length, far, q, k, v, halo, ids, halo_ids, live, h, wo, wu, wd, vec,
            bias_up)
        kept.append((x, u, q, k, v, halo, n1, r1, dg, n2, r2))
        x, h = outs[0], outs[-1]
    hidden_out = x

    gradient = output_gradient.reshape(tokens, width)
    grads = [None] * ENCODER_LAYERS
    for layer in reversed(range(ENCODER_LAYERS)):
        x, u, q, k, v, halo, n1, r1, dg, n2, r2 = kept[layer]
        datt, dfar, dq, dk, dv, dsend = back_near_call(
            layer, sequences, length, gradient, layer == ENCODER_LAYERS - 1, q, k, v, halo, ids,
            halo_ids, live, n1, r1, dg, n2, r2, wo, wu, wd, vec)
        dhalo = lax.ppermute(dsend, "seq", swap)
        dq, dk, dv = back_far_call(sequences, length, q, k, v, dfar, ids, live, dq, dk, dv)
        dk, dv, du, grads[layer] = back_grads_call(
            layer, sequences, length, dq, dk, dv, dhalo, u, x, a, b)
        gradient = back_in_call(layer, sequences, length, datt, dq, dk, dv, du, wqkv, a, b)

    total = sum_over_devices(jnp.concatenate(grads, axis=0))
    token_slots = tokens * lax.axis_size("seq") * lax.axis_size("batch")
    down, up, m_down, v_down, m_up, v_up = adam_call(
        total, None, token_slots, optimizer_step_count, a, b, first_moment_down,
        second_moment_down, jnp.swapaxes(first_moment_up, 2, 3),
        jnp.swapaxes(second_moment_up, 2, 3))
    return (
        hidden_out.reshape(sequences, length, width),
        gradient.reshape(sequences, length, width),
        down,
        jnp.swapaxes(up, 2, 3),
        m_down,
        v_down,
        jnp.swapaxes(m_up, 2, 3),
        jnp.swapaxes(v_up, 2, 3),
    )


def solution(mesh):
    acts, whole = P("batch", "seq", None), P()
    return jax.shard_map(
        shards,
        mesh=mesh,
        in_specs=(acts, acts, P("batch", "seq"), P("batch")) + (whole,) * 13,
        out_specs=(acts, acts) + (whole,) * 6,
        check_vma=False,
    )
```

```python
import jax
import jax.numpy as jnp
from jax import lax
from jax.experimental import pallas as pl
from jax.experimental.pallas import tpu as pltpu
from jax.sharding import PartitionSpec as P

HEADS = 12
ENCODER_LAYERS = 2
HALO = 96
BLOCK = 128
SUB = 64
WINDOW = 256
QUAD = 256
MASKED = -1000000000.0
F32 = jnp.float32
BF16 = jnp.bfloat16


def dot_nn(a, b):
    return lax.dot_general(a, b, (((1,), (0,)), ((), ())), preferred_element_type=F32)


def dot_nt(a, b):
    return lax.dot_general(a, b, (((1,), (1,)), ((), ())), preferred_element_type=F32)


def dot_tn(a, b):
    return lax.dot_general(a, b, (((0,), (0,)), ((), ())), preferred_element_type=F32)


def rows_at(start, size, multiple):
    return pl.ds(pl.multiple_of(start, multiple), size)


def loop(count, body):
    def step(i, carry):
        body(i)
        return carry

    lax.fori_loop(0, count, step, 0)


def column_of(row):
    n = row.shape[1]
    eye = lax.broadcasted_iota(jnp.int32, (n, n), 0) == lax.broadcasted_iota(jnp.int32, (n, n), 1)
    return jnp.sum(jnp.where(eye, row, 0.0), axis=1, keepdims=True)


def head_lanes():
    return lax.broadcasted_iota(jnp.int32, (SUB, QUAD), 1) // 64


def spread_heads(tile, lanes):
    zero = jnp.zeros_like(tile)
    return jnp.concatenate([jnp.where(lanes == h, tile, zero) for h in range(4)], axis=0)


def gather_heads(wide, lanes):
    out = wide[:SUB]
    for h in range(1, 4):
        out = jnp.where(lanes == h, wide[h * SUB:(h + 1) * SUB], out)
    return out


def pipelined(units):
    units = list(units)
    live = []
    while units or live:
        if units:
            live.append(units.pop(0))
        for unit in list(live):
            if next(unit, None) is None:
                live.remove(unit)


class Side:
    def __init__(self, near, length, ids_refs, live_of=None):
        self.near, self.length = near, length
        self.side = lax.axis_index("seq")
        self.row0 = BLOCK * ((1 - self.side) if near else self.side)
        self.query_ids, self.key_ids = ids_refs

    def queries(self, s, sub):
        return rows_at(s * self.length + self.row0 + sub * SUB, SUB, SUB)

    def keys(self, s, sub):
        if self.near:
            return rows_at(s * (WINDOW + SUB) + sub * SUB, WINDOW, SUB)
        return rows_at(s * self.length, WINDOW, WINDOW)

    def diagonal(self, shape, sub, query_dim):
        query = lax.broadcasted_iota(jnp.int32, shape, query_dim)
        key = lax.broadcasted_iota(jnp.int32, shape, 1 - query_dim)
        if self.near:
            return query + HALO == key
        return query + (self.row0 + sub * SUB) == key

    def forward_bias(self, s):
        query = column_of(self.query_ids[pl.ds(s, 1), :])
        key = self.key_ids[pl.ds(s, 1), :]
        out = []
        for sub in range(2):
            keys = key[:, sub * SUB:sub * SUB + WINDOW] if self.near else key
            seen = query[sub * SUB:(sub + 1) * SUB] == keys
            seen = seen | self.diagonal((SUB, WINDOW), sub, 0)
            out.append(jnp.where(seen, 0.0, MASKED))
        return out

    def backward_bias(self, s):
        query = self.query_ids[pl.ds(s, 1), :]
        key = self.key_ids[pl.ds(s, 1), :]
        column = jnp.concatenate(
            [column_of(key[:, i:i + SUB]) for i in range(0, key.shape[1], SUB)], axis=0)
        out = []
        for sub in range(2):
            keys = column[sub * SUB:sub * SUB + WINDOW] if self.near else column
            seen = keys == query[:, sub * SUB:(sub + 1) * SUB]
            seen = seen | self.diagonal((WINDOW, SUB), sub, 1)
            out.append(jnp.where(seen, 0.0, MASKED))
        return out


def attention_forward(where, s, q_ref, k_ref, v_ref, out_ref, out_rows):
    lanes = head_lanes()
    biases = where.forward_bias(s)

    def unit(quad, sub):
        cols = slice(QUAD * quad, QUAD * quad + QUAD)
        keys = where.keys(s, sub)
        q4 = spread_heads(q_ref[where.queries(s, sub), cols], lanes)
        scores = dot_nt(q4, k_ref[keys, cols])
        yield True
        scores = scores + jnp.concatenate([biases[sub]] * 4, axis=0)
        top = jnp.max(scores, axis=1, keepdims=True)
        share = jnp.exp(scores - top)
        total = jnp.sum(share, axis=1, keepdims=True)
        share = share.astype(BF16)
        yield True
        mixed = dot_nn(share, v_ref[keys, cols])
        yield True
        out_ref[out_rows(s, sub), cols] = gather_heads(mixed * (1.0 / total), lanes).astype(BF16)

    width = q_ref.shape[1]
    pipelined(unit(quad, sub) for quad in range(width // QUAD) for sub in range(2))


def attention_backward(where, s, q_ref, k_ref, v_ref, dmix_ref, dmix_rows, dq_ref, dq_rows, done):
    lanes = head_lanes()
    biases = where.backward_bias(s)

    def unit(quad, sub, kept):
        cols = slice(QUAD * quad, QUAD * quad + QUAD)
        keys = where.keys(s, sub)
        q4 = spread_heads(q_ref[where.queries(s, sub), cols], lanes)
        d4 = spread_heads(dmix_ref[dmix_rows(s, sub), cols], lanes)
        key, value = k_ref[keys, cols], v_ref[keys, cols]
        scores = dot_nt(key, q4)
        d_share = dot_nt(value, d4)
        yield True
        scores = scores + jnp.concatenate([biases[sub]] * 4, axis=1)
        top = jnp.max(scores, axis=0, keepdims=True)
        share = jnp.exp(scores - top)
        share = share * (1.0 / jnp.sum(share, axis=0, keepdims=True))
        delta = jnp.sum(share * d_share, axis=0, keepdims=True)
        d_scores = (share * (d_share - delta)).astype(BF16)
        kept.append((share.astype(BF16), d_scores, q4, d4))
        yield True
        d_query = gather_heads(dot_tn(d_scores, key), lanes) * 0.125
        dq_ref[dq_rows(s, sub), cols] = d_query.astype(BF16)
        if sub == 1:
            done(s, cols, kept)

    width = q_ref.shape[1]

    def units():
        for quad in range(width // QUAD):
            kept = []
            for sub in range(2):
                yield unit(quad, sub, kept)

    pipelined(units())


def near_terms(kept, which, other):
    first = dot_nn(kept[0][which], kept[0][other])
    second = dot_nn(kept[1][which], kept[1][other])
    return first[:SUB], first[SUB:] + second[:WINDOW - SUB], second[WINDOW - SUB:]


def near_keys_start(sequences, length, k_ref, v_ref, halo_ref, nk_ref, nv_ref, sems):
    side = lax.axis_index("seq")
    wide, own = WINDOW + SUB, WINDOW + SUB - HALO
    copies = []
    for s in range(sequences):
        for i, (src, dst) in enumerate(((k_ref, nk_ref), (v_ref, nv_ref))):
            for j, (part, first, last, size) in enumerate((
                (src, s * length + (length - own) * (1 - side), s * wide + HALO * side, own),
                (halo_ref.at[i], s * HALO, s * wide + own * (1 - side), HALO),
            )):
                copies.append(pltpu.make_async_copy(
                    part.at[rows_at(first, size, 32)], dst.at[rows_at(last, size, 32)],
                    sems.at[s * 4 + i * 2 + j]))
    for copy in copies:
        copy.start()
    return copies


def norm_forward(values, gain, shift):
    center = values - jnp.mean(values, axis=1, keepdims=True)
    spread = jnp.mean(center * center, axis=1, keepdims=True)
    inverse = lax.rsqrt(spread + 1e-05)
    scaled = center * inverse
    return scaled * gain + shift, scaled, inverse


def norm_backward(gradient, scaled, inverse, gain):
    inner = gradient * gain
    return inverse * (
        inner
        - jnp.mean(inner, axis=1, keepdims=True)
        - scaled * jnp.mean(inner * scaled, axis=1, keepdims=True)
    )


def low_rank(a_ref, b_ref):
    down = jnp.concatenate([a_ref[0], a_ref[1]], axis=0).astype(BF16)
    zero = jnp.zeros_like(b_ref[0])
    up_q = jnp.concatenate([b_ref[0], zero], axis=0).astype(BF16)
    up_v = jnp.concatenate([zero, b_ref[1]], axis=0).astype(BF16)
    return down, up_q, up_v


def project_in(sequences, length, x_ref, w_ref, a_ref, b_ref, vec_ref, q_ref, k_ref, v_ref, u_ref,
               send_ref):
    side = lax.axis_index("seq")
    width = x_ref.shape[1]
    down, up_q, up_v = low_rank(a_ref, b_ref)
    vec = vec_ref[...].astype(F32)

    def one(s):
        rows = rows_at(s * length, length, length)
        x = x_ref[rows, :]
        inner = dot_nt(x, down).astype(BF16)
        u_ref[rows, :] = inner
        q = dot_nn(x, w_ref[:, :width]) + vec[0:1] + 2.0 * dot_nn(inner, up_q)
        q_ref[rows, :] = q.astype(BF16) * jnp.asarray(0.125, BF16)
        k_ref[rows, :] = dot_nn(x, w_ref[:, width:2 * width]).astype(BF16)
        v = dot_nn(x, w_ref[:, 2 * width:]) + vec[1:2] + 2.0 * dot_nn(inner, up_v)
        v_ref[rows, :] = v.astype(BF16)
        taken = rows_at(s * length + (1 - side) * (length - HALO), HALO, 32)
        given = rows_at(s * HALO, HALO, 32)
        send_ref[0, given, :] = k_ref[taken, :]
        send_ref[1, given, :] = v_ref[taken, :]

    loop(sequences, one)


def layer_rest(sequences, length, mix_ref, h_ref, wo_ref, wu_ref, wd_ref, waits, vec_ref, bu_ref,
               one_ref, low_ref, act_ref, n1_ref, r1_ref, dg_ref, n2_ref, r2_ref, h_outs, sent):
    hidden = wu_ref.shape[1]
    waits[0]()
    vec = vec_ref[...].astype(F32)

    def mixed(s):
        rows = rows_at(s * length, length, length)
        attended = dot_nn(mix_ref[rows, :], wo_ref[...]) + vec[2:3] + h_ref[rows, :].astype(F32)
        one, scaled, inverse = norm_forward(attended, vec[4:5], vec[5:6])
        n1_ref[rows, :] = scaled.astype(n1_ref.dtype)
        r1_ref[rows, :] = jnp.broadcast_to(inverse, (length, 128))
        one_ref[rows, :] = one
        low_ref[rows, :] = one.astype(BF16)

    loop(sequences, mixed)
    sent(0)
    waits[1]()
    tile = 512

    def up(j):
        cols = rows_at(j * tile, tile, tile)
        bias = bu_ref[:, cols].astype(F32)
        weights = wu_ref[:, cols]

        def unit(s):
            rows = slice(s * length, (s + 1) * length)
            gate = dot_nn(low_ref[rows, :], weights)
            yield True
            gate = gate + bias
            below = 0.5 * lax.erf(gate * 0.7071067811865476) + 0.5
            act_ref[rows, cols] = (gate * below).astype(BF16)
            density = jnp.exp2(gate * gate * -0.7213475204444817) * 0.3989422804014327
            dg_ref[rows, cols] = (below + gate * density).astype(BF16)

        pipelined(unit(s) for s in range(sequences))

    loop(hidden // tile, up)
    sent(1)
    waits[2]()

    def down(s):
        rows = rows_at(s * length, length, length)
        summed = dot_nn(act_ref[rows, :], wd_ref[...]) + vec[3:4] + one_ref[rows, :]
        out, scaled, inverse = norm_forward(summed, vec[6:7], vec[7:8])
        n2_ref[rows, :] = scaled.astype(n2_ref.dtype)
        r2_ref[rows, :] = jnp.broadcast_to(inverse, (length, 128))
        for h_out in h_outs:
            h_out[rows, :] = out.astype(h_out.dtype)

    loop(sequences, down)
    sent(2)


def layer_rest_back(sequences, length, gradient, waits, n1_ref, r1_ref, dg_ref, n2_ref, r2_ref,
                    wo_ref, wu_ref, wd_ref, vec_ref, two_ref, low_ref, gate_ref, datt_ref):
    hidden = wu_ref.shape[1]
    waits[0]()
    vec = vec_ref[...].astype(F32)

    def second(s):
        rows = rows_at(s * length, length, length)
        two = norm_backward(
            gradient(s, rows), n2_ref[rows, :].astype(F32), r2_ref[rows, 0:1], vec[6:7])
        two_ref[rows, :] = two
        low_ref[rows, :] = two.astype(BF16)

    loop(sequences, second)
    waits[1]()
    tile = 512

    def down(j):
        cols = rows_at(j * tile, tile, tile)
        weights = wd_ref[cols, :]

        def unit(s):
            rows = slice(s * length, (s + 1) * length)
            gate = dot_nt(low_ref[rows, :], weights)
            yield True
            gate_ref[rows, cols] = (gate * dg_ref[rows, cols].astype(F32)).astype(BF16)

        pipelined(unit(s) for s in range(sequences))

    loop(hidden // tile, down)
    waits[2]()
    waits[3]()

    def up(s):
        rows = rows_at(s * length, length, length)
        one = dot_nt(gate_ref[rows, :], wu_ref[...]) + two_ref[rows, :]
        att = norm_backward(one, n1_ref[rows, :].astype(F32), r1_ref[rows, 0:1], vec[4:5])
        datt_ref[rows, :] = att
        low_ref[rows, :] = dot_nt(att.astype(BF16), wo_ref[...]).astype(BF16)

    loop(sequences, up)


def near_backward(sequences, length, ids_refs, q_ref, nk_ref, nv_ref, dmix_ref, dfar_ref, dq_ref,
                  dnk_ref, dnv_ref, dhalo_ref):
    near = Side(True, length, ids_refs)
    side, wide = near.side, WINDOW + SUB

    def done(s, cols, kept):
        for out, which, other in ((dnv_ref, 0, 3), (dnk_ref, 1, 2)):
            first, both, second = near_terms(kept, which, other)
            out[rows_at(s * wide, SUB, SUB), cols] = first
            out[rows_at(s * wide + SUB, WINDOW - SUB, SUB), cols] = both
            out[rows_at(s * wide + WINDOW, SUB, SUB), cols] = second

    def one(s):
        dfar_ref[rows_at(s * BLOCK, BLOCK, BLOCK), :] = dmix_ref[
            rows_at(s * length + side * BLOCK, BLOCK, BLOCK), :]
        attention_backward(
            near, s, q_ref, nk_ref, nv_ref, dmix_ref, near.queries, dq_ref,
            lambda s, sub: rows_at(s * BLOCK + sub * SUB, SUB, SUB), done)
        halo = rows_at(s * wide + (wide - HALO) * (1 - side), HALO, 32)
        dhalo_ref[0, rows_at(s * HALO, HALO, 32), :] = dnk_ref[halo, :].astype(BF16)
        dhalo_ref[1, rows_at(s * HALO, HALO, 32), :] = dnv_ref[halo, :].astype(BF16)

    loop(sequences, one)


def adapter_back(sequences, length, dq_ref, dk_ref, dv_ref, dhalo_ref, u_ref, x_ref, a_ref,
                 b_ref, dkb_ref, dvb_ref, du_ref, grad_ref):
    side = lax.axis_index("seq")
    rank = a_ref.shape[1]
    _, up_q, up_v = low_rank(a_ref, b_ref)

    def one(s):
        rows = rows_at(s * length, length, length)
        taken = rows_at(s * length + (1 - side) * (length - HALO), HALO, 32)
        hrows = rows_at(s * HALO, HALO, 32)
        dk_ref[taken, :] = dk_ref[taken, :] + dhalo_ref[0, hrows, :].astype(F32)
        dv_ref[taken, :] = dv_ref[taken, :] + dhalo_ref[1, hrows, :].astype(F32)
        dkb_ref[rows, :] = dk_ref[rows, :].astype(BF16)
        dv16 = dv_ref[rows, :].astype(BF16)
        dvb_ref[rows, :] = dv16
        du_ref[rows, :] = (2.0 * (dot_nt(dq_ref[rows, :], up_q) + dot_nt(dv16, up_v))).astype(BF16)

    loop(sequences, one)
    u = u_ref[...]
    grad_ref[0:2 * rank, :] = dot_tn(du_ref[...], x_ref[...])
    up_q, up_v = dot_tn(u, dq_ref[...]), dot_tn(u, dvb_ref[...])
    grad_ref[2 * rank:3 * rank, :] = 2.0 * up_q[:rank]
    grad_ref[3 * rank:, :] = 2.0 * up_v[rank:]


def project_back(rows, own_rows, datt_ref, dq_ref, dk_ref, dv_ref, du_ref, w_ref, down):
    width = dq_ref.shape[1]
    out = datt_ref[rows, :] + dot_nn(du_ref[rows, :], down)
    out = out + dot_nt(dq_ref[rows, :], w_ref[:, :width])
    out = out + dot_nt(dk_ref[rows, :], w_ref[:, width:2 * width])
    return out + dot_nt(dv_ref[rows, :], w_ref[:, 2 * width:])


HBM, VMEM, SMEM = pltpu.HBM, pltpu.VMEM, pltpu.SMEM


def call(kernel, name, args, outs, scratch, flops, nbytes, limit, aliases=None):
    scratch = [pltpu.SemaphoreType.DMA((s,)) if isinstance(s, int) else pltpu.VMEM(*s)
               for s in scratch]
    return pl.pallas_call(
        kernel,
        name=name,
        out_shape=tuple(space(shape, dtype) for space, shape, dtype in outs),
        in_specs=[pl.BlockSpec(memory_space=space) for space, _ in args],
        out_specs=tuple(pl.BlockSpec(memory_space=space) for space, _, _ in outs),
        scratch_shapes=scratch,
        input_output_aliases=aliases or {},
        compiler_params=pltpu.CompilerParams(vmem_limit_bytes=limit * 1024 * 1024),
        cost_estimate=pl.CostEstimate(flops=flops, bytes_accessed=nbytes, transcendentals=0),
    )(*[array if space == SMEM else pltpu.with_memory_space_constraint(array, space)
        for space, array in args])


def sds(shape, dtype):
    return jax.ShapeDtypeStruct(shape, dtype)


def copies_of(pairs, sems):
    return [pltpu.make_async_copy(src, dst, sems.at[i]) for i, (src, dst) in enumerate(pairs)]


def start_all(copies):
    for copy in copies:
        copy.start()
    return copies


def wait_for(copies, *which):
    def wait():
        for i in which:
            copies[i].wait()

    return wait


def first_call(layer, sequences, length, x, w, a, b, vec):
    tokens, width = x.shape
    rank = a.shape[2]

    def kernel(x_hbm, w_hbm, a_hbm, b_hbm, vec_hbm, q_ref, k_ref, v_ref, send_ref, u_out, x_ref,
               w_ref, a_ref, b_ref, vec_ref, u_ref, sems, outs):
        copies = start_all(copies_of(
            [(a_hbm.at[layer], a_ref), (b_hbm.at[layer], b_ref), (vec_hbm.at[layer], vec_ref),
             (x_hbm, x_ref), (w_hbm.at[layer], w_ref)], sems))
        wait_for(copies, 0, 1, 2, 3, 4)()
        project_in(sequences, length, x_ref, w_ref, a_ref, b_ref, vec_ref, q_ref, k_ref, v_ref,
                   u_ref, send_ref)
        store = pltpu.make_async_copy(u_ref, u_out, outs.at[0])
        store.start()
        store.wait()

    act, small = (VMEM, (tokens, width), BF16), ((tokens, 2 * rank), BF16)
    return call(
        kernel, "project_in", [(HBM, x), (HBM, w), (HBM, a), (HBM, b), (HBM, vec)],
        [act, act, act, (VMEM, (2, sequences * HALO, width), BF16), (HBM,) + small],
        [((tokens, width), BF16), ((width, 3 * width), BF16), ((2, rank, width), F32),
         ((2, rank, width), F32), ((8, width), BF16), small, 5, 1],
        2 * tokens * width * width * 3, 12000000, 10)


def far_call(sequences, length, q, k, v, ids):
    tokens, width = q.shape

    def kernel(q_ref, k_ref, v_ref, qid_ref, kid_ref, out_ref):
        far = Side(False, length, (qid_ref, kid_ref))
        loop(sequences, lambda s: attention_forward(
            far, s, q_ref, k_ref, v_ref, out_ref,
            lambda s, sub: rows_at(s * BLOCK + sub * SUB, SUB, SUB)))

    return call(
        kernel, "attention_far",
        [(VMEM, q), (VMEM, k), (VMEM, v), (VMEM, ids[2]), (VMEM, ids[3])],
        [(VMEM, (sequences * BLOCK, width), BF16)], [], 2000000000, 6000000, 6)[0]


def near_forward(sequences, length, ids_refs, far_ref, q_ref, k_ref, v_ref, halo_ref, nk_ref,
                 nv_ref, mix_ref, sems):
    copies = near_keys_start(sequences, length, k_ref, v_ref, halo_ref, nk_ref, nv_ref, sems)
    near = Side(True, length, ids_refs)
    for copy in copies:
        copy.wait()

    def one(s):
        mix_ref[rows_at(s * length + near.side * BLOCK, BLOCK, BLOCK), :] = far_ref[
            rows_at(s * BLOCK, BLOCK, BLOCK), :]
        attention_forward(near, s, q_ref, nk_ref, nv_ref, mix_ref, near.queries)

    loop(sequences, one)


def middle_call(layer, sequences, length, ids, far, q, k, v, halo, h, w, a, b, wo, wu, wd, vec,
                bias_up):
    tokens, width = q.shape
    hidden, rank = wu.shape[2], a.shape[2]

    def kernel(qid_ref, kid_ref, far_ref, q_ref, k_ref, v_ref, halo_ref, h_hbm, w_hbm, a_hbm,
               b_hbm, wo_hbm, wu_hbm, wd_hbm, vec_hbm, bu_hbm,
               q2_ref, k2_ref, v2_ref, send_ref,
               u_out, x_out, h_out, n1_out, r1_out, dg_out, n2_out, r2_out, q_out, k_out, v_out,
               nk_out, nv_out,
               h_ref, w_ref, wo_ref, wu_ref, wd_ref, vec_ref, bu_ref, vec2_ref, a_ref, b_ref,
               u_ref, mix_ref, one_ref, low_ref, act_ref,
               n1_ref, r1_ref, dg_ref, n2_ref, r2_ref, nk_ref, nv_ref, ins, outs, sems):
        loads = start_all(copies_of(
            [(h_hbm, h_ref), (vec_hbm.at[layer], vec_ref), (wo_hbm.at[layer], wo_ref),
             (bu_hbm.at[layer], bu_ref), (wu_hbm.at[layer], wu_ref), (wd_hbm.at[layer], wd_ref),
             (w_hbm.at[layer + 1], w_ref), (a_hbm.at[layer + 1], a_ref),
             (b_hbm.at[layer + 1], b_ref), (vec_hbm.at[layer + 1], vec2_ref)], ins))
        stores = copies_of(
            [(q_ref, q_out), (k_ref, k_out), (v_ref, v_out), (nk_ref, nk_out), (nv_ref, nv_out),
             (n1_ref, n1_out), (r1_ref, r1_out), (dg_ref, dg_out), (n2_ref, n2_out),
             (r2_ref, r2_out), (one_ref, h_out), (low_ref, x_out), (u_ref, u_out)], outs)
        near_forward(sequences, length, (qid_ref, kid_ref), far_ref, q_ref, k_ref, v_ref,
                     halo_ref, nk_ref, nv_ref, mix_ref, sems)
        layer_rest(sequences, length, mix_ref, h_ref, wo_ref, wu_ref, wd_ref,
                   [wait_for(loads, 0, 1, 2), wait_for(loads, 3, 4), wait_for(loads, 5)], vec_ref,
                   bu_ref, one_ref, low_ref, act_ref, n1_ref, r1_ref, dg_ref, n2_ref, r2_ref,
                   (one_ref, low_ref),
                   lambda i: start_all((stores[:7], stores[7:8], stores[8:12])[i]))
        wait_for(loads, 6, 7, 8, 9)()
        project_in(sequences, length, low_ref, w_ref, a_ref, b_ref, vec2_ref, q2_ref, k2_ref,
                   v2_ref, u_ref, send_ref)
        stores[12].start()
        for copy in stores:
            copy.wait()

    act, stat = ((tokens, width), BF16), ((tokens, 128), F32)
    wide, deep = ((tokens, width), F32), ((tokens, hidden), BF16)
    near, small = ((sequences * (WINDOW + SUB), width), BF16), ((tokens, 2 * rank), BF16)
    factors = ((2, rank, width), F32)
    return call(
        kernel, "middle",
        [(VMEM, ids[0]), (VMEM, ids[1]), (VMEM, far), (VMEM, q), (VMEM, k), (VMEM, v),
         (VMEM, halo)]
        + [(HBM, item) for item in (h, w, a, b, wo, wu, wd, vec, bias_up)],
        [(VMEM,) + act, (VMEM,) + act, (VMEM,) + act, (VMEM, (2, sequences * HALO, width), BF16)]
        + [(HBM,) + item for item in (small, act, wide, act, stat, deep, act, stat, act, act, act,
                                      near, near)],
        [(h.shape, h.dtype), ((width, 3 * width), BF16), ((width, width), BF16),
         ((width, hidden), BF16), ((hidden, width), BF16), ((8, width), BF16),
         ((1, hidden), BF16), ((8, width), BF16), factors, factors, small, act, wide, act, deep,
         act, stat, deep, act, stat, near, near, 10, 13, 4 * sequences],
        2 * tokens * width * (2 * hidden + 4 * width), 24000000, 42)


def turn_call(layer, sequences, length, ids, live, far, q, k, v, halo, h, gradient, wo, wu, wd,
              vec, bias_up):
    tokens, width = q.shape
    hidden = wu.shape[2]

    def kernel(qid_ref, kid_ref, live_ref, far_ref, q_ref, k_ref, v_ref, halo_ref, h_hbm, g_hbm,
               wo_hbm, wu_hbm, wd_hbm, vec_hbm, bu_hbm,
               datt_ref, dfar_ref, dq_ref, dnk_ref, dnv_ref, dhalo_ref, hidden_out,
               h_ref, g_ref, wo_ref, wu_ref, wd_ref, vec_ref, bu_ref, mix_ref, one_ref, low_ref,
               act_ref, n1_ref, r1_ref, dg_ref, n2_ref, r2_ref, nk_ref, nv_ref, ins, outs, sems):
        loads = start_all(copies_of(
            [(h_hbm, h_ref), (vec_hbm.at[layer], vec_ref), (wo_hbm.at[layer], wo_ref),
             (bu_hbm.at[layer], bu_ref), (wu_hbm.at[layer], wu_ref), (wd_hbm.at[layer], wd_ref),
             (g_hbm, g_ref)], ins))
        store = pltpu.make_async_copy(mix_ref, hidden_out, outs.at[0])
        near_forward(sequences, length, (qid_ref, kid_ref), far_ref, q_ref, k_ref, v_ref,
                     halo_ref, nk_ref, nv_ref, mix_ref, sems)
        side = lax.axis_index("seq")
        layer_rest(sequences, length, mix_ref, h_ref, wo_ref, wu_ref, wd_ref,
                   [wait_for(loads, 0, 1, 2), wait_for(loads, 3, 4), wait_for(loads, 5)], vec_ref,
                   bu_ref, one_ref, low_ref, act_ref, n1_ref, r1_ref, dg_ref, n2_ref, r2_ref,
                   (mix_ref,), lambda i: None)
        store.start()

        def given(s, rows):
            places = lax.broadcasted_iota(jnp.int32, (length, 1), 0) + side * length
            return jnp.where(places < live_ref[s], g_ref[rows, :].astype(F32), 0.0)

        nothing = wait_for(loads)
        layer_rest_back(sequences, length, given,
                        [wait_for(loads, 6), nothing, nothing, nothing], n1_ref,
                        r1_ref, dg_ref, n2_ref, r2_ref, wo_ref, wu_ref, wd_ref, vec_ref, one_ref,
                        low_ref, act_ref, datt_ref)
        near_backward(sequences, length, (qid_ref, kid_ref), q_ref, nk_ref, nv_ref, low_ref,
                      dfar_ref, dq_ref, dnk_ref, dnv_ref, dhalo_ref)
        store.wait()

    act, stat = ((tokens, width), BF16), ((tokens, 128), F32)
    wide, deep = ((tokens, width), F32), ((tokens, hidden), BF16)
    near_rows = sequences * (WINDOW + SUB)
    near, block = ((near_rows, width), BF16), ((sequences * BLOCK, width), BF16)
    return call(
        kernel, "turn",
        [(VMEM, ids[0]), (VMEM, ids[1]), (SMEM, live), (VMEM, far), (VMEM, q), (VMEM, k),
         (VMEM, v), (VMEM, halo)]
        + [(HBM, item) for item in (h, gradient, wo, wu, wd, vec, bias_up)],
        [(VMEM,) + wide, (VMEM,) + block, (VMEM,) + block, (VMEM, (near_rows, width), F32),
         (VMEM, (near_rows, width), F32), (VMEM, (2, sequences * HALO, width), BF16),
         (HBM,) + act],
        [(h.shape, h.dtype), act, ((width, width), BF16), ((width, hidden), BF16),
         ((hidden, width), BF16), ((8, width), BF16), ((1, hidden), BF16), act, wide, act, deep,
         act, stat, deep, act, stat, near, near, 7, 1, 4 * sequences],
        4 * tokens * width * (2 * hidden + width), 24000000, 40)


def back_far_call(sequences, length, ids, q, k, v, dfar, dq_near, dnk, dnv):
    tokens, width = q.shape

    def kernel(qid_ref, kid_ref, q_ref, k_ref, v_ref, dfar_ref, dqn_ref, dnk_ref, dnv_ref, dq_ref,
               dk_ref, dv_ref):
        far = Side(False, length, (qid_ref, kid_ref))
        side, wide, own = far.side, WINDOW + SUB, WINDOW + SUB - HALO

        def done(s, cols, kept):
            for out, which, other in ((dv_ref, 0, 3), (dk_ref, 1, 2)):
                left = jnp.concatenate([kept[0][which], kept[1][which]], axis=1)
                right = jnp.concatenate([kept[0][other], kept[1][other]], axis=0)
                out[far.keys(s, 0), cols] = dot_nn(left, right)

        def one(s):
            attention_backward(
                far, s, q_ref, k_ref, v_ref, dfar_ref,
                lambda s, sub: rows_at(s * BLOCK + sub * SUB, SUB, SUB), dq_ref, far.queries, done)
            dq_ref[rows_at(s * length + (1 - side) * BLOCK, BLOCK, BLOCK), :] = dqn_ref[
                rows_at(s * BLOCK, BLOCK, BLOCK), :]
            mine = rows_at(s * length + (length - own) * (1 - side), own, 32)
            theirs = rows_at(s * wide + HALO * side, own, 32)
            dk_ref[mine, :] = dk_ref[mine, :] + dnk_ref[theirs, :]
            dv_ref[mine, :] = dv_ref[mine, :] + dnv_ref[theirs, :]

        loop(sequences, one)

    wide = (VMEM, (tokens, width), F32)
    return call(
        kernel, "back_far",
        [(VMEM, item) for item in (ids[2], ids[3], q, k, v, dfar, dq_near, dnk, dnv)],
        [(VMEM, (tokens, width), BF16), wide, wide], [], 4000000000, 16000000, 6)


def back_call(layer, sequences, length, ids, dq, dk, dv, dhalo, datt, u, x, saved, w, a, b, wo, wu,
              wd, vec):
    tokens, width = dq.shape
    hidden, rank = wu.shape[2], a.shape[2]

    def kernel(qid_ref, kid_ref, dq_ref, dk_ref, dv_ref, dhalo_ref, datt_ref, u_hbm, x_hbm,
               n1_hbm, r1_hbm, dg_hbm, n2_hbm, r2_hbm, q_hbm, k_hbm, v_hbm, nk_hbm, nv_hbm, w_hbm,
               a_hbm, b_hbm, wo_hbm, wu_hbm, wd_hbm, vec_hbm,
               datt_out, dfar_ref, dqn_ref, dnk_ref, dnv_ref, dhalo_out, q_ref, k_ref, v_ref,
               grad_out,
               u_ref, x_ref, n1_ref, r1_ref, dg_ref, n2_ref, r2_ref, nk_ref, nv_ref, w_ref,
               a_ref, b_ref, wo_ref, wu_ref, wd_ref, vec_ref, dkb_ref, dvb_ref, du_ref, grad_ref,
               two_ref, low_ref, ins, outs):
        loads = start_all(copies_of(
            [(a_hbm.at[layer + 1], a_ref), (b_hbm.at[layer + 1], b_ref), (u_hbm, u_ref),
             (x_hbm, x_ref), (w_hbm.at[layer + 1], w_ref), (vec_hbm.at[layer], vec_ref),
             (n2_hbm, n2_ref), (r2_hbm, r2_ref), (wd_hbm.at[layer], wd_ref), (dg_hbm, dg_ref),
             (wu_hbm.at[layer], wu_ref), (n1_hbm, n1_ref), (r1_hbm, r1_ref),
             (wo_hbm.at[layer], wo_ref), (q_hbm, q_ref), (nk_hbm, nk_ref), (nv_hbm, nv_ref),
             (k_hbm, k_ref), (v_hbm, v_ref)], ins))
        wait_for(loads, 0, 1, 2, 3)()
        adapter_back(sequences, length, dq_ref, dk_ref, dv_ref, dhalo_ref, u_ref, x_ref,
                     a_ref, b_ref, dkb_ref, dvb_ref, du_ref, grad_ref)
        store = pltpu.make_async_copy(grad_ref, grad_out, outs.at[0])
        store.start()
        down, _, _ = low_rank(a_ref, b_ref)

        def given(s, rows):
            return project_back(rows, rows, datt_ref, dq_ref, dkb_ref, dvb_ref, du_ref, w_ref,
                                down)

        layer_rest_back(sequences, length, given,
                        [wait_for(loads, 4, 5, 6, 7), wait_for(loads, 8, 9), wait_for(loads, 10),
                         wait_for(loads, 11, 12, 13)], n1_ref, r1_ref, dg_ref, n2_ref, r2_ref,
                        wo_ref, wu_ref, wd_ref, vec_ref, two_ref, low_ref, dg_ref, datt_out)
        wait_for(loads, 14, 15, 16)()
        near_backward(sequences, length, (qid_ref, kid_ref), q_ref, nk_ref, nv_ref, low_ref,
                      dfar_ref, dqn_ref, dnk_ref, dnv_ref, dhalo_out)
        wait_for(loads, 17, 18)()
        store.wait()

    act, stat = ((tokens, width), BF16), ((tokens, 128), F32)
    wide, deep = ((tokens, width), F32), ((tokens, hidden), BF16)
    near_rows = sequences * (WINDOW + SUB)
    near, block = ((near_rows, width), BF16), ((sequences * BLOCK, width), BF16)
    small, factors = ((tokens, 2 * rank), BF16), ((2, rank, width), F32)
    grad = ((4 * rank, width), F32)
    return call(
        kernel, "back",
        [(VMEM, item) for item in (ids[0], ids[1], dq, dk, dv, dhalo, datt)]
        + [(HBM, item) for item in (u, x, *saved, w, a, b, wo, wu, wd, vec)],
        [(VMEM,) + wide, (VMEM,) + block, (VMEM,) + block,
         (VMEM, (near_rows, width), F32), (VMEM, (near_rows, width), F32),
         (VMEM, (2, sequences * HALO, width), BF16), (VMEM,) + act, (VMEM,) + act, (VMEM,) + act,
         (HBM,) + grad],
        [small, act, act, stat, deep, act, stat, near, near, ((width, 3 * width), BF16), factors,
         factors, ((width, width), BF16), ((width, hidden), BF16), ((hidden, width), BF16),
         ((8, width), BF16), act, act, small, grad, wide, act, 19, 1],
        2 * tokens * width * (2 * hidden + 4 * width), 24000000, 38)


def last_call(layer, sequences, length, dq, dk, dv, dhalo, u, x, w, a, b, other):
    tokens, width = dq.shape
    rank = a.shape[2]

    def kernel(dq_ref, dk_ref, dv_ref, dhalo_ref, u_hbm, x_hbm, w_hbm, a_hbm, b_hbm, other_hbm,
               dkb_ref, dvb_ref, du_ref, w_ref, down_ref, mine_ref, theirs_ref,
               u_ref, x_ref, a_ref, b_ref, other_ref, grad_ref, sems):
        loads = start_all(copies_of(
            [(a_hbm.at[layer], a_ref), (b_hbm.at[layer], b_ref), (u_hbm, u_ref), (x_hbm, x_ref),
             (other_hbm, other_ref), (w_hbm.at[layer], w_ref)], sems))
        wait_for(loads, 0, 1, 2, 3, 4)()
        adapter_back(sequences, length, dq_ref, dk_ref, dv_ref, dhalo_ref, u_ref, x_ref,
                     a_ref, b_ref, dkb_ref, dvb_ref, du_ref, grad_ref)
        down_ref[...] = low_rank(a_ref, b_ref)[0]
        first = lax.axis_index("seq") == layer
        here, there = grad_ref[...], other_ref[...]
        mine_ref[...] = jnp.where(first, here, there)
        theirs_ref[...] = jnp.where(first, there, here)
        wait_for(loads, 5)()

    act, grad = ((tokens, width), BF16), ((4 * rank, width), F32)
    small, factors = ((tokens, 2 * rank), BF16), ((2, rank, width), F32)
    return call(
        kernel, "adapter_back",
        [(VMEM, dq), (VMEM, dk), (VMEM, dv), (VMEM, dhalo)]
        + [(HBM, item) for item in (u, x, w, a, b, other)],
        [(VMEM,) + act, (VMEM,) + act, (VMEM,) + small, (VMEM, (width, 3 * width), BF16),
         (VMEM, (2 * rank, width), BF16), (VMEM,) + grad, (VMEM,) + grad],
        [small, act, factors, factors, grad, grad, 6], 500000000, 12000000, 8)


def project_back_call(s, sequences, length, datt, dq, dk, dv, du, w, down, out):
    tokens, width = dq.shape

    def kernel(datt_ref, dq_ref, dk_ref, dv_ref, du_ref, w_ref, down_ref, *rest):
        out_hbm, out_ref, sems = rest[-3:]
        rows = slice(s * length, (s + 1) * length)
        out_ref[...] = project_back(rows, rows, datt_ref, dq_ref, dk_ref, dv_ref, du_ref, w_ref,
                                    down_ref[...])
        store = pltpu.make_async_copy(out_ref, out_hbm.at[rows], sems.at[0])
        store.start()
        store.wait()

    args = [(VMEM, item) for item in (datt, dq, dk, dv, du, w, down)]
    return call(
        kernel, "project_back", args + ([] if out is None else [(HBM, out)]),
        [(HBM, (tokens, width), F32)], [((length, width), F32), 1],
        2 * length * width * width * 3, 4000000, 6, {} if out is None else {len(args): 0})[0]


def adam_call(mine, theirs, token_slots, steps, down, up, m_down, v_down, m_up, v_up):
    layers, two, rank, width = down.shape

    def kernel(mine_ref, theirs_ref, steps_ref, down_ref, up_ref, md_ref, vd_ref, mu_ref, vu_ref,
               down_out, up_out, md_out, vd_out, mu_out, vu_out):
        side = lax.axis_index("seq")
        for layer in range(layers):
            for which in range(two):
                for group, (w_ref, m_ref, v_ref, w_out, m_out, v_out, rate, decay) in enumerate((
                    (down_ref, md_ref, vd_ref, down_out, md_out, vd_out, 0.03125, 0.1),
                    (up_ref, mu_ref, vu_ref, up_out, mu_out, vu_out, 0.5, 0.0),
                )):
                    rows = slice((group * two + which) * rank, (group * two + which + 1) * rank)
                    grad = jnp.where(side == layer, mine_ref[rows, :], theirs_ref[rows, :])
                    grad = grad / token_slots
                    step = jnp.full((rank, width), steps_ref[layer, which, group], jnp.int32)
                    correction = 1.0 - jnp.exp2(-step.astype(F32))
                    weight = w_ref[layer, which]
                    moment = 0.5 * m_ref[layer, which] + 0.5 * grad
                    velocity = 0.5 * v_ref[layer, which] + 0.5 * grad * grad
                    size = moment / correction / (jnp.sqrt(velocity / correction) + 1e-08)
                    w_out[layer, which] = weight - rate * (size + decay * weight)
                    m_out[layer, which] = moment
                    v_out[layer, which] = velocity

    shapes = [sds(down.shape, F32)] * 6
    vmem = pl.BlockSpec(memory_space=VMEM)
    return pl.pallas_call(
        kernel, name="adam", out_shape=shapes,
        in_specs=[vmem, vmem, pl.BlockSpec(memory_space=SMEM)] + [vmem] * 6, out_specs=[vmem] * 6,
    )(mine, theirs, steps, down, up, m_down, v_down, m_up, v_up)


def together(*values):
    return lax.optimization_barrier(values)


def sum_while(mine, theirs, work):
    batch = lax.axis_size("batch")
    swap = [(0, 1), (1, 0)]
    mine = mine + lax.ppermute(theirs, "seq", swap)
    done, work, step = None, list(work), 1
    while step < batch:
        come = lax.ppermute(mine, "batch", [(i, i ^ step) for i in range(batch)])
        if work:
            done = work.pop(0)(mine, done)
            come, done = together(come, done)
        mine = mine + come
        step *= 2
    for one in work:
        done = one(mine, done)
    return mine, lax.ppermute(mine, "seq", swap), done


def key_and_query_ids(ids, live, length, swap):
    side = lax.axis_index("seq")
    other = lax.ppermute(ids, "seq", swap)
    halo = jnp.where(side == 0, other[:, :HALO], other[:, length - HALO:])
    own = WINDOW + SUB - HALO
    near = jnp.where(side == 0, jnp.concatenate([ids[:, length - own:], halo], 1),
                     jnp.concatenate([halo, ids[:, :own]], 1)).astype(F32)
    places = jnp.arange(WINDOW + SUB) + jnp.where(side == 0, length - own, length - HALO)
    near = jnp.where(places[None] < live[:, None], near, -1.0)
    values = ids.astype(F32)
    places = jnp.arange(length) + side * length
    far = jnp.where(places[None] < live[:, None], values, -1.0)
    low, high = values[:, :BLOCK], values[:, BLOCK:]
    return (jnp.where(side == 0, high, low), near, jnp.where(side == 0, low, high), far)


def shards(
    first_layer_input,
    output_gradient,
    sentence_pair_index,
    sequence_live_length,
    optimizer_step_count,
    query_key_value_weight,
    attention_output_weight,
    feedforward_up_weight,
    feedforward_down_weight,
    layer_bias_gain_rows,
    feedforward_up_bias,
    adapter_down_factors,
    adapter_up_factors,
    first_moment_down,
    second_moment_down,
    first_moment_up,
    second_moment_up,
):
    sequences, length, width = first_layer_input.shape
    tokens = sequences * length
    swap = [(0, 1), (1, 0)]
    live = sequence_live_length
    a, b = adapter_down_factors, jnp.swapaxes(adapter_up_factors, 2, 3)
    vec = layer_bias_gain_rows
    bias_up = feedforward_up_bias[:, None, :]
    wqkv, wo = query_key_value_weight, attention_output_weight
    wu, wd = feedforward_up_weight, feedforward_down_weight
    ids = key_and_query_ids(sentence_pair_index, live, length, swap)
    shape = (sequences, length)

    x1 = first_layer_input.reshape(tokens, width)
    q1, k1, v1, send, u1 = first_call(0, *shape, x1, wqkv, a, b, vec)
    halo = lax.ppermute(send, "seq", swap)
    far = far_call(*shape, q1, k1, v1, ids)
    q2, k2, v2, send, u2, x2, h1, *saved = middle_call(
        0, *shape, ids, far, q1, k1, v1, halo, x1, wqkv, a, b, wo, wu, wd, vec, bias_up)
    halo = lax.ppermute(send, "seq", swap)
    far = far_call(*shape, q2, k2, v2, ids)
    datt, dfar, dqn, dnk, dnv, dsend, hidden_out = turn_call(
        1, *shape, ids, live, far, q2, k2, v2, halo, h1, output_gradient.reshape(tokens, width),
        wo, wu, wd, vec, bias_up)
    dhalo = lax.ppermute(dsend, "seq", swap)
    dq, dk, dv = back_far_call(*shape, ids, q2, k2, v2, dfar, dqn, dnk, dnv)
    datt, dfar, dqn, dnk, dnv, dsend, q1, k1, v1, grad2 = back_call(
        0, *shape, ids, dq, dk, dv, dhalo, datt, u2, x2, saved, wqkv, a, b, wo, wu, wd, vec)
    dhalo = lax.ppermute(dsend, "seq", swap)
    dq, dk, dv = back_far_call(*shape, ids, q1, k1, v1, dfar, dqn, dnk, dnv)
    dk, dv, du, w1, down1, mine, theirs = last_call(
        0, *shape, dq, dk, dv, dhalo, u1, x1, wqkv, a, b, grad2)

    def part(s):
        def work(token, out):
            now, _ = together(datt, token)
            return project_back_call(s, *shape, now, dq, dk, dv, du, w1, down1, out)

        return work

    mine, theirs, gradient = sum_while(mine, theirs, [part(s) for s in range(sequences)])
    token_slots = tokens * lax.axis_size("seq") * lax.axis_size("batch")
    down, up, m_down, v_down, m_up, v_up = adam_call(
        mine, theirs, token_slots, optimizer_step_count, a, b, first_moment_down,
        second_moment_down, jnp.swapaxes(first_moment_up, 2, 3),
        jnp.swapaxes(second_moment_up, 2, 3))
    return (
        hidden_out.reshape(sequences, length, width),
        gradient.reshape(sequences, length, width),
        down,
        jnp.swapaxes(up, 2, 3),
        m_down,
        v_down,
        jnp.swapaxes(m_up, 2, 3),
        jnp.swapaxes(v_up, 2, 3),
    )


def solution(mesh):
    acts, whole = P("batch", "seq", None), P()
    return jax.shard_map(
        shards,
        mesh=mesh,
        in_specs=(acts, acts, P("batch", "seq"), P("batch")) + (whole,) * 13,
        out_specs=(acts, acts) + (whole,) * 6,
        check_vma=False,
    )
```

```python
import jax
import jax.numpy as jnp
from jax import lax
from jax.experimental import pallas as pl
from jax.experimental.pallas import tpu as pltpu
from jax.sharding import PartitionSpec as P

HEADS = 12
ENCODER_LAYERS = 2
HALO = 96
BLOCK = 128
SUB = 64
WINDOW = 256
QUAD = 256
HEAD_ROWS = 16
MASKED = -1000000000.0
LOG2E = 1.4426950408889634
F32 = jnp.float32
BF16 = jnp.bfloat16


def dot_nn(a, b):
    return lax.dot_general(a, b, (((1,), (0,)), ((), ())), preferred_element_type=F32)


def dot_nt(a, b):
    return lax.dot_general(a, b, (((1,), (1,)), ((), ())), preferred_element_type=F32)


def dot_tn(a, b):
    return lax.dot_general(a, b, (((0,), (0,)), ((), ())), preferred_element_type=F32)


def rows_at(start, size, multiple):
    return pl.ds(pl.multiple_of(start, multiple), size)


def loop(count, body):
    def step(i, carry):
        body(i)
        return carry

    lax.fori_loop(0, count, step, 0)


def picked(row_ref, i):
    row = row_ref[...].astype(F32)
    at = lax.broadcasted_iota(jnp.int32, row.shape, 1) == i
    return jnp.sum(jnp.where(at, row, 0.0), axis=1, keepdims=True)


def column_of(row):
    n = row.shape[1]
    eye = lax.broadcasted_iota(jnp.int32, (n, n), 0) == lax.broadcasted_iota(jnp.int32, (n, n), 1)
    return jnp.sum(jnp.where(eye, row, 0.0), axis=1, keepdims=True)


def low_lanes():
    return (lax.broadcasted_iota(jnp.int32, (SUB, 128), 1) < 64).astype(F32).astype(BF16)


def spread_heads(tile, low):
    zero = jnp.zeros((2 * SUB, 128), BF16)
    high = 1 - low
    left, right = tile[:, :128], tile[:, 128:]
    left = jnp.concatenate([left * low, left * high], axis=0)
    right = jnp.concatenate([right * low, right * high], axis=0)
    return jnp.concatenate([jnp.concatenate([left, zero], axis=1),
                            jnp.concatenate([zero, right], axis=1)], axis=0)


def gather_heads(wide):
    low = lax.broadcasted_iota(jnp.int32, (SUB, 128), 1) < 64
    parts = []
    for i in range(2):
        cols, top = slice(128 * i, 128 * i + 128), 2 * SUB * i
        parts.append(jnp.where(low, wide[top:top + SUB, cols],
                               wide[top + SUB:top + 2 * SUB, cols]))
    return jnp.concatenate(parts, axis=1)


def pipelined(units):
    units = list(units)
    live = []
    while units or live:
        if units:
            live.append(units.pop(0))
        for unit in list(live):
            if next(unit, None) is None:
                live.remove(unit)


class Side:
    def __init__(self, near, length, ids_refs):
        self.near, self.length, self.ids_refs = near, length, ids_refs
        self.side = lax.axis_index("seq")
        self.row0 = BLOCK * ((1 - self.side) if near else self.side)

    def ids(self, s):
        own_ref, other_ref, live_ref = self.ids_refs
        own = own_ref[pl.ds(s, 1), :].astype(F32)
        query = jnp.where(self.row0 == 0, own[:, :BLOCK], own[:, BLOCK:])
        if self.near:
            other = other_ref[pl.ds(s, 1), :].astype(F32)
            kept = WINDOW + SUB - HALO
            key = jnp.where(
                self.side == 0,
                jnp.concatenate([own[:, self.length - kept:], other[:, :HALO]], axis=1),
                jnp.concatenate([other[:, self.length - HALO:], own[:, :kept]], axis=1))
            start = jnp.where(self.side == 0, self.length - kept, self.length - HALO)
        else:
            key, start = own, self.side * self.length
        places = lax.broadcasted_iota(jnp.int32, key.shape, 1) + start
        return query, jnp.where(places.astype(F32) < picked(live_ref, s), key, -1.0)

    def queries(self, s, sub):
        return rows_at(s * self.length + self.row0 + sub * SUB, SUB, SUB)

    def keys(self, s, sub):
        if self.near:
            return rows_at(s * (WINDOW + SUB) + sub * SUB, WINDOW, SUB)
        return rows_at(s * self.length, WINDOW, WINDOW)

    def biases(self, sequences, rows_ref, columns_ref):
        lane = lax.broadcasted_iota(jnp.int32, (1, 128), 1)
        place = jnp.where(lane < SUB, lane, lane - SUB)
        key_place = lax.broadcasted_iota(jnp.int32, (WINDOW, 128), 0)
        shape = (SUB, WINDOW)
        apart = lax.broadcasted_iota(jnp.int32, shape, 1) - lax.broadcasted_iota(jnp.int32, shape, 0)

        def one(s):
            query, key = self.ids(s)
            for sub in range(2):
                own = HALO if self.near else self.row0 + sub * SUB
                if rows_ref is not None:
                    keys = key[:, sub * SUB:sub * SUB + WINDOW] if self.near else key
                    queries = column_of(query)[sub * SUB:(sub + 1) * SUB]
                    seen = (queries == keys) | (apart == own)
                    rows_ref[rows_at((s * 2 + sub) * SUB, SUB, SUB), :] = jnp.where(
                        seen, 0.0, MASKED)
                if columns_ref is None:
                    continue
                blocks = (128, 128, SUB) if self.near else (128, 128)
                column = jnp.concatenate(
                    [column_of(key[:, 128 * i:128 * i + n]) for i, n in enumerate(blocks)], axis=0)
                keys = column[sub * SUB:sub * SUB + WINDOW] if self.near else column
                turned = pltpu.roll(query, SUB, 1)
                pair = (query, turned) if sub == 0 else (turned, query)
                seen = (keys == jnp.where(lane < SUB, *pair)) | (key_place == place + own)
                columns_ref[rows_at((s * 2 + sub) * WINDOW, WINDOW, WINDOW), :] = jnp.where(
                    seen, 0.0, MASKED)

        loop(sequences, one)


def bias_shape(sequences, turned):
    return ((sequences * 2 * WINDOW, 128) if turned else (sequences * 2 * SUB, WINDOW)), F32


def half(sub):
    return slice(4 * SUB * sub, 4 * SUB * (sub + 1))


SLOTS = 2


def attention_scratch():
    return [((SLOTS, WINDOW, 4 * SUB), F32), ((SLOTS, WINDOW, 4 * SUB), BF16)]


def attention_forward(where, s, q_ref, k_ref, v_ref, out_ref, out_rows, bias_ref, scratch):
    low = low_lanes()
    scores_ref, share_ref = scratch[:2]

    def unit(quad, sub):
        cols = slice(QUAD * quad, QUAD * quad + QUAD)
        keys = where.keys(s, sub)
        q4 = spread_heads(q_ref[where.queries(s, sub), cols], low)
        slot = (2 * quad + sub) % SLOTS
        scores_ref[slot] = dot_nt(q4, k_ref[keys, cols])
        yield True
        bias = bias_ref[rows_at((s * 2 + sub) * SUB, SUB, SUB), :]
        totals = []
        for h in range(4):
            rows = slice(h * SUB, (h + 1) * SUB)
            scores = scores_ref[slot, rows, :] + bias
            share = jnp.exp2(scores - jnp.max(scores, axis=1, keepdims=True))
            totals.append(1.0 / jnp.sum(share, axis=1, keepdims=True))
            share_ref[slot, rows, :] = share.astype(BF16)
        yield True
        mixed = dot_nn(share_ref[slot], v_ref[keys, cols])
        mixed = jnp.concatenate(
            [mixed[h * SUB:(h + 1) * SUB] * totals[h] for h in range(4)], axis=0)
        yield True
        out_ref[out_rows(s, sub), cols] = gather_heads(mixed).astype(BF16)

    width = q_ref.shape[1]
    pipelined(unit(quad, sub) for quad in range(width // QUAD) for sub in range(2))


def attention_backward(where, s, q_ref, k_ref, v_ref, dmix_ref, dmix_rows, delta_ref, dq_ref,
                       dq_rows, key_terms, bias_ref):
    low = low_lanes()
    delta = delta_ref[rows_at(s * HEAD_ROWS, HEAD_ROWS, HEAD_ROWS), :]
    delta = jnp.where(where.row0 == 0, delta[:, :BLOCK], delta[:, BLOCK:])
    turned = pltpu.roll(delta, SUB, 1)
    first_half = lax.broadcasted_iota(jnp.int32, (1, 2 * SUB), 1) < SUB

    def unit(quad, sub, kept):
        cols = slice(QUAD * quad, QUAD * quad + QUAD)
        keys = where.keys(s, sub)
        q4 = spread_heads(q_ref[where.queries(s, sub), cols], low)
        d4 = spread_heads(dmix_ref[dmix_rows(s, sub), cols], low)
        scores = dot_nt(k_ref[keys, cols], q4)
        d_share = dot_nt(v_ref[keys, cols], d4)
        yield True
        bias = bias_ref[rows_at((s * 2 + sub) * WINDOW, WINDOW, WINDOW), :]
        shares, d_scores = [], []
        left, right = (delta, turned) if sub == 0 else (turned, delta)
        for i in range(2):
            head = 4 * quad + 2 * i
            drop = jnp.where(first_half, left[head:head + 1], right[head + 1:head + 2])
            part = scores[:, 128 * i:128 * i + 128] + bias
            part = jnp.exp2(part - jnp.max(part, axis=0, keepdims=True))
            part = part * (1.0 / jnp.sum(part, axis=0, keepdims=True))
            shares.append(part.astype(BF16))
            d_scores.append((part * (d_share[:, 128 * i:128 * i + 128] - drop)).astype(BF16))
        d_scores = jnp.concatenate(d_scores, axis=1)
        kept.append((jnp.concatenate(shares, axis=1), d_scores, q4, d4))
        yield True
        d_query = gather_heads(dot_tn(d_scores, k_ref[keys, cols])) * 0.125
        dq_ref[dq_rows(s, sub), cols] = d_query.astype(BF16)
        if sub == 1:
            key_terms(s, cols, kept)

    width = q_ref.shape[1]

    def units():
        for quad in range(width // QUAD):
            kept = []
            for sub in range(2):
                yield unit(quad, sub, kept)

    pipelined(units())


def row_deltas(sequences, length, dmix_ref, mix_ref, delta_ref):
    width = dmix_ref.shape[1]
    shape = (HEAD_ROWS, width)
    own = (lax.broadcasted_iota(jnp.int32, shape, 1) // 64
           == lax.broadcasted_iota(jnp.int32, shape, 0)).astype(F32).astype(BF16)

    def one(s):
        rows = rows_at(s * length, length, length)
        product = dmix_ref[rows, :].astype(F32) * mix_ref[rows, :].astype(F32)
        high = product.astype(BF16)
        rest = (product - high.astype(F32)).astype(BF16)
        delta_ref[rows_at(s * HEAD_ROWS, HEAD_ROWS, HEAD_ROWS), :] = (
            dot_nt(own, high) + dot_nt(own, rest))

    loop(sequences, one)


def near_keys(s, length, k_ref, v_ref, halo_ref, nk_ref, nv_ref):
    side = lax.axis_index("seq")
    wide, own = WINDOW + SUB, WINDOW + SUB - HALO
    given = rows_at(s * HALO, HALO, 32)
    for i, (src, dst) in enumerate(((k_ref, nk_ref), (v_ref, nv_ref))):
        dst[rows_at(s * wide + HALO * side, own, 32), :] = src[
            rows_at(s * length + (length - own) * (1 - side), own, 32), :]
        dst[rows_at(s * wide + own * (1 - side), HALO, 32), :] = halo_ref[i, given, :]


def norm_forward(values, gain, shift):
    center = values - jnp.mean(values, axis=1, keepdims=True)
    spread = jnp.mean(center * center, axis=1, keepdims=True)
    inverse = lax.rsqrt(spread + 1e-05)
    scaled = center * inverse
    return scaled * gain + shift, scaled, inverse


def norm_backward(gradient, scaled, inverse, gain):
    inner = gradient * gain
    return inverse * (
        inner
        - jnp.mean(inner, axis=1, keepdims=True)
        - scaled * jnp.mean(inner * scaled, axis=1, keepdims=True)
    )


def low_rank(a_ref, b_ref):
    down = jnp.concatenate([a_ref[0], a_ref[1]], axis=0).astype(BF16)
    zero = jnp.zeros_like(b_ref[0])
    up_q = jnp.concatenate([b_ref[0], zero], axis=0).astype(BF16)
    up_v = jnp.concatenate([zero, b_ref[1]], axis=0).astype(BF16)
    return down, up_q, up_v


def project_in(sequences, length, x_ref, w_ref, waits, a_ref, b_ref, vec_ref, q_ref, k_ref, v_ref,
               u_ref, send_ref, sent):
    side = lax.axis_index("seq")
    width = x_ref.shape[1]
    waits[0]()
    down, up_q, up_v = low_rank(a_ref, b_ref)
    vec = vec_ref[...].astype(F32)

    def send(s, i, ref):
        taken = rows_at(s * length + (1 - side) * (length - HALO), HALO, 32)
        send_ref[i, rows_at(s * HALO, HALO, 32), :] = ref[taken, :]

    def queries(s):
        rows = rows_at(s * length, length, length)
        x = x_ref[rows, :]
        inner = dot_nt(x, down).astype(BF16)
        u_ref[rows, :] = inner
        q = dot_nn(x, w_ref[:, :width]) + vec[0:1] + 2.0 * dot_nn(inner, up_q)
        q_ref[rows, :] = (q * (0.125 * LOG2E)).astype(BF16)

    def keys(s):
        rows = rows_at(s * length, length, length)
        k_ref[rows, :] = dot_nn(x_ref[rows, :], w_ref[:, width:2 * width]).astype(BF16)
        send(s, 0, k_ref)

    def values(s):
        rows = rows_at(s * length, length, length)
        v = dot_nn(x_ref[rows, :], w_ref[:, 2 * width:]) + vec[1:2]
        v_ref[rows, :] = (v + 2.0 * dot_nn(u_ref[rows, :], up_v)).astype(BF16)
        send(s, 1, v_ref)

    loop(sequences, queries)
    sent()
    waits[1]()
    loop(sequences, keys)
    waits[2]()
    loop(sequences, values)


def layer_rest(layer, sequences, length, mix_ref, h_ref, wo_ref, wu_ref, wd_ref, waits, vec_ref, bu_ref,
               one_ref, low_ref, act_ref, n1_ref, r1_ref, dg_ref, n2_ref, r2_ref, h_outs, sent):
    hidden = wu_ref.shape[1]
    waits[0]()
    vec = vec_ref[...].astype(F32)

    def mixed(s):
        rows = rows_at(s * length, length, length)
        attended = dot_nn(mix_ref[rows, :], wo_ref[...]) + vec[2:3] + h_ref[rows, :].astype(F32)
        one, scaled, inverse = norm_forward(attended, vec[4:5], vec[5:6])
        n1_ref[rows, :] = scaled.astype(n1_ref.dtype)
        r1_ref[rows, :] = jnp.broadcast_to(inverse, (length, 128))
        one_ref[rows, :] = one
        low_ref[rows, :] = one.astype(BF16)

    loop(sequences, mixed)
    sent(0)
    waits[1]()
    tile = 512

    def up(j):
        cols = rows_at(j * tile, tile, tile)
        bias = bu_ref[layer:layer + 1, cols].astype(F32)
        weights = wu_ref[:, cols]

        def unit(s):
            rows = slice(s * length, (s + 1) * length)
            gate = dot_nn(low_ref[rows, :], weights)
            yield True
            gate = gate + bias
            below = 0.5 * lax.erf(gate * 0.7071067811865476) + 0.5
            act_ref[rows, cols] = (gate * below).astype(BF16)
            density = jnp.exp2(gate * gate * -0.7213475204444817) * 0.3989422804014327
            dg_ref[rows, cols] = (below + gate * density).astype(BF16)

        pipelined(unit(s) for s in range(sequences))

    loop(hidden // tile, up)
    sent(1)
    waits[2]()

    def down(s):
        rows = rows_at(s * length, length, length)
        summed = dot_nn(act_ref[rows, :], wd_ref[...]) + vec[3:4] + one_ref[rows, :]
        out, scaled, inverse = norm_forward(summed, vec[6:7], vec[7:8])
        n2_ref[rows, :] = scaled.astype(n2_ref.dtype)
        r2_ref[rows, :] = jnp.broadcast_to(inverse, (length, 128))
        for h_out in h_outs:
            h_out[rows, :] = out.astype(h_out.dtype)

    loop(sequences, down)
    sent(2)


def layer_rest_back(sequences, length, gradient, waits, n1_ref, r1_ref, dg_ref, n2_ref, r2_ref,
                    wo_ref, wu_ref, wd_ref, vec_ref, two_ref, low_ref, gate_ref, datt_ref,
                    mix_ref, delta_ref):
    hidden = wu_ref.shape[1]
    waits[0]()
    vec = vec_ref[...].astype(F32)

    def second(s):
        rows = rows_at(s * length, length, length)
        two = norm_backward(
            gradient(s, rows), n2_ref[rows, :].astype(F32), r2_ref[rows, 0:1], vec[6:7])
        two_ref[rows, :] = two
        low_ref[rows, :] = two.astype(BF16)

    loop(sequences, second)
    waits[1]()
    tile = 512

    def down(j):
        cols = rows_at(j * tile, tile, tile)
        weights = wd_ref[cols, :]

        def unit(s):
            rows = slice(s * length, (s + 1) * length)
            gate = dot_nt(low_ref[rows, :], weights)
            yield True
            gate_ref[rows, cols] = (gate * dg_ref[rows, cols].astype(F32)).astype(BF16)

        pipelined(unit(s) for s in range(sequences))

    loop(hidden // tile, down)
    waits[2]()
    waits[3]()

    def up(s):
        rows = rows_at(s * length, length, length)
        one = dot_nt(gate_ref[rows, :], wu_ref[...]) + two_ref[rows, :]
        att = norm_backward(one, n1_ref[rows, :].astype(F32), r1_ref[rows, 0:1], vec[4:5])
        datt_ref[rows, :] = att
        dmix = dot_nt(att.astype(BF16), wo_ref[...]).astype(BF16)
        low_ref[rows, :] = dmix

    loop(sequences, up)
    row_deltas(sequences, length, low_ref, mix_ref, delta_ref)


def near_backward(near, sequences, length, q_ref, nk_ref, nv_ref, dmix_ref, delta_ref,
                  dfar_ref, dq_ref, dnk_ref, dnv_ref, dhalo_ref, bias_ref):
    side, wide = near.side, WINDOW + SUB

    def key_terms(s, cols, kept):
        for out, which, other in ((dnv_ref, 0, 3), (dnk_ref, 1, 2)):
            left, right = [item[which] for item in kept], [item[other] for item in kept]
            out[rows_at(s * wide, SUB, SUB), cols] = dot_nn(left[0][:SUB], right[0])
            both = jnp.concatenate([left[0][SUB:], left[1][:WINDOW - SUB]], axis=1)
            out[rows_at(s * wide + SUB, WINDOW - SUB, SUB), cols] = dot_nn(
                both, jnp.concatenate(right, axis=0))
            out[rows_at(s * wide + WINDOW, SUB, SUB), cols] = dot_nn(
                left[1][WINDOW - SUB:], right[1])

    def one(s):
        dfar_ref[rows_at(s * BLOCK, BLOCK, BLOCK), :] = dmix_ref[
            rows_at(s * length + side * BLOCK, BLOCK, BLOCK), :]
        attention_backward(
            near, s, q_ref, nk_ref, nv_ref, dmix_ref, near.queries, delta_ref, dq_ref,
            lambda s, sub: rows_at(s * BLOCK + sub * SUB, SUB, SUB), key_terms, bias_ref)
        halo = rows_at(s * wide + (wide - HALO) * (1 - side), HALO, 32)
        dhalo_ref[0, rows_at(s * HALO, HALO, 32), :] = (
            dnk_ref[halo, :] * (1.0 / LOG2E)).astype(BF16)
        dhalo_ref[1, rows_at(s * HALO, HALO, 32), :] = dnv_ref[halo, :].astype(BF16)

    loop(sequences, one)


def adapter_back(sequences, length, waits, dq_ref, dk_ref, dv_ref, dhalo_ref, u_ref, x_ref, a_ref,
                 b_ref, dkb_ref, dvb_ref, du_ref, grad_ref):
    side = lax.axis_index("seq")
    rank = a_ref.shape[1]
    waits[0]()
    _, up_q, up_v = low_rank(a_ref, b_ref)

    def one(s):
        rows = rows_at(s * length, length, length)
        taken = rows_at(s * length + (1 - side) * (length - HALO), HALO, 32)
        hrows = rows_at(s * HALO, HALO, 32)
        dk_ref[rows, :] = dk_ref[rows, :] * (1.0 / LOG2E)
        dk_ref[taken, :] = dk_ref[taken, :] + dhalo_ref[0, hrows, :].astype(F32)
        dv_ref[taken, :] = dv_ref[taken, :] + dhalo_ref[1, hrows, :].astype(F32)
        dkb_ref[rows, :] = dk_ref[rows, :].astype(BF16)
        dv16 = dv_ref[rows, :].astype(BF16)
        dvb_ref[rows, :] = dv16
        du_ref[rows, :] = (2.0 * (dot_nt(dq_ref[rows, :], up_q) + dot_nt(dv16, up_v))).astype(BF16)

    loop(sequences, one)
    waits[1]()
    u = u_ref[...]
    grad_ref[0:2 * rank, :] = dot_tn(du_ref[...], x_ref[...])
    up_q, up_v = dot_tn(u, dq_ref[...]), dot_tn(u, dvb_ref[...])
    grad_ref[2 * rank:3 * rank, :] = 2.0 * up_q[:rank]
    grad_ref[3 * rank:, :] = 2.0 * up_v[rank:]


def project_back(rows, own_rows, datt_ref, dq_ref, dk_ref, dv_ref, du_ref, w_ref, down):
    width = dq_ref.shape[1]
    out = datt_ref[rows, :] + dot_nn(du_ref[rows, :], down)
    out = out + dot_nt(dq_ref[rows, :], w_ref[:, :width])
    out = out + dot_nt(dk_ref[rows, :], w_ref[:, width:2 * width])
    return out + dot_nt(dv_ref[rows, :], w_ref[:, 2 * width:])


HBM, VMEM = pltpu.HBM, pltpu.VMEM


def call(kernel, name, args, outs, scratch, flops, nbytes, limit, aliases=None):
    scratch = [pltpu.SemaphoreType.DMA((s,)) if isinstance(s, int) else pltpu.VMEM(*s)
               for s in scratch]
    return pl.pallas_call(
        kernel,
        name=name,
        out_shape=tuple(space(shape, dtype) for space, shape, dtype in outs),
        in_specs=[pl.BlockSpec(memory_space=space) for space, _ in args],
        out_specs=tuple(pl.BlockSpec(memory_space=space) for space, _, _ in outs),
        scratch_shapes=scratch,
        input_output_aliases=aliases or {},
        compiler_params=pltpu.CompilerParams(vmem_limit_bytes=limit * 1024 * 1024),
        cost_estimate=pl.CostEstimate(flops=flops, bytes_accessed=nbytes, transcendentals=0),
    )(*[pltpu.with_memory_space_constraint(array, space) for space, array in args])


def sds(shape, dtype):
    return jax.ShapeDtypeStruct(shape, dtype)


def copies_of(pairs, sems):
    return [pltpu.make_async_copy(src, dst, sems.at[i]) for i, (src, dst) in enumerate(pairs)]


def start_all(copies):
    for copy in copies:
        copy.start()
    return copies


def wait_for(copies, *which):
    def wait():
        for i in which:
            copies[i].wait()

    return wait


def first_call(layer, sequences, length, x, w, a, b, vec):
    tokens, width = x.shape
    rank = a.shape[2]

    def kernel(x_hbm, w_hbm, a_hbm, b_hbm, vec_hbm, q_ref, k_ref, v_ref, send_ref, u_out, x_ref,
               w_ref, a_ref, b_ref, vec_ref, u_ref, sems, outs):
        thirds = [slice(i * width, (i + 1) * width) for i in range(3)]
        copies = start_all(copies_of(
            [(a_hbm.at[layer], a_ref), (b_hbm.at[layer], b_ref), (vec_hbm.at[layer], vec_ref),
             (x_hbm, x_ref)] + [(w_hbm.at[layer, :, part], w_ref.at[:, part]) for part in thirds],
            sems))
        store = pltpu.make_async_copy(u_ref, u_out, outs.at[0])
        project_in(sequences, length, x_ref, w_ref,
                   [wait_for(copies, 0, 1, 2, 3, 4), wait_for(copies, 5), wait_for(copies, 6)],
                   a_ref, b_ref, vec_ref, q_ref, k_ref, v_ref, u_ref, send_ref, store.start)
        store.wait()

    act, small = (VMEM, (tokens, width), BF16), ((tokens, 2 * rank), BF16)
    return call(
        kernel, "project_in", [(HBM, x), (HBM, w), (HBM, a), (HBM, b), (HBM, vec)],
        [act, act, act, (VMEM, (2, sequences * HALO, width), BF16), (HBM,) + small],
        [((tokens, width), BF16), ((width, 3 * width), BF16), ((2, rank, width), F32),
         ((2, rank, width), F32), ((8, width), BF16), small, 7, 1],
        2 * tokens * width * width * 3, 12000000, 10)


def far_call(sequences, length, q, k, v, ids):
    tokens, width = q.shape

    def kernel(q_ref, k_ref, v_ref, own_ref, live_ref, out_ref, bias_ref, *scratch):
        where = Side(False, length, (own_ref, None, live_ref))
        where.biases(sequences, bias_ref, None)
        loop(sequences, lambda s: attention_forward(
            where, s, q_ref, k_ref, v_ref, out_ref,
            lambda s, sub: rows_at(s * BLOCK + sub * SUB, SUB, SUB), bias_ref, scratch))

    return call(
        kernel, "attention_far", [(VMEM, item) for item in (q, k, v, ids[0])] + [(VMEM, ids[2])],
        [(VMEM, (sequences * BLOCK, width), BF16)],
        [bias_shape(sequences, False)] + attention_scratch(), 2000000000, 6000000, 8)[0]


def near_forward(near, sequences, length, far_ref, q_ref, k_ref, v_ref, halo_ref, nk_ref,
                 nv_ref, mix_ref, bias_ref, scratch):
    def one(s):
        near_keys(s, length, k_ref, v_ref, halo_ref, nk_ref, nv_ref)
        mix_ref[rows_at(s * length + near.side * BLOCK, BLOCK, BLOCK), :] = far_ref[
            rows_at(s * BLOCK, BLOCK, BLOCK), :]
        attention_forward(near, s, q_ref, nk_ref, nv_ref, mix_ref, near.queries, bias_ref,
                          scratch)

    loop(sequences, one)


def middle_call(layer, sequences, length, ids, far, q, k, v, halo, h, w, a, b, wo, wu, wd, vec,
                bias_up):
    tokens, width = q.shape
    hidden, rank = wu.shape[2], a.shape[2]

    def kernel(own_ref, other_ref, live_ref, far_ref, q_ref, k_ref, v_ref, halo_ref, h_hbm, w_hbm, a_hbm,
               b_hbm, wo_hbm, wu_hbm, wd_hbm, vec_hbm, bu_hbm,
               q2_ref, k2_ref, v2_ref, send_ref,
               u_out, x_out, h_out, n1_out, r1_out, dg_out, n2_out, r2_out, q_out, k_out, v_out,
               nk_out, nv_out, mix_out,
               h_ref, w_ref, wo_ref, wu_ref, wd_ref, vec_ref, bu_ref, vec2_ref, a_ref, b_ref,
               u_ref, mix_ref, one_ref, low_ref, act_ref,
               n1_ref, r1_ref, dg_ref, n2_ref, r2_ref, nk_ref, nv_ref, ins, outs, bias_ref,
               *scratch):
        loads = start_all(copies_of(
            [(h_hbm, h_ref), (vec_hbm.at[layer], vec_ref), (wo_hbm.at[layer], wo_ref),
             (bu_hbm, bu_ref), (wu_hbm.at[layer], wu_ref), (wd_hbm.at[layer], wd_ref),
             (w_hbm.at[layer + 1], w_ref), (a_hbm.at[layer + 1], a_ref),
             (b_hbm.at[layer + 1], b_ref), (vec_hbm.at[layer + 1], vec2_ref)], ins))
        stores = copies_of(
            [(q_ref, q_out), (k_ref, k_out), (v_ref, v_out), (nk_ref, nk_out), (nv_ref, nv_out),
             (n1_ref, n1_out), (r1_ref, r1_out), (dg_ref, dg_out), (n2_ref, n2_out),
             (r2_ref, r2_out), (one_ref, h_out), (low_ref, x_out), (u_ref, u_out),
             (mix_ref, mix_out)], outs)
        near = Side(True, length, (own_ref, other_ref, live_ref))
        near.biases(sequences, bias_ref, None)
        near_forward(near, sequences, length, far_ref, q_ref, k_ref, v_ref, halo_ref, nk_ref,
                     nv_ref, mix_ref, bias_ref, scratch)
        layer_rest(layer, sequences, length, mix_ref, h_ref, wo_ref, wu_ref, wd_ref,
                   [wait_for(loads, 0, 1, 2), wait_for(loads, 3, 4), wait_for(loads, 5)], vec_ref,
                   bu_ref, one_ref, low_ref, act_ref, n1_ref, r1_ref, dg_ref, n2_ref, r2_ref,
                   (one_ref, low_ref),
                   lambda i: start_all((stores[:7] + stores[13:], stores[7:8], stores[8:12])[i]))
        nothing = wait_for(loads)
        project_in(sequences, length, low_ref, w_ref,
                   [wait_for(loads, 6, 7, 8, 9), nothing, nothing], a_ref, b_ref, vec2_ref, q2_ref,
                   k2_ref, v2_ref, u_ref, send_ref, stores[12].start)
        for copy in stores:
            copy.wait()

    act, stat = ((tokens, width), BF16), ((tokens, 128), F32)
    wide, deep = ((tokens, width), F32), ((tokens, hidden), BF16)
    near, small = ((sequences * (WINDOW + SUB), width), BF16), ((tokens, 2 * rank), BF16)
    factors = ((2, rank, width), F32)
    return call(
        kernel, "middle",
        [(VMEM, ids[0]), (VMEM, ids[1]), (VMEM, ids[2]), (VMEM, far), (VMEM, q), (VMEM, k), (VMEM, v),
         (VMEM, halo)]
        + [(HBM, item) for item in (h, w, a, b, wo, wu, wd, vec, bias_up)],
        [(VMEM,) + act, (VMEM,) + act, (VMEM,) + act, (VMEM, (2, sequences * HALO, width), BF16)]
        + [(HBM,) + item for item in (small, act, wide, act, stat, deep, act, stat, act, act, act,
                                      near, near, act)],
        [(h.shape, h.dtype), ((width, 3 * width), BF16), ((width, width), BF16),
         ((width, hidden), BF16), ((hidden, width), BF16), ((8, width), BF16),
         (bias_up.shape, BF16), ((8, width), BF16), factors, factors, small, act, wide, act, deep,
         act, stat, deep, act, stat, near, near, 10, 14,
         bias_shape(sequences, False)] + attention_scratch(),
        2 * tokens * width * (2 * hidden + 4 * width), 24000000, 42)


def turn_call(layer, sequences, length, ids, far, q, k, v, halo, h, gradient, wo, wu, wd,
              vec, bias_up):
    tokens, width = q.shape
    hidden = wu.shape[2]

    def kernel(own_ref, other_ref, live_ref, far_ref, q_ref, k_ref, v_ref, halo_ref, h_hbm, g_hbm,
               wo_hbm, wu_hbm, wd_hbm, vec_hbm, bu_hbm,
               datt_ref, dfar_ref, dq_ref, dnk_ref, dnv_ref, dhalo_ref, delta_ref, hidden_out,
               h_ref, g_ref, wo_ref, wu_ref, wd_ref, vec_ref, bu_ref, mix_ref, one_ref, low_ref,
               act_ref, n1_ref, r1_ref, dg_ref, n2_ref, r2_ref, nk_ref, nv_ref, last_ref, ins, outs,
               bias_ref, columns_ref, *scratch):
        loads = start_all(copies_of(
            [(h_hbm, h_ref), (vec_hbm.at[layer], vec_ref), (wo_hbm.at[layer], wo_ref),
             (bu_hbm, bu_ref), (wu_hbm.at[layer], wu_ref), (wd_hbm.at[layer], wd_ref),
             (g_hbm, g_ref)], ins))
        store = pltpu.make_async_copy(last_ref, hidden_out, outs.at[0])
        near = Side(True, length, (own_ref, other_ref, live_ref))
        near.biases(sequences, bias_ref, columns_ref)
        near_forward(near, sequences, length, far_ref, q_ref, k_ref, v_ref, halo_ref, nk_ref,
                     nv_ref, mix_ref, bias_ref, scratch)
        side = lax.axis_index("seq")
        layer_rest(layer, sequences, length, mix_ref, h_ref, wo_ref, wu_ref, wd_ref,
                   [wait_for(loads, 0, 1, 2), wait_for(loads, 3, 4), wait_for(loads, 5)], vec_ref,
                   bu_ref, one_ref, low_ref, act_ref, n1_ref, r1_ref, dg_ref, n2_ref, r2_ref,
                   (last_ref,), lambda i: None)
        store.start()

        def given(s, rows):
            places = lax.broadcasted_iota(jnp.int32, (length, 1), 0) + side * length
            return jnp.where(
                places.astype(F32) < picked(live_ref, s), g_ref[rows, :].astype(F32), 0.0)

        nothing = wait_for(loads)
        layer_rest_back(sequences, length, given,
                        [wait_for(loads, 6), nothing, nothing, nothing], n1_ref,
                        r1_ref, dg_ref, n2_ref, r2_ref, wo_ref, wu_ref, wd_ref, vec_ref, one_ref,
                        low_ref, act_ref, datt_ref, mix_ref, delta_ref)
        near_backward(near, sequences, length, q_ref, nk_ref, nv_ref, low_ref,
                      delta_ref, dfar_ref, dq_ref, dnk_ref, dnv_ref, dhalo_ref, columns_ref)
        store.wait()

    act, stat = ((tokens, width), BF16), ((tokens, 128), F32)
    wide, deep = ((tokens, width), F32), ((tokens, hidden), BF16)
    near_rows = sequences * (WINDOW + SUB)
    near, block = ((near_rows, width), BF16), ((sequences * BLOCK, width), BF16)
    return call(
        kernel, "turn",
        [(VMEM, ids[0]), (VMEM, ids[1]), (VMEM, ids[2]), (VMEM, far), (VMEM, q), (VMEM, k),
         (VMEM, v), (VMEM, halo)]
        + [(HBM, item) for item in (h, gradient, wo, wu, wd, vec, bias_up)],
        [(VMEM,) + wide, (VMEM,) + block, (VMEM,) + block, (VMEM, (near_rows, width), F32),
         (VMEM, (near_rows, width), F32), (VMEM, (2, sequences * HALO, width), BF16),
         (VMEM, (HEAD_ROWS * sequences, length), F32), (HBM,) + act],
        [(h.shape, h.dtype), act, ((width, width), BF16), ((width, hidden), BF16),
         ((hidden, width), BF16), ((8, width), BF16), (bias_up.shape, BF16), act, wide, act, deep,
         act, stat, deep, act, stat, near, near, act, 7, 1, bias_shape(sequences, False),
         bias_shape(sequences, True)] + attention_scratch(),
        4 * tokens * width * (2 * hidden + width), 24000000, 42)


def back_far_call(sequences, length, ids, q, k, v, dfar, delta, dq_near, dnk, dnv):
    tokens, width = q.shape

    def kernel(own_ref, live_ref, q_ref, k_ref, v_ref, dfar_ref, delta_ref, dqn_ref, dnk_ref,
               dnv_ref, dq_ref, dk_ref, dv_ref, bias_ref):
        far = Side(False, length, (own_ref, None, live_ref))
        far.biases(sequences, None, bias_ref)
        side, wide, own = far.side, WINDOW + SUB, WINDOW + SUB - HALO

        def key_terms(s, cols, kept):
            for out, which, other in ((dv_ref, 0, 3), (dk_ref, 1, 2)):
                left = jnp.concatenate([item[which] for item in kept], axis=1)
                right = jnp.concatenate([item[other] for item in kept], axis=0)
                out[far.keys(s, 0), cols] = dot_nn(left, right)

        def one(s):
            attention_backward(
                far, s, q_ref, k_ref, v_ref, dfar_ref,
                lambda s, sub: rows_at(s * BLOCK + sub * SUB, SUB, SUB), delta_ref, dq_ref,
                far.queries, key_terms, bias_ref)
            dq_ref[rows_at(s * length + (1 - side) * BLOCK, BLOCK, BLOCK), :] = dqn_ref[
                rows_at(s * BLOCK, BLOCK, BLOCK), :]
            mine = rows_at(s * length + (length - own) * (1 - side), own, 32)
            theirs = rows_at(s * wide + HALO * side, own, 32)
            dk_ref[mine, :] = dk_ref[mine, :] + dnk_ref[theirs, :]
            dv_ref[mine, :] = dv_ref[mine, :] + dnv_ref[theirs, :]

        loop(sequences, one)

    wide = (VMEM, (tokens, width), F32)
    return call(
        kernel, "back_far",
        [(VMEM, ids[0]), (VMEM, ids[2])]
        + [(VMEM, item) for item in (q, k, v, dfar, delta, dq_near, dnk, dnv)],
        [(VMEM, (tokens, width), BF16), wide, wide],
        [bias_shape(sequences, True)], 4000000000, 16000000, 8)


def back_call(layer, sequences, length, ids, dq, dk, dv, dhalo, datt, u, x, saved, w, a, b, wo, wu,
              wd, vec):
    tokens, width = dq.shape
    hidden, rank = wu.shape[2], a.shape[2]

    def kernel(own_ref, other_ref, live_ref, dq_ref, dk_ref, dv_ref, dhalo_ref, datt_ref, u_hbm, x_hbm,
               n1_hbm, r1_hbm, dg_hbm, n2_hbm, r2_hbm, q_hbm, k_hbm, v_hbm, nk_hbm, nv_hbm, mix_hbm,
               w_hbm, a_hbm, b_hbm, wo_hbm, wu_hbm, wd_hbm, vec_hbm,
               datt_out, dfar_ref, dqn_ref, dnk_ref, dnv_ref, dhalo_out, delta_ref, q_ref, k_ref,
               v_ref, grad_out,
               u_ref, x_ref, n1_ref, r1_ref, dg_ref, n2_ref, r2_ref, nk_ref, nv_ref, w_ref,
               a_ref, b_ref, wo_ref, wu_ref, wd_ref, vec_ref, dkb_ref, dvb_ref, du_ref, grad_ref,
               two_ref, low_ref, mix_ref, ins, outs, bias_ref):
        loads = start_all(copies_of(
            [(a_hbm.at[layer + 1], a_ref), (b_hbm.at[layer + 1], b_ref), (u_hbm, u_ref),
             (x_hbm, x_ref), (w_hbm.at[layer + 1], w_ref), (vec_hbm.at[layer], vec_ref),
             (n2_hbm, n2_ref), (r2_hbm, r2_ref), (wd_hbm.at[layer], wd_ref), (dg_hbm, dg_ref),
             (wu_hbm.at[layer], wu_ref), (n1_hbm, n1_ref), (r1_hbm, r1_ref),
             (wo_hbm.at[layer], wo_ref), (q_hbm, q_ref), (nk_hbm, nk_ref), (nv_hbm, nv_ref),
             (k_hbm, k_ref), (v_hbm, v_ref), (mix_hbm, mix_ref)], ins))
        adapter_back(sequences, length, [wait_for(loads, 0, 1), wait_for(loads, 2, 3)], dq_ref, dk_ref, dv_ref, dhalo_ref, u_ref, x_ref,
                     a_ref, b_ref, dkb_ref, dvb_ref, du_ref, grad_ref)
        store = pltpu.make_async_copy(grad_ref, grad_out, outs.at[0])
        store.start()
        down, _, _ = low_rank(a_ref, b_ref)

        def given(s, rows):
            return project_back(rows, rows, datt_ref, dq_ref, dkb_ref, dvb_ref, du_ref, w_ref,
                                down)

        layer_rest_back(sequences, length, given,
                        [wait_for(loads, 4, 5, 6, 7), wait_for(loads, 8, 9), wait_for(loads, 10),
                         wait_for(loads, 11, 12, 13, 19)], n1_ref, r1_ref, dg_ref, n2_ref, r2_ref,
                        wo_ref, wu_ref, wd_ref, vec_ref, two_ref, low_ref, dg_ref, datt_out,
                        mix_ref, delta_ref)
        wait_for(loads, 14, 15, 16)()
        near = Side(True, length, (own_ref, other_ref, live_ref))
        near.biases(sequences, None, bias_ref)
        near_backward(near, sequences, length, q_ref, nk_ref, nv_ref, low_ref,
                      delta_ref, dfar_ref, dqn_ref, dnk_ref, dnv_ref, dhalo_out, bias_ref)
        wait_for(loads, 17, 18)()
        store.wait()

    act, stat = ((tokens, width), BF16), ((tokens, 128), F32)
    wide, deep = ((tokens, width), F32), ((tokens, hidden), BF16)
    near_rows = sequences * (WINDOW + SUB)
    near, block = ((near_rows, width), BF16), ((sequences * BLOCK, width), BF16)
    small, factors = ((tokens, 2 * rank), BF16), ((2, rank, width), F32)
    grad = ((4 * rank, width), F32)
    return call(
        kernel, "back",
        [(VMEM, ids[0]), (VMEM, ids[1]), (VMEM, ids[2])]
        + [(VMEM, item) for item in (dq, dk, dv, dhalo, datt)]
        + [(HBM, item) for item in (u, x, *saved, w, a, b, wo, wu, wd, vec)],
        [(VMEM,) + wide, (VMEM,) + block, (VMEM,) + block,
         (VMEM, (near_rows, width), F32), (VMEM, (near_rows, width), F32),
         (VMEM, (2, sequences * HALO, width), BF16), (VMEM, (HEAD_ROWS * sequences, length), F32),
         (VMEM,) + act, (VMEM,) + act, (VMEM,) + act,
         (HBM,) + grad],
        [small, act, act, stat, deep, act, stat, near, near, ((width, 3 * width), BF16), factors,
         factors, ((width, width), BF16), ((width, hidden), BF16), ((hidden, width), BF16),
         ((8, width), BF16), act, act, small, grad, wide, act, act, 20, 1, bias_shape(sequences, True)],
        2 * tokens * width * (2 * hidden + 4 * width), 24000000, 38)


def last_call(layer, sequences, length, dq, dk, dv, dhalo, u, x, w, a, b, other, *state):
    tokens, width = dq.shape
    rank = a.shape[2]

    def kernel(dq_ref, dk_ref, dv_ref, dhalo_ref, u_hbm, x_hbm, w_hbm, a_hbm, b_hbm, other_hbm,
               *rest):
        given, rest = rest[:len(state)], rest[len(state):]
        (dkb_ref, dvb_ref, du_ref, w_ref, down_ref, mine_ref, theirs_ref), rest = rest[:7], rest[7:]
        taken, rest = rest[:len(state)], rest[len(state):]
        u_ref, x_ref, a_ref, b_ref, other_ref, grad_ref, sems, state_sems = rest
        loads = start_all(copies_of(
            [(a_hbm.at[layer], a_ref), (b_hbm.at[layer], b_ref), (u_hbm, u_ref), (x_hbm, x_ref),
             (other_hbm, other_ref), (w_hbm.at[layer], w_ref)], sems))
        more = start_all(copies_of(zip(given, taken), state_sems))
        adapter_back(sequences, length, [wait_for(loads, 0, 1), wait_for(loads, 2, 3)], dq_ref, dk_ref, dv_ref, dhalo_ref, u_ref, x_ref,
                     a_ref, b_ref, dkb_ref, dvb_ref, du_ref, grad_ref)
        down_ref[...] = low_rank(a_ref, b_ref)[0]
        wait_for(loads, 4)()
        first = lax.axis_index("seq") == layer
        here, there = grad_ref[...], other_ref[...]
        mine_ref[...] = jnp.where(first, here, there)
        theirs_ref[...] = jnp.where(first, there, here)
        wait_for(loads, 5)()
        for copy in more:
            copy.wait()

    act, grad = ((tokens, width), BF16), ((4 * rank, width), F32)
    small, factors = ((tokens, 2 * rank), BF16), ((2, rank, width), F32)
    return call(
        kernel, "adapter_back",
        [(VMEM, dq), (VMEM, dk), (VMEM, dv), (VMEM, dhalo)]
        + [(HBM, item) for item in (u, x, w, a, b, other, *state)],
        [(VMEM,) + act, (VMEM,) + act, (VMEM,) + small, (VMEM, (width, 3 * width), BF16),
         (VMEM, (2 * rank, width), BF16), (VMEM,) + grad, (VMEM,) + grad]
        + [(VMEM, item.shape, F32) for item in state],
        [small, act, factors, factors, grad, grad, 6, len(state)], 500000000, 12000000, 8)


def project_back_call(part, parts, datt, dq, dk, dv, du, w, down, out):
    tokens, width = dq.shape
    length = tokens // parts

    def kernel(datt_ref, dq_ref, dk_ref, dv_ref, du_ref, w_ref, down_ref, *rest):
        out_hbm, out_ref, sems = rest[-3:]
        rows = slice(part * length, (part + 1) * length)
        out_ref[...] = project_back(rows, rows, datt_ref, dq_ref, dk_ref, dv_ref, du_ref, w_ref,
                                    down_ref[...])
        store = pltpu.make_async_copy(out_ref, out_hbm.at[rows], sems.at[0])
        store.start()
        store.wait()

    args = [(VMEM, item) for item in (datt, dq, dk, dv, du, w, down)]
    return call(
        kernel, "project_back", args + ([] if out is None else [(HBM, out)]),
        [(HBM, (tokens, width), F32)], [((length, width), F32), 1],
        2 * length * width * width * 3, 4000000, 6, {} if out is None else {len(args): 0})[0]


def adam_call(mine, theirs, token_slots, steps, down, up, m_down, v_down, m_up, v_up):
    layers, two, rank, width = down.shape

    def kernel(mine_ref, theirs_ref, steps_ref, down_ref, up_ref, md_ref, vd_ref, mu_ref, vu_ref,
               *rest):
        outs, results, sems = rest[:6], rest[6:12], rest[12]
        down_out, up_out, md_out, vd_out, mu_out, vu_out = results
        side = lax.axis_index("seq")
        for layer in range(layers):
            for which in range(two):
                for group, (w_ref, m_ref, v_ref, w_out, m_out, v_out, rate, decay) in enumerate((
                    (down_ref, md_ref, vd_ref, down_out, md_out, vd_out, 0.03125, 0.1),
                    (up_ref, mu_ref, vu_ref, up_out, mu_out, vu_out, 0.5, 0.0),
                )):
                    rows = slice((group * two + which) * rank, (group * two + which + 1) * rank)
                    grad = jnp.where(side == layer, mine_ref[rows, :], theirs_ref[rows, :])
                    grad = grad / token_slots
                    step = picked(steps_ref, (layer * two + which) * 2 + group)
                    correction = jnp.broadcast_to(1.0 - jnp.exp2(-step), (rank, width))
                    weight = w_ref[layer, which]
                    moment = 0.5 * m_ref[layer, which] + 0.5 * grad
                    velocity = 0.5 * v_ref[layer, which] + 0.5 * grad * grad
                    size = moment / correction / (jnp.sqrt(velocity / correction) + 1e-08)
                    w_out[layer, which] = weight - rate * (size + decay * weight)
                    m_out[layer, which] = moment
                    v_out[layer, which] = velocity

        for store in start_all(copies_of(zip(results, outs), sems)):
            store.wait()

    return call(
        kernel, "adam",
        [(VMEM, mine), (VMEM, theirs), (VMEM, steps)]
        + [(VMEM, item) for item in (down, up, m_down, v_down, m_up, v_up)],
        [(HBM, down.shape, F32)] * 6, [(down.shape, F32)] * 6 + [6], 1000000, 2000000, 4)


def together(*values):
    return lax.optimization_barrier(values)


def sum_while(mine, theirs, work):
    batch = lax.axis_size("batch")
    swap = [(0, 1), (1, 0)]
    mine = mine + lax.ppermute(theirs, "seq", swap)
    done, work, step = None, list(work), 1
    while step < batch:
        ways = 4 if batch % (4 * step) == 0 else 2
        given = mine.astype(BF16)
        come = [lax.ppermute(given, "batch", [(i, i ^ (step * d)) for i in range(batch)])
                for d in range(1, ways)]
        if work:
            done = work.pop(0)(mine, done)
            *come, done = together(*come, done)
        mine = mine + sum(item.astype(F32) for item in come)
        step *= ways
    for one in work:
        done = one(mine, done)
    return mine, lax.ppermute(mine, "seq", swap), done


def shards(
    first_layer_input,
    output_gradient,
    sentence_pair_index,
    sequence_live_length,
    optimizer_step_count,
    query_key_value_weight,
    attention_output_weight,
    feedforward_up_weight,
    feedforward_down_weight,
    layer_bias_gain_rows,
    feedforward_up_bias,
    adapter_down_factors,
    adapter_up_factors,
    first_moment_down,
    second_moment_down,
    first_moment_up,
    second_moment_up,
):
    sequences, length, width = first_layer_input.shape
    tokens = sequences * length
    swap = [(0, 1), (1, 0)]
    a, b = adapter_down_factors, jnp.swapaxes(adapter_up_factors, 2, 3)
    vec = layer_bias_gain_rows
    bias_up = feedforward_up_bias
    wqkv, wo = query_key_value_weight, attention_output_weight
    wu, wd = feedforward_up_weight, feedforward_down_weight
    ids = (sentence_pair_index, lax.ppermute(sentence_pair_index, "seq", swap),
           sequence_live_length[None, :])
    shape = (sequences, length)

    x1 = first_layer_input.reshape(tokens, width)
    q1, k1, v1, send, u1 = first_call(0, *shape, x1, wqkv, a, b, vec)
    halo = lax.ppermute(send, "seq", swap)
    far = far_call(*shape, q1, k1, v1, ids)
    q2, k2, v2, send, u2, x2, h1, *saved = middle_call(
        0, *shape, ids, far, q1, k1, v1, halo, x1, wqkv, a, b, wo, wu, wd, vec, bias_up)
    halo = lax.ppermute(send, "seq", swap)
    far = far_call(*shape, q2, k2, v2, ids)
    datt, dfar, dqn, dnk, dnv, dsend, delta, hidden_out = turn_call(
        1, *shape, ids, far, q2, k2, v2, halo, h1, output_gradient.reshape(tokens, width),
        wo, wu, wd, vec, bias_up)
    dhalo = lax.ppermute(dsend, "seq", swap)
    dq, dk, dv = back_far_call(*shape, ids, q2, k2, v2, dfar, delta, dqn, dnk, dnv)
    datt, dfar, dqn, dnk, dnv, dsend, delta, q1, k1, v1, grad2 = back_call(
        0, *shape, ids, dq, dk, dv, dhalo, datt, u2, x2, saved, wqkv, a, b, wo, wu, wd, vec)
    dhalo = lax.ppermute(dsend, "seq", swap)
    dq, dk, dv = back_far_call(*shape, ids, q1, k1, v1, dfar, delta, dqn, dnk, dnv)
    dk, dv, du, w1, down1, mine, theirs, *state = last_call(
        0, *shape, dq, dk, dv, dhalo, u1, x1, wqkv, a, b, grad2, a, b, first_moment_down,
        second_moment_down, jnp.swapaxes(first_moment_up, 2, 3),
        jnp.swapaxes(second_moment_up, 2, 3))

    def part(i, parts):
        def work(token, out):
            now, _ = together(datt, token)
            return project_back_call(i, parts, now, dq, dk, dv, du, w1, down1, out)

        return work

    mine, theirs, gradient = sum_while(mine, theirs, [part(i, 2) for i in range(2)])
    token_slots = tokens * lax.axis_size("seq") * lax.axis_size("batch")
    down, up, m_down, v_down, m_up, v_up = adam_call(
        mine, theirs, token_slots, optimizer_step_count.reshape(1, -1), *state)
    return (
        hidden_out.reshape(sequences, length, width),
        gradient.reshape(sequences, length, width),
        down,
        jnp.swapaxes(up, 2, 3),
        m_down,
        v_down,
        jnp.swapaxes(m_up, 2, 3),
        jnp.swapaxes(v_up, 2, 3),
    )


def solution(mesh):
    acts, whole = P("batch", "seq", None), P()
    return jax.shard_map(
        shards,
        mesh=mesh,
        in_specs=(acts, acts, P("batch", "seq"), P("batch")) + (whole,) * 13,
        out_specs=(acts, acts) + (whole,) * 6,
        check_vma=False,
    )
```

```python
import jax
import jax.numpy as jnp
from jax import lax
from jax.experimental import pallas as pl
from jax.experimental.pallas import tpu as pltpu
from jax.sharding import PartitionSpec as P

HEADS = 12
ENCODER_LAYERS = 2
HALO = 96
BLOCK = 128
SUB = 64
WINDOW = 256
QUAD = 256
HEAD_ROWS = 16
MASKED = -1000000000.0
LOG2E = 1.4426950408889634
HALF_ROOT_PI = 0.886226925452758
ROOT_HALF = 0.7071067811865476
ACTIVE = 0.7978845608028654
SLOPE = 0.5641895835477563
F32 = jnp.float32
BF16 = jnp.bfloat16


def dot_nn(a, b):
    return lax.dot_general(a, b, (((1,), (0,)), ((), ())), preferred_element_type=F32)


def dot_nt(a, b):
    return lax.dot_general(a, b, (((1,), (1,)), ((), ())), preferred_element_type=F32)


def dot_tn(a, b):
    return lax.dot_general(a, b, (((0,), (0,)), ((), ())), preferred_element_type=F32)


def rows_at(start, size, multiple):
    return pl.ds(pl.multiple_of(start, multiple), size)


def loop(count, body):
    def step(i, carry):
        body(i)
        return carry

    lax.fori_loop(0, count, step, 0)


def picked(row_ref, i):
    row = row_ref[...].astype(F32)
    at = lax.broadcasted_iota(jnp.int32, row.shape, 1) == i
    return jnp.sum(jnp.where(at, row, 0.0), axis=1, keepdims=True)


def column_of(row):
    n = row.shape[1]
    eye = lax.broadcasted_iota(jnp.int32, (n, n), 0) == lax.broadcasted_iota(jnp.int32, (n, n), 1)
    return jnp.sum(jnp.where(eye, row, 0.0), axis=1, keepdims=True)


def low_lanes():
    return (lax.broadcasted_iota(jnp.int32, (SUB, 128), 1) < 64).astype(F32).astype(BF16)


def spread_heads(tile, low):
    zero = jnp.zeros((2 * SUB, 128), BF16)
    high = 1 - low
    left, right = tile[:, :128], tile[:, 128:]
    left = jnp.concatenate([left * low, left * high], axis=0)
    right = jnp.concatenate([right * low, right * high], axis=0)
    return jnp.concatenate([jnp.concatenate([left, zero], axis=1),
                            jnp.concatenate([zero, right], axis=1)], axis=0)


def gather_heads(wide):
    low = lax.broadcasted_iota(jnp.int32, (SUB, 128), 1) < 64
    parts = []
    for i in range(2):
        cols, top = slice(128 * i, 128 * i + 128), 2 * SUB * i
        parts.append(jnp.where(low, wide[top:top + SUB, cols],
                               wide[top + SUB:top + 2 * SUB, cols]))
    return jnp.concatenate(parts, axis=1)


def pipelined(units):
    units = list(units)
    live = []
    while units or live:
        if units:
            live.append(units.pop(0))
        for unit in list(live):
            if next(unit, None) is None:
                live.remove(unit)


class Side:
    def __init__(self, near, length, ids_refs):
        self.near, self.length, self.ids_refs = near, length, ids_refs
        self.side = lax.axis_index("seq")
        self.row0 = BLOCK * ((1 - self.side) if near else self.side)

    def ids(self, s):
        own_ref, other_ref, live_ref = self.ids_refs
        own = own_ref[pl.ds(s, 1), :].astype(F32)
        query = jnp.where(self.row0 == 0, own[:, :BLOCK], own[:, BLOCK:])
        if self.near:
            other = other_ref[pl.ds(s, 1), :].astype(F32)
            kept = WINDOW + SUB - HALO
            key = jnp.where(
                self.side == 0,
                jnp.concatenate([own[:, self.length - kept:], other[:, :HALO]], axis=1),
                jnp.concatenate([other[:, self.length - HALO:], own[:, :kept]], axis=1))
            start = jnp.where(self.side == 0, self.length - kept, self.length - HALO)
        else:
            key, start = own, self.side * self.length
        places = lax.broadcasted_iota(jnp.int32, key.shape, 1) + start
        return query, jnp.where(places.astype(F32) < picked(live_ref, s), key, -1.0)

    def queries(self, s, sub):
        return rows_at(s * self.length + self.row0 + sub * SUB, SUB, SUB)

    def keys(self, s, sub):
        if self.near:
            return rows_at(s * (WINDOW + SUB) + sub * SUB, WINDOW, SUB)
        return rows_at(s * self.length, WINDOW, WINDOW)

    def biases(self, sequences, rows_ref, columns_ref):
        lane = lax.broadcasted_iota(jnp.int32, (1, 128), 1)
        place = jnp.where(lane < SUB, lane, lane - SUB)
        key_place = lax.broadcasted_iota(jnp.int32, (WINDOW, 128), 0)
        shape = (SUB, WINDOW)
        apart = lax.broadcasted_iota(jnp.int32, shape, 1) - lax.broadcasted_iota(jnp.int32, shape, 0)

        def one(s):
            query, key = self.ids(s)
            for sub in range(2):
                own = HALO if self.near else self.row0 + sub * SUB
                if rows_ref is not None:
                    keys = key[:, sub * SUB:sub * SUB + WINDOW] if self.near else key
                    queries = column_of(query)[sub * SUB:(sub + 1) * SUB]
                    seen = (queries == keys) | (apart == own)
                    rows_ref[rows_at((s * 2 + sub) * SUB, SUB, SUB), :] = jnp.where(
                        seen, 0.0, MASKED)
                if columns_ref is None:
                    continue
                blocks = (128, 128, SUB) if self.near else (128, 128)
                column = jnp.concatenate(
                    [column_of(key[:, 128 * i:128 * i + n]) for i, n in enumerate(blocks)], axis=0)
                keys = column[sub * SUB:sub * SUB + WINDOW] if self.near else column
                turned = pltpu.roll(query, SUB, 1)
                pair = (query, turned) if sub == 0 else (turned, query)
                seen = (keys == jnp.where(lane < SUB, *pair)) | (key_place == place + own)
                columns_ref[rows_at((s * 2 + sub) * WINDOW, WINDOW, WINDOW), :] = jnp.where(
                    seen, 0.0, MASKED)

        loop(sequences, one)


def bias_shape(sequences, turned):
    return ((sequences * 2 * WINDOW, 128) if turned else (sequences * 2 * SUB, WINDOW)), F32


def half(sub):
    return slice(4 * SUB * sub, 4 * SUB * (sub + 1))


SLOTS = 2


def attention_scratch():
    return [((SLOTS, WINDOW, 4 * SUB), F32), ((SLOTS, WINDOW, 4 * SUB), BF16)]


def attention_forward(where, s, q_ref, k_ref, v_ref, out_ref, out_rows, bias_ref, scratch):
    low = low_lanes()
    scores_ref, share_ref = scratch[:2]

    def unit(quad, sub):
        cols = slice(QUAD * quad, QUAD * quad + QUAD)
        keys = where.keys(s, sub)
        q4 = spread_heads(q_ref[where.queries(s, sub), cols], low)
        slot = (2 * quad + sub) % SLOTS
        scores_ref[slot] = dot_nt(q4, k_ref[keys, cols])
        yield True
        bias = bias_ref[rows_at((s * 2 + sub) * SUB, SUB, SUB), :]
        totals = []
        for h in range(4):
            rows = slice(h * SUB, (h + 1) * SUB)
            scores = scores_ref[slot, rows, :] + bias
            share = jnp.exp2(scores - jnp.max(scores, axis=1, keepdims=True))
            totals.append(1.0 / jnp.sum(share, axis=1, keepdims=True))
            share_ref[slot, rows, :] = share.astype(BF16)
        yield True
        mixed = dot_nn(share_ref[slot], v_ref[keys, cols])
        mixed = jnp.concatenate(
            [mixed[h * SUB:(h + 1) * SUB] * totals[h] for h in range(4)], axis=0)
        yield True
        out_ref[out_rows(s, sub), cols] = gather_heads(mixed).astype(BF16)

    width = q_ref.shape[1]
    pipelined(unit(quad, sub) for quad in range(width // QUAD) for sub in range(2))


def attention_backward(where, s, q_ref, k_ref, v_ref, dmix_ref, dmix_rows, delta_ref, dq_ref,
                       dq_rows, key_terms, bias_ref):
    low = low_lanes()
    delta = delta_ref[rows_at(s * HEAD_ROWS, HEAD_ROWS, HEAD_ROWS), :]
    delta = jnp.where(where.row0 == 0, delta[:, :BLOCK], delta[:, BLOCK:])
    turned = pltpu.roll(delta, SUB, 1)
    first_half = lax.broadcasted_iota(jnp.int32, (1, 2 * SUB), 1) < SUB

    def unit(quad, sub, kept):
        cols = slice(QUAD * quad, QUAD * quad + QUAD)
        keys = where.keys(s, sub)
        q4 = spread_heads(q_ref[where.queries(s, sub), cols], low)
        d4 = spread_heads(dmix_ref[dmix_rows(s, sub), cols], low)
        scores = dot_nt(k_ref[keys, cols], q4)
        d_share = dot_nt(v_ref[keys, cols], d4)
        yield True
        bias = bias_ref[rows_at((s * 2 + sub) * WINDOW, WINDOW, WINDOW), :]
        shares, d_scores = [], []
        left, right = (delta, turned) if sub == 0 else (turned, delta)
        for i in range(2):
            head = 4 * quad + 2 * i
            drop = jnp.where(first_half, left[head:head + 1], right[head + 1:head + 2])
            part = scores[:, 128 * i:128 * i + 128] + bias
            part = jnp.exp2(part - jnp.max(part, axis=0, keepdims=True))
            part = part * (1.0 / jnp.sum(part, axis=0, keepdims=True))
            shares.append(part.astype(BF16))
            d_scores.append((part * (d_share[:, 128 * i:128 * i + 128] - drop)).astype(BF16))
        d_scores = jnp.concatenate(d_scores, axis=1)
        kept.append((jnp.concatenate(shares, axis=1), d_scores, q4, d4))
        yield True
        d_query = gather_heads(dot_tn(d_scores, k_ref[keys, cols])) * 0.125
        dq_ref[dq_rows(s, sub), cols] = d_query.astype(BF16)
        if sub == 1:
            key_terms(s, cols, kept)

    width = q_ref.shape[1]

    def units():
        for quad in range(width // QUAD):
            kept = []
            for sub in range(2):
                yield unit(quad, sub, kept)

    pipelined(units())


def row_deltas(sequences, length, dmix_ref, mix_ref, delta_ref):
    width = dmix_ref.shape[1]
    shape = (HEAD_ROWS, width)
    own = (lax.broadcasted_iota(jnp.int32, shape, 1) // 64
           == lax.broadcasted_iota(jnp.int32, shape, 0)).astype(F32).astype(BF16)

    def one(s):
        rows = rows_at(s * length, length, length)
        product = dmix_ref[rows, :].astype(F32) * mix_ref[rows, :].astype(F32)
        high = product.astype(BF16)
        rest = (product - high.astype(F32)).astype(BF16)
        delta_ref[rows_at(s * HEAD_ROWS, HEAD_ROWS, HEAD_ROWS), :] = (
            dot_nt(own, high) + dot_nt(own, rest))

    loop(sequences, one)


def near_keys(s, length, k_ref, v_ref, halo_ref, nk_ref, nv_ref):
    side = lax.axis_index("seq")
    wide, own = WINDOW + SUB, WINDOW + SUB - HALO
    given = rows_at(s * HALO, HALO, 32)
    for i, (src, dst) in enumerate(((k_ref, nk_ref), (v_ref, nv_ref))):
        dst[rows_at(s * wide + HALO * side, own, 32), :] = src[
            rows_at(s * length + (length - own) * (1 - side), own, 32), :]
        dst[rows_at(s * wide + own * (1 - side), HALO, 32), :] = halo_ref[i, given, :]


def norm_forward(values, gain, shift):
    center = values - jnp.mean(values, axis=1, keepdims=True)
    spread = jnp.mean(center * center, axis=1, keepdims=True)
    inverse = lax.rsqrt(spread + 1e-05)
    scaled = center * inverse
    return scaled * gain + shift, scaled, inverse


def norm_backward(gradient, scaled, inverse, gain):
    inner = gradient * gain
    return inverse * (
        inner
        - jnp.mean(inner, axis=1, keepdims=True)
        - scaled * jnp.mean(inner * scaled, axis=1, keepdims=True)
    )


def low_rank(a_ref, b_ref):
    down = jnp.concatenate([a_ref[0], a_ref[1]], axis=0).astype(BF16)
    zero = jnp.zeros_like(b_ref[0])
    up_q = jnp.concatenate([b_ref[0], zero], axis=0).astype(BF16)
    up_v = jnp.concatenate([zero, b_ref[1]], axis=0).astype(BF16)
    return down, up_q, up_v


def project_in(sequences, length, x_ref, w_ref, waits, a_ref, b_ref, vec_ref, q_ref, k_ref, v_ref,
               u_ref, send_ref, sent):
    side = lax.axis_index("seq")
    width = x_ref.shape[1]
    waits[0]()
    down, up_q, up_v = low_rank(a_ref, b_ref)
    vec = vec_ref[...].astype(F32)

    tall = x_ref.shape[0] // 2

    def queries(i):
        rows = rows_at(i * tall, tall, 128)
        x = x_ref[rows, :]
        inner = dot_nt(x, down).astype(BF16)
        u_ref[rows, :] = inner
        q = dot_nn(x, w_ref[:, :width]) + vec[0:1] + 2.0 * dot_nn(inner, up_q)
        q_ref[rows, :] = (q * (0.125 * LOG2E)).astype(BF16)

    def keys(i):
        rows = rows_at(i * tall, tall, 128)
        k_ref[rows, :] = dot_nn(x_ref[rows, :], w_ref[:, width:2 * width]).astype(BF16)

    def values(i):
        rows = rows_at(i * tall, tall, 128)
        v = dot_nn(x_ref[rows, :], w_ref[:, 2 * width:]) + vec[1:2]
        v_ref[rows, :] = (v + 2.0 * dot_nn(u_ref[rows, :], up_v)).astype(BF16)

    def send(s):
        taken = rows_at(s * length + (1 - side) * (length - HALO), HALO, 32)
        for i, ref in enumerate((k_ref, v_ref)):
            send_ref[i, rows_at(s * HALO, HALO, 32), :] = ref[taken, :]

    loop(2, queries)
    sent()
    waits[1]()
    loop(2, keys)
    waits[2]()
    loop(2, values)
    loop(sequences, send)


def layer_rest(layer, sequences, length, mix_ref, h_ref, wo_ref, wu_ref, wd_ref, waits, vec_ref, bu_ref,
               one_ref, low_ref, act_ref, n1_ref, r1_ref, dg_ref, n2_ref, r2_ref, h_outs, sent):
    tokens, hidden = mix_ref.shape[0], wu_ref.shape[1]
    waits[0]()
    vec = vec_ref[...].astype(F32)
    short, units = 128, 3

    def mixed(i):
        def unit(k):
            rows = rows_at((i * units + k) * short, short, short)
            attended = dot_nn(mix_ref[rows, :], wo_ref[...]) + vec[2:3] + h_ref[rows, :].astype(F32)
            yield True
            one, scaled, inverse = norm_forward(attended, vec[4:5], vec[5:6])
            n1_ref[rows, :] = scaled.astype(n1_ref.dtype)
            r1_ref[rows, :] = jnp.broadcast_to(inverse, (short, 128))
            one_ref[rows, :] = one
            low_ref[rows, :] = (one * ROOT_HALF).astype(BF16)

        pipelined(unit(k) for k in range(units))

    loop(tokens // short // units, mixed)
    sent(0)
    waits[1]()
    tile = 1024

    def up(j):
        cols = rows_at(j * tile, tile, tile)
        bias = bu_ref[layer:layer + 1, cols].astype(F32) * ROOT_HALF
        weights = wu_ref[:, cols]

        def unit(k):
            rows = slice(k * short, (k + 1) * short)
            gate = dot_nn(low_ref[rows, :], weights)
            yield True
            gate = gate + bias
            below = HALF_ROOT_PI * lax.erf(gate) + HALF_ROOT_PI
            act_ref[rows, cols] = (gate * below).astype(BF16)
            density = jnp.exp2(gate * gate * -LOG2E)
            dg_ref[rows, cols] = (below + gate * density).astype(BF16)

        pipelined(unit(k) for k in range(tokens // short))

    loop(hidden // tile, up)
    sent(1)
    waits[2]()

    def down(s):
        rows = rows_at(s * length, length, length)
        summed = dot_nn(act_ref[rows, :], wd_ref[...]) * ACTIVE + vec[3:4] + one_ref[rows, :]
        out, scaled, inverse = norm_forward(summed, vec[6:7], vec[7:8])
        n2_ref[rows, :] = scaled.astype(n2_ref.dtype)
        r2_ref[rows, :] = jnp.broadcast_to(inverse, (length, 128))
        for h_out in h_outs:
            h_out[rows, :] = out.astype(h_out.dtype)

    loop(sequences, down)
    sent(2)


def layer_rest_back(sequences, length, gradient, waits, n1_ref, r1_ref, dg_ref, n2_ref, r2_ref,
                    wo_ref, wu_ref, wd_ref, vec_ref, two_ref, low_ref, gate_ref, datt_ref,
                    mix_ref, delta_ref):
    tokens, hidden = low_ref.shape[0], wu_ref.shape[1]
    waits[0]()
    vec = vec_ref[...].astype(F32)
    tall = tokens // 2

    def second(s):
        rows = rows_at(s * length, length, length)
        two = norm_backward(
            gradient(s, rows), n2_ref[rows, :].astype(F32), r2_ref[rows, 0:1], vec[6:7])
        two_ref[rows, :] = two
        low_ref[rows, :] = (two * SLOPE).astype(BF16)

    loop(sequences, second)
    waits[1]()
    tile = 1024

    def down(j):
        cols = rows_at(j * tile, tile, tile)
        weights = wd_ref[cols, :]

        def unit(s):
            rows = slice(s * length, (s + 1) * length)
            gate = dot_nt(low_ref[rows, :], weights)
            yield True
            gate_ref[rows, cols] = (gate * dg_ref[rows, cols].astype(F32)).astype(BF16)

        pipelined(unit(s) for s in range(sequences))

    loop(hidden // tile, down)
    waits[2]()
    waits[3]()

    def up(i):
        rows = rows_at(i * tall, tall, 128)
        datt_ref[rows, :] = dot_nt(gate_ref[rows, :], wu_ref[...])

    def first(s):
        rows = rows_at(s * length, length, length)
        att = norm_backward(datt_ref[rows, :] + two_ref[rows, :], n1_ref[rows, :].astype(F32),
                            r1_ref[rows, 0:1], vec[4:5])
        datt_ref[rows, :] = att
        low_ref[rows, :] = att.astype(BF16)

    def mixture(i):
        rows = rows_at(i * tall, tall, 128)
        low_ref[rows, :] = dot_nt(low_ref[rows, :], wo_ref[...]).astype(BF16)

    loop(2, up)
    loop(sequences, first)
    loop(2, mixture)
    row_deltas(sequences, length, low_ref, mix_ref, delta_ref)


def near_backward(near, sequences, length, q_ref, nk_ref, nv_ref, dmix_ref, delta_ref,
                  dfar_ref, dq_ref, dnk_ref, dnv_ref, dhalo_ref, bias_ref):
    side, wide = near.side, WINDOW + SUB

    def key_terms(s, cols, kept):
        for out, which, other in ((dnv_ref, 0, 3), (dnk_ref, 1, 2)):
            left, right = [item[which] for item in kept], [item[other] for item in kept]
            out[rows_at(s * wide, SUB, SUB), cols] = dot_nn(left[0][:SUB], right[0])
            both = jnp.concatenate([left[0][SUB:], left[1][:WINDOW - SUB]], axis=1)
            out[rows_at(s * wide + SUB, WINDOW - SUB, SUB), cols] = dot_nn(
                both, jnp.concatenate(right, axis=0))
            out[rows_at(s * wide + WINDOW, SUB, SUB), cols] = dot_nn(
                left[1][WINDOW - SUB:], right[1])

    def one(s):
        dfar_ref[rows_at(s * BLOCK, BLOCK, BLOCK), :] = dmix_ref[
            rows_at(s * length + side * BLOCK, BLOCK, BLOCK), :]
        attention_backward(
            near, s, q_ref, nk_ref, nv_ref, dmix_ref, near.queries, delta_ref, dq_ref,
            lambda s, sub: rows_at(s * BLOCK + sub * SUB, SUB, SUB), key_terms, bias_ref)
        halo = rows_at(s * wide + (wide - HALO) * (1 - side), HALO, 32)
        dhalo_ref[0, rows_at(s * HALO, HALO, 32), :] = (
            dnk_ref[halo, :] * (1.0 / LOG2E)).astype(BF16)
        dhalo_ref[1, rows_at(s * HALO, HALO, 32), :] = dnv_ref[halo, :].astype(BF16)

    loop(sequences, one)


def adapter_back(sequences, length, waits, dq_ref, dk_ref, dv_ref, dhalo_ref, u_ref, x_ref, a_ref,
                 b_ref, dkb_ref, dvb_ref, du_ref, grad_ref):
    side = lax.axis_index("seq")
    rank = a_ref.shape[1]
    waits[0]()
    _, up_q, up_v = low_rank(a_ref, b_ref)

    def one(s):
        rows = rows_at(s * length, length, length)
        taken = rows_at(s * length + (1 - side) * (length - HALO), HALO, 32)
        hrows = rows_at(s * HALO, HALO, 32)
        dk_ref[rows, :] = dk_ref[rows, :] * (1.0 / LOG2E)
        dk_ref[taken, :] = dk_ref[taken, :] + dhalo_ref[0, hrows, :].astype(F32)
        dv_ref[taken, :] = dv_ref[taken, :] + dhalo_ref[1, hrows, :].astype(F32)
        dkb_ref[rows, :] = dk_ref[rows, :].astype(BF16)
        dv16 = dv_ref[rows, :].astype(BF16)
        dvb_ref[rows, :] = dv16
        du_ref[rows, :] = (2.0 * (dot_nt(dq_ref[rows, :], up_q) + dot_nt(dv16, up_v))).astype(BF16)

    loop(sequences, one)
    waits[1]()
    u = u_ref[...]
    grad_ref[0:2 * rank, :] = dot_tn(du_ref[...], x_ref[...])
    up_q, up_v = dot_tn(u, dq_ref[...]), dot_tn(u, dvb_ref[...])
    grad_ref[2 * rank:3 * rank, :] = 2.0 * up_q[:rank]
    grad_ref[3 * rank:, :] = 2.0 * up_v[rank:]


def project_back(rows, own_rows, datt_ref, dq_ref, dk_ref, dv_ref, du_ref, w_ref, down):
    width = dq_ref.shape[1]
    out = datt_ref[rows, :] + dot_nn(du_ref[rows, :], down)
    out = out + dot_nt(dq_ref[rows, :], w_ref[:, :width])
    out = out + dot_nt(dk_ref[rows, :], w_ref[:, width:2 * width])
    return out + dot_nt(dv_ref[rows, :], w_ref[:, 2 * width:])


HBM, VMEM = pltpu.HBM, pltpu.VMEM


def call(kernel, name, args, outs, scratch, flops, nbytes, limit, aliases=None):
    scratch = [pltpu.SemaphoreType.DMA((s,)) if isinstance(s, int) else pltpu.VMEM(*s)
               for s in scratch]
    return pl.pallas_call(
        kernel,
        name=name,
        out_shape=tuple(space(shape, dtype) for space, shape, dtype in outs),
        in_specs=[pl.BlockSpec(memory_space=space) for space, _ in args],
        out_specs=tuple(pl.BlockSpec(memory_space=space) for space, _, _ in outs),
        scratch_shapes=scratch,
        input_output_aliases=aliases or {},
        compiler_params=pltpu.CompilerParams(vmem_limit_bytes=limit * 1024 * 1024),
        cost_estimate=pl.CostEstimate(flops=flops, bytes_accessed=nbytes, transcendentals=0),
    )(*[pltpu.with_memory_space_constraint(array, space) for space, array in args])


def sds(shape, dtype):
    return jax.ShapeDtypeStruct(shape, dtype)


def copies_of(pairs, sems):
    return [pltpu.make_async_copy(src, dst, sems.at[i]) for i, (src, dst) in enumerate(pairs)]


def start_all(copies):
    for copy in copies:
        copy.start()
    return copies


def wait_for(copies, *which):
    def wait():
        for i in which:
            copies[i].wait()

    return wait


def first_call(layer, sequences, length, x, w, a, b, vec):
    tokens, width = x.shape
    rank = a.shape[2]

    def kernel(x_hbm, w_hbm, a_hbm, b_hbm, vec_hbm, q_ref, k_ref, v_ref, send_ref, u_out, x_ref,
               w_ref, a_ref, b_ref, vec_ref, u_ref, sems, outs):
        thirds = [slice(i * width, (i + 1) * width) for i in range(3)]
        copies = start_all(copies_of(
            [(a_hbm.at[layer], a_ref), (b_hbm.at[layer], b_ref), (vec_hbm.at[layer], vec_ref),
             (x_hbm, x_ref)] + [(w_hbm.at[layer, :, part], w_ref.at[:, part]) for part in thirds],
            sems))
        store = pltpu.make_async_copy(u_ref, u_out, outs.at[0])
        project_in(sequences, length, x_ref, w_ref,
                   [wait_for(copies, 0, 1, 2, 3, 4), wait_for(copies, 5), wait_for(copies, 6)],
                   a_ref, b_ref, vec_ref, q_ref, k_ref, v_ref, u_ref, send_ref, store.start)
        store.wait()

    act, small = (VMEM, (tokens, width), BF16), ((tokens, 2 * rank), BF16)
    return call(
        kernel, "project_in", [(HBM, x), (HBM, w), (HBM, a), (HBM, b), (HBM, vec)],
        [act, act, act, (VMEM, (2, sequences * HALO, width), BF16), (HBM,) + small],
        [((tokens, width), BF16), ((width, 3 * width), BF16), ((2, rank, width), F32),
         ((2, rank, width), F32), ((8, width), BF16), small, 7, 1],
        2 * tokens * width * width * 3, 12000000, 10)


def far_call(sequences, length, q, k, v, ids):
    tokens, width = q.shape

    def kernel(q_ref, k_ref, v_ref, own_ref, live_ref, out_ref, bias_ref, *scratch):
        where = Side(False, length, (own_ref, None, live_ref))
        where.biases(sequences, bias_ref, None)
        loop(sequences, lambda s: attention_forward(
            where, s, q_ref, k_ref, v_ref, out_ref,
            lambda s, sub: rows_at(s * BLOCK + sub * SUB, SUB, SUB), bias_ref, scratch))

    return call(
        kernel, "attention_far", [(VMEM, item) for item in (q, k, v, ids[0])] + [(VMEM, ids[2])],
        [(VMEM, (sequences * BLOCK, width), BF16)],
        [bias_shape(sequences, False)] + attention_scratch(), 2000000000, 6000000, 8)[0]


def near_forward(near, sequences, length, far_ref, q_ref, k_ref, v_ref, halo_ref, nk_ref,
                 nv_ref, mix_ref, bias_ref, scratch):
    def one(s):
        near_keys(s, length, k_ref, v_ref, halo_ref, nk_ref, nv_ref)
        mix_ref[rows_at(s * length + near.side * BLOCK, BLOCK, BLOCK), :] = far_ref[
            rows_at(s * BLOCK, BLOCK, BLOCK), :]
        attention_forward(near, s, q_ref, nk_ref, nv_ref, mix_ref, near.queries, bias_ref,
                          scratch)

    loop(sequences, one)


def middle_call(layer, sequences, length, ids, far, q, k, v, halo, h, w, a, b, wo, wu, wd, vec,
                bias_up):
    tokens, width = q.shape
    hidden, rank = wu.shape[2], a.shape[2]

    def kernel(own_ref, other_ref, live_ref, far_ref, q_ref, k_ref, v_ref, halo_ref, h_hbm, w_hbm, a_hbm,
               b_hbm, wo_hbm, wu_hbm, wd_hbm, vec_hbm, bu_hbm,
               q2_ref, k2_ref, v2_ref, send_ref,
               u_out, x_out, h_out, n1_out, r1_out, dg_out, n2_out, r2_out, q_out, k_out, v_out,
               nk_out, nv_out, mix_out,
               h_ref, w_ref, wo_ref, wu_ref, wd_ref, vec_ref, bu_ref, vec2_ref, a_ref, b_ref,
               u_ref, mix_ref, one_ref, low_ref, act_ref,
               n1_ref, r1_ref, dg_ref, n2_ref, r2_ref, nk_ref, nv_ref, ins, outs, bias_ref,
               *scratch):
        loads = start_all(copies_of(
            [(h_hbm, h_ref), (vec_hbm.at[layer], vec_ref), (wo_hbm.at[layer], wo_ref),
             (bu_hbm, bu_ref), (wu_hbm.at[layer], wu_ref), (wd_hbm.at[layer], wd_ref),
             (w_hbm.at[layer + 1], w_ref), (a_hbm.at[layer + 1], a_ref),
             (b_hbm.at[layer + 1], b_ref), (vec_hbm.at[layer + 1], vec2_ref)], ins))
        stores = copies_of(
            [(q_ref, q_out), (k_ref, k_out), (v_ref, v_out), (nk_ref, nk_out), (nv_ref, nv_out),
             (n1_ref, n1_out), (r1_ref, r1_out), (dg_ref, dg_out), (n2_ref, n2_out),
             (r2_ref, r2_out), (one_ref, h_out), (low_ref, x_out), (u_ref, u_out),
             (mix_ref, mix_out)], outs)
        near = Side(True, length, (own_ref, other_ref, live_ref))
        near.biases(sequences, bias_ref, None)
        near_forward(near, sequences, length, far_ref, q_ref, k_ref, v_ref, halo_ref, nk_ref,
                     nv_ref, mix_ref, bias_ref, scratch)
        layer_rest(layer, sequences, length, mix_ref, h_ref, wo_ref, wu_ref, wd_ref,
                   [wait_for(loads, 0, 1, 2), wait_for(loads, 3, 4), wait_for(loads, 5)], vec_ref,
                   bu_ref, one_ref, low_ref, act_ref, n1_ref, r1_ref, dg_ref, n2_ref, r2_ref,
                   (one_ref, low_ref),
                   lambda i: start_all((stores[:7] + stores[13:], stores[7:8], stores[8:12])[i]))
        nothing = wait_for(loads)
        project_in(sequences, length, low_ref, w_ref,
                   [wait_for(loads, 6, 7, 8, 9), nothing, nothing], a_ref, b_ref, vec2_ref, q2_ref,
                   k2_ref, v2_ref, u_ref, send_ref, stores[12].start)
        for copy in stores:
            copy.wait()

    act, stat = ((tokens, width), BF16), ((tokens, 128), F32)
    wide, deep = ((tokens, width), F32), ((tokens, hidden), BF16)
    near, small = ((sequences * (WINDOW + SUB), width), BF16), ((tokens, 2 * rank), BF16)
    factors = ((2, rank, width), F32)
    return call(
        kernel, "middle",
        [(VMEM, ids[0]), (VMEM, ids[1]), (VMEM, ids[2]), (VMEM, far), (VMEM, q), (VMEM, k), (VMEM, v),
         (VMEM, halo)]
        + [(HBM, item) for item in (h, w, a, b, wo, wu, wd, vec, bias_up)],
        [(VMEM,) + act, (VMEM,) + act, (VMEM,) + act, (VMEM, (2, sequences * HALO, width), BF16)]
        + [(HBM,) + item for item in (small, act, wide, act, stat, deep, act, stat, act, act, act,
                                      near, near, act)],
        [(h.shape, h.dtype), ((width, 3 * width), BF16), ((width, width), BF16),
         ((width, hidden), BF16), ((hidden, width), BF16), ((8, width), BF16),
         (bias_up.shape, BF16), ((8, width), BF16), factors, factors, small, act, wide, act, deep,
         act, stat, deep, act, stat, near, near, 10, 14,
         bias_shape(sequences, False)] + attention_scratch(),
        2 * tokens * width * (2 * hidden + 4 * width), 24000000, 42)


def turn_call(layer, sequences, length, ids, far, q, k, v, halo, h, gradient, wo, wu, wd,
              vec, bias_up):
    tokens, width = q.shape
    hidden = wu.shape[2]

    def kernel(own_ref, other_ref, live_ref, far_ref, q_ref, k_ref, v_ref, halo_ref, h_hbm, g_hbm,
               wo_hbm, wu_hbm, wd_hbm, vec_hbm, bu_hbm,
               datt_ref, dfar_ref, dq_ref, dnk_ref, dnv_ref, dhalo_ref, delta_ref, hidden_out,
               h_ref, g_ref, wo_ref, wu_ref, wd_ref, vec_ref, bu_ref, mix_ref, one_ref, low_ref,
               act_ref, n1_ref, r1_ref, dg_ref, n2_ref, r2_ref, nk_ref, nv_ref, last_ref, ins, outs,
               bias_ref, columns_ref, *scratch):
        loads = start_all(copies_of(
            [(h_hbm, h_ref), (vec_hbm.at[layer], vec_ref), (wo_hbm.at[layer], wo_ref),
             (bu_hbm, bu_ref), (wu_hbm.at[layer], wu_ref), (wd_hbm.at[layer], wd_ref),
             (g_hbm, g_ref)], ins))
        store = pltpu.make_async_copy(last_ref, hidden_out, outs.at[0])
        near = Side(True, length, (own_ref, other_ref, live_ref))
        near.biases(sequences, bias_ref, columns_ref)
        near_forward(near, sequences, length, far_ref, q_ref, k_ref, v_ref, halo_ref, nk_ref,
                     nv_ref, mix_ref, bias_ref, scratch)
        side = lax.axis_index("seq")
        layer_rest(layer, sequences, length, mix_ref, h_ref, wo_ref, wu_ref, wd_ref,
                   [wait_for(loads, 0, 1, 2), wait_for(loads, 3, 4), wait_for(loads, 5)], vec_ref,
                   bu_ref, one_ref, low_ref, act_ref, n1_ref, r1_ref, dg_ref, n2_ref, r2_ref,
                   (last_ref,), lambda i: None)
        store.start()

        def given(s, rows):
            places = lax.broadcasted_iota(jnp.int32, (length, 1), 0) + side * length
            return jnp.where(
                places.astype(F32) < picked(live_ref, s), g_ref[rows, :].astype(F32), 0.0)

        nothing = wait_for(loads)
        layer_rest_back(sequences, length, given,
                        [wait_for(loads, 6), nothing, nothing, nothing], n1_ref,
                        r1_ref, dg_ref, n2_ref, r2_ref, wo_ref, wu_ref, wd_ref, vec_ref, one_ref,
                        low_ref, act_ref, datt_ref, mix_ref, delta_ref)
        near_backward(near, sequences, length, q_ref, nk_ref, nv_ref, low_ref,
                      delta_ref, dfar_ref, dq_ref, dnk_ref, dnv_ref, dhalo_ref, columns_ref)
        store.wait()

    act, stat = ((tokens, width), BF16), ((tokens, 128), F32)
    wide, deep = ((tokens, width), F32), ((tokens, hidden), BF16)
    near_rows = sequences * (WINDOW + SUB)
    near, block = ((near_rows, width), BF16), ((sequences * BLOCK, width), BF16)
    return call(
        kernel, "turn",
        [(VMEM, ids[0]), (VMEM, ids[1]), (VMEM, ids[2]), (VMEM, far), (VMEM, q), (VMEM, k),
         (VMEM, v), (VMEM, halo)]
        + [(HBM, item) for item in (h, gradient, wo, wu, wd, vec, bias_up)],
        [(VMEM,) + wide, (VMEM,) + block, (VMEM,) + block, (VMEM, (near_rows, width), F32),
         (VMEM, (near_rows, width), F32), (VMEM, (2, sequences * HALO, width), BF16),
         (VMEM, (HEAD_ROWS * sequences, length), F32), (HBM,) + act],
        [(h.shape, h.dtype), act, ((width, width), BF16), ((width, hidden), BF16),
         ((hidden, width), BF16), ((8, width), BF16), (bias_up.shape, BF16), act, wide, act, deep,
         act, stat, deep, act, stat, near, near, act, 7, 1, bias_shape(sequences, False),
         bias_shape(sequences, True)] + attention_scratch(),
        4 * tokens * width * (2 * hidden + width), 24000000, 42)


def back_far_call(sequences, length, ids, q, k, v, dfar, delta, dq_near, dnk, dnv):
    tokens, width = q.shape

    def kernel(own_ref, live_ref, q_ref, k_ref, v_ref, dfar_ref, delta_ref, dqn_ref, dnk_ref,
               dnv_ref, dq_ref, dk_ref, dv_ref, bias_ref):
        far = Side(False, length, (own_ref, None, live_ref))
        far.biases(sequences, None, bias_ref)
        side, wide, own = far.side, WINDOW + SUB, WINDOW + SUB - HALO

        def key_terms(s, cols, kept):
            for out, which, other in ((dv_ref, 0, 3), (dk_ref, 1, 2)):
                left = jnp.concatenate([item[which] for item in kept], axis=1)
                right = jnp.concatenate([item[other] for item in kept], axis=0)
                out[far.keys(s, 0), cols] = dot_nn(left, right)

        def one(s):
            attention_backward(
                far, s, q_ref, k_ref, v_ref, dfar_ref,
                lambda s, sub: rows_at(s * BLOCK + sub * SUB, SUB, SUB), delta_ref, dq_ref,
                far.queries, key_terms, bias_ref)
            dq_ref[rows_at(s * length + (1 - side) * BLOCK, BLOCK, BLOCK), :] = dqn_ref[
                rows_at(s * BLOCK, BLOCK, BLOCK), :]
            mine = rows_at(s * length + (length - own) * (1 - side), own, 32)
            theirs = rows_at(s * wide + HALO * side, own, 32)
            dk_ref[mine, :] = dk_ref[mine, :] + dnk_ref[theirs, :]
            dv_ref[mine, :] = dv_ref[mine, :] + dnv_ref[theirs, :]

        loop(sequences, one)

    wide = (VMEM, (tokens, width), F32)
    return call(
        kernel, "back_far",
        [(VMEM, ids[0]), (VMEM, ids[2])]
        + [(VMEM, item) for item in (q, k, v, dfar, delta, dq_near, dnk, dnv)],
        [(VMEM, (tokens, width), BF16), wide, wide],
        [bias_shape(sequences, True)], 4000000000, 16000000, 8)


def back_call(layer, sequences, length, ids, dq, dk, dv, dhalo, datt, u, x, saved, w, a, b, wo, wu,
              wd, vec):
    tokens, width = dq.shape
    hidden, rank = wu.shape[2], a.shape[2]

    def kernel(own_ref, other_ref, live_ref, dq_ref, dk_ref, dv_ref, dhalo_ref, datt_ref, u_hbm, x_hbm,
               n1_hbm, r1_hbm, dg_hbm, n2_hbm, r2_hbm, q_hbm, k_hbm, v_hbm, nk_hbm, nv_hbm, mix_hbm,
               w_hbm, a_hbm, b_hbm, wo_hbm, wu_hbm, wd_hbm, vec_hbm,
               datt_out, dfar_ref, dqn_ref, dnk_ref, dnv_ref, dhalo_out, delta_ref, q_ref, k_ref,
               v_ref, grad_out,
               u_ref, x_ref, n1_ref, r1_ref, dg_ref, n2_ref, r2_ref, nk_ref, nv_ref, w_ref,
               a_ref, b_ref, wo_ref, wu_ref, wd_ref, vec_ref, dkb_ref, dvb_ref, du_ref, grad_ref,
               two_ref, low_ref, mix_ref, ins, outs, bias_ref):
        loads = start_all(copies_of(
            [(a_hbm.at[layer + 1], a_ref), (b_hbm.at[layer + 1], b_ref), (u_hbm, u_ref),
             (x_hbm, x_ref), (w_hbm.at[layer + 1], w_ref), (vec_hbm.at[layer], vec_ref),
             (n2_hbm, n2_ref), (r2_hbm, r2_ref), (wd_hbm.at[layer], wd_ref), (dg_hbm, dg_ref),
             (wu_hbm.at[layer], wu_ref), (n1_hbm, n1_ref), (r1_hbm, r1_ref),
             (wo_hbm.at[layer], wo_ref), (q_hbm, q_ref), (nk_hbm, nk_ref), (nv_hbm, nv_ref),
             (k_hbm, k_ref), (v_hbm, v_ref), (mix_hbm, mix_ref)], ins))
        adapter_back(sequences, length, [wait_for(loads, 0, 1), wait_for(loads, 2, 3)], dq_ref, dk_ref, dv_ref, dhalo_ref, u_ref, x_ref,
                     a_ref, b_ref, dkb_ref, dvb_ref, du_ref, grad_ref)
        store = pltpu.make_async_copy(grad_ref, grad_out, outs.at[0])
        store.start()
        down, _, _ = low_rank(a_ref, b_ref)

        wait_for(loads, 4)()
        tall = tokens // 2

        def given(s, rows):
            return two_ref[rows, :]

        def project(i):
            rows = rows_at(i * tall, tall, 128)
            two_ref[rows, :] = project_back(rows, rows, datt_ref, dq_ref, dkb_ref, dvb_ref, du_ref,
                                            w_ref, down)

        loop(2, project)
        layer_rest_back(sequences, length, given,
                        [wait_for(loads, 5, 6, 7), wait_for(loads, 8, 9), wait_for(loads, 10),
                         wait_for(loads, 11, 12, 13, 19)], n1_ref, r1_ref, dg_ref, n2_ref, r2_ref,
                        wo_ref, wu_ref, wd_ref, vec_ref, two_ref, low_ref, dg_ref, datt_out,
                        mix_ref, delta_ref)
        wait_for(loads, 14, 15, 16)()
        near = Side(True, length, (own_ref, other_ref, live_ref))
        near.biases(sequences, None, bias_ref)
        near_backward(near, sequences, length, q_ref, nk_ref, nv_ref, low_ref,
                      delta_ref, dfar_ref, dqn_ref, dnk_ref, dnv_ref, dhalo_out, bias_ref)
        wait_for(loads, 17, 18)()
        store.wait()

    act, stat = ((tokens, width), BF16), ((tokens, 128), F32)
    wide, deep = ((tokens, width), F32), ((tokens, hidden), BF16)
    near_rows = sequences * (WINDOW + SUB)
    near, block = ((near_rows, width), BF16), ((sequences * BLOCK, width), BF16)
    small, factors = ((tokens, 2 * rank), BF16), ((2, rank, width), F32)
    grad = ((4 * rank, width), F32)
    return call(
        kernel, "back",
        [(VMEM, ids[0]), (VMEM, ids[1]), (VMEM, ids[2])]
        + [(VMEM, item) for item in (dq, dk, dv, dhalo, datt)]
        + [(HBM, item) for item in (u, x, *saved, w, a, b, wo, wu, wd, vec)],
        [(VMEM,) + wide, (VMEM,) + block, (VMEM,) + block,
         (VMEM, (near_rows, width), F32), (VMEM, (near_rows, width), F32),
         (VMEM, (2, sequences * HALO, width), BF16), (VMEM, (HEAD_ROWS * sequences, length), F32),
         (VMEM,) + act, (VMEM,) + act, (VMEM,) + act,
         (HBM,) + grad],
        [small, act, act, stat, deep, act, stat, near, near, ((width, 3 * width), BF16), factors,
         factors, ((width, width), BF16), ((width, hidden), BF16), ((hidden, width), BF16),
         ((8, width), BF16), act, act, small, grad, wide, act, act, 20, 1, bias_shape(sequences, True)],
        2 * tokens * width * (2 * hidden + 4 * width), 24000000, 38)


def last_call(layer, sequences, length, dq, dk, dv, dhalo, u, x, w, a, b, other, *state):
    tokens, width = dq.shape
    rank = a.shape[2]

    def kernel(dq_ref, dk_ref, dv_ref, dhalo_ref, u_hbm, x_hbm, w_hbm, a_hbm, b_hbm, other_hbm,
               *rest):
        given, rest = rest[:len(state)], rest[len(state):]
        (dkb_ref, dvb_ref, du_ref, w_ref, down_ref, mine_ref, theirs_ref), rest = rest[:7], rest[7:]
        taken, rest = rest[:len(state)], rest[len(state):]
        u_ref, x_ref, a_ref, b_ref, other_ref, grad_ref, sems, state_sems = rest
        loads = start_all(copies_of(
            [(a_hbm.at[layer], a_ref), (b_hbm.at[layer], b_ref), (u_hbm, u_ref), (x_hbm, x_ref),
             (other_hbm, other_ref), (w_hbm.at[layer], w_ref)], sems))
        more = start_all(copies_of(zip(given, taken), state_sems))
        adapter_back(sequences, length, [wait_for(loads, 0, 1), wait_for(loads, 2, 3)], dq_ref, dk_ref, dv_ref, dhalo_ref, u_ref, x_ref,
                     a_ref, b_ref, dkb_ref, dvb_ref, du_ref, grad_ref)
        down_ref[...] = low_rank(a_ref, b_ref)[0]
        wait_for(loads, 4)()
        first = lax.axis_index("seq") == layer
        here, there = grad_ref[...], other_ref[...]
        mine_ref[...] = jnp.where(first, here, there)
        theirs_ref[...] = jnp.where(first, there, here)
        wait_for(loads, 5)()
        for copy in more:
            copy.wait()

    act, grad = ((tokens, width), BF16), ((4 * rank, width), F32)
    small, factors = ((tokens, 2 * rank), BF16), ((2, rank, width), F32)
    return call(
        kernel, "adapter_back",
        [(VMEM, dq), (VMEM, dk), (VMEM, dv), (VMEM, dhalo)]
        + [(HBM, item) for item in (u, x, w, a, b, other, *state)],
        [(VMEM,) + act, (VMEM,) + act, (VMEM,) + small, (VMEM, (width, 3 * width), BF16),
         (VMEM, (2 * rank, width), BF16), (VMEM,) + grad, (VMEM,) + grad]
        + [(VMEM, item.shape, F32) for item in state],
        [small, act, factors, factors, grad, grad, 6, len(state)], 500000000, 12000000, 8)


def project_back_call(datt, dq, dk, dv, du, w, down):
    tokens, width = dq.shape
    parts = 2
    length = tokens // parts

    def kernel(datt_ref, dq_ref, dk_ref, dv_ref, du_ref, w_ref, down_ref, out_hbm, out_ref, sems):
        def part(i):
            rows = rows_at(i * length, length, 128)
            return pltpu.make_async_copy(out_ref.at[rows], out_hbm.at[rows], sems.at[i])

        def one(i):
            rows = rows_at(i * length, length, 128)
            out_ref[rows, :] = project_back(rows, rows, datt_ref, dq_ref, dk_ref, dv_ref, du_ref,
                                            w_ref, down_ref[...])
            part(i).start()

        loop(parts, one)
        for i in range(parts):
            part(i).wait()

    return call(
        kernel, "project_back", [(VMEM, item) for item in (datt, dq, dk, dv, du, w, down)],
        [(HBM, (tokens, width), F32)], [((tokens, width), F32), parts],
        2 * tokens * width * width * 3, 4000000, 6)[0]


def adam_call(mine, theirs, token_slots, steps, down, up, m_down, v_down, m_up, v_up):
    layers, two, rank, width = down.shape

    def kernel(mine_ref, theirs_ref, steps_ref, down_ref, up_ref, md_ref, vd_ref, mu_ref, vu_ref,
               *rest):
        outs, results, sems = rest[:6], rest[6:12], rest[12]
        down_out, up_out, md_out, vd_out, mu_out, vu_out = results
        side = lax.axis_index("seq")
        for layer in range(layers):
            for which in range(two):
                for group, (w_ref, m_ref, v_ref, w_out, m_out, v_out, rate, decay) in enumerate((
                    (down_ref, md_ref, vd_ref, down_out, md_out, vd_out, 0.03125, 0.1),
                    (up_ref, mu_ref, vu_ref, up_out, mu_out, vu_out, 0.5, 0.0),
                )):
                    rows = slice((group * two + which) * rank, (group * two + which + 1) * rank)
                    grad = jnp.where(side == layer, mine_ref[rows, :], theirs_ref[rows, :])
                    grad = grad / token_slots
                    step = picked(steps_ref, (layer * two + which) * 2 + group)
                    correction = jnp.broadcast_to(1.0 - jnp.exp2(-step), (rank, width))
                    weight = w_ref[layer, which]
                    moment = 0.5 * m_ref[layer, which] + 0.5 * grad
                    velocity = 0.5 * v_ref[layer, which] + 0.5 * grad * grad
                    size = moment / correction / (jnp.sqrt(velocity / correction) + 1e-08)
                    w_out[layer, which] = weight - rate * (size + decay * weight)
                    m_out[layer, which] = moment
                    v_out[layer, which] = velocity

        for store in start_all(copies_of(zip(results, outs), sems)):
            store.wait()

    return call(
        kernel, "adam",
        [(VMEM, mine), (VMEM, theirs), (VMEM, steps)]
        + [(VMEM, item) for item in (down, up, m_down, v_down, m_up, v_up)],
        [(HBM, down.shape, F32)] * 6, [(down.shape, F32)] * 6 + [6], 1000000, 2000000, 4)


def together(*values):
    return lax.optimization_barrier(values)


def sum_while(mine, theirs, work):
    batch = lax.axis_size("batch")
    swap = [(0, 1), (1, 0)]
    mine = mine + lax.ppermute(theirs, "seq", swap)
    done, work, step = None, list(work), 1
    while step < batch:
        ways = 4 if batch % (4 * step) == 0 else 2
        given = mine.astype(BF16)
        come = [lax.ppermute(given, "batch", [(i, i ^ (step * d)) for i in range(batch)])
                for d in range(1, ways)]
        if work:
            done = work.pop(0)(mine, done)
            *come, done = together(*come, done)
        mine = mine + sum(item.astype(F32) for item in come)
        step *= ways
    for one in work:
        done = one(mine, done)
    return mine, lax.ppermute(mine, "seq", swap), done


def shards(
    first_layer_input,
    output_gradient,
    sentence_pair_index,
    sequence_live_length,
    optimizer_step_count,
    query_key_value_weight,
    attention_output_weight,
    feedforward_up_weight,
    feedforward_down_weight,
    layer_bias_gain_rows,
    feedforward_up_bias,
    adapter_down_factors,
    adapter_up_factors,
    first_moment_down,
    second_moment_down,
    first_moment_up,
    second_moment_up,
):
    sequences, length, width = first_layer_input.shape
    tokens = sequences * length
    swap = [(0, 1), (1, 0)]
    a, b = adapter_down_factors, jnp.swapaxes(adapter_up_factors, 2, 3)
    vec = layer_bias_gain_rows
    bias_up = feedforward_up_bias
    wqkv, wo = query_key_value_weight, attention_output_weight
    wu, wd = feedforward_up_weight, feedforward_down_weight
    ids = (sentence_pair_index, lax.ppermute(sentence_pair_index, "seq", swap),
           sequence_live_length[None, :])
    shape = (sequences, length)

    x1 = first_layer_input.reshape(tokens, width)
    q1, k1, v1, send, u1 = first_call(0, *shape, x1, wqkv, a, b, vec)
    halo = lax.ppermute(send, "seq", swap)
    far = far_call(*shape, q1, k1, v1, ids)
    q2, k2, v2, send, u2, x2, h1, *saved = middle_call(
        0, *shape, ids, far, q1, k1, v1, halo, x1, wqkv, a, b, wo, wu, wd, vec, bias_up)
    halo = lax.ppermute(send, "seq", swap)
    far = far_call(*shape, q2, k2, v2, ids)
    datt, dfar, dqn, dnk, dnv, dsend, delta, hidden_out = turn_call(
        1, *shape, ids, far, q2, k2, v2, halo, h1, output_gradient.reshape(tokens, width),
        wo, wu, wd, vec, bias_up)
    dhalo = lax.ppermute(dsend, "seq", swap)
    dq, dk, dv = back_far_call(*shape, ids, q2, k2, v2, dfar, delta, dqn, dnk, dnv)
    datt, dfar, dqn, dnk, dnv, dsend, delta, q1, k1, v1, grad2 = back_call(
        0, *shape, ids, dq, dk, dv, dhalo, datt, u2, x2, saved, wqkv, a, b, wo, wu, wd, vec)
    dhalo = lax.ppermute(dsend, "seq", swap)
    dq, dk, dv = back_far_call(*shape, ids, q1, k1, v1, dfar, delta, dqn, dnk, dnv)
    dk, dv, du, w1, down1, mine, theirs, *state = last_call(
        0, *shape, dq, dk, dv, dhalo, u1, x1, wqkv, a, b, grad2, a, b, first_moment_down,
        second_moment_down, jnp.swapaxes(first_moment_up, 2, 3),
        jnp.swapaxes(second_moment_up, 2, 3))

    def work(token, out):
        now, _ = together(datt, token)
        return project_back_call(now, dq, dk, dv, du, w1, down1)

    mine, theirs, gradient = sum_while(mine, theirs, [work])
    token_slots = tokens * lax.axis_size("seq") * lax.axis_size("batch")
    down, up, m_down, v_down, m_up, v_up = adam_call(
        mine, theirs, token_slots, optimizer_step_count.reshape(1, -1), *state)
    return (
        hidden_out.reshape(sequences, length, width),
        gradient.reshape(sequences, length, width),
        down,
        jnp.swapaxes(up, 2, 3),
        m_down,
        v_down,
        jnp.swapaxes(m_up, 2, 3),
        jnp.swapaxes(v_up, 2, 3),
    )


def solution(mesh):
    acts, whole = P("batch", "seq", None), P()
    return jax.shard_map(
        shards,
        mesh=mesh,
        in_specs=(acts, acts, P("batch", "seq"), P("batch")) + (whole,) * 13,
        out_specs=(acts, acts) + (whole,) * 6,
        check_vma=False,
    )
```

```python
import jax
import jax.numpy as jnp
from jax import lax
from jax.experimental import pallas as pl
from jax.experimental.pallas import tpu as pltpu
from jax.sharding import PartitionSpec as P

HEADS = 12
ENCODER_LAYERS = 2
HALO = 96
BLOCK = 128
SUB = 64
WINDOW = 256
QUAD = 256
HEAD_ROWS = 16
MASKED = -1000000000.0
LOG2E = 1.4426950408889634
HALF_ROOT_PI = 0.886226925452758
ROOT_HALF = 0.7071067811865476
ACTIVE = 0.7978845608028654
SLOPE = 0.5641895835477563
F32 = jnp.float32
BF16 = jnp.bfloat16


def dot_nn(a, b):
    return lax.dot_general(a, b, (((1,), (0,)), ((), ())), preferred_element_type=F32)


def dot_nt(a, b):
    return lax.dot_general(a, b, (((1,), (1,)), ((), ())), preferred_element_type=F32)


def dot_tn(a, b):
    return lax.dot_general(a, b, (((0,), (0,)), ((), ())), preferred_element_type=F32)


def rows_at(start, size, multiple):
    return pl.ds(pl.multiple_of(start, multiple), size)


def loop(count, body):
    def step(i, carry):
        body(i)
        return carry

    lax.fori_loop(0, count, step, 0)


def picked(row_ref, i):
    row = row_ref[...].astype(F32)
    at = lax.broadcasted_iota(jnp.int32, row.shape, 1) == i
    return jnp.sum(jnp.where(at, row, 0.0), axis=1, keepdims=True)


def column_of(row):
    n = row.shape[1]
    eye = lax.broadcasted_iota(jnp.int32, (n, n), 0) == lax.broadcasted_iota(jnp.int32, (n, n), 1)
    return jnp.sum(jnp.where(eye, row, 0.0), axis=1, keepdims=True)


def low_lanes():
    return (lax.broadcasted_iota(jnp.int32, (SUB, 128), 1) < 64).astype(F32).astype(BF16)


def spread_heads(tile, low):
    zero = jnp.zeros((2 * SUB, 128), BF16)
    high = 1 - low
    left, right = tile[:, :128], tile[:, 128:]
    left = jnp.concatenate([left * low, left * high], axis=0)
    right = jnp.concatenate([right * low, right * high], axis=0)
    return jnp.concatenate([jnp.concatenate([left, zero], axis=1),
                            jnp.concatenate([zero, right], axis=1)], axis=0)


def gather_heads(wide):
    low = lax.broadcasted_iota(jnp.int32, (SUB, 128), 1) < 64
    parts = []
    for i in range(2):
        cols, top = slice(128 * i, 128 * i + 128), 2 * SUB * i
        parts.append(jnp.where(low, wide[top:top + SUB, cols],
                               wide[top + SUB:top + 2 * SUB, cols]))
    return jnp.concatenate(parts, axis=1)


def pipelined(units):
    units = list(units)
    live = []
    while units or live:
        if units:
            live.append(units.pop(0))
        for unit in reversed(list(live)):
            if next(unit, None) is None:
                live.remove(unit)


class Side:
    def __init__(self, near, length, ids_refs):
        self.near, self.length, self.ids_refs = near, length, ids_refs
        self.side = lax.axis_index("seq")
        self.row0 = BLOCK * ((1 - self.side) if near else self.side)

    def ids(self, s):
        own_ref, other_ref, live_ref = self.ids_refs
        own = own_ref[pl.ds(s, 1), :].astype(F32)
        query = jnp.where(self.row0 == 0, own[:, :BLOCK], own[:, BLOCK:])
        if self.near:
            other = other_ref[pl.ds(s, 1), :].astype(F32)
            kept = WINDOW + SUB - HALO
            key = jnp.where(
                self.side == 0,
                jnp.concatenate([own[:, self.length - kept:], other[:, :HALO]], axis=1),
                jnp.concatenate([other[:, self.length - HALO:], own[:, :kept]], axis=1))
            start = jnp.where(self.side == 0, self.length - kept, self.length - HALO)
        else:
            key, start = own, self.side * self.length
        places = lax.broadcasted_iota(jnp.int32, key.shape, 1) + start
        return query, jnp.where(places.astype(F32) < picked(live_ref, s), key, -1.0)

    def queries(self, s, sub):
        return rows_at(s * self.length + self.row0 + sub * SUB, SUB, SUB)

    def keys(self, s, sub):
        if self.near:
            return rows_at(s * (WINDOW + SUB) + sub * SUB, WINDOW, SUB)
        return rows_at(s * self.length, WINDOW, WINDOW)

    def biases(self, sequences, rows_ref, columns_ref):
        lane = lax.broadcasted_iota(jnp.int32, (1, 128), 1)
        place = jnp.where(lane < SUB, lane, lane - SUB)
        key_place = lax.broadcasted_iota(jnp.int32, (WINDOW, 128), 0)
        shape = (SUB, WINDOW)
        apart = lax.broadcasted_iota(jnp.int32, shape, 1) - lax.broadcasted_iota(jnp.int32, shape, 0)

        def one(s):
            query, key = self.ids(s)
            for sub in range(2):
                own = HALO if self.near else self.row0 + sub * SUB
                if rows_ref is not None:
                    keys = key[:, sub * SUB:sub * SUB + WINDOW] if self.near else key
                    queries = column_of(query)[sub * SUB:(sub + 1) * SUB]
                    seen = (queries == keys) | (apart == own)
                    rows_ref[rows_at((s * 2 + sub) * SUB, SUB, SUB), :] = jnp.where(
                        seen, 0.0, MASKED)
                if columns_ref is None:
                    continue
                blocks = (128, 128, SUB) if self.near else (128, 128)
                column = jnp.concatenate(
                    [column_of(key[:, 128 * i:128 * i + n]) for i, n in enumerate(blocks)], axis=0)
                keys = column[sub * SUB:sub * SUB + WINDOW] if self.near else column
                turned = pltpu.roll(query, SUB, 1)
                pair = (query, turned) if sub == 0 else (turned, query)
                seen = (keys == jnp.where(lane < SUB, *pair)) | (key_place == place + own)
                columns_ref[rows_at((s * 2 + sub) * WINDOW, WINDOW, WINDOW), :] = jnp.where(
                    seen, 0.0, MASKED)

        loop(sequences, one)


def bias_shape(sequences, turned):
    return ((sequences * 2 * WINDOW, 128) if turned else (sequences * 2 * SUB, WINDOW)), F32


def half(sub):
    return slice(4 * SUB * sub, 4 * SUB * (sub + 1))


SLOTS = 2


def attention_scratch(backward=False):
    pair = [((SLOTS, WINDOW, 4 * SUB), F32), ((SLOTS, WINDOW, 4 * SUB), BF16)]
    return pair * 2 if backward else pair


def attention_forward(where, s, q_ref, k_ref, v_ref, out_ref, out_rows, bias_ref, scratch):
    low = low_lanes()
    scores_ref, share_ref = scratch[:2]

    def unit(quad, sub):
        cols = slice(QUAD * quad, QUAD * quad + QUAD)
        keys = where.keys(s, sub)
        q4 = spread_heads(q_ref[where.queries(s, sub), cols], low)
        slot = (2 * quad + sub) % SLOTS
        scores_ref[slot] = dot_nt(q4, k_ref[keys, cols])
        yield True
        bias = bias_ref[rows_at((s * 2 + sub) * SUB, SUB, SUB), :]
        totals = []
        for h in range(4):
            rows = slice(h * SUB, (h + 1) * SUB)
            scores = scores_ref[slot, rows, :] + bias
            share = jnp.exp2(scores - jnp.max(scores, axis=1, keepdims=True))
            totals.append(1.0 / jnp.sum(share, axis=1, keepdims=True))
            share_ref[slot, rows, :] = share.astype(BF16)
        yield True
        mixed = dot_nn(share_ref[slot], v_ref[keys, cols])
        mixed = jnp.concatenate(
            [mixed[h * SUB:(h + 1) * SUB] * totals[h] for h in range(4)], axis=0)
        yield True
        out_ref[out_rows(s, sub), cols] = gather_heads(mixed).astype(BF16)

    width = q_ref.shape[1]
    pipelined(unit(quad, sub) for quad in range(width // QUAD) for sub in range(2))


def attention_backward(where, s, q_ref, k_ref, v_ref, dmix_ref, dmix_rows, delta_ref, dq_ref,
                       dq_rows, key_terms, bias_ref, scratch):
    low = low_lanes()
    scores_ref, share_ref, d_share_ref, d_scores_ref = scratch
    delta = delta_ref[rows_at(s * HEAD_ROWS, HEAD_ROWS, HEAD_ROWS), :]
    delta = jnp.where(where.row0 == 0, delta[:, :BLOCK], delta[:, BLOCK:])
    turned = pltpu.roll(delta, SUB, 1)
    first_half = lax.broadcasted_iota(jnp.int32, (1, 2 * SUB), 1) < SUB

    def unit(quad, sub, kept):
        cols = slice(QUAD * quad, QUAD * quad + QUAD)
        keys = where.keys(s, sub)
        slot = (2 * quad + sub) % SLOTS
        q4 = spread_heads(q_ref[where.queries(s, sub), cols], low)
        d4 = spread_heads(dmix_ref[dmix_rows(s, sub), cols], low)
        scores_ref[slot] = dot_nt(k_ref[keys, cols], q4)
        d_share_ref[slot] = dot_nt(v_ref[keys, cols], d4)
        yield True
        bias = bias_ref[rows_at((s * 2 + sub) * WINDOW, WINDOW, WINDOW), :]
        shares, d_scores = [], []
        left, right = (delta, turned) if sub == 0 else (turned, delta)
        for i in range(2):
            head = 4 * quad + 2 * i
            drop = jnp.where(first_half, left[head:head + 1], right[head + 1:head + 2])
            part = scores_ref[slot, :, 128 * i:128 * i + 128] + bias
            part = jnp.exp2(part - jnp.max(part, axis=0, keepdims=True))
            part = part * (1.0 / jnp.sum(part, axis=0, keepdims=True))
            shares.append(part.astype(BF16))
            d_scores.append((part * (d_share_ref[slot, :, 128 * i:128 * i + 128] - drop)).astype(BF16))
        d_scores = jnp.concatenate(d_scores, axis=1)
        kept.append((jnp.concatenate(shares, axis=1), d_scores, q4, d4))
        yield True
        if sub == 1:
            key_terms(s, cols, kept)
        yield True
        d_query = gather_heads(dot_tn(d_scores, k_ref[keys, cols])) * 0.125
        dq_ref[dq_rows(s, sub), cols] = d_query.astype(BF16)

    width = q_ref.shape[1]

    def units():
        for quad in range(width // QUAD):
            kept = []
            for sub in range(2):
                yield unit(quad, sub, kept)

    pipelined(units())


def row_deltas(sequences, length, dmix_ref, mix_ref, delta_ref):
    width = dmix_ref.shape[1]
    shape = (HEAD_ROWS, width)
    own = (lax.broadcasted_iota(jnp.int32, shape, 1) // 64
           == lax.broadcasted_iota(jnp.int32, shape, 0)).astype(F32).astype(BF16)

    def one(s):
        rows = rows_at(s * length, length, length)
        product = dmix_ref[rows, :].astype(F32) * mix_ref[rows, :].astype(F32)
        high = product.astype(BF16)
        rest = (product - high.astype(F32)).astype(BF16)
        delta_ref[rows_at(s * HEAD_ROWS, HEAD_ROWS, HEAD_ROWS), :] = (
            dot_nt(own, high) + dot_nt(own, rest))

    loop(sequences, one)


def near_keys(s, length, k_ref, v_ref, halo_ref, nk_ref, nv_ref):
    side = lax.axis_index("seq")
    wide, own = WINDOW + SUB, WINDOW + SUB - HALO
    given = rows_at(s * HALO, HALO, 32)
    for i, (src, dst) in enumerate(((k_ref, nk_ref), (v_ref, nv_ref))):
        dst[rows_at(s * wide + HALO * side, own, 32), :] = src[
            rows_at(s * length + (length - own) * (1 - side), own, 32), :]
        dst[rows_at(s * wide + own * (1 - side), HALO, 32), :] = halo_ref[i, given, :]


def norm_forward(values, gain, shift):
    center = values - jnp.mean(values, axis=1, keepdims=True)
    spread = jnp.mean(center * center, axis=1, keepdims=True)
    inverse = lax.rsqrt(spread + 1e-05)
    scaled = center * inverse
    return scaled * gain + shift, scaled, inverse


def norm_backward(gradient, scaled, inverse, gain):
    inner = gradient * gain
    return inverse * (
        inner
        - jnp.mean(inner, axis=1, keepdims=True)
        - scaled * jnp.mean(inner * scaled, axis=1, keepdims=True)
    )


def low_rank(a_ref, b_ref):
    down = jnp.concatenate([a_ref[0], a_ref[1]], axis=0).astype(BF16)
    zero = jnp.zeros_like(b_ref[0])
    up_q = jnp.concatenate([b_ref[0], zero], axis=0).astype(BF16)
    up_v = jnp.concatenate([zero, b_ref[1]], axis=0).astype(BF16)
    return down, up_q, up_v


def project_in(sequences, length, x_ref, w_ref, waits, a_ref, b_ref, vec_ref, q_ref, k_ref, v_ref,
               u_ref, send_ref, sent):
    side = lax.axis_index("seq")
    width = x_ref.shape[1]
    waits[0]()
    down, up_q, up_v = low_rank(a_ref, b_ref)
    vec = vec_ref[...].astype(F32)

    tall = x_ref.shape[0] // 2

    def queries(i):
        rows = rows_at(i * tall, tall, 128)
        x = x_ref[rows, :]
        inner = dot_nt(x, down).astype(BF16)
        u_ref[rows, :] = inner
        q = dot_nn(x, w_ref[:, :width]) + vec[0:1] + 2.0 * dot_nn(inner, up_q)
        q_ref[rows, :] = (q * (0.125 * LOG2E)).astype(BF16)

    def keys(i):
        rows = rows_at(i * tall, tall, 128)
        k_ref[rows, :] = dot_nn(x_ref[rows, :], w_ref[:, width:2 * width]).astype(BF16)

    def values(i):
        rows = rows_at(i * tall, tall, 128)
        v = dot_nn(x_ref[rows, :], w_ref[:, 2 * width:]) + vec[1:2]
        v_ref[rows, :] = (v + 2.0 * dot_nn(u_ref[rows, :], up_v)).astype(BF16)

    def send(s):
        taken = rows_at(s * length + (1 - side) * (length - HALO), HALO, 32)
        for i, ref in enumerate((k_ref, v_ref)):
            send_ref[i, rows_at(s * HALO, HALO, 32), :] = ref[taken, :]

    loop(2, queries)
    sent()
    waits[1]()
    loop(2, keys)
    waits[2]()
    loop(2, values)
    loop(sequences, send)


def layer_rest(layer, sequences, length, mix_ref, h_ref, wo_ref, wu_ref, wd_ref, waits, vec_ref, bu_ref,
               one_ref, low_ref, act_ref, n1_ref, r1_ref, dg_ref, n2_ref, r2_ref, h_outs, sent):
    tokens, hidden = mix_ref.shape[0], wu_ref.shape[1]
    waits[0]()
    vec = vec_ref[...].astype(F32)
    short, units = 128, 3

    def mixed(i):
        def unit(k):
            rows = rows_at((i * units + k) * short, short, short)
            attended = dot_nn(mix_ref[rows, :], wo_ref[...]) + vec[2:3] + h_ref[rows, :].astype(F32)
            yield True
            one, scaled, inverse = norm_forward(attended, vec[4:5], vec[5:6])
            n1_ref[rows, :] = scaled.astype(n1_ref.dtype)
            r1_ref[rows, :] = jnp.broadcast_to(inverse, (short, 128))
            one_ref[rows, :] = one
            low_ref[rows, :] = (one * ROOT_HALF).astype(BF16)

        pipelined(unit(k) for k in range(units))

    loop(tokens // short // units, mixed)
    sent(0)
    waits[1]()
    tile = 1024

    def up(j):
        cols = rows_at(j * tile, tile, tile)
        bias = bu_ref[layer:layer + 1, cols].astype(F32) * ROOT_HALF
        weights = wu_ref[:, cols]

        def unit(k):
            rows = slice(k * short, (k + 1) * short)
            gate = dot_nn(low_ref[rows, :], weights)
            yield True
            gate = gate + bias
            below = HALF_ROOT_PI * lax.erf(gate) + HALF_ROOT_PI
            act_ref[rows, cols] = (gate * below).astype(BF16)
            density = jnp.exp2(gate * gate * -LOG2E)
            dg_ref[rows, cols] = (below + gate * density).astype(BF16)

        pipelined(unit(k) for k in range(tokens // short))

    loop(hidden // tile, up)
    sent(1)
    waits[2]()

    def down(s):
        rows = rows_at(s * length, length, length)
        summed = dot_nn(act_ref[rows, :], wd_ref[...]) * ACTIVE + vec[3:4] + one_ref[rows, :]
        out, scaled, inverse = norm_forward(summed, vec[6:7], vec[7:8])
        n2_ref[rows, :] = scaled.astype(n2_ref.dtype)
        r2_ref[rows, :] = jnp.broadcast_to(inverse, (length, 128))
        for h_out in h_outs:
            h_out[rows, :] = out.astype(h_out.dtype)

    loop(sequences, down)
    sent(2)


def layer_rest_back(sequences, length, gradient, waits, n1_ref, r1_ref, dg_ref, n2_ref, r2_ref,
                    wo_ref, wu_ref, wd_ref, vec_ref, two_ref, low_ref, gate_ref, datt_ref,
                    mix_ref, delta_ref):
    tokens, hidden = low_ref.shape[0], wu_ref.shape[1]
    waits[0]()
    vec = vec_ref[...].astype(F32)
    tall = tokens // 2

    def second(s):
        rows = rows_at(s * length, length, length)
        two = norm_backward(
            gradient(s, rows), n2_ref[rows, :].astype(F32), r2_ref[rows, 0:1], vec[6:7])
        two_ref[rows, :] = two
        low_ref[rows, :] = (two * SLOPE).astype(BF16)

    loop(sequences, second)
    waits[1]()
    tile = 1024

    def down(j):
        cols = rows_at(j * tile, tile, tile)
        weights = wd_ref[cols, :]

        def unit(s):
            rows = slice(s * length, (s + 1) * length)
            gate = dot_nt(low_ref[rows, :], weights)
            yield True
            gate_ref[rows, cols] = (gate * dg_ref[rows, cols].astype(F32)).astype(BF16)

        pipelined(unit(s) for s in range(sequences))

    loop(hidden // tile, down)
    waits[2]()
    waits[3]()

    def up(i):
        rows = rows_at(i * tall, tall, 128)
        datt_ref[rows, :] = dot_nt(gate_ref[rows, :], wu_ref[...])

    def first(s):
        rows = rows_at(s * length, length, length)
        att = norm_backward(datt_ref[rows, :] + two_ref[rows, :], n1_ref[rows, :].astype(F32),
                            r1_ref[rows, 0:1], vec[4:5])
        datt_ref[rows, :] = att
        low_ref[rows, :] = att.astype(BF16)

    def mixture(i):
        rows = rows_at(i * tall, tall, 128)
        low_ref[rows, :] = dot_nt(low_ref[rows, :], wo_ref[...]).astype(BF16)

    loop(2, up)
    loop(sequences, first)
    loop(2, mixture)
    row_deltas(sequences, length, low_ref, mix_ref, delta_ref)


def near_backward(near, sequences, length, q_ref, nk_ref, nv_ref, dmix_ref, delta_ref,
                  dfar_ref, dq_ref, dnk_ref, dnv_ref, dhalo_ref, bias_ref, scratch):
    side, wide = near.side, WINDOW + SUB

    def key_terms(s, cols, kept):
        for out, which, other in ((dnv_ref, 0, 3), (dnk_ref, 1, 2)):
            left, right = [item[which] for item in kept], [item[other] for item in kept]
            out[rows_at(s * wide, SUB, SUB), cols] = dot_nn(left[0][:SUB], right[0])
            both = jnp.concatenate([left[0][SUB:], left[1][:WINDOW - SUB]], axis=1)
            out[rows_at(s * wide + SUB, WINDOW - SUB, SUB), cols] = dot_nn(
                both, jnp.concatenate(right, axis=0))
            out[rows_at(s * wide + WINDOW, SUB, SUB), cols] = dot_nn(
                left[1][WINDOW - SUB:], right[1])

    def one(s):
        dfar_ref[rows_at(s * BLOCK, BLOCK, BLOCK), :] = dmix_ref[
            rows_at(s * length + side * BLOCK, BLOCK, BLOCK), :]
        attention_backward(
            near, s, q_ref, nk_ref, nv_ref, dmix_ref, near.queries, delta_ref, dq_ref,
            lambda s, sub: rows_at(s * BLOCK + sub * SUB, SUB, SUB), key_terms, bias_ref,
            scratch)
        halo = rows_at(s * wide + (wide - HALO) * (1 - side), HALO, 32)
        dhalo_ref[0, rows_at(s * HALO, HALO, 32), :] = (
            dnk_ref[halo, :] * (1.0 / LOG2E)).astype(BF16)
        dhalo_ref[1, rows_at(s * HALO, HALO, 32), :] = dnv_ref[halo, :].astype(BF16)

    loop(sequences, one)


def adapter_back(sequences, length, waits, dq_ref, dk_ref, dv_ref, dhalo_ref, u_ref, x_ref, a_ref,
                 b_ref, dkb_ref, dvb_ref, du_ref, grad_ref):
    side = lax.axis_index("seq")
    rank = a_ref.shape[1]
    waits[0]()
    _, up_q, up_v = low_rank(a_ref, b_ref)

    def one(s):
        rows = rows_at(s * length, length, length)
        taken = rows_at(s * length + (1 - side) * (length - HALO), HALO, 32)
        hrows = rows_at(s * HALO, HALO, 32)
        dk_ref[rows, :] = dk_ref[rows, :] * (1.0 / LOG2E)
        dk_ref[taken, :] = dk_ref[taken, :] + dhalo_ref[0, hrows, :].astype(F32)
        dv_ref[taken, :] = dv_ref[taken, :] + dhalo_ref[1, hrows, :].astype(F32)
        dkb_ref[rows, :] = dk_ref[rows, :].astype(BF16)
        dv16 = dv_ref[rows, :].astype(BF16)
        dvb_ref[rows, :] = dv16
        du_ref[rows, :] = (2.0 * (dot_nt(dq_ref[rows, :], up_q) + dot_nt(dv16, up_v))).astype(BF16)

    loop(sequences, one)
    waits[1]()
    u = u_ref[...]
    grad_ref[0:2 * rank, :] = dot_tn(du_ref[...], x_ref[...])
    up_q, up_v = dot_tn(u, dq_ref[...]), dot_tn(u, dvb_ref[...])
    grad_ref[2 * rank:3 * rank, :] = 2.0 * up_q[:rank]
    grad_ref[3 * rank:, :] = 2.0 * up_v[rank:]


def project_back(rows, own_rows, datt_ref, dq_ref, dk_ref, dv_ref, du_ref, w_ref, down):
    width = dq_ref.shape[1]
    out = datt_ref[rows, :] + dot_nn(du_ref[rows, :], down)
    out = out + dot_nt(dq_ref[rows, :], w_ref[:, :width])
    out = out + dot_nt(dk_ref[rows, :], w_ref[:, width:2 * width])
    return out + dot_nt(dv_ref[rows, :], w_ref[:, 2 * width:])


HBM, VMEM = pltpu.HBM, pltpu.VMEM


def call(kernel, name, args, outs, scratch, flops, nbytes, limit, aliases=None):
    scratch = [pltpu.SemaphoreType.DMA((s,)) if isinstance(s, int) else pltpu.VMEM(*s)
               for s in scratch]
    return pl.pallas_call(
        kernel,
        name=name,
        out_shape=tuple(space(shape, dtype) for space, shape, dtype in outs),
        in_specs=[pl.BlockSpec(memory_space=space) for space, _ in args],
        out_specs=tuple(pl.BlockSpec(memory_space=space) for space, _, _ in outs),
        scratch_shapes=scratch,
        input_output_aliases=aliases or {},
        compiler_params=pltpu.CompilerParams(vmem_limit_bytes=limit * 1024 * 1024),
        cost_estimate=pl.CostEstimate(flops=flops, bytes_accessed=nbytes, transcendentals=0),
    )(*[pltpu.with_memory_space_constraint(array, space) for space, array in args])


def sds(shape, dtype):
    return jax.ShapeDtypeStruct(shape, dtype)


def copies_of(pairs, sems):
    return [pltpu.make_async_copy(src, dst, sems.at[i]) for i, (src, dst) in enumerate(pairs)]


def start_all(copies):
    for copy in copies:
        copy.start()
    return copies


def wait_for(copies, *which):
    def wait():
        for i in which:
            copies[i].wait()

    return wait


def first_call(layer, sequences, length, x, w, a, b, vec):
    tokens, width = x.shape
    rank = a.shape[2]

    def kernel(x_hbm, w_hbm, a_hbm, b_hbm, vec_hbm, q_ref, k_ref, v_ref, send_ref, u_out, x_ref,
               w_ref, a_ref, b_ref, vec_ref, u_ref, sems, outs):
        thirds = [slice(i * width, (i + 1) * width) for i in range(3)]
        copies = start_all(copies_of(
            [(a_hbm.at[layer], a_ref), (b_hbm.at[layer], b_ref), (vec_hbm.at[layer], vec_ref),
             (x_hbm, x_ref)] + [(w_hbm.at[layer, :, part], w_ref.at[:, part]) for part in thirds],
            sems))
        store = pltpu.make_async_copy(u_ref, u_out, outs.at[0])
        project_in(sequences, length, x_ref, w_ref,
                   [wait_for(copies, 0, 1, 2, 3, 4), wait_for(copies, 5), wait_for(copies, 6)],
                   a_ref, b_ref, vec_ref, q_ref, k_ref, v_ref, u_ref, send_ref, store.start)
        store.wait()

    act, small = (VMEM, (tokens, width), BF16), ((tokens, 2 * rank), BF16)
    return call(
        kernel, "project_in", [(HBM, x), (HBM, w), (HBM, a), (HBM, b), (HBM, vec)],
        [act, act, act, (VMEM, (2, sequences * HALO, width), BF16), (HBM,) + small],
        [((tokens, width), BF16), ((width, 3 * width), BF16), ((2, rank, width), F32),
         ((2, rank, width), F32), ((8, width), BF16), small, 7, 1],
        2 * tokens * width * width * 3, 12000000, 10)


def far_call(sequences, length, q, k, v, ids):
    tokens, width = q.shape

    def kernel(q_ref, k_ref, v_ref, own_ref, live_ref, out_ref, bias_ref, *scratch):
        where = Side(False, length, (own_ref, None, live_ref))
        where.biases(sequences, bias_ref, None)
        loop(sequences, lambda s: attention_forward(
            where, s, q_ref, k_ref, v_ref, out_ref,
            lambda s, sub: rows_at(s * BLOCK + sub * SUB, SUB, SUB), bias_ref, scratch))

    return call(
        kernel, "attention_far", [(VMEM, item) for item in (q, k, v, ids[0])] + [(VMEM, ids[2])],
        [(VMEM, (sequences * BLOCK, width), BF16)],
        [bias_shape(sequences, False)] + attention_scratch(), 2000000000, 6000000, 8)[0]


def near_forward(near, sequences, length, far_ref, q_ref, k_ref, v_ref, halo_ref, nk_ref,
                 nv_ref, mix_ref, bias_ref, scratch):
    def one(s):
        near_keys(s, length, k_ref, v_ref, halo_ref, nk_ref, nv_ref)
        mix_ref[rows_at(s * length + near.side * BLOCK, BLOCK, BLOCK), :] = far_ref[
            rows_at(s * BLOCK, BLOCK, BLOCK), :]
        attention_forward(near, s, q_ref, nk_ref, nv_ref, mix_ref, near.queries, bias_ref,
                          scratch)

    loop(sequences, one)


def middle_call(layer, sequences, length, ids, far, q, k, v, halo, h, w, a, b, wo, wu, wd, vec,
                bias_up):
    tokens, width = q.shape
    hidden, rank = wu.shape[2], a.shape[2]

    def kernel(own_ref, other_ref, live_ref, far_ref, q_ref, k_ref, v_ref, halo_ref, h_hbm, w_hbm, a_hbm,
               b_hbm, wo_hbm, wu_hbm, wd_hbm, vec_hbm, bu_hbm,
               q2_ref, k2_ref, v2_ref, send_ref,
               u_out, x_out, h_out, n1_out, r1_out, dg_out, n2_out, r2_out, q_out, k_out, v_out,
               nk_out, nv_out, mix_out,
               h_ref, w_ref, wo_ref, wu_ref, wd_ref, vec_ref, bu_ref, vec2_ref, a_ref, b_ref,
               u_ref, mix_ref, one_ref, low_ref, act_ref,
               n1_ref, r1_ref, dg_ref, n2_ref, r2_ref, nk_ref, nv_ref, ins, outs, bias_ref,
               *scratch):
        loads = start_all(copies_of(
            [(h_hbm, h_ref), (vec_hbm.at[layer], vec_ref), (wo_hbm.at[layer], wo_ref),
             (bu_hbm, bu_ref), (wu_hbm.at[layer], wu_ref), (wd_hbm.at[layer], wd_ref),
             (w_hbm.at[layer + 1], w_ref), (a_hbm.at[layer + 1], a_ref),
             (b_hbm.at[layer + 1], b_ref), (vec_hbm.at[layer + 1], vec2_ref)], ins))
        stores = copies_of(
            [(q_ref, q_out), (k_ref, k_out), (v_ref, v_out), (nk_ref, nk_out), (nv_ref, nv_out),
             (n1_ref, n1_out), (r1_ref, r1_out), (dg_ref, dg_out), (n2_ref, n2_out),
             (r2_ref, r2_out), (one_ref, h_out), (low_ref, x_out), (u_ref, u_out),
             (mix_ref, mix_out)], outs)
        near = Side(True, length, (own_ref, other_ref, live_ref))
        near.biases(sequences, bias_ref, None)
        near_forward(near, sequences, length, far_ref, q_ref, k_ref, v_ref, halo_ref, nk_ref,
                     nv_ref, mix_ref, bias_ref, scratch)
        layer_rest(layer, sequences, length, mix_ref, h_ref, wo_ref, wu_ref, wd_ref,
                   [wait_for(loads, 0, 1, 2), wait_for(loads, 3, 4), wait_for(loads, 5)], vec_ref,
                   bu_ref, one_ref, low_ref, act_ref, n1_ref, r1_ref, dg_ref, n2_ref, r2_ref,
                   (one_ref, low_ref),
                   lambda i: start_all((stores[:7] + stores[13:], stores[7:8], stores[8:12])[i]))
        nothing = wait_for(loads)
        project_in(sequences, length, low_ref, w_ref,
                   [wait_for(loads, 6, 7, 8, 9), nothing, nothing], a_ref, b_ref, vec2_ref, q2_ref,
                   k2_ref, v2_ref, u_ref, send_ref, stores[12].start)
        for copy in stores:
            copy.wait()

    act, stat = ((tokens, width), BF16), ((tokens, 128), F32)
    wide, deep = ((tokens, width), F32), ((tokens, hidden), BF16)
    near, small = ((sequences * (WINDOW + SUB), width), BF16), ((tokens, 2 * rank), BF16)
    factors = ((2, rank, width), F32)
    return call(
        kernel, "middle",
        [(VMEM, ids[0]), (VMEM, ids[1]), (VMEM, ids[2]), (VMEM, far), (VMEM, q), (VMEM, k), (VMEM, v),
         (VMEM, halo)]
        + [(HBM, item) for item in (h, w, a, b, wo, wu, wd, vec, bias_up)],
        [(VMEM,) + act, (VMEM,) + act, (VMEM,) + act, (VMEM, (2, sequences * HALO, width), BF16)]
        + [(HBM,) + item for item in (small, act, wide, act, stat, deep, act, stat, act, act, act,
                                      near, near, act)],
        [(h.shape, h.dtype), ((width, 3 * width), BF16), ((width, width), BF16),
         ((width, hidden), BF16), ((hidden, width), BF16), ((8, width), BF16),
         (bias_up.shape, BF16), ((8, width), BF16), factors, factors, small, act, wide, act, deep,
         act, stat, deep, act, stat, near, near, 10, 14,
         bias_shape(sequences, False)] + attention_scratch(),
        2 * tokens * width * (2 * hidden + 4 * width), 24000000, 42)


def turn_call(layer, sequences, length, ids, far, q, k, v, halo, h, gradient, wo, wu, wd,
              vec, bias_up):
    tokens, width = q.shape
    hidden = wu.shape[2]

    def kernel(own_ref, other_ref, live_ref, far_ref, q_ref, k_ref, v_ref, halo_ref, h_hbm, g_hbm,
               wo_hbm, wu_hbm, wd_hbm, vec_hbm, bu_hbm,
               datt_ref, dfar_ref, dq_ref, dnk_ref, dnv_ref, dhalo_ref, delta_ref, hidden_out,
               h_ref, g_ref, wo_ref, wu_ref, wd_ref, vec_ref, bu_ref, mix_ref, one_ref, low_ref,
               act_ref, n1_ref, r1_ref, dg_ref, n2_ref, r2_ref, nk_ref, nv_ref, last_ref, ins, outs,
               bias_ref, columns_ref, *scratch):
        loads = start_all(copies_of(
            [(h_hbm, h_ref), (vec_hbm.at[layer], vec_ref), (wo_hbm.at[layer], wo_ref),
             (bu_hbm, bu_ref), (wu_hbm.at[layer], wu_ref), (wd_hbm.at[layer], wd_ref),
             (g_hbm, g_ref)], ins))
        store = pltpu.make_async_copy(last_ref, hidden_out, outs.at[0])
        near = Side(True, length, (own_ref, other_ref, live_ref))
        near.biases(sequences, bias_ref, columns_ref)
        near_forward(near, sequences, length, far_ref, q_ref, k_ref, v_ref, halo_ref, nk_ref,
                     nv_ref, mix_ref, bias_ref, scratch)
        side = lax.axis_index("seq")
        layer_rest(layer, sequences, length, mix_ref, h_ref, wo_ref, wu_ref, wd_ref,
                   [wait_for(loads, 0, 1, 2), wait_for(loads, 3, 4), wait_for(loads, 5)], vec_ref,
                   bu_ref, one_ref, low_ref, act_ref, n1_ref, r1_ref, dg_ref, n2_ref, r2_ref,
                   (last_ref,), lambda i: None)
        store.start()

        def given(s, rows):
            places = lax.broadcasted_iota(jnp.int32, (length, 1), 0) + side * length
            return jnp.where(
                places.astype(F32) < picked(live_ref, s), g_ref[rows, :].astype(F32), 0.0)

        nothing = wait_for(loads)
        layer_rest_back(sequences, length, given,
                        [wait_for(loads, 6), nothing, nothing, nothing], n1_ref,
                        r1_ref, dg_ref, n2_ref, r2_ref, wo_ref, wu_ref, wd_ref, vec_ref, one_ref,
                        low_ref, act_ref, datt_ref, mix_ref, delta_ref)
        near_backward(near, sequences, length, q_ref, nk_ref, nv_ref, low_ref,
                      delta_ref, dfar_ref, dq_ref, dnk_ref, dnv_ref, dhalo_ref, columns_ref, scratch)
        store.wait()

    act, stat = ((tokens, width), BF16), ((tokens, 128), F32)
    wide, deep = ((tokens, width), F32), ((tokens, hidden), BF16)
    near_rows = sequences * (WINDOW + SUB)
    near, block = ((near_rows, width), BF16), ((sequences * BLOCK, width), BF16)
    return call(
        kernel, "turn",
        [(VMEM, ids[0]), (VMEM, ids[1]), (VMEM, ids[2]), (VMEM, far), (VMEM, q), (VMEM, k),
         (VMEM, v), (VMEM, halo)]
        + [(HBM, item) for item in (h, gradient, wo, wu, wd, vec, bias_up)],
        [(VMEM,) + wide, (VMEM,) + block, (VMEM,) + block, (VMEM, (near_rows, width), F32),
         (VMEM, (near_rows, width), F32), (VMEM, (2, sequences * HALO, width), BF16),
         (VMEM, (HEAD_ROWS * sequences, length), F32), (HBM,) + act],
        [(h.shape, h.dtype), act, ((width, width), BF16), ((width, hidden), BF16),
         ((hidden, width), BF16), ((8, width), BF16), (bias_up.shape, BF16), act, wide, act, deep,
         act, stat, deep, act, stat, near, near, act, 7, 1, bias_shape(sequences, False),
         bias_shape(sequences, True)] + attention_scratch(True),
        4 * tokens * width * (2 * hidden + width), 24000000, 42)


def back_far_call(sequences, length, ids, q, k, v, dfar, delta, dq_near, dnk, dnv):
    tokens, width = q.shape

    def kernel(own_ref, live_ref, q_ref, k_ref, v_ref, dfar_ref, delta_ref, dqn_ref, dnk_ref,
               dnv_ref, dq_ref, dk_ref, dv_ref, bias_ref,
               *scratch):
        far = Side(False, length, (own_ref, None, live_ref))
        far.biases(sequences, None, bias_ref)
        side, wide, own = far.side, WINDOW + SUB, WINDOW + SUB - HALO

        def key_terms(s, cols, kept):
            for out, which, other in ((dv_ref, 0, 3), (dk_ref, 1, 2)):
                left = jnp.concatenate([item[which] for item in kept], axis=1)
                right = jnp.concatenate([item[other] for item in kept], axis=0)
                out[far.keys(s, 0), cols] = dot_nn(left, right)

        def one(s):
            attention_backward(
                far, s, q_ref, k_ref, v_ref, dfar_ref,
                lambda s, sub: rows_at(s * BLOCK + sub * SUB, SUB, SUB), delta_ref, dq_ref,
                far.queries, key_terms, bias_ref, scratch)
            dq_ref[rows_at(s * length + (1 - side) * BLOCK, BLOCK, BLOCK), :] = dqn_ref[
                rows_at(s * BLOCK, BLOCK, BLOCK), :]
            mine = rows_at(s * length + (length - own) * (1 - side), own, 32)
            theirs = rows_at(s * wide + HALO * side, own, 32)
            dk_ref[mine, :] = dk_ref[mine, :] + dnk_ref[theirs, :]
            dv_ref[mine, :] = dv_ref[mine, :] + dnv_ref[theirs, :]

        loop(sequences, one)

    wide = (VMEM, (tokens, width), F32)
    return call(
        kernel, "back_far",
        [(VMEM, ids[0]), (VMEM, ids[2])]
        + [(VMEM, item) for item in (q, k, v, dfar, delta, dq_near, dnk, dnv)],
        [(VMEM, (tokens, width), BF16), wide, wide],
        [bias_shape(sequences, True)] + attention_scratch(True), 4000000000, 16000000, 8)


def back_call(layer, sequences, length, ids, dq, dk, dv, dhalo, datt, u, x, saved, w, a, b, wo, wu,
              wd, vec):
    tokens, width = dq.shape
    hidden, rank = wu.shape[2], a.shape[2]

    def kernel(own_ref, other_ref, live_ref, dq_ref, dk_ref, dv_ref, dhalo_ref, datt_ref, u_hbm, x_hbm,
               n1_hbm, r1_hbm, dg_hbm, n2_hbm, r2_hbm, q_hbm, k_hbm, v_hbm, nk_hbm, nv_hbm, mix_hbm,
               w_hbm, a_hbm, b_hbm, wo_hbm, wu_hbm, wd_hbm, vec_hbm,
               datt_out, dfar_ref, dqn_ref, dnk_ref, dnv_ref, dhalo_out, delta_ref, q_ref, k_ref,
               v_ref, grad_out,
               u_ref, x_ref, n1_ref, r1_ref, dg_ref, n2_ref, r2_ref, nk_ref, nv_ref, w_ref,
               a_ref, b_ref, wo_ref, wu_ref, wd_ref, vec_ref, dkb_ref, dvb_ref, du_ref, grad_ref,
               two_ref, low_ref, mix_ref, ins, outs, bias_ref, *scratch):
        loads = start_all(copies_of(
            [(a_hbm.at[layer + 1], a_ref), (b_hbm.at[layer + 1], b_ref), (u_hbm, u_ref),
             (x_hbm, x_ref), (w_hbm.at[layer + 1], w_ref), (vec_hbm.at[layer], vec_ref),
             (n2_hbm, n2_ref), (r2_hbm, r2_ref), (wd_hbm.at[layer], wd_ref), (dg_hbm, dg_ref),
             (wu_hbm.at[layer], wu_ref), (n1_hbm, n1_ref), (r1_hbm, r1_ref),
             (wo_hbm.at[layer], wo_ref), (q_hbm, q_ref), (nk_hbm, nk_ref), (nv_hbm, nv_ref),
             (k_hbm, k_ref), (v_hbm, v_ref), (mix_hbm, mix_ref)], ins))
        adapter_back(sequences, length, [wait_for(loads, 0, 1), wait_for(loads, 2, 3)], dq_ref, dk_ref, dv_ref, dhalo_ref, u_ref, x_ref,
                     a_ref, b_ref, dkb_ref, dvb_ref, du_ref, grad_ref)
        store = pltpu.make_async_copy(grad_ref, grad_out, outs.at[0])
        store.start()
        down, _, _ = low_rank(a_ref, b_ref)

        wait_for(loads, 4)()
        tall = tokens // 2

        def given(s, rows):
            return two_ref[rows, :]

        def project(i):
            rows = rows_at(i * tall, tall, 128)
            two_ref[rows, :] = project_back(rows, rows, datt_ref, dq_ref, dkb_ref, dvb_ref, du_ref,
                                            w_ref, down)

        loop(2, project)
        layer_rest_back(sequences, length, given,
                        [wait_for(loads, 5, 6, 7), wait_for(loads, 8, 9), wait_for(loads, 10),
                         wait_for(loads, 11, 12, 13, 19)], n1_ref, r1_ref, dg_ref, n2_ref, r2_ref,
                        wo_ref, wu_ref, wd_ref, vec_ref, two_ref, low_ref, dg_ref, datt_out,
                        mix_ref, delta_ref)
        wait_for(loads, 14, 15, 16)()
        near = Side(True, length, (own_ref, other_ref, live_ref))
        near.biases(sequences, None, bias_ref)
        near_backward(near, sequences, length, q_ref, nk_ref, nv_ref, low_ref,
                      delta_ref, dfar_ref, dqn_ref, dnk_ref, dnv_ref, dhalo_out, bias_ref, scratch)
        wait_for(loads, 17, 18)()
        store.wait()

    act, stat = ((tokens, width), BF16), ((tokens, 128), F32)
    wide, deep = ((tokens, width), F32), ((tokens, hidden), BF16)
    near_rows = sequences * (WINDOW + SUB)
    near, block = ((near_rows, width), BF16), ((sequences * BLOCK, width), BF16)
    small, factors = ((tokens, 2 * rank), BF16), ((2, rank, width), F32)
    grad = ((4 * rank, width), F32)
    return call(
        kernel, "back",
        [(VMEM, ids[0]), (VMEM, ids[1]), (VMEM, ids[2])]
        + [(VMEM, item) for item in (dq, dk, dv, dhalo, datt)]
        + [(HBM, item) for item in (u, x, *saved, w, a, b, wo, wu, wd, vec)],
        [(VMEM,) + wide, (VMEM,) + block, (VMEM,) + block,
         (VMEM, (near_rows, width), F32), (VMEM, (near_rows, width), F32),
         (VMEM, (2, sequences * HALO, width), BF16), (VMEM, (HEAD_ROWS * sequences, length), F32),
         (VMEM,) + act, (VMEM,) + act, (VMEM,) + act,
         (HBM,) + grad],
        [small, act, act, stat, deep, act, stat, near, near, ((width, 3 * width), BF16), factors,
         factors, ((width, width), BF16), ((width, hidden), BF16), ((hidden, width), BF16),
         ((8, width), BF16), act, act, small, grad, wide, act, act, 20, 1, bias_shape(sequences, True)]
        + attention_scratch(True),
        2 * tokens * width * (2 * hidden + 4 * width), 24000000, 38)


def last_call(layer, sequences, length, dq, dk, dv, dhalo, u, x, w, a, b, other, *state):
    tokens, width = dq.shape
    rank = a.shape[2]

    def kernel(dq_ref, dk_ref, dv_ref, dhalo_ref, u_hbm, x_hbm, w_hbm, a_hbm, b_hbm, other_hbm,
               *rest):
        given, rest = rest[:len(state)], rest[len(state):]
        (dkb_ref, dvb_ref, du_ref, w_ref, down_ref, mine_ref, theirs_ref), rest = rest[:7], rest[7:]
        taken, rest = rest[:len(state)], rest[len(state):]
        u_ref, x_ref, a_ref, b_ref, other_ref, grad_ref, sems, state_sems = rest
        loads = start_all(copies_of(
            [(a_hbm.at[layer], a_ref), (b_hbm.at[layer], b_ref), (u_hbm, u_ref), (x_hbm, x_ref),
             (other_hbm, other_ref), (w_hbm.at[layer], w_ref)], sems))
        more = start_all(copies_of(zip(given, taken), state_sems))
        adapter_back(sequences, length, [wait_for(loads, 0, 1), wait_for(loads, 2, 3)], dq_ref, dk_ref, dv_ref, dhalo_ref, u_ref, x_ref,
                     a_ref, b_ref, dkb_ref, dvb_ref, du_ref, grad_ref)
        down_ref[...] = low_rank(a_ref, b_ref)[0]
        wait_for(loads, 4)()
        first = lax.axis_index("seq") == layer
        here, there = grad_ref[...], other_ref[...]
        mine_ref[...] = jnp.where(first, here, there)
        theirs_ref[...] = jnp.where(first, there, here)
        wait_for(loads, 5)()
        for copy in more:
            copy.wait()

    act, grad = ((tokens, width), BF16), ((4 * rank, width), F32)
    small, factors = ((tokens, 2 * rank), BF16), ((2, rank, width), F32)
    return call(
        kernel, "adapter_back",
        [(VMEM, dq), (VMEM, dk), (VMEM, dv), (VMEM, dhalo)]
        + [(HBM, item) for item in (u, x, w, a, b, other, *state)],
        [(VMEM,) + act, (VMEM,) + act, (VMEM,) + small, (VMEM, (width, 3 * width), BF16),
         (VMEM, (2 * rank, width), BF16), (VMEM,) + grad, (VMEM,) + grad]
        + [(VMEM, item.shape, F32) for item in state],
        [small, act, factors, factors, grad, grad, 6, len(state)], 500000000, 12000000, 8)


def project_back_call(datt, dq, dk, dv, du, w, down):
    tokens, width = dq.shape
    parts = 2
    length = tokens // parts

    def kernel(datt_ref, dq_ref, dk_ref, dv_ref, du_ref, w_ref, down_ref, out_hbm, out_ref, sems):
        def part(i):
            rows = rows_at(i * length, length, 128)
            return pltpu.make_async_copy(out_ref.at[rows], out_hbm.at[rows], sems.at[i])

        def one(i):
            rows = rows_at(i * length, length, 128)
            out_ref[rows, :] = project_back(rows, rows, datt_ref, dq_ref, dk_ref, dv_ref, du_ref,
                                            w_ref, down_ref[...])
            part(i).start()

        loop(parts, one)
        for i in range(parts):
            part(i).wait()

    return call(
        kernel, "project_back", [(VMEM, item) for item in (datt, dq, dk, dv, du, w, down)],
        [(HBM, (tokens, width), F32)], [((tokens, width), F32), parts],
        2 * tokens * width * width * 3, 4000000, 6)[0]


def adam_call(mine, theirs, token_slots, steps, down, up, m_down, v_down, m_up, v_up):
    layers, two, rank, width = down.shape

    def kernel(mine_ref, theirs_ref, steps_ref, down_ref, up_ref, md_ref, vd_ref, mu_ref, vu_ref,
               *rest):
        outs, results, sems = rest[:6], rest[6:12], rest[12]
        down_out, up_out, md_out, vd_out, mu_out, vu_out = results
        side = lax.axis_index("seq")
        for layer in range(layers):
            for which in range(two):
                for group, (w_ref, m_ref, v_ref, w_out, m_out, v_out, rate, decay) in enumerate((
                    (down_ref, md_ref, vd_ref, down_out, md_out, vd_out, 0.03125, 0.1),
                    (up_ref, mu_ref, vu_ref, up_out, mu_out, vu_out, 0.5, 0.0),
                )):
                    rows = slice((group * two + which) * rank, (group * two + which + 1) * rank)
                    grad = jnp.where(side == layer, mine_ref[rows, :], theirs_ref[rows, :])
                    grad = grad / token_slots
                    step = picked(steps_ref, (layer * two + which) * 2 + group)
                    correction = jnp.broadcast_to(1.0 - jnp.exp2(-step), (rank, width))
                    weight = w_ref[layer, which]
                    moment = 0.5 * m_ref[layer, which] + 0.5 * grad
                    velocity = 0.5 * v_ref[layer, which] + 0.5 * grad * grad
                    size = moment / correction / (jnp.sqrt(velocity / correction) + 1e-08)
                    w_out[layer, which] = weight - rate * (size + decay * weight)
                    m_out[layer, which] = moment
                    v_out[layer, which] = velocity

        for store in start_all(copies_of(zip(results, outs), sems)):
            store.wait()

    return call(
        kernel, "adam",
        [(VMEM, mine), (VMEM, theirs), (VMEM, steps)]
        + [(VMEM, item) for item in (down, up, m_down, v_down, m_up, v_up)],
        [(HBM, down.shape, F32)] * 6, [(down.shape, F32)] * 6 + [6], 1000000, 2000000, 4)


def together(*values):
    return lax.optimization_barrier(values)


def sum_while(mine, theirs, work):
    batch = lax.axis_size("batch")
    swap = [(0, 1), (1, 0)]
    mine = mine + lax.ppermute(theirs, "seq", swap)
    done, work, step = None, list(work), 1
    while step < batch:
        ways = 4 if batch % (4 * step) == 0 else 2
        given = mine.astype(BF16)
        come = [lax.ppermute(given, "batch", [(i, i ^ (step * d)) for i in range(batch)])
                for d in range(1, ways)]
        if work:
            done = work.pop(0)(mine, done)
            *come, done = together(*come, done)
        mine = mine + sum(item.astype(F32) for item in come)
        step *= ways
    for one in work:
        done = one(mine, done)
    return mine, lax.ppermute(mine, "seq", swap), done


def shards(
    first_layer_input,
    output_gradient,
    sentence_pair_index,
    sequence_live_length,
    optimizer_step_count,
    query_key_value_weight,
    attention_output_weight,
    feedforward_up_weight,
    feedforward_down_weight,
    layer_bias_gain_rows,
    feedforward_up_bias,
    adapter_down_factors,
    adapter_up_factors,
    first_moment_down,
    second_moment_down,
    first_moment_up,
    second_moment_up,
):
    sequences, length, width = first_layer_input.shape
    tokens = sequences * length
    swap = [(0, 1), (1, 0)]
    a, b = adapter_down_factors, jnp.swapaxes(adapter_up_factors, 2, 3)
    vec = layer_bias_gain_rows
    bias_up = feedforward_up_bias
    wqkv, wo = query_key_value_weight, attention_output_weight
    wu, wd = feedforward_up_weight, feedforward_down_weight
    ids = (sentence_pair_index, lax.ppermute(sentence_pair_index, "seq", swap),
           sequence_live_length[None, :])
    shape = (sequences, length)

    x1 = first_layer_input.reshape(tokens, width)
    q1, k1, v1, send, u1 = first_call(0, *shape, x1, wqkv, a, b, vec)
    halo = lax.ppermute(send, "seq", swap)
    far = far_call(*shape, q1, k1, v1, ids)
    q2, k2, v2, send, u2, x2, h1, *saved = middle_call(
        0, *shape, ids, far, q1, k1, v1, halo, x1, wqkv, a, b, wo, wu, wd, vec, bias_up)
    halo = lax.ppermute(send, "seq", swap)
    far = far_call(*shape, q2, k2, v2, ids)
    datt, dfar, dqn, dnk, dnv, dsend, delta, hidden_out = turn_call(
        1, *shape, ids, far, q2, k2, v2, halo, h1, output_gradient.reshape(tokens, width),
        wo, wu, wd, vec, bias_up)
    dhalo = lax.ppermute(dsend, "seq", swap)
    dq, dk, dv = back_far_call(*shape, ids, q2, k2, v2, dfar, delta, dqn, dnk, dnv)
    datt, dfar, dqn, dnk, dnv, dsend, delta, q1, k1, v1, grad2 = back_call(
        0, *shape, ids, dq, dk, dv, dhalo, datt, u2, x2, saved, wqkv, a, b, wo, wu, wd, vec)
    dhalo = lax.ppermute(dsend, "seq", swap)
    dq, dk, dv = back_far_call(*shape, ids, q1, k1, v1, dfar, delta, dqn, dnk, dnv)
    dk, dv, du, w1, down1, mine, theirs, *state = last_call(
        0, *shape, dq, dk, dv, dhalo, u1, x1, wqkv, a, b, grad2, a, b, first_moment_down,
        second_moment_down, jnp.swapaxes(first_moment_up, 2, 3),
        jnp.swapaxes(second_moment_up, 2, 3))

    def work(token, out):
        now, _ = together(datt, token)
        return project_back_call(now, dq, dk, dv, du, w1, down1)

    mine, theirs, gradient = sum_while(mine, theirs, [work])
    token_slots = tokens * lax.axis_size("seq") * lax.axis_size("batch")
    down, up, m_down, v_down, m_up, v_up = adam_call(
        mine, theirs, token_slots, optimizer_step_count.reshape(1, -1), *state)
    return (
        hidden_out.reshape(sequences, length, width),
        gradient.reshape(sequences, length, width),
        down,
        jnp.swapaxes(up, 2, 3),
        m_down,
        v_down,
        jnp.swapaxes(m_up, 2, 3),
        jnp.swapaxes(v_up, 2, 3),
    )


def solution(mesh):
    acts, whole = P("batch", "seq", None), P()
    return jax.shard_map(
        shards,
        mesh=mesh,
        in_specs=(acts, acts, P("batch", "seq"), P("batch")) + (whole,) * 13,
        out_specs=(acts, acts) + (whole,) * 6,
        check_vma=False,
    )
```

```python
import jax
import jax.numpy as jnp
from jax import lax
from jax.experimental import pallas as pl
from jax.experimental.pallas import tpu as pltpu
from jax.sharding import PartitionSpec as P

HEADS = 12
ENCODER_LAYERS = 2
HALO = 96
BLOCK = 128
SUB = 64
WINDOW = 256
QUAD = 256
HEAD_ROWS = 16
MASKED = -1000000000.0
LOG2E = 1.4426950408889634
HALF_ROOT_PI = 0.886226925452758
ROOT_HALF = 0.7071067811865476
ACTIVE = 0.7978845608028654
SLOPE = 0.5641895835477563
F32 = jnp.float32
BF16 = jnp.bfloat16


def dot_nn(a, b):
    return lax.dot_general(a, b, (((1,), (0,)), ((), ())), preferred_element_type=F32)


def dot_nt(a, b):
    return lax.dot_general(a, b, (((1,), (1,)), ((), ())), preferred_element_type=F32)


def dot_tn(a, b):
    return lax.dot_general(a, b, (((0,), (0,)), ((), ())), preferred_element_type=F32)


def rows_at(start, size, multiple):
    return pl.ds(pl.multiple_of(start, multiple), size)


def loop(count, body):
    def step(i, carry):
        body(i)
        return carry

    lax.fori_loop(0, count, step, 0)


def picked(row_ref, i):
    row = row_ref[...].astype(F32)
    at = lax.broadcasted_iota(jnp.int32, row.shape, 1) == i
    return jnp.sum(jnp.where(at, row, 0.0), axis=1, keepdims=True)


def column_of(row):
    n = row.shape[1]
    eye = lax.broadcasted_iota(jnp.int32, (n, n), 0) == lax.broadcasted_iota(jnp.int32, (n, n), 1)
    return jnp.sum(jnp.where(eye, row, 0.0), axis=1, keepdims=True)


def low_lanes():
    return (lax.broadcasted_iota(jnp.int32, (SUB, 128), 1) < 64).astype(F32).astype(BF16)


def spread_heads(tile, low):
    zero = jnp.zeros((2 * SUB, 128), BF16)
    high = 1 - low
    left, right = tile[:, :128], tile[:, 128:]
    left = jnp.concatenate([left * low, left * high], axis=0)
    right = jnp.concatenate([right * low, right * high], axis=0)
    return jnp.concatenate([jnp.concatenate([left, zero], axis=1),
                            jnp.concatenate([zero, right], axis=1)], axis=0)


def gather_heads(wide):
    low = lax.broadcasted_iota(jnp.int32, (SUB, 128), 1) < 64
    parts = []
    for i in range(2):
        cols, top = slice(128 * i, 128 * i + 128), 2 * SUB * i
        parts.append(jnp.where(low, wide[top:top + SUB, cols],
                               wide[top + SUB:top + 2 * SUB, cols]))
    return jnp.concatenate(parts, axis=1)


def pipelined(units):
    units = list(units)
    live = []
    while units or live:
        if units:
            live.append(units.pop(0))
        for unit in reversed(list(live)):
            if next(unit, None) is None:
                live.remove(unit)


class Side:
    def __init__(self, near, length, ids_refs):
        self.near, self.length, self.ids_refs = near, length, ids_refs
        self.side = lax.axis_index("seq")
        self.row0 = BLOCK * ((1 - self.side) if near else self.side)

    def ids(self, s):
        own_ref, other_ref, live_ref = self.ids_refs
        own = own_ref[pl.ds(s, 1), :].astype(F32)
        query = jnp.where(self.row0 == 0, own[:, :BLOCK], own[:, BLOCK:])
        if self.near:
            other = other_ref[pl.ds(s, 1), :].astype(F32)
            kept = WINDOW + SUB - HALO
            key = jnp.where(
                self.side == 0,
                jnp.concatenate([own[:, self.length - kept:], other[:, :HALO]], axis=1),
                jnp.concatenate([other[:, self.length - HALO:], own[:, :kept]], axis=1))
            start = jnp.where(self.side == 0, self.length - kept, self.length - HALO)
        else:
            key, start = own, self.side * self.length
        places = lax.broadcasted_iota(jnp.int32, key.shape, 1) + start
        return query, jnp.where(places.astype(F32) < picked(live_ref, s), key, -1.0)

    def queries(self, s, sub):
        return rows_at(s * self.length + self.row0 + sub * SUB, SUB, SUB)

    def keys(self, s, sub):
        if self.near:
            return rows_at(s * (WINDOW + SUB) + sub * SUB, WINDOW, SUB)
        return rows_at(s * self.length, WINDOW, WINDOW)

    def biases(self, s, rows_ref=None, columns_ref=None):
        lane = lax.broadcasted_iota(jnp.int32, (1, 128), 1)
        place = jnp.where(lane < SUB, lane, lane - SUB)
        key_place = lax.broadcasted_iota(jnp.int32, (WINDOW, 128), 0)
        shape = (SUB, WINDOW)
        apart = lax.broadcasted_iota(jnp.int32, shape, 1) - lax.broadcasted_iota(jnp.int32, shape, 0)
        query, key = self.ids(s)
        if rows_ref is None:
            blocks = (128, 128, SUB) if self.near else (128, 128)
            column = jnp.concatenate(
                [column_of(key[:, 128 * i:128 * i + n]) for i, n in enumerate(blocks)], axis=0)
            turned = pltpu.roll(query, SUB, 1)
        for sub in range(2):
            own = HALO if self.near else self.row0 + sub * SUB
            if rows_ref is not None:
                keys = key[:, sub * SUB:sub * SUB + WINDOW] if self.near else key
                queries = column_of(query)[sub * SUB:(sub + 1) * SUB]
                seen = (queries == keys) | (apart == own)
                rows_ref[sub * SUB:(sub + 1) * SUB, :] = jnp.where(seen, 0.0, MASKED)
                continue
            keys = column[sub * SUB:sub * SUB + WINDOW] if self.near else column
            pair = (query, turned) if sub == 0 else (turned, query)
            seen = (keys == jnp.where(lane < SUB, *pair)) | (key_place == place + own)
            columns_ref[sub * WINDOW:(sub + 1) * WINDOW, :] = jnp.where(seen, 0.0, MASKED)


def bias_shape(turned):
    return ((2 * WINDOW, 128) if turned else (2 * SUB, WINDOW)), F32


def half(sub):
    return slice(4 * SUB * sub, 4 * SUB * (sub + 1))


SLOTS = 2


def attention_scratch(backward=False):
    pair = [((SLOTS, WINDOW, 4 * SUB), F32), ((SLOTS, WINDOW, 4 * SUB), BF16)]
    return pair * 2 if backward else pair


def attention_forward(where, s, q_ref, k_ref, v_ref, out_ref, out_rows, bias_ref, scratch):
    low = low_lanes()
    scores_ref, share_ref = scratch[:2]

    def unit(quad, sub):
        cols = slice(QUAD * quad, QUAD * quad + QUAD)
        keys = where.keys(s, sub)
        q4 = spread_heads(q_ref[where.queries(s, sub), cols], low)
        slot = (2 * quad + sub) % SLOTS
        scores_ref[slot] = dot_nt(q4, k_ref[keys, cols])
        yield True
        bias = bias_ref[sub * SUB:(sub + 1) * SUB, :]
        totals = []
        for h in range(4):
            rows = slice(h * SUB, (h + 1) * SUB)
            scores = scores_ref[slot, rows, :] + bias
            share = jnp.exp2(scores - jnp.max(scores, axis=1, keepdims=True))
            totals.append(1.0 / jnp.sum(share, axis=1, keepdims=True))
            share_ref[slot, rows, :] = share.astype(BF16)
        yield True
        mixed = dot_nn(share_ref[slot], v_ref[keys, cols])
        mixed = jnp.concatenate(
            [mixed[h * SUB:(h + 1) * SUB] * totals[h] for h in range(4)], axis=0)
        yield True
        out_ref[out_rows(s, sub), cols] = gather_heads(mixed).astype(BF16)

    width = q_ref.shape[1]
    pipelined(unit(quad, sub) for quad in range(width // QUAD) for sub in range(2))


def attention_backward(where, s, q_ref, k_ref, v_ref, dmix_ref, dmix_rows, delta, dq_ref,
                       dq_rows, key_terms, bias_ref, scratch):
    low = low_lanes()
    scores_ref, share_ref, d_share_ref, d_scores_ref = scratch
    delta = jnp.where(where.row0 == 0, delta[:, :BLOCK], delta[:, BLOCK:])
    turned = pltpu.roll(delta, SUB, 1)
    first_half = lax.broadcasted_iota(jnp.int32, (1, 2 * SUB), 1) < SUB

    def unit(quad, sub, kept):
        cols = slice(QUAD * quad, QUAD * quad + QUAD)
        keys = where.keys(s, sub)
        slot = (2 * quad + sub) % SLOTS
        q4 = spread_heads(q_ref[where.queries(s, sub), cols], low)
        d4 = spread_heads(dmix_ref[dmix_rows(s, sub), cols], low)
        scores_ref[slot] = dot_nt(k_ref[keys, cols], q4)
        d_share_ref[slot] = dot_nt(v_ref[keys, cols], d4)
        yield True
        bias = bias_ref[sub * WINDOW:(sub + 1) * WINDOW, :]
        shares, d_scores = [], []
        left, right = (delta, turned) if sub == 0 else (turned, delta)
        for i in range(2):
            head = 4 * quad + 2 * i
            drop = jnp.where(first_half, left[head:head + 1], right[head + 1:head + 2])
            part = scores_ref[slot, :, 128 * i:128 * i + 128] + bias
            part = jnp.exp2(part - jnp.max(part, axis=0, keepdims=True))
            part = part * (1.0 / jnp.sum(part, axis=0, keepdims=True))
            shares.append(part.astype(BF16))
            d_scores.append((part * (d_share_ref[slot, :, 128 * i:128 * i + 128] - drop)).astype(BF16))
        d_scores = jnp.concatenate(d_scores, axis=1)
        kept.append((jnp.concatenate(shares, axis=1), d_scores, q4, d4))
        yield True
        if sub == 1:
            key_terms(s, cols, kept)
        yield True
        d_query = gather_heads(dot_tn(d_scores, k_ref[keys, cols])) * 0.125
        dq_ref[dq_rows(s, sub), cols] = d_query.astype(BF16)

    width = q_ref.shape[1]

    def units():
        for quad in range(width // QUAD):
            kept = []
            for sub in range(2):
                yield unit(quad, sub, kept)

    pipelined(units())


def row_deltas(dmix, mix):
    shape = (HEAD_ROWS, dmix.shape[1])
    own = (lax.broadcasted_iota(jnp.int32, shape, 1) // 64
           == lax.broadcasted_iota(jnp.int32, shape, 0)).astype(F32).astype(BF16)
    product = dmix.astype(F32) * mix.astype(F32)
    high = product.astype(BF16)
    rest = (product - high.astype(F32)).astype(BF16)
    return dot_nt(own, high) + dot_nt(own, rest)


def near_keys(s, length, k_ref, v_ref, halo_ref, nk_ref, nv_ref):
    side = lax.axis_index("seq")
    wide, own = WINDOW + SUB, WINDOW + SUB - HALO
    given = rows_at(s * HALO, HALO, 32)
    for i, (src, dst) in enumerate(((k_ref, nk_ref), (v_ref, nv_ref))):
        dst[rows_at(s * wide + HALO * side, own, 32), :] = src[
            rows_at(s * length + (length - own) * (1 - side), own, 32), :]
        dst[rows_at(s * wide + own * (1 - side), HALO, 32), :] = halo_ref[i, given, :]


def norm_forward(values, gain, shift):
    center = values - jnp.mean(values, axis=1, keepdims=True)
    spread = jnp.mean(center * center, axis=1, keepdims=True)
    inverse = lax.rsqrt(spread + 1e-05)
    scaled = center * inverse
    return scaled * gain + shift, scaled, inverse


def norm_backward(gradient, scaled, inverse, gain):
    inner = gradient * gain
    return inverse * (
        inner
        - jnp.mean(inner, axis=1, keepdims=True)
        - scaled * jnp.mean(inner * scaled, axis=1, keepdims=True)
    )


def low_rank(a_ref, b_ref):
    down = jnp.concatenate([a_ref[0], a_ref[1]], axis=0).astype(BF16)
    zero = jnp.zeros_like(b_ref[0])
    up_q = jnp.concatenate([b_ref[0], zero], axis=0).astype(BF16)
    up_v = jnp.concatenate([zero, b_ref[1]], axis=0).astype(BF16)
    return down, up_q, up_v


def project_in(sequences, length, x_ref, w_ref, waits, a_ref, b_ref, vec_ref, q_ref, k_ref, v_ref,
               u_ref, send_ref, sent):
    side = lax.axis_index("seq")
    width = x_ref.shape[1]
    waits[0]()
    down, up_q, up_v = low_rank(a_ref, b_ref)
    vec = vec_ref[...].astype(F32)

    tall = x_ref.shape[0] // 2

    def queries(i):
        rows = rows_at(i * tall, tall, 128)
        x = x_ref[rows, :]
        inner = dot_nt(x, down).astype(BF16)
        u_ref[rows, :] = inner
        q = dot_nn(x, w_ref[:, :width]) + vec[0:1] + 2.0 * dot_nn(inner, up_q)
        q_ref[rows, :] = (q * (0.125 * LOG2E)).astype(BF16)

    def keys(i):
        rows = rows_at(i * tall, tall, 128)
        k_ref[rows, :] = dot_nn(x_ref[rows, :], w_ref[:, width:2 * width]).astype(BF16)

    def values(i):
        rows = rows_at(i * tall, tall, 128)
        v = dot_nn(x_ref[rows, :], w_ref[:, 2 * width:]) + vec[1:2]
        v_ref[rows, :] = (v + 2.0 * dot_nn(u_ref[rows, :], up_v)).astype(BF16)

    def send(s):
        taken = rows_at(s * length + (1 - side) * (length - HALO), HALO, 32)
        for i, ref in enumerate((k_ref, v_ref)):
            send_ref[i, rows_at(s * HALO, HALO, 32), :] = ref[taken, :]

    loop(2, queries)
    sent()
    waits[1]()
    loop(2, keys)
    waits[2]()
    loop(2, values)
    loop(sequences, send)


def layer_rest(layer, sequences, length, mix_ref, h_ref, wo_ref, wu_ref, wd_ref, waits, vec_ref, bu_ref,
               one_ref, low_ref, act_ref, n1_ref, r1_ref, dg_ref, n2_ref, r2_ref, h_outs, sent):
    tokens, hidden = mix_ref.shape[0], wu_ref.shape[1]
    waits[0]()
    vec = vec_ref[...].astype(F32)
    short, units = 128, 3

    def mixed(i):
        def unit(k):
            rows = rows_at((i * units + k) * short, short, short)
            attended = dot_nn(mix_ref[rows, :], wo_ref[...]) + vec[2:3] + h_ref[rows, :].astype(F32)
            yield True
            one, scaled, inverse = norm_forward(attended, vec[4:5], vec[5:6])
            n1_ref[rows, :] = scaled.astype(n1_ref.dtype)
            r1_ref[rows, :] = jnp.broadcast_to(inverse, (short, 128))
            one_ref[rows, :] = one
            low_ref[rows, :] = (one * ROOT_HALF).astype(BF16)

        pipelined(unit(k) for k in range(units))

    loop(tokens // short // units, mixed)
    sent(0)
    waits[1]()
    tile = 1024

    def up(j):
        cols = rows_at(j * tile, tile, tile)
        bias = bu_ref[layer:layer + 1, cols].astype(F32) * ROOT_HALF
        weights = wu_ref[:, cols]

        def unit(k):
            rows = slice(k * short, (k + 1) * short)
            gate = dot_nn(low_ref[rows, :], weights)
            yield True
            gate = gate + bias
            below = HALF_ROOT_PI * lax.erf(gate) + HALF_ROOT_PI
            act_ref[rows, cols] = (gate * below).astype(BF16)
            density = jnp.exp2(gate * gate * -LOG2E)
            dg_ref[rows, cols] = (below + gate * density).astype(BF16)

        pipelined(unit(k) for k in range(tokens // short))

    loop(hidden // tile, up)
    sent(1)
    waits[2]()

    def down(s):
        rows = rows_at(s * length, length, length)
        summed = dot_nn(act_ref[rows, :], wd_ref[...]) * ACTIVE + vec[3:4] + one_ref[rows, :]
        out, scaled, inverse = norm_forward(summed, vec[6:7], vec[7:8])
        n2_ref[rows, :] = scaled.astype(n2_ref.dtype)
        r2_ref[rows, :] = jnp.broadcast_to(inverse, (length, 128))
        for h_out in h_outs:
            h_out[rows, :] = out.astype(h_out.dtype)

    loop(sequences, down)
    sent(2)


def layer_rest_back(sequences, length, gradient, waits, n1_ref, r1_ref, dg_ref, n2_ref, r2_ref,
                    wo_ref, wu_ref, wd_ref, vec_ref, two_ref, low_ref, gate_ref, datt_ref):
    tokens, hidden = low_ref.shape[0], wu_ref.shape[1]
    waits[0]()
    vec = vec_ref[...].astype(F32)
    tall = tokens // 2

    def second(s):
        rows = rows_at(s * length, length, length)
        two = norm_backward(
            gradient(s, rows), n2_ref[rows, :].astype(F32), r2_ref[rows, 0:1], vec[6:7])
        two_ref[rows, :] = two
        low_ref[rows, :] = (two * SLOPE).astype(BF16)

    loop(sequences, second)
    waits[1]()
    tile = 1024

    def down(j):
        cols = rows_at(j * tile, tile, tile)
        weights = wd_ref[cols, :]

        def unit(s):
            rows = slice(s * length, (s + 1) * length)
            gate = dot_nt(low_ref[rows, :], weights)
            yield True
            gate_ref[rows, cols] = (gate * dg_ref[rows, cols].astype(F32)).astype(BF16)

        pipelined(unit(s) for s in range(sequences))

    loop(hidden // tile, down)
    waits[2]()
    waits[3]()

    def up(i):
        rows = rows_at(i * tall, tall, 128)
        datt_ref[rows, :] = dot_nt(gate_ref[rows, :], wu_ref[...])

    def first(s):
        rows = rows_at(s * length, length, length)
        att = norm_backward(datt_ref[rows, :] + two_ref[rows, :], n1_ref[rows, :].astype(F32),
                            r1_ref[rows, 0:1], vec[4:5])
        datt_ref[rows, :] = att
        low_ref[rows, :] = att.astype(BF16)

    def mixture(i):
        rows = rows_at(i * tall, tall, 128)
        low_ref[rows, :] = dot_nt(low_ref[rows, :], wo_ref[...]).astype(BF16)

    loop(2, up)
    loop(sequences, first)
    loop(2, mixture)


def near_backward(near, sequences, length, q_ref, nk_ref, nv_ref, dmix_ref, mix_ref,
                  delta_ref, dfar_ref, dq_ref, dnk_ref, dnv_ref, dhalo_ref, bias_ref, scratch):
    side, all_rows = near.side, length + HALO
    width = q_ref.shape[1]

    def key_terms(s, cols, kept):
        for out, which, other in ((dnv_ref, 0, 3), (dnk_ref, 1, 2)):
            left, right = [item[which] for item in kept], [item[other] for item in kept]
            start = s * all_rows + (length + HALO - WINDOW - SUB) * (1 - side)
            out[rows_at(start, SUB, 32), cols] = dot_nn(left[0][:SUB], right[0])
            both = jnp.concatenate([left[0][SUB:], left[1][:WINDOW - SUB]], axis=1)
            out[rows_at(start + SUB, WINDOW - SUB, 32), cols] = dot_nn(
                both, jnp.concatenate(right, axis=0))
            out[rows_at(start + WINDOW, SUB, 32), cols] = dot_nn(
                left[1][WINDOW - SUB:], right[1])

    def one(s):
        dfar_ref[rows_at(s * BLOCK, BLOCK, BLOCK), :] = dmix_ref[
            rows_at(s * length + side * BLOCK, BLOCK, BLOCK), :]
        near.biases(s, None, bias_ref)
        rows = rows_at(s * length, length, length)
        delta = row_deltas(dmix_ref[rows, :], mix_ref[rows, :])
        delta_ref[rows_at(s * HEAD_ROWS, HEAD_ROWS, HEAD_ROWS), :] = delta
        attention_backward(
            near, s, q_ref, nk_ref, nv_ref, dmix_ref, near.queries, delta, dq_ref,
            lambda s, sub: rows_at(s * BLOCK + sub * SUB, SUB, SUB), key_terms, bias_ref,
            scratch)
        unseen = rows_at(s * all_rows + (WINDOW + SUB) * side, all_rows - WINDOW - SUB, 32)
        for out in (dnk_ref, dnv_ref):
            out[unseen, :] = jnp.zeros((all_rows - WINDOW - SUB, width), F32)
        halo = rows_at(s * all_rows + length * (1 - side), HALO, 32)
        dhalo_ref[0, rows_at(s * HALO, HALO, 32), :] = (
            dnk_ref[halo, :] * (1.0 / LOG2E)).astype(BF16)
        dhalo_ref[1, rows_at(s * HALO, HALO, 32), :] = dnv_ref[halo, :].astype(BF16)

    loop(sequences, one)


def adapter_back(sequences, length, waits, dq_ref, dk_ref, dv_ref, dhalo_ref, u_ref, x_ref, a_ref,
                 b_ref, dkb_ref, dvb_ref, du_ref, grad_ref):
    side = lax.axis_index("seq")
    rank = a_ref.shape[1]
    waits[0]()
    _, up_q, up_v = low_rank(a_ref, b_ref)

    def one(s):
        rows = rows_at(s * length, length, length)
        taken = rows_at(s * length + (1 - side) * (length - HALO), HALO, 32)
        hrows = rows_at(s * HALO, HALO, 32)
        dvb_ref[rows, :] = dv_ref[rows, :].astype(BF16)
        dvb_ref[taken, :] = (dv_ref[taken, :] + dhalo_ref[1, hrows, :].astype(F32)).astype(BF16)
        dkb_ref[rows, :] = (dk_ref[rows, :] * (1.0 / LOG2E)).astype(BF16)
        dkb_ref[taken, :] = (
            dk_ref[taken, :] * (1.0 / LOG2E) + dhalo_ref[0, hrows, :].astype(F32)).astype(BF16)
        dv16 = dvb_ref[rows, :]
        du_ref[rows, :] = (2.0 * (dot_nt(dq_ref[rows, :], up_q) + dot_nt(dv16, up_v))).astype(BF16)

    loop(sequences, one)
    waits[1]()
    u = u_ref[...]
    grad_ref[0:2 * rank, :] = dot_tn(du_ref[...], x_ref[...])
    up_q, up_v = dot_tn(u, dq_ref[...]), dot_tn(u, dvb_ref[...])
    grad_ref[2 * rank:3 * rank, :] = 2.0 * up_q[:rank]
    grad_ref[3 * rank:, :] = 2.0 * up_v[rank:]


def project_back(rows, own_rows, datt_ref, dq_ref, dk_ref, dv_ref, du_ref, w_ref, down):
    width = dq_ref.shape[1]
    out = datt_ref[rows, :] + dot_nn(du_ref[rows, :], down)
    out = out + dot_nt(dq_ref[rows, :], w_ref[:, :width])
    out = out + dot_nt(dk_ref[rows, :], w_ref[:, width:2 * width])
    return out + dot_nt(dv_ref[rows, :], w_ref[:, 2 * width:])


HBM, VMEM = pltpu.HBM, pltpu.VMEM


def call(kernel, name, args, outs, scratch, flops, nbytes, limit, aliases=None):
    scratch = [pltpu.SemaphoreType.DMA((s,)) if isinstance(s, int) else pltpu.VMEM(*s)
               for s in scratch]
    return pl.pallas_call(
        kernel,
        name=name,
        out_shape=tuple(space(shape, dtype) for space, shape, dtype in outs),
        in_specs=[pl.BlockSpec(memory_space=space) for space, _ in args],
        out_specs=tuple(pl.BlockSpec(memory_space=space) for space, _, _ in outs),
        scratch_shapes=scratch,
        input_output_aliases=aliases or {},
        compiler_params=pltpu.CompilerParams(vmem_limit_bytes=limit * 1024 * 1024),
        cost_estimate=pl.CostEstimate(flops=flops, bytes_accessed=nbytes, transcendentals=0),
    )(*[pltpu.with_memory_space_constraint(array, space) for space, array in args])


def sds(shape, dtype):
    return jax.ShapeDtypeStruct(shape, dtype)


def copies_of(pairs, sems):
    return [pltpu.make_async_copy(src, dst, sems.at[i]) for i, (src, dst) in enumerate(pairs)]


def start_all(copies):
    for copy in copies:
        copy.start()
    return copies


def wait_for(copies, *which):
    def wait():
        for i in which:
            copies[i].wait()

    return wait


def first_call(layer, sequences, length, x, w, a, b, vec):
    tokens, width = x.shape
    rank = a.shape[2]

    def kernel(x_hbm, w_hbm, a_hbm, b_hbm, vec_hbm, q_ref, k_ref, v_ref, send_ref, u_out, x_ref,
               w_ref, a_ref, b_ref, vec_ref, u_ref, sems, outs):
        thirds = [slice(i * width, (i + 1) * width) for i in range(3)]
        copies = start_all(copies_of(
            [(a_hbm.at[layer], a_ref), (b_hbm.at[layer], b_ref), (vec_hbm.at[layer], vec_ref),
             (x_hbm, x_ref)] + [(w_hbm.at[layer, :, part], w_ref.at[:, part]) for part in thirds],
            sems))
        store = pltpu.make_async_copy(u_ref, u_out, outs.at[0])
        project_in(sequences, length, x_ref, w_ref,
                   [wait_for(copies, 0, 1, 2, 3, 4), wait_for(copies, 5), wait_for(copies, 6)],
                   a_ref, b_ref, vec_ref, q_ref, k_ref, v_ref, u_ref, send_ref, store.start)
        store.wait()

    act, small = (VMEM, (tokens, width), BF16), ((tokens, 2 * rank), BF16)
    return call(
        kernel, "project_in", [(HBM, x), (HBM, w), (HBM, a), (HBM, b), (HBM, vec)],
        [act, act, act, (VMEM, (2, sequences * HALO, width), BF16), (HBM,) + small],
        [((tokens, width), BF16), ((width, 3 * width), BF16), ((2, rank, width), F32),
         ((2, rank, width), F32), ((8, width), BF16), small, 7, 1],
        2 * tokens * width * width * 3, 12000000, 10)


def far_call(sequences, length, q, k, v, ids):
    tokens, width = q.shape

    def kernel(q_ref, k_ref, v_ref, own_ref, live_ref, out_ref, bias_ref, *scratch):
        where = Side(False, length, (own_ref, None, live_ref))

        def one(s):
            where.biases(s, bias_ref)
            attention_forward(
                where, s, q_ref, k_ref, v_ref, out_ref,
                lambda s, sub: rows_at(s * BLOCK + sub * SUB, SUB, SUB), bias_ref, scratch)

        loop(sequences, one)

    return call(
        kernel, "attention_far", [(VMEM, item) for item in (q, k, v, ids[0])] + [(VMEM, ids[2])],
        [(VMEM, (sequences * BLOCK, width), BF16)],
        [bias_shape(False)] + attention_scratch(), 2000000000, 6000000, 8)[0]


def near_forward(near, sequences, length, far_ref, q_ref, k_ref, v_ref, halo_ref, nk_ref,
                 nv_ref, mix_ref, bias_ref, scratch):
    def one(s):
        near.biases(s, bias_ref)
        near_keys(s, length, k_ref, v_ref, halo_ref, nk_ref, nv_ref)
        mix_ref[rows_at(s * length + near.side * BLOCK, BLOCK, BLOCK), :] = far_ref[
            rows_at(s * BLOCK, BLOCK, BLOCK), :]
        attention_forward(near, s, q_ref, nk_ref, nv_ref, mix_ref, near.queries, bias_ref,
                          scratch)

    loop(sequences, one)


def middle_call(layer, sequences, length, ids, far, q, k, v, halo, h, w, a, b, wo, wu, wd, vec,
                bias_up):
    tokens, width = q.shape
    hidden, rank = wu.shape[2], a.shape[2]

    def kernel(own_ref, other_ref, live_ref, far_ref, q_ref, k_ref, v_ref, halo_ref, h_hbm, w_hbm, a_hbm,
               b_hbm, wo_hbm, wu_hbm, wd_hbm, vec_hbm, bu_hbm,
               q2_ref, k2_ref, v2_ref, send_ref,
               u_out, x_out, h_out, n1_out, r1_out, dg_out, n2_out, r2_out, q_out, k_out, v_out,
               nk_out, nv_out, mix_out,
               h_ref, w_ref, wo_ref, wu_ref, wd_ref, vec_ref, bu_ref, vec2_ref, a_ref, b_ref,
               u_ref, mix_ref, one_ref, low_ref, act_ref,
               n1_ref, r1_ref, dg_ref, n2_ref, r2_ref, nk_ref, nv_ref, ins, outs, bias_ref,
               *scratch):
        loads = start_all(copies_of(
            [(h_hbm, h_ref), (vec_hbm.at[layer], vec_ref), (wo_hbm.at[layer], wo_ref),
             (bu_hbm, bu_ref), (wu_hbm.at[layer], wu_ref), (wd_hbm.at[layer], wd_ref),
             (w_hbm.at[layer + 1], w_ref), (a_hbm.at[layer + 1], a_ref),
             (b_hbm.at[layer + 1], b_ref), (vec_hbm.at[layer + 1], vec2_ref)], ins))
        stores = copies_of(
            [(q_ref, q_out), (k_ref, k_out), (v_ref, v_out), (nk_ref, nk_out), (nv_ref, nv_out),
             (n1_ref, n1_out), (r1_ref, r1_out), (dg_ref, dg_out), (n2_ref, n2_out),
             (r2_ref, r2_out), (one_ref, h_out), (low_ref, x_out), (u_ref, u_out),
             (mix_ref, mix_out)], outs)
        near = Side(True, length, (own_ref, other_ref, live_ref))
        near_forward(near, sequences, length, far_ref, q_ref, k_ref, v_ref, halo_ref, nk_ref,
                     nv_ref, mix_ref, bias_ref, scratch)
        layer_rest(layer, sequences, length, mix_ref, h_ref, wo_ref, wu_ref, wd_ref,
                   [wait_for(loads, 0, 1, 2), wait_for(loads, 3, 4), wait_for(loads, 5)], vec_ref,
                   bu_ref, one_ref, low_ref, act_ref, n1_ref, r1_ref, dg_ref, n2_ref, r2_ref,
                   (one_ref, low_ref),
                   lambda i: start_all((stores[:7] + stores[13:], stores[7:8], stores[8:12])[i]))
        nothing = wait_for(loads)
        project_in(sequences, length, low_ref, w_ref,
                   [wait_for(loads, 6, 7, 8, 9), nothing, nothing], a_ref, b_ref, vec2_ref, q2_ref,
                   k2_ref, v2_ref, u_ref, send_ref, stores[12].start)
        for copy in stores:
            copy.wait()

    act, stat = ((tokens, width), BF16), ((tokens, 128), F32)
    wide, deep = ((tokens, width), F32), ((tokens, hidden), BF16)
    near, small = ((sequences * (WINDOW + SUB), width), BF16), ((tokens, 2 * rank), BF16)
    factors = ((2, rank, width), F32)
    return call(
        kernel, "middle",
        [(VMEM, ids[0]), (VMEM, ids[1]), (VMEM, ids[2]), (VMEM, far), (VMEM, q), (VMEM, k), (VMEM, v),
         (VMEM, halo)]
        + [(HBM, item) for item in (h, w, a, b, wo, wu, wd, vec, bias_up)],
        [(VMEM,) + act, (VMEM,) + act, (VMEM,) + act, (VMEM, (2, sequences * HALO, width), BF16)]
        + [(HBM,) + item for item in (small, act, wide, act, stat, deep, act, stat, act, act, act,
                                      near, near, act)],
        [(h.shape, h.dtype), ((width, 3 * width), BF16), ((width, width), BF16),
         ((width, hidden), BF16), ((hidden, width), BF16), ((8, width), BF16),
         (bias_up.shape, BF16), ((8, width), BF16), factors, factors, small, act, wide, act, deep,
         act, stat, deep, act, stat, near, near, 10, 14,
         bias_shape(False)] + attention_scratch(),
        2 * tokens * width * (2 * hidden + 4 * width), 24000000, 42)


def turn_call(layer, sequences, length, ids, far, q, k, v, halo, h, gradient, wo, wu, wd,
              vec, bias_up):
    tokens, width = q.shape
    hidden = wu.shape[2]

    def kernel(own_ref, other_ref, live_ref, far_ref, q_ref, k_ref, v_ref, halo_ref, h_hbm, g_hbm,
               wo_hbm, wu_hbm, wd_hbm, vec_hbm, bu_hbm,
               datt_ref, dfar_ref, dq_ref, dnk_ref, dnv_ref, dhalo_ref, delta_ref, hidden_out,
               h_ref, g_ref, wo_ref, wu_ref, wd_ref, vec_ref, bu_ref, mix_ref, one_ref, low_ref,
               act_ref, n1_ref, r1_ref, dg_ref, n2_ref, r2_ref, nk_ref, nv_ref, last_ref, ins, outs,
               bias_ref, columns_ref, *scratch):
        loads = start_all(copies_of(
            [(h_hbm, h_ref), (vec_hbm.at[layer], vec_ref), (wo_hbm.at[layer], wo_ref),
             (bu_hbm, bu_ref), (wu_hbm.at[layer], wu_ref), (wd_hbm.at[layer], wd_ref),
             (g_hbm, g_ref)], ins))
        store = pltpu.make_async_copy(last_ref, hidden_out, outs.at[0])
        near = Side(True, length, (own_ref, other_ref, live_ref))
        near_forward(near, sequences, length, far_ref, q_ref, k_ref, v_ref, halo_ref, nk_ref,
                     nv_ref, mix_ref, bias_ref, scratch)
        side = lax.axis_index("seq")
        layer_rest(layer, sequences, length, mix_ref, h_ref, wo_ref, wu_ref, wd_ref,
                   [wait_for(loads, 0, 1, 2), wait_for(loads, 3, 4), wait_for(loads, 5)], vec_ref,
                   bu_ref, one_ref, low_ref, act_ref, n1_ref, r1_ref, dg_ref, n2_ref, r2_ref,
                   (last_ref,), lambda i: None)
        store.start()

        def given(s, rows):
            places = lax.broadcasted_iota(jnp.int32, (length, 1), 0) + side * length
            return jnp.where(
                places.astype(F32) < picked(live_ref, s), g_ref[rows, :].astype(F32), 0.0)

        nothing = wait_for(loads)
        layer_rest_back(sequences, length, given,
                        [wait_for(loads, 6), nothing, nothing, nothing], n1_ref,
                        r1_ref, dg_ref, n2_ref, r2_ref, wo_ref, wu_ref, wd_ref, vec_ref, one_ref,
                        low_ref, act_ref, datt_ref)
        near_backward(near, sequences, length, q_ref, nk_ref, nv_ref, low_ref, mix_ref,
                      delta_ref, dfar_ref, dq_ref, dnk_ref, dnv_ref, dhalo_ref, columns_ref, scratch)
        store.wait()

    act, stat = ((tokens, width), BF16), ((tokens, 128), F32)
    wide, deep = ((tokens, width), F32), ((tokens, hidden), BF16)
    near_rows, ordered = sequences * (WINDOW + SUB), sequences * (length + HALO)
    near, block = ((near_rows, width), BF16), ((sequences * BLOCK, width), BF16)
    return call(
        kernel, "turn",
        [(VMEM, ids[0]), (VMEM, ids[1]), (VMEM, ids[2]), (VMEM, far), (VMEM, q), (VMEM, k),
         (VMEM, v), (VMEM, halo)]
        + [(HBM, item) for item in (h, gradient, wo, wu, wd, vec, bias_up)],
        [(VMEM,) + wide, (VMEM,) + block, (VMEM,) + block, (VMEM, (ordered, width), F32),
         (VMEM, (ordered, width), F32), (VMEM, (2, sequences * HALO, width), BF16),
         (VMEM, (HEAD_ROWS * sequences, length), F32), (HBM,) + act],
        [(h.shape, h.dtype), act, ((width, width), BF16), ((width, hidden), BF16),
         ((hidden, width), BF16), ((8, width), BF16), (bias_up.shape, BF16), act, wide, act, deep,
         act, stat, deep, act, stat, near, near, act, 7, 1, bias_shape(False),
         bias_shape(True)] + attention_scratch(True),
        4 * tokens * width * (2 * hidden + width), 24000000, 42)


def back_far_call(sequences, length, ids, q, k, v, dfar, delta, dq_near, dnk, dnv):
    tokens, width = q.shape

    def kernel(own_ref, live_ref, q_ref, k_ref, v_ref, dfar_ref, delta_ref, dqn_ref, dnk_ref,
               dnv_ref, dq_ref, dk_ref, dv_ref, bias_ref,
               *scratch):
        far = Side(False, length, (own_ref, None, live_ref))
        side = far.side

        def key_terms(s, cols, kept):
            near = rows_at(s * (length + HALO) + HALO * side, length, 32)
            for out, term, which, other in ((dv_ref, dnv_ref, 0, 3), (dk_ref, dnk_ref, 1, 2)):
                left = jnp.concatenate([item[which] for item in kept], axis=1)
                right = jnp.concatenate([item[other] for item in kept], axis=0)
                out[far.keys(s, 0), cols] = dot_nn(left, right) + term[near, cols]

        def one(s):
            far.biases(s, None, bias_ref)
            delta = delta_ref[rows_at(s * HEAD_ROWS, HEAD_ROWS, HEAD_ROWS), :]
            attention_backward(
                far, s, q_ref, k_ref, v_ref, dfar_ref,
                lambda s, sub: rows_at(s * BLOCK + sub * SUB, SUB, SUB), delta, dq_ref,
                far.queries, key_terms, bias_ref, scratch)
            dq_ref[rows_at(s * length + (1 - side) * BLOCK, BLOCK, BLOCK), :] = dqn_ref[
                rows_at(s * BLOCK, BLOCK, BLOCK), :]

        loop(sequences, one)

    wide = (VMEM, (tokens, width), F32)
    return call(
        kernel, "back_far",
        [(VMEM, ids[0]), (VMEM, ids[2])]
        + [(VMEM, item) for item in (q, k, v, dfar, delta, dq_near, dnk, dnv)],
        [(VMEM, (tokens, width), BF16), wide, wide],
        [bias_shape(True)] + attention_scratch(True), 4000000000, 16000000, 8)


def back_call(layer, sequences, length, ids, dq, dk, dv, dhalo, datt, u, x, saved, w, a, b, wo, wu,
              wd, vec):
    tokens, width = dq.shape
    hidden, rank = wu.shape[2], a.shape[2]

    def kernel(own_ref, other_ref, live_ref, dq_ref, dk_ref, dv_ref, dhalo_ref, datt_ref, u_hbm, x_hbm,
               n1_hbm, r1_hbm, dg_hbm, n2_hbm, r2_hbm, q_hbm, k_hbm, v_hbm, nk_hbm, nv_hbm, mix_hbm,
               w_hbm, a_hbm, b_hbm, wo_hbm, wu_hbm, wd_hbm, vec_hbm,
               datt_out, dfar_ref, dqn_ref, dnk_ref, dnv_ref, dhalo_out, delta_ref, q_ref, k_ref,
               v_ref, grad_out,
               u_ref, x_ref, n1_ref, r1_ref, dg_ref, n2_ref, r2_ref, nk_ref, nv_ref, w_ref,
               a_ref, b_ref, wo_ref, wu_ref, wd_ref, vec_ref, dkb_ref, dvb_ref, du_ref, grad_ref,
               two_ref, low_ref, mix_ref, ins, outs, bias_ref, *scratch):
        loads = start_all(copies_of(
            [(a_hbm.at[layer + 1], a_ref), (b_hbm.at[layer + 1], b_ref), (u_hbm, u_ref),
             (x_hbm, x_ref), (w_hbm.at[layer + 1], w_ref), (vec_hbm.at[layer], vec_ref),
             (n2_hbm, n2_ref), (r2_hbm, r2_ref), (wd_hbm.at[layer], wd_ref), (dg_hbm, dg_ref),
             (wu_hbm.at[layer], wu_ref), (n1_hbm, n1_ref), (r1_hbm, r1_ref),
             (wo_hbm.at[layer], wo_ref), (q_hbm, q_ref), (nk_hbm, nk_ref), (nv_hbm, nv_ref),
             (k_hbm, k_ref), (v_hbm, v_ref), (mix_hbm, mix_ref)], ins))
        adapter_back(sequences, length, [wait_for(loads, 0, 1), wait_for(loads, 2, 3)], dq_ref, dk_ref, dv_ref, dhalo_ref, u_ref, x_ref,
                     a_ref, b_ref, dkb_ref, dvb_ref, du_ref, grad_ref)
        store = pltpu.make_async_copy(grad_ref, grad_out, outs.at[0])
        store.start()
        down, _, _ = low_rank(a_ref, b_ref)

        wait_for(loads, 4)()
        tall = tokens // 2

        def given(s, rows):
            return two_ref[rows, :]

        def project(i):
            rows = rows_at(i * tall, tall, 128)
            two_ref[rows, :] = project_back(rows, rows, datt_ref, dq_ref, dkb_ref, dvb_ref, du_ref,
                                            w_ref, down)

        loop(2, project)
        layer_rest_back(sequences, length, given,
                        [wait_for(loads, 5, 6, 7), wait_for(loads, 8, 9), wait_for(loads, 10),
                         wait_for(loads, 11, 12, 13, 19)], n1_ref, r1_ref, dg_ref, n2_ref, r2_ref,
                        wo_ref, wu_ref, wd_ref, vec_ref, two_ref, low_ref, dg_ref, datt_out)
        wait_for(loads, 14, 15, 16)()
        near = Side(True, length, (own_ref, other_ref, live_ref))
        near_backward(near, sequences, length, q_ref, nk_ref, nv_ref, low_ref, mix_ref,
                      delta_ref, dfar_ref, dqn_ref, dnk_ref, dnv_ref, dhalo_out, bias_ref, scratch)
        wait_for(loads, 17, 18)()
        store.wait()

    act, stat = ((tokens, width), BF16), ((tokens, 128), F32)
    wide, deep = ((tokens, width), F32), ((tokens, hidden), BF16)
    near_rows, ordered = sequences * (WINDOW + SUB), sequences * (length + HALO)
    near, block = ((near_rows, width), BF16), ((sequences * BLOCK, width), BF16)
    small, factors = ((tokens, 2 * rank), BF16), ((2, rank, width), F32)
    grad = ((4 * rank, width), F32)
    return call(
        kernel, "back",
        [(VMEM, ids[0]), (VMEM, ids[1]), (VMEM, ids[2])]
        + [(VMEM, item) for item in (dq, dk, dv, dhalo, datt)]
        + [(HBM, item) for item in (u, x, *saved, w, a, b, wo, wu, wd, vec)],
        [(VMEM,) + wide, (VMEM,) + block, (VMEM,) + block,
         (VMEM, (ordered, width), F32), (VMEM, (ordered, width), F32),
         (VMEM, (2, sequences * HALO, width), BF16), (VMEM, (HEAD_ROWS * sequences, length), F32),
         (VMEM,) + act, (VMEM,) + act, (VMEM,) + act,
         (HBM,) + grad],
        [small, act, act, stat, deep, act, stat, near, near, ((width, 3 * width), BF16), factors,
         factors, ((width, width), BF16), ((width, hidden), BF16), ((hidden, width), BF16),
         ((8, width), BF16), act, act, small, grad, wide, act, act, 20, 1, bias_shape(True)]
        + attention_scratch(True),
        2 * tokens * width * (2 * hidden + 4 * width), 24000000, 38)


def last_call(layer, sequences, length, dq, dk, dv, dhalo, u, x, w, a, b, other, *state):
    tokens, width = dq.shape
    rank = a.shape[2]

    def kernel(dq_ref, dk_ref, dv_ref, dhalo_ref, u_hbm, x_hbm, w_hbm, a_hbm, b_hbm, other_hbm,
               *rest):
        given, rest = rest[:len(state)], rest[len(state):]
        (dkb_ref, dvb_ref, du_ref, w_ref, down_ref, mine_ref, theirs_ref), rest = rest[:7], rest[7:]
        taken, rest = rest[:len(state)], rest[len(state):]
        u_ref, x_ref, a_ref, b_ref, other_ref, grad_ref, sems, state_sems = rest
        loads = start_all(copies_of(
            [(a_hbm.at[layer], a_ref), (b_hbm.at[layer], b_ref), (u_hbm, u_ref), (x_hbm, x_ref),
             (other_hbm, other_ref), (w_hbm.at[layer], w_ref)], sems))
        more = start_all(copies_of(zip(given, taken), state_sems))
        adapter_back(sequences, length, [wait_for(loads, 0, 1), wait_for(loads, 2, 3)], dq_ref, dk_ref, dv_ref, dhalo_ref, u_ref, x_ref,
                     a_ref, b_ref, dkb_ref, dvb_ref, du_ref, grad_ref)
        down_ref[...] = low_rank(a_ref, b_ref)[0]
        wait_for(loads, 4)()
        first = lax.axis_index("seq") == layer
        here, there = grad_ref[...], other_ref[...]
        mine_ref[...] = jnp.where(first, here, there)
        theirs_ref[...] = jnp.where(first, there, here)
        wait_for(loads, 5)()
        for copy in more:
            copy.wait()

    act, grad = ((tokens, width), BF16), ((4 * rank, width), F32)
    small, factors = ((tokens, 2 * rank), BF16), ((2, rank, width), F32)
    return call(
        kernel, "adapter_back",
        [(VMEM, dq), (VMEM, dk), (VMEM, dv), (VMEM, dhalo)]
        + [(HBM, item) for item in (u, x, w, a, b, other, *state)],
        [(VMEM,) + act, (VMEM,) + act, (VMEM,) + small, (VMEM, (width, 3 * width), BF16),
         (VMEM, (2 * rank, width), BF16), (VMEM,) + grad, (VMEM,) + grad]
        + [(VMEM, item.shape, F32) for item in state],
        [small, act, factors, factors, grad, grad, 6, len(state)], 500000000, 12000000, 8)


def project_back_call(datt, dq, dk, dv, du, w, down):
    tokens, width = dq.shape
    parts = 2
    length = tokens // parts

    def kernel(datt_ref, dq_ref, dk_ref, dv_ref, du_ref, w_ref, down_ref, out_hbm, out_ref, sems):
        def part(i):
            rows = rows_at(i * length, length, 128)
            return pltpu.make_async_copy(out_ref.at[rows], out_hbm.at[rows], sems.at[i])

        def one(i):
            rows = rows_at(i * length, length, 128)
            out_ref[rows, :] = project_back(rows, rows, datt_ref, dq_ref, dk_ref, dv_ref, du_ref,
                                            w_ref, down_ref[...])
            part(i).start()

        loop(parts, one)
        for i in range(parts):
            part(i).wait()

    return call(
        kernel, "project_back", [(VMEM, item) for item in (datt, dq, dk, dv, du, w, down)],
        [(HBM, (tokens, width), F32)], [((tokens, width), F32), parts],
        2 * tokens * width * width * 3, 4000000, 6)[0]


def adam_call(mine, theirs, token_slots, steps, down, up, m_down, v_down, m_up, v_up):
    layers, two, rank, width = down.shape

    def kernel(mine_ref, theirs_ref, steps_ref, down_ref, up_ref, md_ref, vd_ref, mu_ref, vu_ref,
               *rest):
        outs, results, sems = rest[:6], rest[6:12], rest[12]
        down_out, up_out, md_out, vd_out, mu_out, vu_out = results
        side = lax.axis_index("seq")
        for layer in range(layers):
            for which in range(two):
                for group, (w_ref, m_ref, v_ref, w_out, m_out, v_out, rate, decay) in enumerate((
                    (down_ref, md_ref, vd_ref, down_out, md_out, vd_out, 0.03125, 0.1),
                    (up_ref, mu_ref, vu_ref, up_out, mu_out, vu_out, 0.5, 0.0),
                )):
                    rows = slice((group * two + which) * rank, (group * two + which + 1) * rank)
                    grad = jnp.where(side == layer, mine_ref[rows, :], theirs_ref[rows, :])
                    grad = grad / token_slots
                    step = picked(steps_ref, (layer * two + which) * 2 + group)
                    correction = jnp.broadcast_to(1.0 - jnp.exp2(-step), (rank, width))
                    weight = w_ref[layer, which]
                    moment = 0.5 * m_ref[layer, which] + 0.5 * grad
                    velocity = 0.5 * v_ref[layer, which] + 0.5 * grad * grad
                    size = moment / correction / (jnp.sqrt(velocity / correction) + 1e-08)
                    w_out[layer, which] = weight - rate * (size + decay * weight)
                    m_out[layer, which] = moment
                    v_out[layer, which] = velocity

        for store in start_all(copies_of(zip(results, outs), sems)):
            store.wait()

    return call(
        kernel, "adam",
        [(VMEM, mine), (VMEM, theirs), (VMEM, steps)]
        + [(VMEM, item) for item in (down, up, m_down, v_down, m_up, v_up)],
        [(HBM, down.shape, F32)] * 6, [(down.shape, F32)] * 6 + [6], 1000000, 2000000, 4)


def together(*values):
    return lax.optimization_barrier(values)


def sum_while(mine, theirs, work):
    batch = lax.axis_size("batch")
    swap = [(0, 1), (1, 0)]
    mine = mine + lax.ppermute(theirs, "seq", swap)
    done, work, step = None, list(work), 1
    while step < batch:
        ways = 4 if batch % (4 * step) == 0 else 2
        given = mine.astype(BF16)
        come = [lax.ppermute(given, "batch", [(i, i ^ (step * d)) for i in range(batch)])
                for d in range(1, ways)]
        if work:
            done = work.pop(0)(mine, done)
            *come, done = together(*come, done)
        mine = mine + sum(item.astype(F32) for item in come)
        step *= ways
    for one in work:
        done = one(mine, done)
    return mine, lax.ppermute(mine, "seq", swap), done


def shards(
    first_layer_input,
    output_gradient,
    sentence_pair_index,
    sequence_live_length,
    optimizer_step_count,
    query_key_value_weight,
    attention_output_weight,
    feedforward_up_weight,
    feedforward_down_weight,
    layer_bias_gain_rows,
    feedforward_up_bias,
    adapter_down_factors,
    adapter_up_factors,
    first_moment_down,
    second_moment_down,
    first_moment_up,
    second_moment_up,
):
    sequences, length, width = first_layer_input.shape
    tokens = sequences * length
    swap = [(0, 1), (1, 0)]
    a, b = adapter_down_factors, jnp.swapaxes(adapter_up_factors, 2, 3)
    vec = layer_bias_gain_rows
    bias_up = feedforward_up_bias
    wqkv, wo = query_key_value_weight, attention_output_weight
    wu, wd = feedforward_up_weight, feedforward_down_weight
    ids = (sentence_pair_index, lax.ppermute(sentence_pair_index, "seq", swap),
           sequence_live_length[None, :])
    shape = (sequences, length)

    x1 = first_layer_input.reshape(tokens, width)
    q1, k1, v1, send, u1 = first_call(0, *shape, x1, wqkv, a, b, vec)
    halo = lax.ppermute(send, "seq", swap)
    far = far_call(*shape, q1, k1, v1, ids)
    q2, k2, v2, send, u2, x2, h1, *saved = middle_call(
        0, *shape, ids, far, q1, k1, v1, halo, x1, wqkv, a, b, wo, wu, wd, vec, bias_up)
    halo = lax.ppermute(send, "seq", swap)
    far = far_call(*shape, q2, k2, v2, ids)
    datt, dfar, dqn, dnk, dnv, dsend, delta, hidden_out = turn_call(
        1, *shape, ids, far, q2, k2, v2, halo, h1, output_gradient.reshape(tokens, width),
        wo, wu, wd, vec, bias_up)
    dhalo = lax.ppermute(dsend, "seq", swap)
    dq, dk, dv = back_far_call(*shape, ids, q2, k2, v2, dfar, delta, dqn, dnk, dnv)
    datt, dfar, dqn, dnk, dnv, dsend, delta, q1, k1, v1, grad2 = back_call(
        0, *shape, ids, dq, dk, dv, dhalo, datt, u2, x2, saved, wqkv, a, b, wo, wu, wd, vec)
    dhalo = lax.ppermute(dsend, "seq", swap)
    dq, dk, dv = back_far_call(*shape, ids, q1, k1, v1, dfar, delta, dqn, dnk, dnv)
    dk, dv, du, w1, down1, mine, theirs, *state = last_call(
        0, *shape, dq, dk, dv, dhalo, u1, x1, wqkv, a, b, grad2, a, b, first_moment_down,
        second_moment_down, jnp.swapaxes(first_moment_up, 2, 3),
        jnp.swapaxes(second_moment_up, 2, 3))

    def work(token, out):
        now, _ = together(datt, token)
        return project_back_call(now, dq, dk, dv, du, w1, down1)

    mine, theirs, gradient = sum_while(mine, theirs, [work])
    token_slots = tokens * lax.axis_size("seq") * lax.axis_size("batch")
    down, up, m_down, v_down, m_up, v_up = adam_call(
        mine, theirs, token_slots, optimizer_step_count.reshape(1, -1), *state)
    return (
        hidden_out.reshape(sequences, length, width),
        gradient.reshape(sequences, length, width),
        down,
        jnp.swapaxes(up, 2, 3),
        m_down,
        v_down,
        jnp.swapaxes(m_up, 2, 3),
        jnp.swapaxes(v_up, 2, 3),
    )


def solution(mesh):
    acts, whole = P("batch", "seq", None), P()
    return jax.shard_map(
        shards,
        mesh=mesh,
        in_specs=(acts, acts, P("batch", "seq"), P("batch")) + (whole,) * 13,
        out_specs=(acts, acts) + (whole,) * 6,
        check_vma=False,
    )
```

```python
import jax
import jax.numpy as jnp
from jax import lax
from jax.experimental import pallas as pl
from jax.experimental.pallas import tpu as pltpu
from jax.sharding import PartitionSpec as P

HEADS = 12
ENCODER_LAYERS = 2
HALO = 96
BLOCK = 128
SUB = 64
WINDOW = 256
QUAD = 256
HEAD_ROWS = 16
MASKED = -1000000000.0
LOG2E = 1.4426950408889634
HALF_ROOT_PI = 0.886226925452758
ROOT_HALF = 0.7071067811865476
ACTIVE = 0.7978845608028654
SLOPE = 0.5641895835477563
F32 = jnp.float32
BF16 = jnp.bfloat16


def dot_nn(a, b):
    return lax.dot_general(a, b, (((1,), (0,)), ((), ())), preferred_element_type=F32)


def dot_nt(a, b):
    return lax.dot_general(a, b, (((1,), (1,)), ((), ())), preferred_element_type=F32)


def dot_tn(a, b):
    return lax.dot_general(a, b, (((0,), (0,)), ((), ())), preferred_element_type=F32)


def rows_at(start, size, multiple):
    return pl.ds(pl.multiple_of(start, multiple), size)


def loop(count, body):
    def step(i, carry):
        body(i)
        return carry

    lax.fori_loop(0, count, step, 0)


def picked(row_ref, i):
    row = row_ref[...].astype(F32)
    at = lax.broadcasted_iota(jnp.int32, row.shape, 1) == i
    return jnp.sum(jnp.where(at, row, 0.0), axis=1, keepdims=True)


def column_of(row):
    n = row.shape[1]
    eye = lax.broadcasted_iota(jnp.int32, (n, n), 0) == lax.broadcasted_iota(jnp.int32, (n, n), 1)
    return jnp.sum(jnp.where(eye, row, 0.0), axis=1, keepdims=True)


def low_lanes():
    return (lax.broadcasted_iota(jnp.int32, (SUB, 128), 1) < 64).astype(F32).astype(BF16)


def spread_heads(tile, low):
    zero = jnp.zeros((2 * SUB, 128), BF16)
    high = 1 - low
    left, right = tile[:, :128], tile[:, 128:]
    left = jnp.concatenate([left * low, left * high], axis=0)
    right = jnp.concatenate([right * low, right * high], axis=0)
    return jnp.concatenate([jnp.concatenate([left, zero], axis=1),
                            jnp.concatenate([zero, right], axis=1)], axis=0)


def gather_heads(wide):
    low = lax.broadcasted_iota(jnp.int32, (SUB, 128), 1) < 64
    parts = []
    for i in range(2):
        cols, top = slice(128 * i, 128 * i + 128), 2 * SUB * i
        parts.append(jnp.where(low, wide[top:top + SUB, cols],
                               wide[top + SUB:top + 2 * SUB, cols]))
    return jnp.concatenate(parts, axis=1)


def pipelined(units):
    units = list(units)
    live = []
    while units or live:
        if units:
            live.append(units.pop(0))
        for unit in reversed(list(live)):
            if next(unit, None) is None:
                live.remove(unit)


class Side:
    def __init__(self, near, length, ids_refs):
        self.near, self.length, self.ids_refs = near, length, ids_refs
        self.side = lax.axis_index("seq")
        self.row0 = BLOCK * ((1 - self.side) if near else self.side)

    def ids(self, s):
        own_ref, other_ref, live_ref = self.ids_refs
        own = own_ref[pl.ds(s, 1), :].astype(F32)
        query = jnp.where(self.row0 == 0, own[:, :BLOCK], own[:, BLOCK:])
        if self.near:
            other = other_ref[pl.ds(s, 1), :].astype(F32)
            kept = WINDOW + SUB - HALO
            key = jnp.where(
                self.side == 0,
                jnp.concatenate([own[:, self.length - kept:], other[:, :HALO]], axis=1),
                jnp.concatenate([other[:, self.length - HALO:], own[:, :kept]], axis=1))
            start = jnp.where(self.side == 0, self.length - kept, self.length - HALO)
        else:
            key, start = own, self.side * self.length
        places = lax.broadcasted_iota(jnp.int32, key.shape, 1) + start
        return query, jnp.where(places.astype(F32) < picked(live_ref, s), key, -1.0)

    def queries(self, s, sub):
        return rows_at(s * self.length + self.row0 + sub * SUB, SUB, SUB)

    def keys(self, s, sub):
        if self.near:
            return rows_at(s * (WINDOW + SUB) + sub * SUB, WINDOW, SUB)
        return rows_at(s * self.length, WINDOW, WINDOW)

    def biases(self, s, rows_ref=None, columns_ref=None):
        lane = lax.broadcasted_iota(jnp.int32, (1, 128), 1)
        place = jnp.where(lane < SUB, lane, lane - SUB)
        key_place = lax.broadcasted_iota(jnp.int32, (WINDOW, 128), 0)
        shape = (SUB, WINDOW)
        apart = lax.broadcasted_iota(jnp.int32, shape, 1) - lax.broadcasted_iota(jnp.int32, shape, 0)
        query, key = self.ids(s)
        if rows_ref is None:
            blocks = (128, 128, SUB) if self.near else (128, 128)
            column = jnp.concatenate(
                [column_of(key[:, 128 * i:128 * i + n]) for i, n in enumerate(blocks)], axis=0)
            turned = pltpu.roll(query, SUB, 1)
        for sub in range(2):
            own = HALO if self.near else self.row0 + sub * SUB
            if rows_ref is not None:
                keys = key[:, sub * SUB:sub * SUB + WINDOW] if self.near else key
                queries = column_of(query)[sub * SUB:(sub + 1) * SUB]
                seen = (queries == keys) | (apart == own)
                rows_ref[sub * SUB:(sub + 1) * SUB, :] = jnp.where(seen, 0.0, MASKED)
                continue
            keys = column[sub * SUB:sub * SUB + WINDOW] if self.near else column
            pair = (query, turned) if sub == 0 else (turned, query)
            seen = (keys == jnp.where(lane < SUB, *pair)) | (key_place == place + own)
            columns_ref[sub * WINDOW:(sub + 1) * WINDOW, :] = jnp.where(seen, 0.0, MASKED)


def bias_shape(turned):
    return ((2 * WINDOW, 128) if turned else (2 * SUB, WINDOW)), F32


def half(sub):
    return slice(4 * SUB * sub, 4 * SUB * (sub + 1))


SLOTS = 2


def attention_scratch(backward=False):
    pair = [((SLOTS, WINDOW, 4 * SUB), F32), ((SLOTS, WINDOW, 4 * SUB), BF16)]
    return pair * 2 if backward else pair


def attention_forward(where, s, q_ref, k_ref, v_ref, out_ref, out_rows, bias_ref, scratch):
    low = low_lanes()
    scores_ref, share_ref = scratch[:2]

    def unit(quad, sub):
        cols = slice(QUAD * quad, QUAD * quad + QUAD)
        keys = where.keys(s, sub)
        q4 = spread_heads(q_ref[where.queries(s, sub), cols], low)
        slot = (2 * quad + sub) % SLOTS
        scores_ref[slot] = dot_nt(q4, k_ref[keys, cols])
        yield True
        bias = bias_ref[sub * SUB:(sub + 1) * SUB, :]
        totals = []
        for h in range(4):
            rows = slice(h * SUB, (h + 1) * SUB)
            scores = scores_ref[slot, rows, :] + bias
            share = jnp.exp2(scores - jnp.max(scores, axis=1, keepdims=True))
            totals.append(1.0 / jnp.sum(share, axis=1, keepdims=True))
            share_ref[slot, rows, :] = share.astype(BF16)
        yield True
        mixed = dot_nn(share_ref[slot], v_ref[keys, cols])
        mixed = jnp.concatenate(
            [mixed[h * SUB:(h + 1) * SUB] * totals[h] for h in range(4)], axis=0)
        yield True
        out_ref[out_rows(s, sub), cols] = gather_heads(mixed).astype(BF16)

    width = q_ref.shape[1]
    pipelined(unit(quad, sub) for quad in range(width // QUAD) for sub in range(2))


def attention_backward(where, s, q_ref, k_ref, v_ref, dmix_ref, dmix_rows, delta, dq_ref,
                       dq_rows, key_terms, bias_ref, scratch):
    low = low_lanes()
    scores_ref, share_ref, d_share_ref, d_scores_ref = scratch
    delta = jnp.where(where.row0 == 0, delta[:, :BLOCK], delta[:, BLOCK:])
    turned = pltpu.roll(delta, SUB, 1)
    first_half = lax.broadcasted_iota(jnp.int32, (1, 2 * SUB), 1) < SUB

    def unit(quad, sub, kept):
        cols = slice(QUAD * quad, QUAD * quad + QUAD)
        keys = where.keys(s, sub)
        slot = (2 * quad + sub) % SLOTS
        q4 = spread_heads(q_ref[where.queries(s, sub), cols], low)
        d4 = spread_heads(dmix_ref[dmix_rows(s, sub), cols], low)
        scores_ref[slot] = dot_nt(k_ref[keys, cols], q4)
        d_share_ref[slot] = dot_nt(v_ref[keys, cols], d4)
        yield True
        bias = bias_ref[sub * WINDOW:(sub + 1) * WINDOW, :]
        shares, d_scores = [], []
        left, right = (delta, turned) if sub == 0 else (turned, delta)
        for i in range(2):
            head = 4 * quad + 2 * i
            drop = jnp.where(first_half, left[head:head + 1], right[head + 1:head + 2])
            part = scores_ref[slot, :, 128 * i:128 * i + 128] + bias
            part = jnp.exp2(part - jnp.max(part, axis=0, keepdims=True))
            part = part * (1.0 / jnp.sum(part, axis=0, keepdims=True))
            shares.append(part.astype(BF16))
            d_scores.append((part * (d_share_ref[slot, :, 128 * i:128 * i + 128] - drop)).astype(BF16))
        d_scores = jnp.concatenate(d_scores, axis=1)
        kept.append((jnp.concatenate(shares, axis=1), d_scores, q4, d4))
        yield True
        if sub == 1:
            key_terms(s, cols, kept)
        yield True
        d_query = gather_heads(dot_tn(d_scores, k_ref[keys, cols])) * 0.125
        dq_ref[dq_rows(s, sub), cols] = d_query.astype(BF16)

    width = q_ref.shape[1]

    def units():
        for quad in range(width // QUAD):
            kept = []
            for sub in range(2):
                yield unit(quad, sub, kept)

    pipelined(units())


def row_deltas(dmix, mix):
    shape = (HEAD_ROWS, dmix.shape[1])
    own = (lax.broadcasted_iota(jnp.int32, shape, 1) // 64
           == lax.broadcasted_iota(jnp.int32, shape, 0)).astype(F32).astype(BF16)
    product = dmix.astype(F32) * mix.astype(F32)
    high = product.astype(BF16)
    rest = (product - high.astype(F32)).astype(BF16)
    return dot_nt(own, high) + dot_nt(own, rest)


def near_keys(s, length, k_ref, v_ref, halo_ref, nk_ref, nv_ref):
    side = lax.axis_index("seq")
    wide, own = WINDOW + SUB, WINDOW + SUB - HALO
    given = rows_at(s * HALO, HALO, 32)
    for i, (src, dst) in enumerate(((k_ref, nk_ref), (v_ref, nv_ref))):
        dst[rows_at(s * wide + HALO * side, own, 32), :] = src[
            rows_at(s * length + (length - own) * (1 - side), own, 32), :]
        dst[rows_at(s * wide + own * (1 - side), HALO, 32), :] = halo_ref[i, given, :]


def norm_forward(values, gain, shift):
    center = values - jnp.mean(values, axis=1, keepdims=True)
    spread = jnp.mean(center * center, axis=1, keepdims=True)
    inverse = lax.rsqrt(spread + 1e-05)
    scaled = center * inverse
    return scaled * gain + shift, scaled, inverse


def norm_backward(gradient, scaled, inverse, gain):
    inner = gradient * gain
    return inverse * (
        inner
        - jnp.mean(inner, axis=1, keepdims=True)
        - scaled * jnp.mean(inner * scaled, axis=1, keepdims=True)
    )


def low_rank(a_ref, b_ref):
    down = jnp.concatenate([a_ref[0], a_ref[1]], axis=0).astype(BF16)
    zero = jnp.zeros_like(b_ref[0])
    up_q = jnp.concatenate([b_ref[0], zero], axis=0).astype(BF16)
    up_v = jnp.concatenate([zero, b_ref[1]], axis=0).astype(BF16)
    return down, up_q, up_v


def project_in(sequences, length, x_ref, w_ref, waits, a_ref, b_ref, vec_ref, q_ref, k_ref, v_ref,
               u_ref, send_ref, sent):
    side = lax.axis_index("seq")
    width = x_ref.shape[1]
    waits[0]()
    down, up_q, up_v = low_rank(a_ref, b_ref)
    vec = vec_ref[...].astype(F32)

    tall = x_ref.shape[0] // 2

    def queries(i):
        rows = rows_at(i * tall, tall, 128)
        x = x_ref[rows, :]
        inner = dot_nt(x, down).astype(BF16)
        u_ref[rows, :] = inner
        q = dot_nn(x, w_ref[:, :width]) + vec[0:1] + 2.0 * dot_nn(inner, up_q)
        q_ref[rows, :] = (q * (0.125 * LOG2E)).astype(BF16)

    def keys(i):
        rows = rows_at(i * tall, tall, 128)
        k_ref[rows, :] = dot_nn(x_ref[rows, :], w_ref[:, width:2 * width]).astype(BF16)

    def values(i):
        rows = rows_at(i * tall, tall, 128)
        v = dot_nn(x_ref[rows, :], w_ref[:, 2 * width:]) + vec[1:2]
        v_ref[rows, :] = (v + 2.0 * dot_nn(u_ref[rows, :], up_v)).astype(BF16)

    def send(s):
        taken = rows_at(s * length + (1 - side) * (length - HALO), HALO, 32)
        for i, ref in enumerate((k_ref, v_ref)):
            send_ref[i, rows_at(s * HALO, HALO, 32), :] = ref[taken, :]

    loop(2, queries)
    sent()
    waits[1]()
    loop(2, keys)
    waits[2]()
    loop(2, values)
    loop(sequences, send)


def layer_rest(layer, sequences, length, mix_ref, h_ref, wo_ref, wu_ref, wd_ref, waits, vec_ref, bu_ref,
               one_ref, low_ref, act_ref, n1_ref, r1_ref, dg_ref, n2_ref, r2_ref, h_outs, sent):
    tokens, hidden = mix_ref.shape[0], wu_ref.shape[1]
    waits[0]()
    vec = vec_ref[...].astype(F32)
    short, units = 128, 3

    def mixed(i):
        def unit(k):
            rows = rows_at((i * units + k) * short, short, short)
            attended = dot_nn(mix_ref[rows, :], wo_ref[...]) + vec[2:3] + h_ref[rows, :].astype(F32)
            yield True
            one, scaled, inverse = norm_forward(attended, vec[4:5], vec[5:6])
            n1_ref[rows, :] = scaled.astype(n1_ref.dtype)
            r1_ref[rows, :] = jnp.broadcast_to(inverse, (short, 128))
            one_ref[rows, :] = one
            low_ref[rows, :] = (one * ROOT_HALF).astype(BF16)

        pipelined(unit(k) for k in range(units))

    loop(tokens // short // units, mixed)
    sent(0)
    waits[1]()
    tile = 1024

    def up(j):
        cols = rows_at(j * tile, tile, tile)
        bias = bu_ref[layer:layer + 1, cols].astype(F32) * ROOT_HALF
        weights = wu_ref[:, cols]

        def unit(k):
            rows = slice(k * short, (k + 1) * short)
            gate = dot_nn(low_ref[rows, :], weights)
            yield True
            gate = gate + bias
            below = HALF_ROOT_PI * lax.erf(gate) + HALF_ROOT_PI
            act_ref[rows, cols] = (gate * below).astype(BF16)
            density = jnp.exp2(gate * gate * -LOG2E)
            dg_ref[rows, cols] = (below + gate * density).astype(BF16)

        pipelined(unit(k) for k in range(tokens // short))

    loop(hidden // tile, up)
    sent(1)
    waits[2]()

    def down(s):
        rows = rows_at(s * length, length, length)
        summed = dot_nn(act_ref[rows, :], wd_ref[...]) * ACTIVE + vec[3:4] + one_ref[rows, :]
        out, scaled, inverse = norm_forward(summed, vec[6:7], vec[7:8])
        n2_ref[rows, :] = scaled.astype(n2_ref.dtype)
        r2_ref[rows, :] = jnp.broadcast_to(inverse, (length, 128))
        for h_out in h_outs:
            h_out[rows, :] = out.astype(h_out.dtype)

    loop(sequences, down)
    sent(2)


def layer_rest_back(sequences, length, gradient, waits, n1_ref, r1_ref, dg_ref, n2_ref, r2_ref,
                    wo_ref, wu_ref, wd_ref, vec_ref, two_ref, low_ref, gate_ref, datt_ref):
    tokens, hidden = low_ref.shape[0], wu_ref.shape[1]
    waits[0]()
    vec = vec_ref[...].astype(F32)
    tall = tokens // 2

    def second(s):
        rows = rows_at(s * length, length, length)
        two = norm_backward(
            gradient(s, rows), n2_ref[rows, :].astype(F32), r2_ref[rows, 0:1], vec[6:7])
        two_ref[rows, :] = two
        low_ref[rows, :] = (two * SLOPE).astype(BF16)

    loop(sequences, second)
    waits[1]()
    tile = 1024

    def down(j):
        cols = rows_at(j * tile, tile, tile)
        weights = wd_ref[cols, :]

        def unit(s):
            rows = slice(s * length, (s + 1) * length)
            gate = dot_nt(low_ref[rows, :], weights)
            yield True
            gate_ref[rows, cols] = (gate * dg_ref[rows, cols].astype(F32)).astype(BF16)

        pipelined(unit(s) for s in range(sequences))

    loop(hidden // tile, down)
    waits[2]()
    waits[3]()

    def up(i):
        rows = rows_at(i * tall, tall, 128)
        datt_ref[rows, :] = dot_nt(gate_ref[rows, :], wu_ref[...])

    def first(s):
        rows = slice(s * length, (s + 1) * length)
        att = norm_backward(datt_ref[rows, :] + two_ref[rows, :], n1_ref[rows, :].astype(F32),
                            r1_ref[rows, 0:1], vec[4:5])
        datt_ref[rows, :] = att
        att = att.astype(BF16)
        yield True
        low_ref[rows, :] = dot_nt(att, wo_ref[...]).astype(BF16)

    loop(2, up)
    pipelined(first(s) for s in range(sequences))


def near_backward(near, sequences, length, q_ref, nk_ref, nv_ref, dmix_ref, mix_ref,
                  delta_ref, dfar_ref, dq_ref, dnk_ref, dnv_ref, dhalo_ref, bias_ref, scratch):
    side, all_rows = near.side, length + HALO
    width = q_ref.shape[1]

    def key_terms(s, cols, kept):
        for out, which, other in ((dnv_ref, 0, 3), (dnk_ref, 1, 2)):
            left, right = [item[which] for item in kept], [item[other] for item in kept]
            start = s * all_rows + (length + HALO - WINDOW - SUB) * (1 - side)
            out[rows_at(start, SUB, 32), cols] = dot_nn(left[0][:SUB], right[0])
            both = jnp.concatenate([left[0][SUB:], left[1][:WINDOW - SUB]], axis=1)
            out[rows_at(start + SUB, WINDOW - SUB, 32), cols] = dot_nn(
                both, jnp.concatenate(right, axis=0))
            out[rows_at(start + WINDOW, SUB, 32), cols] = dot_nn(
                left[1][WINDOW - SUB:], right[1])

    def one(s):
        dfar_ref[rows_at(s * BLOCK, BLOCK, BLOCK), :] = dmix_ref[
            rows_at(s * length + side * BLOCK, BLOCK, BLOCK), :]
        near.biases(s, None, bias_ref)
        rows = rows_at(s * length, length, length)
        delta = row_deltas(dmix_ref[rows, :], mix_ref[rows, :])
        delta_ref[rows_at(s * HEAD_ROWS, HEAD_ROWS, HEAD_ROWS), :] = delta
        attention_backward(
            near, s, q_ref, nk_ref, nv_ref, dmix_ref, near.queries, delta, dq_ref,
            lambda s, sub: rows_at(s * BLOCK + sub * SUB, SUB, SUB), key_terms, bias_ref,
            scratch)
        unseen = rows_at(s * all_rows + (WINDOW + SUB) * side, all_rows - WINDOW - SUB, 32)
        for out in (dnk_ref, dnv_ref):
            out[unseen, :] = jnp.zeros((all_rows - WINDOW - SUB, width), F32)
        halo = rows_at(s * all_rows + length * (1 - side), HALO, 32)
        dhalo_ref[0, rows_at(s * HALO, HALO, 32), :] = (
            dnk_ref[halo, :] * (1.0 / LOG2E)).astype(BF16)
        dhalo_ref[1, rows_at(s * HALO, HALO, 32), :] = dnv_ref[halo, :].astype(BF16)

    loop(sequences, one)


def adapter_back(sequences, length, waits, dq_ref, dk_ref, dv_ref, dhalo_ref, u_ref, x_ref, a_ref,
                 b_ref, dkb_ref, dvb_ref, du_ref, grad_ref):
    side = lax.axis_index("seq")
    rank = a_ref.shape[1]
    waits[0]()
    _, up_q, up_v = low_rank(a_ref, b_ref)

    def one(s):
        rows = rows_at(s * length, length, length)
        taken = rows_at(s * length + (1 - side) * (length - HALO), HALO, 32)
        hrows = rows_at(s * HALO, HALO, 32)
        dvb_ref[rows, :] = dv_ref[rows, :].astype(BF16)
        dvb_ref[taken, :] = (dv_ref[taken, :] + dhalo_ref[1, hrows, :].astype(F32)).astype(BF16)
        dkb_ref[rows, :] = (dk_ref[rows, :] * (1.0 / LOG2E)).astype(BF16)
        dkb_ref[taken, :] = (
            dk_ref[taken, :] * (1.0 / LOG2E) + dhalo_ref[0, hrows, :].astype(F32)).astype(BF16)
        dv16 = dvb_ref[rows, :]
        du_ref[rows, :] = (2.0 * (dot_nt(dq_ref[rows, :], up_q) + dot_nt(dv16, up_v))).astype(BF16)

    loop(sequences, one)
    waits[1]()
    u = u_ref[...]
    grad_ref[0:2 * rank, :] = dot_tn(du_ref[...], x_ref[...])
    up_q, up_v = dot_tn(u, dq_ref[...]), dot_tn(u, dvb_ref[...])
    grad_ref[2 * rank:3 * rank, :] = 2.0 * up_q[:rank]
    grad_ref[3 * rank:, :] = 2.0 * up_v[rank:]


def project_back(rows, own_rows, datt_ref, dq_ref, dk_ref, dv_ref, du_ref, w_ref, down):
    width = dq_ref.shape[1]
    out = datt_ref[rows, :] + dot_nn(du_ref[rows, :], down)
    out = out + dot_nt(dq_ref[rows, :], w_ref[:, :width])
    out = out + dot_nt(dk_ref[rows, :], w_ref[:, width:2 * width])
    return out + dot_nt(dv_ref[rows, :], w_ref[:, 2 * width:])


HBM, VMEM = pltpu.HBM, pltpu.VMEM


def call(kernel, name, args, outs, scratch, flops, nbytes, limit, aliases=None):
    scratch = [pltpu.SemaphoreType.DMA((s,)) if isinstance(s, int) else pltpu.VMEM(*s)
               for s in scratch]
    return pl.pallas_call(
        kernel,
        name=name,
        out_shape=tuple(space(shape, dtype) for space, shape, dtype in outs),
        in_specs=[pl.BlockSpec(memory_space=space) for space, _ in args],
        out_specs=tuple(pl.BlockSpec(memory_space=space) for space, _, _ in outs),
        scratch_shapes=scratch,
        input_output_aliases=aliases or {},
        compiler_params=pltpu.CompilerParams(vmem_limit_bytes=limit * 1024 * 1024),
        cost_estimate=pl.CostEstimate(flops=flops, bytes_accessed=nbytes, transcendentals=0),
    )(*[pltpu.with_memory_space_constraint(array, space) for space, array in args])


def sds(shape, dtype):
    return jax.ShapeDtypeStruct(shape, dtype)


def copies_of(pairs, sems):
    return [pltpu.make_async_copy(src, dst, sems.at[i]) for i, (src, dst) in enumerate(pairs)]


def start_all(copies):
    for copy in copies:
        copy.start()
    return copies


def wait_for(copies, *which):
    def wait():
        for i in which:
            copies[i].wait()

    return wait


def first_call(layer, sequences, length, x, w, a, b, vec):
    tokens, width = x.shape
    rank = a.shape[2]

    def kernel(x_hbm, w_hbm, a_hbm, b_hbm, vec_hbm, q_ref, k_ref, v_ref, send_ref, u_out, x_ref,
               w_ref, a_ref, b_ref, vec_ref, u_ref, sems, outs):
        thirds = [slice(i * width, (i + 1) * width) for i in range(3)]
        copies = start_all(copies_of(
            [(a_hbm.at[layer], a_ref), (b_hbm.at[layer], b_ref), (vec_hbm.at[layer], vec_ref),
             (x_hbm, x_ref)] + [(w_hbm.at[layer, :, part], w_ref.at[:, part]) for part in thirds],
            sems))
        store = pltpu.make_async_copy(u_ref, u_out, outs.at[0])
        project_in(sequences, length, x_ref, w_ref,
                   [wait_for(copies, 0, 1, 2, 3, 4), wait_for(copies, 5), wait_for(copies, 6)],
                   a_ref, b_ref, vec_ref, q_ref, k_ref, v_ref, u_ref, send_ref, store.start)
        store.wait()

    act, small = (VMEM, (tokens, width), BF16), ((tokens, 2 * rank), BF16)
    return call(
        kernel, "project_in", [(HBM, x), (HBM, w), (HBM, a), (HBM, b), (HBM, vec)],
        [act, act, act, (VMEM, (2, sequences * HALO, width), BF16), (HBM,) + small],
        [((tokens, width), BF16), ((width, 3 * width), BF16), ((2, rank, width), F32),
         ((2, rank, width), F32), ((8, width), BF16), small, 7, 1],
        2 * tokens * width * width * 3, 12000000, 10)


def far_call(sequences, length, q, k, v, ids):
    tokens, width = q.shape

    def kernel(q_ref, k_ref, v_ref, own_ref, live_ref, out_ref, bias_ref, *scratch):
        where = Side(False, length, (own_ref, None, live_ref))

        def one(s):
            where.biases(s, bias_ref)
            attention_forward(
                where, s, q_ref, k_ref, v_ref, out_ref,
                lambda s, sub: rows_at(s * BLOCK + sub * SUB, SUB, SUB), bias_ref, scratch)

        loop(sequences, one)

    return call(
        kernel, "attention_far", [(VMEM, item) for item in (q, k, v, ids[0])] + [(VMEM, ids[2])],
        [(VMEM, (sequences * BLOCK, width), BF16)],
        [bias_shape(False)] + attention_scratch(), 2000000000, 6000000, 8)[0]


def near_forward(near, sequences, length, far_ref, q_ref, k_ref, v_ref, halo_ref, nk_ref,
                 nv_ref, mix_ref, bias_ref, scratch):
    def one(s):
        near.biases(s, bias_ref)
        near_keys(s, length, k_ref, v_ref, halo_ref, nk_ref, nv_ref)
        mix_ref[rows_at(s * length + near.side * BLOCK, BLOCK, BLOCK), :] = far_ref[
            rows_at(s * BLOCK, BLOCK, BLOCK), :]
        attention_forward(near, s, q_ref, nk_ref, nv_ref, mix_ref, near.queries, bias_ref,
                          scratch)

    loop(sequences, one)


def middle_call(layer, sequences, length, ids, far, q, k, v, halo, h, w, a, b, wo, wu, wd, vec,
                bias_up):
    tokens, width = q.shape
    hidden, rank = wu.shape[2], a.shape[2]

    def kernel(own_ref, other_ref, live_ref, far_ref, q_ref, k_ref, v_ref, halo_ref, h_hbm, w_hbm, a_hbm,
               b_hbm, wo_hbm, wu_hbm, wd_hbm, vec_hbm, bu_hbm,
               q2_ref, k2_ref, v2_ref, send_ref,
               u_out, x_out, h_out, n1_out, r1_out, dg_out, n2_out, r2_out, q_out, k_out, v_out,
               nk_out, nv_out, mix_out,
               h_ref, w_ref, wo_ref, wu_ref, wd_ref, vec_ref, bu_ref, vec2_ref, a_ref, b_ref,
               u_ref, mix_ref, one_ref, low_ref, act_ref,
               n1_ref, r1_ref, dg_ref, n2_ref, r2_ref, nk_ref, nv_ref, ins, outs, bias_ref,
               *scratch):
        loads = start_all(copies_of(
            [(h_hbm, h_ref), (vec_hbm.at[layer], vec_ref), (wo_hbm.at[layer], wo_ref),
             (bu_hbm, bu_ref), (wu_hbm.at[layer], wu_ref), (wd_hbm.at[layer], wd_ref),
             (w_hbm.at[layer + 1], w_ref), (a_hbm.at[layer + 1], a_ref),
             (b_hbm.at[layer + 1], b_ref), (vec_hbm.at[layer + 1], vec2_ref)], ins))
        stores = copies_of(
            [(q_ref, q_out), (k_ref, k_out), (v_ref, v_out), (nk_ref, nk_out), (nv_ref, nv_out),
             (n1_ref, n1_out), (r1_ref, r1_out), (dg_ref, dg_out), (n2_ref, n2_out),
             (r2_ref, r2_out), (one_ref, h_out), (low_ref, x_out), (u_ref, u_out),
             (mix_ref, mix_out)], outs)
        near = Side(True, length, (own_ref, other_ref, live_ref))
        near_forward(near, sequences, length, far_ref, q_ref, k_ref, v_ref, halo_ref, nk_ref,
                     nv_ref, mix_ref, bias_ref, scratch)
        layer_rest(layer, sequences, length, mix_ref, h_ref, wo_ref, wu_ref, wd_ref,
                   [wait_for(loads, 0, 1, 2), wait_for(loads, 3, 4), wait_for(loads, 5)], vec_ref,
                   bu_ref, one_ref, low_ref, act_ref, n1_ref, r1_ref, dg_ref, n2_ref, r2_ref,
                   (one_ref, low_ref),
                   lambda i: start_all((stores[:7] + stores[13:], stores[7:8], stores[8:12])[i]))
        nothing = wait_for(loads)
        project_in(sequences, length, low_ref, w_ref,
                   [wait_for(loads, 6, 7, 8, 9), nothing, nothing], a_ref, b_ref, vec2_ref, q2_ref,
                   k2_ref, v2_ref, u_ref, send_ref, stores[12].start)
        for copy in stores:
            copy.wait()

    act, stat = ((tokens, width), BF16), ((tokens, 128), F32)
    wide, deep = ((tokens, width), F32), ((tokens, hidden), BF16)
    near, small = ((sequences * (WINDOW + SUB), width), BF16), ((tokens, 2 * rank), BF16)
    factors = ((2, rank, width), F32)
    return call(
        kernel, "middle",
        [(VMEM, ids[0]), (VMEM, ids[1]), (VMEM, ids[2]), (VMEM, far), (VMEM, q), (VMEM, k), (VMEM, v),
         (VMEM, halo)]
        + [(HBM, item) for item in (h, w, a, b, wo, wu, wd, vec, bias_up)],
        [(VMEM,) + act, (VMEM,) + act, (VMEM,) + act, (VMEM, (2, sequences * HALO, width), BF16)]
        + [(HBM,) + item for item in (small, act, wide, act, stat, deep, act, stat, act, act, act,
                                      near, near, act)],
        [(h.shape, h.dtype), ((width, 3 * width), BF16), ((width, width), BF16),
         ((width, hidden), BF16), ((hidden, width), BF16), ((8, width), BF16),
         (bias_up.shape, BF16), ((8, width), BF16), factors, factors, small, act, wide, act, deep,
         act, stat, deep, act, stat, near, near, 10, 14,
         bias_shape(False)] + attention_scratch(),
        2 * tokens * width * (2 * hidden + 4 * width), 24000000, 42)


def turn_call(layer, sequences, length, ids, far, q, k, v, halo, h, gradient, wo, wu, wd,
              vec, bias_up):
    tokens, width = q.shape
    hidden = wu.shape[2]

    def kernel(own_ref, other_ref, live_ref, far_ref, q_ref, k_ref, v_ref, halo_ref, h_hbm, g_hbm,
               wo_hbm, wu_hbm, wd_hbm, vec_hbm, bu_hbm,
               datt_ref, dfar_ref, dq_ref, dnk_ref, dnv_ref, dhalo_ref, delta_ref, hidden_out,
               h_ref, g_ref, wo_ref, wu_ref, wd_ref, vec_ref, bu_ref, mix_ref, one_ref, low_ref,
               act_ref, n1_ref, r1_ref, dg_ref, n2_ref, r2_ref, nk_ref, nv_ref, last_ref, ins, outs,
               bias_ref, columns_ref, *scratch):
        loads = start_all(copies_of(
            [(h_hbm, h_ref), (vec_hbm.at[layer], vec_ref), (wo_hbm.at[layer], wo_ref),
             (bu_hbm, bu_ref), (wu_hbm.at[layer], wu_ref), (wd_hbm.at[layer], wd_ref),
             (g_hbm, g_ref)], ins))
        store = pltpu.make_async_copy(last_ref, hidden_out, outs.at[0])
        near = Side(True, length, (own_ref, other_ref, live_ref))
        near_forward(near, sequences, length, far_ref, q_ref, k_ref, v_ref, halo_ref, nk_ref,
                     nv_ref, mix_ref, bias_ref, scratch)
        side = lax.axis_index("seq")
        layer_rest(layer, sequences, length, mix_ref, h_ref, wo_ref, wu_ref, wd_ref,
                   [wait_for(loads, 0, 1, 2), wait_for(loads, 3, 4), wait_for(loads, 5)], vec_ref,
                   bu_ref, one_ref, low_ref, act_ref, n1_ref, r1_ref, dg_ref, n2_ref, r2_ref,
                   (last_ref,), lambda i: None)
        store.start()

        def given(s, rows):
            places = lax.broadcasted_iota(jnp.int32, (length, 1), 0) + side * length
            return jnp.where(
                places.astype(F32) < picked(live_ref, s), g_ref[rows, :].astype(F32), 0.0)

        nothing = wait_for(loads)
        layer_rest_back(sequences, length, given,
                        [wait_for(loads, 6), nothing, nothing, nothing], n1_ref,
                        r1_ref, dg_ref, n2_ref, r2_ref, wo_ref, wu_ref, wd_ref, vec_ref, one_ref,
                        low_ref, act_ref, datt_ref)
        near_backward(near, sequences, length, q_ref, nk_ref, nv_ref, low_ref, mix_ref,
                      delta_ref, dfar_ref, dq_ref, dnk_ref, dnv_ref, dhalo_ref, columns_ref, scratch)
        store.wait()

    act, stat = ((tokens, width), BF16), ((tokens, 128), F32)
    wide, deep = ((tokens, width), F32), ((tokens, hidden), BF16)
    near_rows, ordered = sequences * (WINDOW + SUB), sequences * (length + HALO)
    near, block = ((near_rows, width), BF16), ((sequences * BLOCK, width), BF16)
    return call(
        kernel, "turn",
        [(VMEM, ids[0]), (VMEM, ids[1]), (VMEM, ids[2]), (VMEM, far), (VMEM, q), (VMEM, k),
         (VMEM, v), (VMEM, halo)]
        + [(HBM, item) for item in (h, gradient, wo, wu, wd, vec, bias_up)],
        [(VMEM,) + wide, (VMEM,) + block, (VMEM,) + block, (VMEM, (ordered, width), F32),
         (VMEM, (ordered, width), F32), (VMEM, (2, sequences * HALO, width), BF16),
         (VMEM, (HEAD_ROWS * sequences, length), F32), (HBM,) + act],
        [(h.shape, h.dtype), act, ((width, width), BF16), ((width, hidden), BF16),
         ((hidden, width), BF16), ((8, width), BF16), (bias_up.shape, BF16), act, wide, act, deep,
         act, stat, deep, act, stat, near, near, act, 7, 1, bias_shape(False),
         bias_shape(True)] + attention_scratch(True),
        4 * tokens * width * (2 * hidden + width), 24000000, 42)


def back_far_call(sequences, length, ids, q, k, v, dfar, delta, dq_near, dnk, dnv):
    tokens, width = q.shape

    def kernel(own_ref, live_ref, q_ref, k_ref, v_ref, dfar_ref, delta_ref, dqn_ref, dnk_ref,
               dnv_ref, dq_ref, dk_ref, dv_ref, bias_ref,
               *scratch):
        far = Side(False, length, (own_ref, None, live_ref))
        side = far.side

        def key_terms(s, cols, kept):
            near = rows_at(s * (length + HALO) + HALO * side, length, 32)
            for out, term, which, other in ((dv_ref, dnv_ref, 0, 3), (dk_ref, dnk_ref, 1, 2)):
                left = jnp.concatenate([item[which] for item in kept], axis=1)
                right = jnp.concatenate([item[other] for item in kept], axis=0)
                out[far.keys(s, 0), cols] = dot_nn(left, right) + term[near, cols]

        def one(s):
            far.biases(s, None, bias_ref)
            delta = delta_ref[rows_at(s * HEAD_ROWS, HEAD_ROWS, HEAD_ROWS), :]
            attention_backward(
                far, s, q_ref, k_ref, v_ref, dfar_ref,
                lambda s, sub: rows_at(s * BLOCK + sub * SUB, SUB, SUB), delta, dq_ref,
                far.queries, key_terms, bias_ref, scratch)
            dq_ref[rows_at(s * length + (1 - side) * BLOCK, BLOCK, BLOCK), :] = dqn_ref[
                rows_at(s * BLOCK, BLOCK, BLOCK), :]

        loop(sequences, one)

    wide = (VMEM, (tokens, width), F32)
    return call(
        kernel, "back_far",
        [(VMEM, ids[0]), (VMEM, ids[2])]
        + [(VMEM, item) for item in (q, k, v, dfar, delta, dq_near, dnk, dnv)],
        [(VMEM, (tokens, width), BF16), wide, wide],
        [bias_shape(True)] + attention_scratch(True), 4000000000, 16000000, 8)


def back_call(layer, sequences, length, ids, dq, dk, dv, dhalo, datt, u, x, saved, w, a, b, wo, wu,
              wd, vec):
    tokens, width = dq.shape
    hidden, rank = wu.shape[2], a.shape[2]

    def kernel(own_ref, other_ref, live_ref, dq_ref, dk_ref, dv_ref, dhalo_ref, datt_ref, u_hbm, x_hbm,
               n1_hbm, r1_hbm, dg_hbm, n2_hbm, r2_hbm, q_hbm, k_hbm, v_hbm, nk_hbm, nv_hbm, mix_hbm,
               w_hbm, a_hbm, b_hbm, wo_hbm, wu_hbm, wd_hbm, vec_hbm,
               datt_out, dfar_ref, dqn_ref, dnk_ref, dnv_ref, dhalo_out, delta_ref, q_ref, k_ref,
               v_ref, grad_out,
               u_ref, x_ref, n1_ref, r1_ref, dg_ref, n2_ref, r2_ref, nk_ref, nv_ref, w_ref,
               a_ref, b_ref, wo_ref, wu_ref, wd_ref, vec_ref, dkb_ref, dvb_ref, du_ref, grad_ref,
               two_ref, low_ref, mix_ref, ins, outs, bias_ref, *scratch):
        loads = start_all(copies_of(
            [(a_hbm.at[layer + 1], a_ref), (b_hbm.at[layer + 1], b_ref), (u_hbm, u_ref),
             (x_hbm, x_ref), (w_hbm.at[layer + 1], w_ref), (vec_hbm.at[layer], vec_ref),
             (n2_hbm, n2_ref), (r2_hbm, r2_ref), (wd_hbm.at[layer], wd_ref), (dg_hbm, dg_ref),
             (wu_hbm.at[layer], wu_ref), (n1_hbm, n1_ref), (r1_hbm, r1_ref),
             (wo_hbm.at[layer], wo_ref), (q_hbm, q_ref), (nk_hbm, nk_ref), (nv_hbm, nv_ref),
             (k_hbm, k_ref), (v_hbm, v_ref), (mix_hbm, mix_ref)], ins))
        adapter_back(sequences, length, [wait_for(loads, 0, 1), wait_for(loads, 2, 3)], dq_ref, dk_ref, dv_ref, dhalo_ref, u_ref, x_ref,
                     a_ref, b_ref, dkb_ref, dvb_ref, du_ref, grad_ref)
        store = pltpu.make_async_copy(grad_ref, grad_out, outs.at[0])
        store.start()
        down, _, _ = low_rank(a_ref, b_ref)

        wait_for(loads, 4)()
        tall = tokens // 2

        def given(s, rows):
            return two_ref[rows, :]

        def project(i):
            rows = rows_at(i * tall, tall, 128)
            two_ref[rows, :] = project_back(rows, rows, datt_ref, dq_ref, dkb_ref, dvb_ref, du_ref,
                                            w_ref, down)

        loop(2, project)
        layer_rest_back(sequences, length, given,
                        [wait_for(loads, 5, 6, 7), wait_for(loads, 8, 9), wait_for(loads, 10),
                         wait_for(loads, 11, 12, 13, 19)], n1_ref, r1_ref, dg_ref, n2_ref, r2_ref,
                        wo_ref, wu_ref, wd_ref, vec_ref, two_ref, low_ref, dg_ref, datt_out)
        wait_for(loads, 14, 15, 16)()
        near = Side(True, length, (own_ref, other_ref, live_ref))
        near_backward(near, sequences, length, q_ref, nk_ref, nv_ref, low_ref, mix_ref,
                      delta_ref, dfar_ref, dqn_ref, dnk_ref, dnv_ref, dhalo_out, bias_ref, scratch)
        wait_for(loads, 17, 18)()
        store.wait()

    act, stat = ((tokens, width), BF16), ((tokens, 128), F32)
    wide, deep = ((tokens, width), F32), ((tokens, hidden), BF16)
    near_rows, ordered = sequences * (WINDOW + SUB), sequences * (length + HALO)
    near, block = ((near_rows, width), BF16), ((sequences * BLOCK, width), BF16)
    small, factors = ((tokens, 2 * rank), BF16), ((2, rank, width), F32)
    grad = ((4 * rank, width), F32)
    return call(
        kernel, "back",
        [(VMEM, ids[0]), (VMEM, ids[1]), (VMEM, ids[2])]
        + [(VMEM, item) for item in (dq, dk, dv, dhalo, datt)]
        + [(HBM, item) for item in (u, x, *saved, w, a, b, wo, wu, wd, vec)],
        [(VMEM,) + wide, (VMEM,) + block, (VMEM,) + block,
         (VMEM, (ordered, width), F32), (VMEM, (ordered, width), F32),
         (VMEM, (2, sequences * HALO, width), BF16), (VMEM, (HEAD_ROWS * sequences, length), F32),
         (VMEM,) + act, (VMEM,) + act, (VMEM,) + act,
         (HBM,) + grad],
        [small, act, act, stat, deep, act, stat, near, near, ((width, 3 * width), BF16), factors,
         factors, ((width, width), BF16), ((width, hidden), BF16), ((hidden, width), BF16),
         ((8, width), BF16), act, act, small, grad, wide, act, act, 20, 1, bias_shape(True)]
        + attention_scratch(True),
        2 * tokens * width * (2 * hidden + 4 * width), 24000000, 38)


def last_call(layer, sequences, length, dq, dk, dv, dhalo, u, x, w, a, b, other, *state):
    tokens, width = dq.shape
    rank = a.shape[2]

    def kernel(dq_ref, dk_ref, dv_ref, dhalo_ref, u_hbm, x_hbm, w_hbm, a_hbm, b_hbm, other_hbm,
               *rest):
        given, rest = rest[:len(state)], rest[len(state):]
        (dkb_ref, dvb_ref, du_ref, w_ref, down_ref, mine_ref, theirs_ref), rest = rest[:7], rest[7:]
        taken, rest = rest[:len(state)], rest[len(state):]
        u_ref, x_ref, a_ref, b_ref, other_ref, grad_ref, sems, state_sems = rest
        loads = start_all(copies_of(
            [(a_hbm.at[layer], a_ref), (b_hbm.at[layer], b_ref), (u_hbm, u_ref), (x_hbm, x_ref),
             (other_hbm, other_ref), (w_hbm.at[layer], w_ref)], sems))
        more = start_all(copies_of(zip(given, taken), state_sems))
        adapter_back(sequences, length, [wait_for(loads, 0, 1), wait_for(loads, 2, 3)], dq_ref, dk_ref, dv_ref, dhalo_ref, u_ref, x_ref,
                     a_ref, b_ref, dkb_ref, dvb_ref, du_ref, grad_ref)
        down_ref[...] = low_rank(a_ref, b_ref)[0]
        wait_for(loads, 4)()
        first = lax.axis_index("seq") == layer
        here, there = grad_ref[...], other_ref[...]
        mine_ref[...] = jnp.where(first, here, there)
        theirs_ref[...] = jnp.where(first, there, here)
        wait_for(loads, 5)()
        for copy in more:
            copy.wait()

    act, grad = ((tokens, width), BF16), ((4 * rank, width), F32)
    small, factors = ((tokens, 2 * rank), BF16), ((2, rank, width), F32)
    return call(
        kernel, "adapter_back",
        [(VMEM, dq), (VMEM, dk), (VMEM, dv), (VMEM, dhalo)]
        + [(HBM, item) for item in (u, x, w, a, b, other, *state)],
        [(VMEM,) + act, (VMEM,) + act, (VMEM,) + small, (VMEM, (width, 3 * width), BF16),
         (VMEM, (2 * rank, width), BF16), (VMEM,) + grad, (VMEM,) + grad]
        + [(VMEM, item.shape, F32) for item in state],
        [small, act, factors, factors, grad, grad, 6, len(state)], 500000000, 12000000, 8)


def project_back_call(datt, dq, dk, dv, du, w, down):
    tokens, width = dq.shape
    parts = 2
    length = tokens // parts

    def kernel(datt_ref, dq_ref, dk_ref, dv_ref, du_ref, w_ref, down_ref, out_hbm, out_ref, sems):
        def part(i):
            rows = rows_at(i * length, length, 128)
            return pltpu.make_async_copy(out_ref.at[rows], out_hbm.at[rows], sems.at[i])

        def one(i):
            rows = rows_at(i * length, length, 128)
            out_ref[rows, :] = project_back(rows, rows, datt_ref, dq_ref, dk_ref, dv_ref, du_ref,
                                            w_ref, down_ref[...])
            part(i).start()

        loop(parts, one)
        for i in range(parts):
            part(i).wait()

    return call(
        kernel, "project_back", [(VMEM, item) for item in (datt, dq, dk, dv, du, w, down)],
        [(HBM, (tokens, width), F32)], [((tokens, width), F32), parts],
        2 * tokens * width * width * 3, 4000000, 6)[0]


def adam_call(mine, theirs, token_slots, steps, down, up, m_down, v_down, m_up, v_up):
    layers, two, rank, width = down.shape

    def kernel(mine_ref, theirs_ref, steps_ref, down_ref, up_ref, md_ref, vd_ref, mu_ref, vu_ref,
               *rest):
        outs, results, sems = rest[:6], rest[6:12], rest[12]
        down_out, up_out, md_out, vd_out, mu_out, vu_out = results
        side = lax.axis_index("seq")
        for layer in range(layers):
            for which in range(two):
                for group, (w_ref, m_ref, v_ref, w_out, m_out, v_out, rate, decay) in enumerate((
                    (down_ref, md_ref, vd_ref, down_out, md_out, vd_out, 0.03125, 0.1),
                    (up_ref, mu_ref, vu_ref, up_out, mu_out, vu_out, 0.5, 0.0),
                )):
                    rows = slice((group * two + which) * rank, (group * two + which + 1) * rank)
                    grad = jnp.where(side == layer, mine_ref[rows, :], theirs_ref[rows, :])
                    grad = grad / token_slots
                    step = picked(steps_ref, (layer * two + which) * 2 + group)
                    correction = jnp.broadcast_to(1.0 - jnp.exp2(-step), (rank, width))
                    weight = w_ref[layer, which]
                    moment = 0.5 * m_ref[layer, which] + 0.5 * grad
                    velocity = 0.5 * v_ref[layer, which] + 0.5 * grad * grad
                    size = moment / correction / (jnp.sqrt(velocity / correction) + 1e-08)
                    w_out[layer, which] = weight - rate * (size + decay * weight)
                    m_out[layer, which] = moment
                    v_out[layer, which] = velocity

        for store in start_all(copies_of(zip(results, outs), sems)):
            store.wait()

    return call(
        kernel, "adam",
        [(VMEM, mine), (VMEM, theirs), (VMEM, steps)]
        + [(VMEM, item) for item in (down, up, m_down, v_down, m_up, v_up)],
        [(HBM, down.shape, F32)] * 6, [(down.shape, F32)] * 6 + [6], 1000000, 2000000, 4)


def together(*values):
    return lax.optimization_barrier(values)


def sum_while(mine, theirs, work):
    batch = lax.axis_size("batch")
    swap = [(0, 1), (1, 0)]
    mine = mine + lax.ppermute(theirs, "seq", swap)
    done, work, step = None, list(work), 1
    while step < batch:
        ways = 4 if batch % (4 * step) == 0 else 2
        given = mine.astype(BF16)
        come = [lax.ppermute(given, "batch", [(i, i ^ (step * d)) for i in range(batch)])
                for d in range(1, ways)]
        if work:
            done = work.pop(0)(mine, done)
            *come, done = together(*come, done)
        mine = mine + sum(item.astype(F32) for item in come)
        step *= ways
    for one in work:
        done = one(mine, done)
    return mine, lax.ppermute(mine, "seq", swap), done


def shards(
    first_layer_input,
    output_gradient,
    sentence_pair_index,
    sequence_live_length,
    optimizer_step_count,
    query_key_value_weight,
    attention_output_weight,
    feedforward_up_weight,
    feedforward_down_weight,
    layer_bias_gain_rows,
    feedforward_up_bias,
    adapter_down_factors,
    adapter_up_factors,
    first_moment_down,
    second_moment_down,
    first_moment_up,
    second_moment_up,
):
    sequences, length, width = first_layer_input.shape
    tokens = sequences * length
    swap = [(0, 1), (1, 0)]
    a, b = adapter_down_factors, jnp.swapaxes(adapter_up_factors, 2, 3)
    vec = layer_bias_gain_rows
    bias_up = feedforward_up_bias
    wqkv, wo = query_key_value_weight, attention_output_weight
    wu, wd = feedforward_up_weight, feedforward_down_weight
    ids = (sentence_pair_index, lax.ppermute(sentence_pair_index, "seq", swap),
           sequence_live_length[None, :])
    shape = (sequences, length)

    x1 = first_layer_input.reshape(tokens, width)
    q1, k1, v1, send, u1 = first_call(0, *shape, x1, wqkv, a, b, vec)
    halo = lax.ppermute(send, "seq", swap)
    far = far_call(*shape, q1, k1, v1, ids)
    q2, k2, v2, send, u2, x2, h1, *saved = middle_call(
        0, *shape, ids, far, q1, k1, v1, halo, x1, wqkv, a, b, wo, wu, wd, vec, bias_up)
    halo = lax.ppermute(send, "seq", swap)
    far = far_call(*shape, q2, k2, v2, ids)
    datt, dfar, dqn, dnk, dnv, dsend, delta, hidden_out = turn_call(
        1, *shape, ids, far, q2, k2, v2, halo, h1, output_gradient.reshape(tokens, width),
        wo, wu, wd, vec, bias_up)
    dhalo = lax.ppermute(dsend, "seq", swap)
    dq, dk, dv = back_far_call(*shape, ids, q2, k2, v2, dfar, delta, dqn, dnk, dnv)
    datt, dfar, dqn, dnk, dnv, dsend, delta, q1, k1, v1, grad2 = back_call(
        0, *shape, ids, dq, dk, dv, dhalo, datt, u2, x2, saved, wqkv, a, b, wo, wu, wd, vec)
    dhalo = lax.ppermute(dsend, "seq", swap)
    dq, dk, dv = back_far_call(*shape, ids, q1, k1, v1, dfar, delta, dqn, dnk, dnv)
    dk, dv, du, w1, down1, mine, theirs, *state = last_call(
        0, *shape, dq, dk, dv, dhalo, u1, x1, wqkv, a, b, grad2, a, b, first_moment_down,
        second_moment_down, jnp.swapaxes(first_moment_up, 2, 3),
        jnp.swapaxes(second_moment_up, 2, 3))

    def work(token, out):
        now, _ = together(datt, token)
        return project_back_call(now, dq, dk, dv, du, w1, down1)

    mine, theirs, gradient = sum_while(mine, theirs, [work])
    token_slots = tokens * lax.axis_size("seq") * lax.axis_size("batch")
    down, up, m_down, v_down, m_up, v_up = adam_call(
        mine, theirs, token_slots, optimizer_step_count.reshape(1, -1), *state)
    return (
        hidden_out.reshape(sequences, length, width),
        gradient.reshape(sequences, length, width),
        down,
        jnp.swapaxes(up, 2, 3),
        m_down,
        v_down,
        jnp.swapaxes(m_up, 2, 3),
        jnp.swapaxes(v_up, 2, 3),
    )


def solution(mesh):
    acts, whole = P("batch", "seq", None), P()
    return jax.shard_map(
        shards,
        mesh=mesh,
        in_specs=(acts, acts, P("batch", "seq"), P("batch")) + (whole,) * 13,
        out_specs=(acts, acts) + (whole,) * 6,
        check_vma=False,
    )
```

```python
import jax
import jax.numpy as jnp
from jax import lax
from jax.experimental import pallas as pl
from jax.experimental.pallas import tpu as pltpu
from jax.sharding import PartitionSpec as P

HEADS = 12
ENCODER_LAYERS = 2
HALO = 96
BLOCK = 128
SUB = 64
WINDOW = 256
QUAD = 256
HEAD_ROWS = 16
MASKED = -1000000000.0
LOG2E = 1.4426950408889634
HALF_ROOT_PI = 0.886226925452758
ROOT_HALF = 0.7071067811865476
ACTIVE = 0.7978845608028654
SLOPE = 0.5641895835477563
F32 = jnp.float32
BF16 = jnp.bfloat16


def dot_nn(a, b):
    return lax.dot_general(a, b, (((1,), (0,)), ((), ())), preferred_element_type=F32)


def dot_nt(a, b):
    return lax.dot_general(a, b, (((1,), (1,)), ((), ())), preferred_element_type=F32)


def dot_tn(a, b):
    return lax.dot_general(a, b, (((0,), (0,)), ((), ())), preferred_element_type=F32)


def rows_at(start, size, multiple):
    return pl.ds(pl.multiple_of(start, multiple), size)


def loop(count, body):
    def step(i, carry):
        body(i)
        return carry

    lax.fori_loop(0, count, step, 0)


def picked(row_ref, i):
    row = row_ref[...].astype(F32)
    at = lax.broadcasted_iota(jnp.int32, row.shape, 1) == i
    return jnp.sum(jnp.where(at, row, 0.0), axis=1, keepdims=True)


def column_of(row):
    n = row.shape[1]
    eye = lax.broadcasted_iota(jnp.int32, (n, n), 0) == lax.broadcasted_iota(jnp.int32, (n, n), 1)
    return jnp.sum(jnp.where(eye, row, 0.0), axis=1, keepdims=True)


def low_lanes():
    return (lax.broadcasted_iota(jnp.int32, (SUB, 128), 1) < 64).astype(F32).astype(BF16)


def spread_heads(tile, low):
    zero = jnp.zeros((2 * SUB, 128), BF16)
    high = 1 - low
    left, right = tile[:, :128], tile[:, 128:]
    left = jnp.concatenate([left * low, left * high], axis=0)
    right = jnp.concatenate([right * low, right * high], axis=0)
    return jnp.concatenate([jnp.concatenate([left, zero], axis=1),
                            jnp.concatenate([zero, right], axis=1)], axis=0)


def gather_heads(wide):
    low = lax.broadcasted_iota(jnp.int32, (SUB, 128), 1) < 64
    parts = []
    for i in range(2):
        cols, top = slice(128 * i, 128 * i + 128), 2 * SUB * i
        parts.append(jnp.where(low, wide[top:top + SUB, cols],
                               wide[top + SUB:top + 2 * SUB, cols]))
    return jnp.concatenate(parts, axis=1)


def pipelined(units):
    units = list(units)
    live = []
    while units or live:
        if units:
            live.append(units.pop(0))
        for unit in reversed(list(live)):
            if next(unit, None) is None:
                live.remove(unit)


class Side:
    def __init__(self, near, length, ids_refs):
        self.near, self.length, self.ids_refs = near, length, ids_refs
        self.side = lax.axis_index("seq")
        self.row0 = BLOCK * ((1 - self.side) if near else self.side)

    def ids(self, s):
        own_ref, other_ref, live_ref = self.ids_refs
        own = own_ref[pl.ds(s, 1), :].astype(F32)
        query = jnp.where(self.row0 == 0, own[:, :BLOCK], own[:, BLOCK:])
        if self.near:
            other = other_ref[pl.ds(s, 1), :].astype(F32)
            kept = WINDOW + SUB - HALO
            key = jnp.where(
                self.side == 0,
                jnp.concatenate([own[:, self.length - kept:], other[:, :HALO]], axis=1),
                jnp.concatenate([other[:, self.length - HALO:], own[:, :kept]], axis=1))
            start = jnp.where(self.side == 0, self.length - kept, self.length - HALO)
        else:
            key, start = own, self.side * self.length
        places = lax.broadcasted_iota(jnp.int32, key.shape, 1) + start
        return query, jnp.where(places.astype(F32) < picked(live_ref, s), key, -1.0)

    def queries(self, s, sub):
        return rows_at(s * self.length + self.row0 + sub * SUB, SUB, SUB)

    def keys(self, s, sub):
        if self.near:
            return rows_at(s * (WINDOW + SUB) + sub * SUB, WINDOW, SUB)
        return rows_at(s * self.length, WINDOW, WINDOW)

    def biases(self, s, rows_ref=None, columns_ref=None):
        lane = lax.broadcasted_iota(jnp.int32, (1, 128), 1)
        place = jnp.where(lane < SUB, lane, lane - SUB)
        key_place = lax.broadcasted_iota(jnp.int32, (WINDOW, 128), 0)
        shape = (SUB, WINDOW)
        apart = lax.broadcasted_iota(jnp.int32, shape, 1) - lax.broadcasted_iota(jnp.int32, shape, 0)
        query, key = self.ids(s)
        if rows_ref is None:
            blocks = (128, 128, SUB) if self.near else (128, 128)
            column = jnp.concatenate(
                [column_of(key[:, 128 * i:128 * i + n]) for i, n in enumerate(blocks)], axis=0)
            turned = pltpu.roll(query, SUB, 1)
        for sub in range(2):
            own = HALO if self.near else self.row0 + sub * SUB
            if rows_ref is not None:
                keys = key[:, sub * SUB:sub * SUB + WINDOW] if self.near else key
                queries = column_of(query)[sub * SUB:(sub + 1) * SUB]
                seen = (queries == keys) | (apart == own)
                rows_ref[sub * SUB:(sub + 1) * SUB, :] = jnp.where(seen, 0.0, MASKED)
                continue
            keys = column[sub * SUB:sub * SUB + WINDOW] if self.near else column
            pair = (query, turned) if sub == 0 else (turned, query)
            seen = (keys == jnp.where(lane < SUB, *pair)) | (key_place == place + own)
            columns_ref[sub * WINDOW:(sub + 1) * WINDOW, :] = jnp.where(seen, 0.0, MASKED)


def bias_shape(turned):
    return ((2 * WINDOW, 128) if turned else (2 * SUB, WINDOW)), F32


def half(sub):
    return slice(4 * SUB * sub, 4 * SUB * (sub + 1))


SLOTS = 2


def attention_scratch(backward=False):
    pair = [((SLOTS, WINDOW, 4 * SUB), F32), ((SLOTS, WINDOW, 4 * SUB), BF16)]
    return pair * 2 if backward else pair


def attention_forward(where, s, q_ref, k_ref, v_ref, out_ref, out_rows, bias_ref, scratch):
    low = low_lanes()
    scores_ref, share_ref = scratch[:2]

    def unit(quad, sub):
        cols = slice(QUAD * quad, QUAD * quad + QUAD)
        keys = where.keys(s, sub)
        q4 = spread_heads(q_ref[where.queries(s, sub), cols], low)
        slot = (2 * quad + sub) % SLOTS
        scores_ref[slot] = dot_nt(q4, k_ref[keys, cols])
        yield True
        bias = bias_ref[sub * SUB:(sub + 1) * SUB, :]
        totals = []
        for h in range(4):
            rows = slice(h * SUB, (h + 1) * SUB)
            scores = scores_ref[slot, rows, :] + bias
            share = jnp.exp2(scores - jnp.max(scores, axis=1, keepdims=True))
            totals.append(1.0 / jnp.sum(share, axis=1, keepdims=True))
            share_ref[slot, rows, :] = share.astype(BF16)
        yield True
        mixed = dot_nn(share_ref[slot], v_ref[keys, cols])
        mixed = jnp.concatenate(
            [mixed[h * SUB:(h + 1) * SUB] * totals[h] for h in range(4)], axis=0)
        yield True
        out_ref[out_rows(s, sub), cols] = gather_heads(mixed).astype(BF16)

    width = q_ref.shape[1]
    pipelined(unit(quad, sub) for quad in range(width // QUAD) for sub in range(2))


def attention_backward(where, s, q_ref, k_ref, v_ref, dmix_ref, dmix_rows, delta, dq_ref,
                       dq_rows, key_terms, bias_ref, scratch):
    low = low_lanes()
    scores_ref, share_ref, d_share_ref, d_scores_ref = scratch
    delta = jnp.where(where.row0 == 0, delta[:, :BLOCK], delta[:, BLOCK:])
    turned = pltpu.roll(delta, SUB, 1)
    first_half = lax.broadcasted_iota(jnp.int32, (1, 2 * SUB), 1) < SUB

    def unit(quad, sub, kept):
        cols = slice(QUAD * quad, QUAD * quad + QUAD)
        keys = where.keys(s, sub)
        slot = (2 * quad + sub) % SLOTS
        q4 = spread_heads(q_ref[where.queries(s, sub), cols], low)
        d4 = spread_heads(dmix_ref[dmix_rows(s, sub), cols], low)
        scores_ref[slot] = dot_nt(k_ref[keys, cols], q4)
        d_share_ref[slot] = dot_nt(v_ref[keys, cols], d4)
        yield True
        bias = bias_ref[sub * WINDOW:(sub + 1) * WINDOW, :]
        shares, d_scores = [], []
        left, right = (delta, turned) if sub == 0 else (turned, delta)
        for i in range(2):
            head = 4 * quad + 2 * i
            drop = jnp.where(first_half, left[head:head + 1], right[head + 1:head + 2])
            part = scores_ref[slot, :, 128 * i:128 * i + 128] + bias
            part = jnp.exp2(part - jnp.max(part, axis=0, keepdims=True))
            part = part * (1.0 / jnp.sum(part, axis=0, keepdims=True))
            shares.append(part.astype(BF16))
            d_scores.append((part * (d_share_ref[slot, :, 128 * i:128 * i + 128] - drop)).astype(BF16))
        d_scores = jnp.concatenate(d_scores, axis=1)
        kept.append((jnp.concatenate(shares, axis=1), d_scores, q4, d4))
        yield True
        if sub == 1:
            key_terms(s, cols, kept)
        yield True
        d_query = gather_heads(dot_tn(d_scores, k_ref[keys, cols])) * 0.125
        dq_ref[dq_rows(s, sub), cols] = d_query.astype(BF16)

    width = q_ref.shape[1]

    def units():
        for quad in range(width // QUAD):
            kept = []
            for sub in range(2):
                yield unit(quad, sub, kept)

    pipelined(units())


def row_deltas(dmix, mix):
    shape = (HEAD_ROWS, dmix.shape[1])
    own = (lax.broadcasted_iota(jnp.int32, shape, 1) // 64
           == lax.broadcasted_iota(jnp.int32, shape, 0)).astype(F32).astype(BF16)
    product = dmix.astype(F32) * mix.astype(F32)
    high = product.astype(BF16)
    rest = (product - high.astype(F32)).astype(BF16)
    return dot_nt(own, high) + dot_nt(own, rest)


def near_keys(s, length, k_ref, v_ref, halo_ref, nk_ref, nv_ref):
    side = lax.axis_index("seq")
    wide, own = WINDOW + SUB, WINDOW + SUB - HALO
    given = rows_at(s * HALO, HALO, 32)
    for i, (src, dst) in enumerate(((k_ref, nk_ref), (v_ref, nv_ref))):
        dst[rows_at(s * wide + HALO * side, own, 32), :] = src[
            rows_at(s * length + (length - own) * (1 - side), own, 32), :]
        dst[rows_at(s * wide + own * (1 - side), HALO, 32), :] = halo_ref[i, given, :]


def norm_forward(values, gain, shift):
    center = values - jnp.mean(values, axis=1, keepdims=True)
    spread = jnp.mean(center * center, axis=1, keepdims=True)
    inverse = lax.rsqrt(spread + 1e-05)
    scaled = center * inverse
    return scaled * gain + shift, scaled, inverse


def norm_backward(gradient, scaled, inverse, gain):
    inner = gradient * gain
    return inverse * (
        inner
        - jnp.mean(inner, axis=1, keepdims=True)
        - scaled * jnp.mean(inner * scaled, axis=1, keepdims=True)
    )


def low_rank(a_ref, b_ref):
    down = jnp.concatenate([a_ref[0], a_ref[1]], axis=0).astype(BF16)
    zero = jnp.zeros_like(b_ref[0])
    up_q = jnp.concatenate([b_ref[0], zero], axis=0).astype(BF16)
    up_v = jnp.concatenate([zero, b_ref[1]], axis=0).astype(BF16)
    return down, up_q, up_v


def project_in(sequences, length, x_ref, w_ref, waits, a_ref, b_ref, vec_ref, q_ref, k_ref, v_ref,
               u_ref, send_ref, sent):
    side = lax.axis_index("seq")
    width = x_ref.shape[1]
    waits[0]()
    down, up_q, up_v = low_rank(a_ref, b_ref)
    vec = vec_ref[...].astype(F32)

    tall = x_ref.shape[0] // 2

    def queries(i):
        rows = rows_at(i * tall, tall, 128)
        x = x_ref[rows, :]
        inner = dot_nt(x, down).astype(BF16)
        u_ref[rows, :] = inner
        q = dot_nn(x, w_ref[:, :width]) + vec[0:1] + 2.0 * dot_nn(inner, up_q)
        q_ref[rows, :] = (q * (0.125 * LOG2E)).astype(BF16)

    def keys(i):
        rows = rows_at(i * tall, tall, 128)
        k_ref[rows, :] = dot_nn(x_ref[rows, :], w_ref[:, width:2 * width]).astype(BF16)

    def values(i):
        rows = rows_at(i * tall, tall, 128)
        v = dot_nn(x_ref[rows, :], w_ref[:, 2 * width:]) + vec[1:2]
        v_ref[rows, :] = (v + 2.0 * dot_nn(u_ref[rows, :], up_v)).astype(BF16)

    def send(s):
        taken = rows_at(s * length + (1 - side) * (length - HALO), HALO, 32)
        for i, ref in enumerate((k_ref, v_ref)):
            send_ref[i, rows_at(s * HALO, HALO, 32), :] = ref[taken, :]

    loop(2, queries)
    sent()
    waits[1]()
    loop(2, keys)
    waits[2]()
    loop(2, values)
    loop(sequences, send)


def layer_rest(layer, sequences, length, mix_ref, h_ref, wo_ref, wu_ref, wd_ref, waits, vec_ref, bu_ref,
               one_ref, low_ref, act_ref, n1_ref, r1_ref, dg_ref, n2_ref, r2_ref, h_outs, sent):
    tokens, hidden = mix_ref.shape[0], wu_ref.shape[1]
    waits[0]()
    vec = vec_ref[...].astype(F32)
    short, units = 128, 3

    def mixed(i):
        def unit(k):
            rows = rows_at((i * units + k) * short, short, short)
            attended = dot_nn(mix_ref[rows, :], wo_ref[...]) + vec[2:3] + h_ref[rows, :].astype(F32)
            yield True
            one, scaled, inverse = norm_forward(attended, vec[4:5], vec[5:6])
            n1_ref[rows, :] = scaled.astype(n1_ref.dtype)
            r1_ref[rows, :] = jnp.broadcast_to(inverse, (short, 128))
            one_ref[rows, :] = one
            low_ref[rows, :] = (one * ROOT_HALF).astype(BF16)

        pipelined(unit(k) for k in range(units))

    loop(tokens // short // units, mixed)
    sent(0)
    waits[1]()
    tile = 1024

    def up(j):
        cols = rows_at(j * tile, tile, tile)
        bias = bu_ref[layer:layer + 1, cols].astype(F32) * ROOT_HALF
        weights = wu_ref[:, cols]

        def unit(k):
            rows = slice(k * short, (k + 1) * short)
            gate = dot_nn(low_ref[rows, :], weights)
            yield True
            gate = gate + bias
            below = HALF_ROOT_PI * lax.erf(gate) + HALF_ROOT_PI
            act_ref[rows, cols] = (gate * below).astype(BF16)
            density = jnp.exp2(gate * gate * -LOG2E)
            dg_ref[rows, cols] = (below + gate * density).astype(BF16)

        pipelined(unit(k) for k in range(tokens // short))

    loop(hidden // tile, up)
    sent(1)
    waits[2]()

    def down(s):
        rows = rows_at(s * length, length, length)
        summed = dot_nn(act_ref[rows, :], wd_ref[...]) * ACTIVE + vec[3:4] + one_ref[rows, :]
        out, scaled, inverse = norm_forward(summed, vec[6:7], vec[7:8])
        n2_ref[rows, :] = scaled.astype(n2_ref.dtype)
        r2_ref[rows, :] = jnp.broadcast_to(inverse, (length, 128))
        for h_out in h_outs:
            h_out[rows, :] = out.astype(h_out.dtype)

    loop(sequences, down)
    sent(2)


def layer_rest_back(sequences, length, gradient, waits, n1_ref, r1_ref, dg_ref, n2_ref, r2_ref,
                    wo_ref, wu_ref, wd_ref, vec_ref, two_ref, low_ref, gate_ref, datt_ref):
    tokens, hidden = low_ref.shape[0], wu_ref.shape[1]
    waits[0]()
    vec = vec_ref[...].astype(F32)
    tall = tokens // 2

    def second(s):
        rows = rows_at(s * length, length, length)
        two = norm_backward(
            gradient(s, rows), n2_ref[rows, :].astype(F32), r2_ref[rows, 0:1], vec[6:7])
        two_ref[rows, :] = two
        low_ref[rows, :] = (two * SLOPE).astype(BF16)

    loop(sequences, second)
    waits[1]()
    tile = 1024

    def down(j):
        cols = rows_at(j * tile, tile, tile)
        weights = wd_ref[cols, :]

        def unit(s):
            rows = slice(s * length, (s + 1) * length)
            gate = dot_nt(low_ref[rows, :], weights)
            yield True
            gate_ref[rows, cols] = (gate * dg_ref[rows, cols].astype(F32)).astype(BF16)

        pipelined(unit(s) for s in range(sequences))

    loop(hidden // tile, down)
    waits[2]()
    waits[3]()

    def up(i):
        rows = rows_at(i * tall, tall, 128)
        datt_ref[rows, :] = dot_nt(gate_ref[rows, :], wu_ref[...])

    def first(s):
        rows = slice(s * length, (s + 1) * length)
        att = norm_backward(datt_ref[rows, :] + two_ref[rows, :], n1_ref[rows, :].astype(F32),
                            r1_ref[rows, 0:1], vec[4:5])
        datt_ref[rows, :] = att
        att = att.astype(BF16)
        yield True
        low_ref[rows, :] = dot_nt(att, wo_ref[...]).astype(BF16)

    loop(2, up)
    pipelined(first(s) for s in range(sequences))


def near_backward(near, sequences, length, q_ref, nk_ref, nv_ref, dmix_ref, mix_ref,
                  delta_ref, dfar_ref, dq_ref, dnk_ref, dnv_ref, dhalo_ref, bias_ref, scratch):
    side, all_rows = near.side, length + HALO
    width = q_ref.shape[1]

    def key_terms(s, cols, kept):
        for out, which, other in ((dnv_ref, 0, 3), (dnk_ref, 1, 2)):
            left, right = [item[which] for item in kept], [item[other] for item in kept]
            start = s * all_rows + (length + HALO - WINDOW - SUB) * (1 - side)
            out[rows_at(start, SUB, 32), cols] = dot_nn(left[0][:SUB], right[0])
            both = jnp.concatenate([left[0][SUB:], left[1][:WINDOW - SUB]], axis=1)
            out[rows_at(start + SUB, WINDOW - SUB, 32), cols] = dot_nn(
                both, jnp.concatenate(right, axis=0))
            out[rows_at(start + WINDOW, SUB, 32), cols] = dot_nn(
                left[1][WINDOW - SUB:], right[1])

    def one(s):
        dfar_ref[rows_at(s * BLOCK, BLOCK, BLOCK), :] = dmix_ref[
            rows_at(s * length + side * BLOCK, BLOCK, BLOCK), :]
        near.biases(s, None, bias_ref)
        rows = rows_at(s * length, length, length)
        delta = row_deltas(dmix_ref[rows, :], mix_ref[rows, :])
        delta_ref[rows_at(s * HEAD_ROWS, HEAD_ROWS, HEAD_ROWS), :] = delta
        attention_backward(
            near, s, q_ref, nk_ref, nv_ref, dmix_ref, near.queries, delta, dq_ref,
            lambda s, sub: rows_at(s * BLOCK + sub * SUB, SUB, SUB), key_terms, bias_ref,
            scratch)
        unseen = rows_at(s * all_rows + (WINDOW + SUB) * side, all_rows - WINDOW - SUB, 32)
        for out in (dnk_ref, dnv_ref):
            out[unseen, :] = jnp.zeros((all_rows - WINDOW - SUB, width), F32)
        halo = rows_at(s * all_rows + length * (1 - side), HALO, 32)
        dhalo_ref[0, rows_at(s * HALO, HALO, 32), :] = (
            dnk_ref[halo, :] * (1.0 / LOG2E)).astype(BF16)
        dhalo_ref[1, rows_at(s * HALO, HALO, 32), :] = dnv_ref[halo, :].astype(BF16)

    loop(sequences, one)


def adapter_back(sequences, length, waits, dq_ref, dk_ref, dv_ref, dhalo_ref, u_ref, x_ref, a_ref,
                 b_ref, dkb_ref, dvb_ref, du_ref, grad_ref):
    side = lax.axis_index("seq")
    rank = a_ref.shape[1]
    waits[0]()
    _, up_q, up_v = low_rank(a_ref, b_ref)

    def one(s):
        rows = rows_at(s * length, length, length)
        taken = rows_at(s * length + (1 - side) * (length - HALO), HALO, 32)
        hrows = rows_at(s * HALO, HALO, 32)
        dvb_ref[rows, :] = dv_ref[rows, :].astype(BF16)
        dvb_ref[taken, :] = (dv_ref[taken, :] + dhalo_ref[1, hrows, :].astype(F32)).astype(BF16)
        dkb_ref[rows, :] = (dk_ref[rows, :] * (1.0 / LOG2E)).astype(BF16)
        dkb_ref[taken, :] = (
            dk_ref[taken, :] * (1.0 / LOG2E) + dhalo_ref[0, hrows, :].astype(F32)).astype(BF16)
        dv16 = dvb_ref[rows, :]
        du_ref[rows, :] = (2.0 * (dot_nt(dq_ref[rows, :], up_q) + dot_nt(dv16, up_v))).astype(BF16)

    loop(sequences, one)
    waits[1]()
    u = u_ref[...]
    grad_ref[0:2 * rank, :] = dot_tn(du_ref[...], x_ref[...])
    up_q, up_v = dot_tn(u, dq_ref[...]), dot_tn(u, dvb_ref[...])
    grad_ref[2 * rank:3 * rank, :] = 2.0 * up_q[:rank]
    grad_ref[3 * rank:, :] = 2.0 * up_v[rank:]


def project_back(rows, own_rows, datt_ref, dq_ref, dk_ref, dv_ref, du_ref, w_ref, down):
    width = dq_ref.shape[1]
    out = datt_ref[rows, :] + dot_nn(du_ref[rows, :], down)
    out = out + dot_nt(dq_ref[rows, :], w_ref[:, :width])
    out = out + dot_nt(dk_ref[rows, :], w_ref[:, width:2 * width])
    return out + dot_nt(dv_ref[rows, :], w_ref[:, 2 * width:])


HBM, VMEM = pltpu.HBM, pltpu.VMEM


def call(kernel, name, args, outs, scratch, flops, nbytes, limit, aliases=None):
    scratch = [pltpu.SemaphoreType.DMA((s,)) if isinstance(s, int) else pltpu.VMEM(*s)
               for s in scratch]
    return pl.pallas_call(
        kernel,
        name=name,
        out_shape=tuple(space(shape, dtype) for space, shape, dtype in outs),
        in_specs=[pl.BlockSpec(memory_space=space) for space, _ in args],
        out_specs=tuple(pl.BlockSpec(memory_space=space) for space, _, _ in outs),
        scratch_shapes=scratch,
        input_output_aliases=aliases or {},
        compiler_params=pltpu.CompilerParams(vmem_limit_bytes=limit * 1024 * 1024),
        cost_estimate=pl.CostEstimate(flops=flops, bytes_accessed=nbytes, transcendentals=0),
    )(*[pltpu.with_memory_space_constraint(array, space) for space, array in args])


def sds(shape, dtype):
    return jax.ShapeDtypeStruct(shape, dtype)


def copies_of(pairs, sems):
    return [pltpu.make_async_copy(src, dst, sems.at[i]) for i, (src, dst) in enumerate(pairs)]


def start_all(copies):
    for copy in copies:
        copy.start()
    return copies


def wait_for(copies, *which):
    def wait():
        for i in which:
            copies[i].wait()

    return wait


def first_call(layer, sequences, length, x, w, a, b, vec):
    tokens, width = x.shape
    rank = a.shape[2]

    def kernel(x_hbm, w_hbm, a_hbm, b_hbm, vec_hbm, q_ref, k_ref, v_ref, send_ref, u_out, x_ref,
               w_ref, a_ref, b_ref, vec_ref, u_ref, sems, outs):
        thirds = [slice(i * width, (i + 1) * width) for i in range(3)]
        copies = start_all(copies_of(
            [(a_hbm.at[layer], a_ref), (b_hbm.at[layer], b_ref), (vec_hbm.at[layer], vec_ref),
             (x_hbm, x_ref)] + [(w_hbm.at[layer, :, part], w_ref.at[:, part]) for part in thirds],
            sems))
        store = pltpu.make_async_copy(u_ref, u_out, outs.at[0])
        project_in(sequences, length, x_ref, w_ref,
                   [wait_for(copies, 0, 1, 2, 3, 4), wait_for(copies, 5), wait_for(copies, 6)],
                   a_ref, b_ref, vec_ref, q_ref, k_ref, v_ref, u_ref, send_ref, store.start)
        store.wait()

    act, small = (VMEM, (tokens, width), BF16), ((tokens, 2 * rank), BF16)
    return call(
        kernel, "project_in", [(HBM, x), (HBM, w), (HBM, a), (HBM, b), (HBM, vec)],
        [act, act, act, (VMEM, (2, sequences * HALO, width), BF16), (HBM,) + small],
        [((tokens, width), BF16), ((width, 3 * width), BF16), ((2, rank, width), F32),
         ((2, rank, width), F32), ((8, width), BF16), small, 7, 1],
        2 * tokens * width * width * 3, 12000000, 10)


def far_call(sequences, length, q, k, v, ids):
    tokens, width = q.shape

    def kernel(q_ref, k_ref, v_ref, own_ref, live_ref, out_ref, bias_ref, *scratch):
        where = Side(False, length, (own_ref, None, live_ref))

        def one(s):
            where.biases(s, bias_ref)
            attention_forward(
                where, s, q_ref, k_ref, v_ref, out_ref,
                lambda s, sub: rows_at(s * BLOCK + sub * SUB, SUB, SUB), bias_ref, scratch)

        loop(sequences, one)

    return call(
        kernel, "attention_far", [(VMEM, item) for item in (q, k, v, ids[0])] + [(VMEM, ids[2])],
        [(VMEM, (sequences * BLOCK, width), BF16)],
        [bias_shape(False)] + attention_scratch(), 2000000000, 6000000, 8)[0]


def near_forward(near, sequences, length, far_ref, q_ref, k_ref, v_ref, halo_ref, nk_ref,
                 nv_ref, mix_ref, bias_ref, scratch):
    def one(s):
        near.biases(s, bias_ref)
        near_keys(s, length, k_ref, v_ref, halo_ref, nk_ref, nv_ref)
        mix_ref[rows_at(s * length + near.side * BLOCK, BLOCK, BLOCK), :] = far_ref[
            rows_at(s * BLOCK, BLOCK, BLOCK), :]
        attention_forward(near, s, q_ref, nk_ref, nv_ref, mix_ref, near.queries, bias_ref,
                          scratch)

    loop(sequences, one)


def middle_call(layer, sequences, length, ids, far, q, k, v, halo, h, w, a, b, wo, wu, wd, vec,
                bias_up):
    tokens, width = q.shape
    hidden, rank = wu.shape[2], a.shape[2]

    def kernel(own_ref, other_ref, live_ref, far_ref, q_ref, k_ref, v_ref, halo_ref, h_hbm, w_hbm, a_hbm,
               b_hbm, wo_hbm, wu_hbm, wd_hbm, vec_hbm, bu_hbm,
               q2_ref, k2_ref, v2_ref, send_ref,
               u_out, x_out, h_out, n1_out, r1_out, dg_out, n2_out, r2_out, q_out, k_out, v_out,
               nk_out, nv_out, mix_out,
               h_ref, w_ref, wo_ref, wu_ref, wd_ref, vec_ref, bu_ref, vec2_ref, a_ref, b_ref,
               u_ref, mix_ref, one_ref, low_ref, act_ref,
               n1_ref, r1_ref, dg_ref, n2_ref, r2_ref, nk_ref, nv_ref, ins, outs, bias_ref,
               *scratch):
        loads = start_all(copies_of(
            [(h_hbm, h_ref), (vec_hbm.at[layer], vec_ref), (wo_hbm.at[layer], wo_ref),
             (bu_hbm, bu_ref), (wu_hbm.at[layer], wu_ref), (wd_hbm.at[layer], wd_ref),
             (w_hbm.at[layer + 1], w_ref), (a_hbm.at[layer + 1], a_ref),
             (b_hbm.at[layer + 1], b_ref), (vec_hbm.at[layer + 1], vec2_ref)], ins))
        stores = copies_of(
            [(q_ref, q_out), (k_ref, k_out), (v_ref, v_out), (nk_ref, nk_out), (nv_ref, nv_out),
             (n1_ref, n1_out), (r1_ref, r1_out), (dg_ref, dg_out), (n2_ref, n2_out),
             (r2_ref, r2_out), (one_ref, h_out), (low_ref, x_out), (u_ref, u_out),
             (mix_ref, mix_out)], outs)
        near = Side(True, length, (own_ref, other_ref, live_ref))
        near_forward(near, sequences, length, far_ref, q_ref, k_ref, v_ref, halo_ref, nk_ref,
                     nv_ref, mix_ref, bias_ref, scratch)
        layer_rest(layer, sequences, length, mix_ref, h_ref, wo_ref, wu_ref, wd_ref,
                   [wait_for(loads, 0, 1, 2), wait_for(loads, 3, 4), wait_for(loads, 5)], vec_ref,
                   bu_ref, one_ref, low_ref, act_ref, n1_ref, r1_ref, dg_ref, n2_ref, r2_ref,
                   (one_ref, low_ref),
                   lambda i: start_all((stores[:7] + stores[13:], stores[7:8], stores[8:12])[i]))
        nothing = wait_for(loads)
        project_in(sequences, length, low_ref, w_ref,
                   [wait_for(loads, 6, 7, 8, 9), nothing, nothing], a_ref, b_ref, vec2_ref, q2_ref,
                   k2_ref, v2_ref, u_ref, send_ref, stores[12].start)
        for copy in stores:
            copy.wait()

    act, stat = ((tokens, width), BF16), ((tokens, 128), F32)
    wide, deep = ((tokens, width), F32), ((tokens, hidden), BF16)
    near, small = ((sequences * (WINDOW + SUB), width), BF16), ((tokens, 2 * rank), BF16)
    factors = ((2, rank, width), F32)
    return call(
        kernel, "middle",
        [(VMEM, ids[0]), (VMEM, ids[1]), (VMEM, ids[2]), (VMEM, far), (VMEM, q), (VMEM, k), (VMEM, v),
         (VMEM, halo)]
        + [(HBM, item) for item in (h, w, a, b, wo, wu, wd, vec, bias_up)],
        [(VMEM,) + act, (VMEM,) + act, (VMEM,) + act, (VMEM, (2, sequences * HALO, width), BF16)]
        + [(HBM,) + item for item in (small, act, wide, act, stat, deep, act, stat, act, act, act,
                                      near, near, act)],
        [(h.shape, h.dtype), ((width, 3 * width), BF16), ((width, width), BF16),
         ((width, hidden), BF16), ((hidden, width), BF16), ((8, width), BF16),
         (bias_up.shape, BF16), ((8, width), BF16), factors, factors, small, act, wide, act, deep,
         act, stat, deep, act, stat, near, near, 10, 14,
         bias_shape(False)] + attention_scratch(),
        2 * tokens * width * (2 * hidden + 4 * width), 24000000, 42)


def turn_call(layer, sequences, length, ids, far, q, k, v, halo, h, gradient, wo, wu, wd,
              vec, bias_up):
    tokens, width = q.shape
    hidden = wu.shape[2]

    def kernel(own_ref, other_ref, live_ref, far_ref, q_ref, k_ref, v_ref, halo_ref, h_hbm, g_hbm,
               wo_hbm, wu_hbm, wd_hbm, vec_hbm, bu_hbm,
               datt_ref, dfar_ref, dq_ref, dnk_ref, dnv_ref, dhalo_ref, delta_ref, hidden_out,
               h_ref, g_ref, wo_ref, wu_ref, wd_ref, vec_ref, bu_ref, mix_ref, one_ref, low_ref,
               act_ref, n1_ref, r1_ref, dg_ref, n2_ref, r2_ref, nk_ref, nv_ref, last_ref, ins, outs,
               bias_ref, columns_ref, *scratch):
        loads = start_all(copies_of(
            [(h_hbm, h_ref), (vec_hbm.at[layer], vec_ref), (wo_hbm.at[layer], wo_ref),
             (bu_hbm, bu_ref), (wu_hbm.at[layer], wu_ref), (wd_hbm.at[layer], wd_ref),
             (g_hbm, g_ref)], ins))
        store = pltpu.make_async_copy(last_ref, hidden_out, outs.at[0])
        near = Side(True, length, (own_ref, other_ref, live_ref))
        near_forward(near, sequences, length, far_ref, q_ref, k_ref, v_ref, halo_ref, nk_ref,
                     nv_ref, mix_ref, bias_ref, scratch)
        side = lax.axis_index("seq")
        layer_rest(layer, sequences, length, mix_ref, h_ref, wo_ref, wu_ref, wd_ref,
                   [wait_for(loads, 0, 1, 2), wait_for(loads, 3, 4), wait_for(loads, 5)], vec_ref,
                   bu_ref, one_ref, low_ref, act_ref, n1_ref, r1_ref, dg_ref, n2_ref, r2_ref,
                   (last_ref,), lambda i: None)
        store.start()

        def given(s, rows):
            places = lax.broadcasted_iota(jnp.int32, (length, 1), 0) + side * length
            return jnp.where(
                places.astype(F32) < picked(live_ref, s), g_ref[rows, :].astype(F32), 0.0)

        nothing = wait_for(loads)
        layer_rest_back(sequences, length, given,
                        [wait_for(loads, 6), nothing, nothing, nothing], n1_ref,
                        r1_ref, dg_ref, n2_ref, r2_ref, wo_ref, wu_ref, wd_ref, vec_ref, one_ref,
                        low_ref, act_ref, datt_ref)
        near_backward(near, sequences, length, q_ref, nk_ref, nv_ref, low_ref, mix_ref,
                      delta_ref, dfar_ref, dq_ref, dnk_ref, dnv_ref, dhalo_ref, columns_ref, scratch)
        store.wait()

    act, stat = ((tokens, width), BF16), ((tokens, 128), F32)
    wide, deep = ((tokens, width), F32), ((tokens, hidden), BF16)
    near_rows, ordered = sequences * (WINDOW + SUB), sequences * (length + HALO)
    near, block = ((near_rows, width), BF16), ((sequences * BLOCK, width), BF16)
    return call(
        kernel, "turn",
        [(VMEM, ids[0]), (VMEM, ids[1]), (VMEM, ids[2]), (VMEM, far), (VMEM, q), (VMEM, k),
         (VMEM, v), (VMEM, halo)]
        + [(HBM, item) for item in (h, gradient, wo, wu, wd, vec, bias_up)],
        [(VMEM,) + wide, (VMEM,) + block, (VMEM,) + block, (VMEM, (ordered, width), F32),
         (VMEM, (ordered, width), F32), (VMEM, (2, sequences * HALO, width), BF16),
         (VMEM, (HEAD_ROWS * sequences, length), F32), (HBM,) + act],
        [(h.shape, h.dtype), act, ((width, width), BF16), ((width, hidden), BF16),
         ((hidden, width), BF16), ((8, width), BF16), (bias_up.shape, BF16), act, wide, act, deep,
         act, stat, deep, act, stat, near, near, act, 7, 1, bias_shape(False),
         bias_shape(True)] + attention_scratch(True),
        4 * tokens * width * (2 * hidden + width), 24000000, 42)


def back_far_call(sequences, length, ids, q, k, v, dfar, delta, dq_near, dnk, dnv):
    tokens, width = q.shape

    def kernel(own_ref, live_ref, q_ref, k_ref, v_ref, dfar_ref, delta_ref, dqn_ref, dnk_ref,
               dnv_ref, dq_ref, dk_ref, dv_ref, bias_ref,
               *scratch):
        far = Side(False, length, (own_ref, None, live_ref))
        side = far.side

        def key_terms(s, cols, kept):
            near = rows_at(s * (length + HALO) + HALO * side, length, 32)
            for out, term, which, other in ((dv_ref, dnv_ref, 0, 3), (dk_ref, dnk_ref, 1, 2)):
                left = jnp.concatenate([item[which] for item in kept], axis=1)
                right = jnp.concatenate([item[other] for item in kept], axis=0)
                out[far.keys(s, 0), cols] = dot_nn(left, right) + term[near, cols]

        def one(s):
            far.biases(s, None, bias_ref)
            delta = delta_ref[rows_at(s * HEAD_ROWS, HEAD_ROWS, HEAD_ROWS), :]
            attention_backward(
                far, s, q_ref, k_ref, v_ref, dfar_ref,
                lambda s, sub: rows_at(s * BLOCK + sub * SUB, SUB, SUB), delta, dq_ref,
                far.queries, key_terms, bias_ref, scratch)
            dq_ref[rows_at(s * length + (1 - side) * BLOCK, BLOCK, BLOCK), :] = dqn_ref[
                rows_at(s * BLOCK, BLOCK, BLOCK), :]

        loop(sequences, one)

    wide = (VMEM, (tokens, width), F32)
    return call(
        kernel, "back_far",
        [(VMEM, ids[0]), (VMEM, ids[2])]
        + [(VMEM, item) for item in (q, k, v, dfar, delta, dq_near, dnk, dnv)],
        [(VMEM, (tokens, width), BF16), wide, wide],
        [bias_shape(True)] + attention_scratch(True), 4000000000, 16000000, 8)


def back_call(layer, sequences, length, ids, dq, dk, dv, dhalo, datt, u, x, saved, w, a, b, wo, wu,
              wd, vec):
    tokens, width = dq.shape
    hidden, rank = wu.shape[2], a.shape[2]

    def kernel(own_ref, other_ref, live_ref, dq_ref, dk_ref, dv_ref, dhalo_ref, datt_ref, u_hbm, x_hbm,
               n1_hbm, r1_hbm, dg_hbm, n2_hbm, r2_hbm, q_hbm, k_hbm, v_hbm, nk_hbm, nv_hbm, mix_hbm,
               w_hbm, a_hbm, b_hbm, wo_hbm, wu_hbm, wd_hbm, vec_hbm,
               datt_out, dfar_ref, dqn_ref, dnk_ref, dnv_ref, dhalo_out, delta_ref, q_ref, k_ref,
               v_ref, grad_out,
               u_ref, x_ref, n1_ref, r1_ref, dg_ref, n2_ref, r2_ref, nk_ref, nv_ref, w_ref,
               a_ref, b_ref, wo_ref, wu_ref, wd_ref, vec_ref, dkb_ref, dvb_ref, du_ref, grad_ref,
               two_ref, low_ref, mix_ref, ins, outs, bias_ref, *scratch):
        loads = start_all(copies_of(
            [(a_hbm.at[layer + 1], a_ref), (b_hbm.at[layer + 1], b_ref), (u_hbm, u_ref),
             (x_hbm, x_ref), (w_hbm.at[layer + 1], w_ref), (vec_hbm.at[layer], vec_ref),
             (n2_hbm, n2_ref), (r2_hbm, r2_ref), (wd_hbm.at[layer], wd_ref), (dg_hbm, dg_ref),
             (wu_hbm.at[layer], wu_ref), (n1_hbm, n1_ref), (r1_hbm, r1_ref),
             (wo_hbm.at[layer], wo_ref), (q_hbm, q_ref), (nk_hbm, nk_ref), (nv_hbm, nv_ref),
             (k_hbm, k_ref), (v_hbm, v_ref), (mix_hbm, mix_ref)], ins))
        adapter_back(sequences, length, [wait_for(loads, 0, 1), wait_for(loads, 2, 3)], dq_ref, dk_ref, dv_ref, dhalo_ref, u_ref, x_ref,
                     a_ref, b_ref, dkb_ref, dvb_ref, du_ref, grad_ref)
        store = pltpu.make_async_copy(grad_ref, grad_out, outs.at[0])
        store.start()
        down, _, _ = low_rank(a_ref, b_ref)

        wait_for(loads, 4)()
        tall = tokens // 2

        def given(s, rows):
            return two_ref[rows, :]

        def project(i):
            rows = rows_at(i * tall, tall, 128)
            two_ref[rows, :] = project_back(rows, rows, datt_ref, dq_ref, dkb_ref, dvb_ref, du_ref,
                                            w_ref, down)

        loop(2, project)
        layer_rest_back(sequences, length, given,
                        [wait_for(loads, 5, 6, 7), wait_for(loads, 8, 9), wait_for(loads, 10),
                         wait_for(loads, 11, 12, 13, 19)], n1_ref, r1_ref, dg_ref, n2_ref, r2_ref,
                        wo_ref, wu_ref, wd_ref, vec_ref, two_ref, low_ref, dg_ref, datt_out)
        wait_for(loads, 14, 15, 16)()
        near = Side(True, length, (own_ref, other_ref, live_ref))
        near_backward(near, sequences, length, q_ref, nk_ref, nv_ref, low_ref, mix_ref,
                      delta_ref, dfar_ref, dqn_ref, dnk_ref, dnv_ref, dhalo_out, bias_ref, scratch)
        wait_for(loads, 17, 18)()
        store.wait()

    act, stat = ((tokens, width), BF16), ((tokens, 128), F32)
    wide, deep = ((tokens, width), F32), ((tokens, hidden), BF16)
    near_rows, ordered = sequences * (WINDOW + SUB), sequences * (length + HALO)
    near, block = ((near_rows, width), BF16), ((sequences * BLOCK, width), BF16)
    small, factors = ((tokens, 2 * rank), BF16), ((2, rank, width), F32)
    grad = ((4 * rank, width), F32)
    return call(
        kernel, "back",
        [(VMEM, ids[0]), (VMEM, ids[1]), (VMEM, ids[2])]
        + [(VMEM, item) for item in (dq, dk, dv, dhalo, datt)]
        + [(HBM, item) for item in (u, x, *saved, w, a, b, wo, wu, wd, vec)],
        [(VMEM,) + wide, (VMEM,) + block, (VMEM,) + block,
         (VMEM, (ordered, width), F32), (VMEM, (ordered, width), F32),
         (VMEM, (2, sequences * HALO, width), BF16), (VMEM, (HEAD_ROWS * sequences, length), F32),
         (VMEM,) + act, (VMEM,) + act, (VMEM,) + act,
         (HBM,) + grad],
        [small, act, act, stat, deep, act, stat, near, near, ((width, 3 * width), BF16), factors,
         factors, ((width, width), BF16), ((width, hidden), BF16), ((hidden, width), BF16),
         ((8, width), BF16), act, act, small, grad, wide, act, act, 20, 1, bias_shape(True)]
        + attention_scratch(True),
        2 * tokens * width * (2 * hidden + 4 * width), 24000000, 38)


def last_call(layer, sequences, length, dq, dk, dv, dhalo, u, x, w, a, b, other, *state):
    tokens, width = dq.shape
    rank = a.shape[2]

    def kernel(dq_ref, dk_ref, dv_ref, dhalo_ref, u_hbm, x_hbm, w_hbm, a_hbm, b_hbm, other_hbm,
               *rest):
        given, rest = rest[:len(state)], rest[len(state):]
        (dkb_ref, dvb_ref, du_ref, w_ref, down_ref, mine_ref, theirs_ref), rest = rest[:7], rest[7:]
        taken, rest = rest[:len(state)], rest[len(state):]
        u_ref, x_ref, a_ref, b_ref, other_ref, grad_ref, sems, state_sems = rest
        loads = start_all(copies_of(
            [(a_hbm.at[layer], a_ref), (b_hbm.at[layer], b_ref), (u_hbm, u_ref), (x_hbm, x_ref),
             (other_hbm, other_ref), (w_hbm.at[layer], w_ref)], sems))
        more = start_all(copies_of(zip(given, taken), state_sems))
        adapter_back(sequences, length, [wait_for(loads, 0, 1), wait_for(loads, 2, 3)], dq_ref, dk_ref, dv_ref, dhalo_ref, u_ref, x_ref,
                     a_ref, b_ref, dkb_ref, dvb_ref, du_ref, grad_ref)
        down_ref[...] = low_rank(a_ref, b_ref)[0]
        wait_for(loads, 4)()
        first = lax.axis_index("seq") == layer
        here, there = grad_ref[...], other_ref[...]
        mine_ref[...] = jnp.where(first, here, there)
        theirs_ref[...] = jnp.where(first, there, here)
        wait_for(loads, 5)()
        for copy in more:
            copy.wait()

    act, grad = ((tokens, width), BF16), ((4 * rank, width), F32)
    small, factors = ((tokens, 2 * rank), BF16), ((2, rank, width), F32)
    return call(
        kernel, "adapter_back",
        [(VMEM, dq), (VMEM, dk), (VMEM, dv), (VMEM, dhalo)]
        + [(HBM, item) for item in (u, x, w, a, b, other, *state)],
        [(VMEM,) + act, (VMEM,) + act, (VMEM,) + small, (VMEM, (width, 3 * width), BF16),
         (VMEM, (2 * rank, width), BF16), (VMEM,) + grad, (VMEM,) + grad]
        + [(VMEM, item.shape, F32) for item in state],
        [small, act, factors, factors, grad, grad, 6, len(state)], 500000000, 12000000, 8)


def project_back_call(datt, dq, dk, dv, du, w, down):
    tokens, width = dq.shape
    parts = 2
    length = tokens // parts

    def kernel(datt_ref, dq_ref, dk_ref, dv_ref, du_ref, w_ref, down_ref, out_hbm, out_ref, sems):
        def part(i):
            rows = rows_at(i * length, length, 128)
            return pltpu.make_async_copy(out_ref.at[rows], out_hbm.at[rows], sems.at[i])

        def one(i):
            rows = rows_at(i * length, length, 128)
            out_ref[rows, :] = project_back(rows, rows, datt_ref, dq_ref, dk_ref, dv_ref, du_ref,
                                            w_ref, down_ref[...])
            part(i).start()

        loop(parts, one)
        for i in range(parts):
            part(i).wait()

    return call(
        kernel, "project_back", [(VMEM, item) for item in (datt, dq, dk, dv, du, w, down)],
        [(HBM, (tokens, width), F32)], [((tokens, width), F32), parts],
        2 * tokens * width * width * 3, 4000000, 6)[0]


def adam_call(mine, theirs, token_slots, steps, down, up, m_down, v_down, m_up, v_up):
    layers, two, rank, width = down.shape

    def kernel(mine_ref, theirs_ref, steps_ref, down_ref, up_ref, md_ref, vd_ref, mu_ref, vu_ref,
               *rest):
        outs, results, sems = rest[:6], rest[6:12], rest[12]
        down_out, up_out, md_out, vd_out, mu_out, vu_out = results
        side = lax.axis_index("seq")
        for layer in range(layers):
            for which in range(two):
                for group, (w_ref, m_ref, v_ref, w_out, m_out, v_out, rate, decay) in enumerate((
                    (down_ref, md_ref, vd_ref, down_out, md_out, vd_out, 0.03125, 0.1),
                    (up_ref, mu_ref, vu_ref, up_out, mu_out, vu_out, 0.5, 0.0),
                )):
                    rows = slice((group * two + which) * rank, (group * two + which + 1) * rank)
                    grad = jnp.where(side == layer, mine_ref[rows, :], theirs_ref[rows, :])
                    grad = grad / token_slots
                    step = picked(steps_ref, (layer * two + which) * 2 + group)
                    correction = jnp.broadcast_to(1.0 - jnp.exp2(-step), (rank, width))
                    weight = w_ref[layer, which]
                    moment = 0.5 * m_ref[layer, which] + 0.5 * grad
                    velocity = 0.5 * v_ref[layer, which] + 0.5 * grad * grad
                    size = moment / correction / (jnp.sqrt(velocity / correction) + 1e-08)
                    w_out[layer, which] = weight - rate * (size + decay * weight)
                    m_out[layer, which] = moment
                    v_out[layer, which] = velocity

        for store in start_all(copies_of(zip(results, outs), sems)):
            store.wait()

    return call(
        kernel, "adam",
        [(VMEM, mine), (VMEM, theirs), (VMEM, steps)]
        + [(VMEM, item) for item in (down, up, m_down, v_down, m_up, v_up)],
        [(HBM, down.shape, F32)] * 6, [(down.shape, F32)] * 6 + [6], 1000000, 2000000, 4)


def together(*values):
    return lax.optimization_barrier(values)


def sum_while(mine, theirs, work):
    batch = lax.axis_size("batch")
    swap = [(0, 1), (1, 0)]
    mine = mine + lax.ppermute(theirs, "seq", swap)
    done, work, step = None, list(work), 1
    while step < batch:
        ways = 4 if batch % (4 * step) == 0 else 2
        given = mine.astype(BF16)
        come = [lax.ppermute(given, "batch", [(i, i ^ (step * d)) for i in range(batch)])
                for d in range(1, ways)]
        if work and step * ways >= batch:
            done = work.pop(0)(mine, done)
            *come, done = together(*come, done)
        mine = mine + sum(item.astype(F32) for item in come)
        step *= ways
    for one in work:
        done = one(mine, done)
    return mine, lax.ppermute(mine, "seq", swap), done


def shards(
    first_layer_input,
    output_gradient,
    sentence_pair_index,
    sequence_live_length,
    optimizer_step_count,
    query_key_value_weight,
    attention_output_weight,
    feedforward_up_weight,
    feedforward_down_weight,
    layer_bias_gain_rows,
    feedforward_up_bias,
    adapter_down_factors,
    adapter_up_factors,
    first_moment_down,
    second_moment_down,
    first_moment_up,
    second_moment_up,
):
    sequences, length, width = first_layer_input.shape
    tokens = sequences * length
    swap = [(0, 1), (1, 0)]
    a, b = adapter_down_factors, jnp.swapaxes(adapter_up_factors, 2, 3)
    vec = layer_bias_gain_rows
    bias_up = feedforward_up_bias
    wqkv, wo = query_key_value_weight, attention_output_weight
    wu, wd = feedforward_up_weight, feedforward_down_weight
    ids = (sentence_pair_index, lax.ppermute(sentence_pair_index, "seq", swap),
           sequence_live_length[None, :])
    shape = (sequences, length)

    x1 = first_layer_input.reshape(tokens, width)
    q1, k1, v1, send, u1 = first_call(0, *shape, x1, wqkv, a, b, vec)
    halo = lax.ppermute(send, "seq", swap)
    far = far_call(*shape, q1, k1, v1, ids)
    q2, k2, v2, send, u2, x2, h1, *saved = middle_call(
        0, *shape, ids, far, q1, k1, v1, halo, x1, wqkv, a, b, wo, wu, wd, vec, bias_up)
    halo = lax.ppermute(send, "seq", swap)
    far = far_call(*shape, q2, k2, v2, ids)
    datt, dfar, dqn, dnk, dnv, dsend, delta, hidden_out = turn_call(
        1, *shape, ids, far, q2, k2, v2, halo, h1, output_gradient.reshape(tokens, width),
        wo, wu, wd, vec, bias_up)
    dhalo = lax.ppermute(dsend, "seq", swap)
    dq, dk, dv = back_far_call(*shape, ids, q2, k2, v2, dfar, delta, dqn, dnk, dnv)
    datt, dfar, dqn, dnk, dnv, dsend, delta, q1, k1, v1, grad2 = back_call(
        0, *shape, ids, dq, dk, dv, dhalo, datt, u2, x2, saved, wqkv, a, b, wo, wu, wd, vec)
    dhalo = lax.ppermute(dsend, "seq", swap)
    dq, dk, dv = back_far_call(*shape, ids, q1, k1, v1, dfar, delta, dqn, dnk, dnv)
    dk, dv, du, w1, down1, mine, theirs, *state = last_call(
        0, *shape, dq, dk, dv, dhalo, u1, x1, wqkv, a, b, grad2, a, b, first_moment_down,
        second_moment_down, jnp.swapaxes(first_moment_up, 2, 3),
        jnp.swapaxes(second_moment_up, 2, 3))

    def work(token, out):
        now, _ = together(datt, token)
        return project_back_call(now, dq, dk, dv, du, w1, down1)

    mine, theirs, gradient = sum_while(mine, theirs, [work])
    token_slots = tokens * lax.axis_size("seq") * lax.axis_size("batch")
    down, up, m_down, v_down, m_up, v_up = adam_call(
        mine, theirs, token_slots, optimizer_step_count.reshape(1, -1), *state)
    return (
        hidden_out.reshape(sequences, length, width),
        gradient.reshape(sequences, length, width),
        down,
        jnp.swapaxes(up, 2, 3),
        m_down,
        v_down,
        jnp.swapaxes(m_up, 2, 3),
        jnp.swapaxes(v_up, 2, 3),
    )


def solution(mesh):
    acts, whole = P("batch", "seq", None), P()
    return jax.shard_map(
        shards,
        mesh=mesh,
        in_specs=(acts, acts, P("batch", "seq"), P("batch")) + (whole,) * 13,
        out_specs=(acts, acts) + (whole,) * 6,
        check_vma=False,
    )
```
